32 devices in a mesh: dp: 4 (over y, x), ffn: 8 (over z, core).
Axes of the slice: x: 2, y: 2, z: 4, core: 2. Of those that a mesh axis runs over, the one named last changes fastest.
Arguments:
- tokens: bfloat16 [2, 8, 512, 1024], P(None, 'ffn', 'dp'), may hold values from -6 to 6
- seq_lens: int32 [2, 8], P(None, 'ffn'), may hold values from 256 to 512, as said below
- qkv_weight: bfloat16 [3, 1024, 1024], P(None, ('dp', 'ffn')), may hold values from -0.1875 to 0.1875
- out_weight: bfloat16 [1024, 1024], P(('dp', 'ffn')), may hold values from -0.1875 to 0.1875
- head_scale: float32 [16], replicated, may hold values from 0.25 to 2
- gains: bfloat16 [3, 1024], P(None, ('dp', 'ffn')), may hold values from 0.25 to 1.75
- biases: bfloat16 [7, 1024], P(None, ('dp', 'ffn')), may hold values from -3 to 3
- ffn_in: bfloat16 [1024, 4096], P('dp', 'ffn'), may hold values from -0.1875 to 0.1875
- ffn_bias: bfloat16 [4096], P('ffn'), may hold values from -3 to 3
- mid_gain: bfloat16 [4096], P('ffn'), may hold values from 0.25 to 1.75
- mid_bias: bfloat16 [4096], P('ffn'), may hold values from -3 to 3
- ffn_out: bfloat16 [4096, 1024], P('ffn', 'dp'), may hold values from -0.09375 to 0.09375
- out_cotangent: bfloat16 [2, 8, 512, 1024], P(None, 'ffn', 'dp'), may hold values from -6 to 6
Outputs:
- output: bfloat16 [2, 8, 512, 1024], P(None, 'ffn', 'dp')
- tokens_grad: float32 [2, 8, 512, 1024], P(None, 'ffn', 'dp')
- qkv_grad: float32 [3, 1024, 1024], P(None, ('dp', 'ffn'))
- out_weight_grad: float32 [1024, 1024], P(('dp', 'ffn'))
- head_scale_grad: float32 [16], replicated
- gains_grad: float32 [3, 1024], P(None, ('dp', 'ffn'))
- biases_grad: float32 [7, 1024], P(None, ('dp', 'ffn'))
- ffn_in_grad: float32 [1024, 4096], P('dp', 'ffn')
- ffn_bias_grad: float32 [4096], P('ffn')
- mid_gain_grad: float32 [4096], P('ffn')
- mid_bias_grad: float32 [4096], P('ffn')
- ffn_out_grad: float32 [4096, 1024], P('ffn', 'dp')
The draws below stay inside these ranges and needn't reach their ends.
Inputs may be any that keep to these rules, and one draw needn't show every extreme that they name: `seq_lens`: every length is a multiple of 64; in every draw some sequence fills its whole slot and some has 256 positions.
All inputs are finite; a program needn't handle non-finite values.
Results may differ from the reference program's by a relative error of at most 0.012.
Values may be sent and summed in bfloat16 or wider, within the bound.
A program may use at most 384 MiB of HBM per device.

```python
import math
import jax
import jax.numpy as jnp
from jax import lax

D = 1024
HEADS = 16
HDIM = 64
FF = 4096
MB = 2
SLOT = 512
GROUPS = 8


def draw_seq_lens(key, part):
    count = MB * GROUPS
    unit = SLOT // 8
    steps = jax.random.randint(jax.random.fold_in(key, 11), (count,), 0, 5)
    lengths = SLOT // 2 + unit * steps
    order = jax.random.permutation(jax.random.fold_in(key, 12), count)
    lengths = lengths.at[order[0]].set(SLOT)
    lengths = lengths.at[order[1]].set(SLOT // 2)
    return lengths.reshape(MB, GROUPS).astype(jnp.int32)


def block_levels(key, extent, shards, least, largest):
    loudness, own = 1.0, jax.random.fold_in(key, 6)
    for position, parts in shards:
        steps = jnp.exp(jax.random.uniform(jax.random.fold_in(own, position), (parts,), jnp.float32, least / len(shards), largest / len(shards)))
        loudness = loudness * jnp.repeat(steps, extent[position] // parts).reshape([-1 if axis == position else 1 for axis in range(len(extent))])
    return loudness


def gaussian(stream_key, extent, scale, limit, split=(), kind=jnp.bfloat16):
    values = jax.random.normal(stream_key, extent, jnp.float32) * scale
    if len(split) > 0:
        values = block_levels(stream_key, extent, split, -0.22, 0.18) * values
    return jnp.clip(values, min=-limit, max=limit).astype(kind)


def setup_inputs(seed: int = 0) -> dict:
    splits = jax.random.split(jax.random.key(seed), 14)
    tokens = gaussian(splits[0], (MB, GROUPS, SLOT, D), 1.0, 6.0, ((1, 8), (2, 4)))
    seq_lens = draw_seq_lens(jax.random.fold_in(splits[13], 71), 0)
    qkv_weight = gaussian(splits[2], (3, D, D), D ** -0.5, 0.1875, ((1, 32),))
    out_weight = gaussian(splits[3], (D, D), D ** -0.5, 0.1875, ((0, 32),))
    head_scale = jnp.clip(jnp.exp(jax.random.uniform(splits[4], (HEADS,), jnp.float32, math.log(0.25), math.log(2.0))), 0.25, 2.0)
    gains = jnp.clip(1.0 + 0.15 * jax.random.normal(splits[5], (3, D), jnp.float32), 0.25, 1.75).astype(jnp.bfloat16)
    biases = gaussian(splits[6], (7, D), 0.5, 3.0, ((1, 32),))
    ffn_in = gaussian(splits[7], (D, FF), D ** -0.5, 0.1875, ((0, 4), (1, 8)))
    ffn_bias = gaussian(splits[8], (FF,), 0.5, 3.0, ((0, 8),))
    mid_gain = jnp.clip(1.0 + 0.15 * jax.random.normal(splits[9], (FF,), jnp.float32), 0.25, 1.75).astype(jnp.bfloat16)
    mid_bias = gaussian(splits[10], (FF,), 0.5, 3.0, ((0, 8),))
    ffn_out = gaussian(splits[11], (FF, D), FF ** -0.5, 0.09375, ((0, 8), (1, 4)))
    out_cotangent = gaussian(splits[12], (MB, GROUPS, SLOT, D), 1.0, 6.0, ((1, 8), (2, 4)))
    return {"tokens": tokens, "seq_lens": seq_lens, "qkv_weight": qkv_weight, "out_weight": out_weight, "head_scale": head_scale, "gains": gains, "biases": biases, "ffn_in": ffn_in, "ffn_bias": ffn_bias, "mid_gain": mid_gain, "mid_bias": mid_bias, "ffn_out": ffn_out, "out_cotangent": out_cotangent}


EPS = 1e-05
HIGH = lax.Precision.HIGHEST

@jax.custom_vjp
def low(v):
    return lax.optimization_barrier(v.astype(jnp.bfloat16)).astype(jnp.float32)

@jax.custom_vjp
def low_back(v):
    return v

def low_keep(v):
    return (low(v), None)

def low_pass(kept, grad):
    return (grad,)

def back_keep(v):
    return (v, None)

def back_low(kept, grad):
    return (low(grad),)
low.defvjp(low_keep, low_pass)
low_back.defvjp(back_keep, back_low)

def matmul(left, right):
    return jnp.dot(left, right, precision=HIGH)

def layer_norm(values, gain, shift):
    center = values - lax.optimization_barrier(jnp.mean(values, axis=-1, keepdims=True))
    spread = lax.optimization_barrier(jnp.mean(center * center, axis=-1, keepdims=True))
    return center * lax.rsqrt(spread + EPS) * gain + shift

def attend(queries, keys, values, length):
    q_heads = queries.reshape(SLOT, HEADS, HDIM)
    k_heads = keys.reshape(SLOT, HEADS, HDIM)
    v_heads = values.reshape(SLOT, HEADS, HDIM)
    scores = jnp.einsum('qhd,khd->hqk', q_heads, k_heads, precision=HIGH) * HDIM ** (-0.5)
    scores = low_back(scores)
    where_at = jnp.arange(SLOT, dtype=jnp.int32)
    mask = (where_at[None, :] <= where_at[:, None]) & (where_at[None, :] < length)
    scores = jnp.where(mask[None], scores, -1e+30)
    probs = low(jax.nn.softmax(scores, axis=-1))
    return jnp.einsum('hqk,khd->qhd', probs, v_heads, precision=HIGH)

def layer(inputs, length, params):
    qkv_w, out_w, head_scale, gains, biases, ffn_in, ffn_bias, mid_gain, mid_bias, ffn_out = params
    normed = low(layer_norm(inputs, gains[0], biases[0]))
    queries = low(low_back(matmul(normed, qkv_w[0]) + biases[1]))
    keys = low(low_back(matmul(normed, qkv_w[1])))
    values = low(low_back(matmul(normed, qkv_w[2]) + biases[2]))
    attended = low_back(attend(queries, keys, values, length))
    joined = low((attended * head_scale[None, :, None]).reshape(SLOT, D))
    pre_norm = low_back(matmul(joined, out_w) + biases[3])
    mid_rows = inputs + layer_norm(pre_norm, gains[1], biases[4])
    second_in = low(layer_norm(mid_rows, gains[2], biases[5]))
    hidden = low_back(matmul(second_in, ffn_in) + ffn_bias)
    active = jax.nn.gelu(hidden, approximate=False)
    mean = lax.optimization_barrier(jnp.mean(active, axis=-1, keepdims=True))
    spread = lax.optimization_barrier(jnp.mean(active * active, axis=-1, keepdims=True)) - mean * mean
    mixed = low((active - mean) * lax.rsqrt(spread + EPS) * mid_gain + mid_bias)
    return mid_rows + matmul(mixed, ffn_out) + biases[6]

def reference(tokens, seq_lens, qkv_weight, out_weight, head_scale, gains, biases, ffn_in, ffn_bias, mid_gain, mid_bias, ffn_out, out_cotangent):
    params = (qkv_weight.astype(jnp.float32), out_weight.astype(jnp.float32), head_scale.astype(jnp.float32), gains.astype(jnp.float32), biases.astype(jnp.float32), ffn_in.astype(jnp.float32), ffn_bias.astype(jnp.float32), mid_gain.astype(jnp.float32), mid_bias.astype(jnp.float32), ffn_out.astype(jnp.float32))
    count = MB * GROUPS
    inputs_all = tokens.reshape(count, SLOT, D).astype(jnp.float32)
    cot_all = out_cotangent.reshape(count, SLOT, D).astype(jnp.float32)
    lengths = seq_lens.reshape(count)
    where_at = jnp.arange(SLOT, dtype=jnp.int32)

    def one(totals, item):
        inputs, cot, length = item
        result, back = jax.vjp(lambda values, weights: layer(values, length, weights), inputs, params)
        valid = (where_at < length)[:, None]
        grad_inputs, grad_params = back(jnp.where(valid, cot, jnp.zeros_like(cot)))
        summed = jax.tree.map(lambda a, b: a + b, totals, grad_params)
        return (summed, (result.astype(jnp.bfloat16), grad_inputs))
    start = jax.tree.map(jnp.zeros_like, params)
    totals, (results, input_grads) = lax.scan(one, start, (inputs_all, cot_all, lengths))
    return (results.reshape(MB, GROUPS, SLOT, D), input_grads.reshape(MB, GROUPS, SLOT, D), totals[0], totals[1], totals[2], totals[3], totals[4], totals[5], totals[6], totals[7], totals[8], totals[9])
```

```python
import jax
import jax.numpy as jnp
from jax import lax
from jax.sharding import PartitionSpec as P

HDIM = 64
EPS = 1e-05
LOW = jnp.bfloat16
F32 = jnp.float32


def layer_norm(values, gain, shift):
    center = values - jnp.mean(values, axis=-1, keepdims=True)
    spread = jnp.mean(center * center, axis=-1, keepdims=True)
    return center * lax.rsqrt(spread + EPS) * gain + shift


def dot(left, right):
    return jnp.dot(left, right, preferred_element_type=F32)


def dot_nt(left, right):
    return lax.dot_general(left, right, (((1,), (1,)), ((), ())), preferred_element_type=F32)


def dot_tn(left, right):
    return lax.dot_general(left, right, (((0,), (0,)), ((), ())), preferred_element_type=F32)


def exact_gelu(values):
    return jax.nn.gelu(values, approximate=False)


def add_up(total, term):
    return term if total is None else total + term


def on_device(
    tokens,
    seq_lens,
    qkv_weight,
    out_weight,
    head_scale,
    gains,
    biases,
    ffn_in,
    ffn_bias,
    mid_gain,
    mid_bias,
    ffn_out,
    out_cotangent,
):
    n = lax.axis_size("dp")
    nf = lax.axis_size("ffn")
    me = lax.axis_index("dp")
    batch, _, tok, width = tokens.shape
    heads = head_scale.shape[0]
    own_heads = heads // n
    cols = own_heads * HDIM
    rows = qkv_weight.shape[1]
    hid = ffn_in.shape[1]
    part = hid // n
    ff = hid * nf
    factor = HDIM ** (-0.5)

    def swap(value, i):
        return lax.ppermute(value, "dp", [(j, j ^ i) for j in range(n)])

    def by_xor(stack):
        bit = 1
        while bit < n:
            flipped = jnp.concatenate([stack[i ^ bit][None] for i in range(n)])
            stack = jnp.where((me & bit) != 0, flipped, stack)
            bit *= 2
        return stack

    def exchange(blocks):
        near = by_xor(blocks)
        got = jnp.stack([near[0]] + [swap(near[i], i) for i in range(1, n)])
        return by_xor(got)

    qkv_blocks = exchange(
        qkv_weight.reshape(3, rows, n, cols).transpose(2, 1, 0, 3).reshape(n, rows, 3 * cols)
    )
    w_qkv = lax.all_gather(qkv_blocks, "ffn", axis=1, tiled=True).reshape(width, 3 * cols)
    small = jnp.concatenate([gains, biases])
    small_all = jnp.stack([small] + [swap(small, i) for i in range(1, n)])
    small_all = by_xor(small_all).reshape(-1)
    vectors = lax.dynamic_index_in_dim(
        jnp.stack([ffn_bias, mid_gain, mid_bias]).reshape(3, n, part), me, 1, keepdims=False
    ).reshape(-1)
    count = 10 * n * rows
    flat = jnp.concatenate([small_all, vectors])
    extra = -(-flat.shape[0] // width)
    flat = jnp.pad(flat, (0, extra * width - flat.shape[0])).reshape(extra, width)
    packed = lax.all_gather(jnp.concatenate([out_weight, flat]), "ffn", axis=0)
    w_out = packed[:, :rows].reshape(nf * rows, width)
    flat_all = packed[:, rows:].reshape(nf, extra * width)
    wide = flat_all[:, :count].reshape(nf, n, 10, rows).transpose(2, 1, 0, 3).reshape(10, width)
    wide = wide.astype(F32)
    gain_rows, bias_rows = wide[:3], wide[3:]
    mids = flat_all[:, count : count + 3 * part].reshape(nf, 3, part).transpose(1, 0, 2)
    mids = mids.reshape(3, nf * part).astype(F32)
    first_bias, mid_scale, mid_shift = mids[0], mids[1], mids[2]
    own_bias = lax.dynamic_slice_in_dim(bias_rows[1:3], me * cols, cols, 1)
    ffn_blocks = jnp.stack(
        [ffn_in.T.reshape(n, part, width // n), ffn_out.reshape(n, part, width // n)], axis=1
    )
    ffn_blocks = exchange(ffn_blocks).transpose(1, 2, 0, 3).reshape(2, part, width)
    w_first = lax.all_gather(ffn_blocks[0], "ffn", axis=0, tiled=True)
    w_second = lax.all_gather(ffn_blocks[1], "ffn", axis=0, tiled=True)
    own_scale = lax.dynamic_slice_in_dim(head_scale, me * own_heads, own_heads)

    def gather(value):
        return jnp.concatenate([value] + [swap(value, i) for i in range(1, n)])

    def scatter_sum(value):
        low = value.astype(LOW)
        total = value[:tok]
        for i in range(1, n):
            total = total + swap(low[i * tok : (i + 1) * tok], i).astype(F32)
        return total

    def moment_sum(first, second):
        sums = jnp.stack([first, second]).reshape(2, n, tok)
        total = sums
        for i in range(1, n):
            other = swap(sums, i)
            total = total + jnp.stack([other[:, j ^ i] for j in range(n)], axis=1)
        total = total.reshape(2, n * tok)
        return total[0][:, None], total[1][:, None]

    slot = n * tok
    own_positions = me * tok + jnp.arange(tok, dtype=jnp.int32)
    positions = jnp.concatenate(
        [(me ^ i) * tok + jnp.arange(tok, dtype=jnp.int32) for i in range(n)]
    )
    causal = positions[None, :] <= positions[:, None]
    outputs = []
    input_grads = []
    acc = {}

    def keep(name, term):
        acc[name] = add_up(acc.get(name), term)

    for micro in range(batch):
        length = seq_lens[micro, 0]
        own_low = tokens[micro, 0]
        inputs = own_low.astype(F32)
        all_in = gather(own_low).astype(F32)
        grad_low = jnp.where(
            (own_positions < length)[:, None], out_cotangent[micro, 0], jnp.zeros((), LOW)
        )
        grad_all = gather(grad_low)
        h_low = layer_norm(all_in, gain_rows[0], bias_rows[0]).astype(LOW)
        qkv = dot(h_low, w_qkv).reshape(slot, 3, cols)
        q_low = (qkv[:, 0] + own_bias[0]).astype(LOW).reshape(slot, own_heads, HDIM)
        k_low = qkv[:, 1].astype(LOW).reshape(slot, own_heads, HDIM)
        v_low = (qkv[:, 2] + own_bias[1]).astype(LOW).reshape(slot, own_heads, HDIM)
        mask = causal & (positions[None, :] < length)
        scores = jnp.einsum("qhd,khd->hqk", q_low, k_low, preferred_element_type=F32) * factor
        scores = jnp.where(mask[None], scores, -1e30)
        top = jnp.max(scores, axis=-1, keepdims=True)
        expo = jnp.exp(scores - top)
        probs = expo / jnp.sum(expo, axis=-1, keepdims=True)
        probs_low = probs.astype(LOW)
        attended = jnp.einsum("hqk,khd->qhd", probs_low, v_low, preferred_element_type=F32)
        scale_col = own_scale[None, :, None]
        a_low = (attended * scale_col).reshape(slot, cols).astype(LOW)
        pre_norm = scatter_sum(dot(a_low, w_out)) + bias_rows[3]
        branch, post_back = jax.vjp(layer_norm, pre_norm, gain_rows[1], bias_rows[4])
        mid_rows = inputs + branch
        second_in, second_back = jax.vjp(layer_norm, mid_rows, gain_rows[2], bias_rows[5])
        rows_all = gather(second_in.astype(LOW))
        hidden = dot_nt(rows_all, w_first) + first_bias
        active = exact_gelu(hidden)
        total, squares = moment_sum(jnp.sum(active, axis=-1), jnp.sum(active * active, axis=-1))
        mean = total / ff
        inverse = lax.rsqrt(squares / ff - mean * mean + EPS)
        normed = (active - mean) * inverse
        mixed = (normed * mid_scale + mid_shift).astype(LOW)
        ffn_term = scatter_sum(dot(mixed, w_second))
        outputs.append((mid_rows + ffn_term + bias_rows[6]).astype(LOW))
        grad_mixed = dot_nt(grad_all, w_second)
        grad_normed = grad_mixed * mid_scale
        total, squares = moment_sum(
            jnp.sum(grad_normed, axis=-1), jnp.sum(grad_normed * normed, axis=-1)
        )
        grad_active = inverse * (grad_normed - total / ff - normed * (squares / ff))
        grad_hidden = jax.vjp(exact_gelu, hidden)[1](grad_active)[0].astype(LOW)
        keep(
            "mid",
            jnp.stack(
                [
                    jnp.sum(grad_hidden.astype(F32), axis=0),
                    jnp.sum(grad_mixed * normed, axis=0),
                    jnp.sum(grad_mixed, axis=0),
                ]
            ),
        )
        keep("second", dot_tn(mixed, grad_all))
        keep("first", dot_tn(grad_hidden, rows_all))
        grad_h2 = scatter_sum(dot(grad_hidden, w_first))
        dx_mid, grad_gain2, grad_shift2 = second_back(grad_h2)
        grad_out = grad_low.astype(F32)
        grad_mid = grad_out + dx_mid
        grad_pre, grad_gain1, grad_shift1 = post_back(grad_mid)
        grad_pre_low = grad_pre.astype(LOW)
        pre_all = gather(grad_pre_low)
        keep("out", dot_tn(a_low, pre_all))
        grad_att = dot_nt(pre_all, w_out).reshape(slot, own_heads, HDIM)
        keep("scale", jnp.sum(grad_att * attended, axis=(0, 2)))
        grad_heads = (grad_att * scale_col).astype(LOW)
        grad_probs = jnp.einsum("qhd,khd->hqk", grad_heads, v_low, preferred_element_type=F32)
        grad_scores = (
            probs * (grad_probs - jnp.sum(probs * grad_probs, axis=-1, keepdims=True))
        ).astype(LOW)
        grad_q = jnp.einsum("hqk,khd->qhd", grad_scores, k_low, preferred_element_type=F32)
        grad_k = jnp.einsum("hqk,qhd->khd", grad_scores, q_low, preferred_element_type=F32)
        grad_v = jnp.einsum("hqk,qhd->khd", probs_low, grad_heads, preferred_element_type=F32)
        grad_qkv = jnp.concatenate(
            [
                (grad_q * factor).reshape(slot, cols).astype(LOW),
                (grad_k * factor).reshape(slot, cols).astype(LOW),
                grad_v.reshape(slot, cols).astype(LOW),
            ],
            axis=1,
        )
        keep("qkv", dot_tn(h_low, grad_qkv))
        grad_h = scatter_sum(dot_nt(grad_qkv, w_qkv))
        first_back = jax.vjp(layer_norm, inputs, gain_rows[0], bias_rows[0])[1]
        dx_in, grad_gain0, grad_shift0 = first_back(grad_h)
        input_grads.append(grad_mid + dx_in)
        sums = jnp.sum(grad_qkv.astype(F32), axis=0)
        keep("heads", jnp.stack([sums[:cols], sums[2 * cols :]]))
        keep(
            "rows",
            jnp.stack(
                [
                    grad_gain0,
                    grad_gain1,
                    grad_gain2,
                    grad_shift0,
                    jnp.sum(grad_pre_low.astype(F32), axis=0),
                    grad_shift1,
                    grad_shift2,
                    jnp.sum(grad_out, axis=0),
                ]
            ),
        )

    def to_owner(value):
        return lax.psum_scatter(value.astype(LOW), "ffn", scatter_dimension=0, tiled=True)

    second = to_owner(acc["second"])
    first = to_owner(acc["first"])
    second = exchange(second.reshape(part, n, width // n).transpose(1, 0, 2))
    first = exchange(first.reshape(part, n, width // n).transpose(1, 0, 2))
    ffn_out_grad = second.reshape(hid, width // n).astype(F32)
    ffn_in_grad = first.reshape(hid, width // n).T.astype(F32)
    out_grad = to_owner(acc["out"])
    out_weight_grad = out_grad.astype(F32)
    qkv_grad = lax.psum_scatter(
        acc["qkv"].astype(LOW).reshape(n, nf * rows, 3 * cols),
        "ffn",
        scatter_dimension=1,
        tiled=True,
    )
    qkv_grad = exchange(qkv_grad).reshape(n, rows, 3, cols).transpose(2, 1, 0, 3)
    qkv_grad = qkv_grad.reshape(3, rows, width).astype(F32)

    head_rows = lax.dynamic_update_slice_in_dim(
        jnp.zeros((2, width), F32), acc["heads"], me * cols, 1
    )
    vec = jnp.concatenate([acc["rows"][:4], head_rows, acc["rows"][4:]])
    vec = vec.reshape(10, n, nf, rows).transpose(2, 1, 0, 3).reshape(nf, count)
    mid = acc["mid"].reshape(3, nf, part).transpose(1, 0, 2).reshape(nf, 3 * part)
    scale = jnp.broadcast_to(acc["scale"][None], (nf, own_heads))
    vec = jnp.concatenate([vec, mid, scale], axis=1)
    length = vec.shape[1]
    vec = jnp.pad(vec, ((0, 0), (0, -length % 128)))
    vec = lax.psum_scatter(vec, "ffn", scatter_dimension=0, tiled=True)
    vec = by_xor(jnp.concatenate([vec] + [swap(vec, i) for i in range(1, n)]))
    own = lax.dynamic_index_in_dim(
        vec[:, :count].reshape(n, n, 10, rows), me, 1, keepdims=False
    ).sum(axis=0)
    mid = vec[:, count : count + 3 * part].reshape(n, 3, part).transpose(1, 0, 2).reshape(3, hid)
    scale = vec[:, count + 3 * part : count + 3 * part + own_heads].reshape(heads)
    return (
        jnp.stack(outputs)[:, None],
        jnp.stack(input_grads)[:, None],
        qkv_grad,
        out_weight_grad,
        scale,
        own[:3],
        own[3:],
        ffn_in_grad,
        mid[0],
        mid[1],
        mid[2],
        ffn_out_grad,
    )


def solution(mesh):
    seqs = P(None, "ffn", "dp", None)
    wide = P(None, ("dp", "ffn"))
    hidden = P("ffn")
    return jax.shard_map(
        on_device,
        mesh=mesh,
        in_specs=(
            seqs,
            P(None, "ffn"),
            P(None, ("dp", "ffn"), None),
            P(("dp", "ffn"), None),
            P(),
            wide,
            wide,
            P("dp", "ffn"),
            hidden,
            hidden,
            hidden,
            P("ffn", "dp"),
            seqs,
        ),
        out_specs=(
            seqs,
            seqs,
            P(None, ("dp", "ffn"), None),
            P(("dp", "ffn"), None),
            P(),
            wide,
            wide,
            P("dp", "ffn"),
            hidden,
            hidden,
            hidden,
            P("ffn", "dp"),
        ),
        check_vma=False,
    )
```

```python
import jax
import jax.numpy as jnp
from jax import lax
from jax.experimental import pallas as pl
from jax.experimental.pallas import tpu as pltpu
from jax.sharding import PartitionSpec as P

HDIM = 64
EPS = 1e-05
LOW = jnp.bfloat16
F32 = jnp.float32
ANY = pl.BlockSpec(memory_space=pl.ANY)
VMEM = pl.BlockSpec(memory_space=pltpu.VMEM)
SMEM = pl.BlockSpec(memory_space=pltpu.SMEM)
MESH = pl.DeviceIdType.MESH
DMA = pltpu.SemaphoreType.DMA


def dot(left, right):
    return jnp.dot(left, right, preferred_element_type=F32)


def dot_nt(left, right):
    return lax.dot_general(left, right, (((1,), (1,)), ((), ())), preferred_element_type=F32)


def dot_tn(left, right):
    return lax.dot_general(left, right, (((0,), (0,)), ((), ())), preferred_element_type=F32)


def shape(dims, kind):
    return jax.ShapeDtypeStruct(tuple(dims), kind)


def at(start, size, unit=128):
    return pl.ds(pl.multiple_of(start, unit), size)


def send(src, dst, sems, index, where):
    return pltpu.make_async_remote_copy(
        src_ref=src,
        dst_ref=dst,
        send_sem=sems.at[(0, *index)],
        recv_sem=sems.at[(1, *index)],
        device_id=where,
        device_id_type=MESH,
    )


def greet(peers):
    barrier = pltpu.get_barrier_semaphore()
    for peer in peers:
        pl.semaphore_signal(barrier, inc=1, device_id=peer, device_id_type=MESH)


def meet(peers):
    pl.semaphore_wait(pltpu.get_barrier_semaphore(), len(peers))


def dp_peers(n, me):
    return [{"dp": me ^ i} for i in range(1, n)]


def ffn_peers(nf, f):
    return [{"ffn": f ^ (2 * j)} for j in range(1, nf // 2)] + [{"ffn": f ^ 1}]


def start(copies):
    for copy in copies:
        copy.start()


def wait(copies):
    for copy in copies:
        copy.wait()


def normal(values):
    center = values - jnp.mean(values, axis=-1, keepdims=True)
    inverse = lax.rsqrt(jnp.mean(center * center, axis=-1, keepdims=True) + EPS)
    return center * inverse, inverse


def normal_back(grad, normed, inverse):
    return inverse * (
        grad
        - jnp.mean(grad, axis=-1, keepdims=True)
        - normed * jnp.mean(grad * normed, axis=-1, keepdims=True)
    )


def column_sum(values):
    return jnp.sum(values, axis=0, keepdims=True)


def spread_kernel(
    n, nf, part, x_ref, block_ref, wout_ref, small_ref, first_ref, second_ref,
    x_all, w_all, out_stage, ffn_stage, wide_ref, mid_ref,
    stage, stage_small, small_all, d_sems, x_sems, z_sems, f_sems, own_sems,
):
    me = lax.axis_index("dp")
    f = lax.axis_index("ffn")
    nz = nf // 2
    peers = dp_peers(n, me) + ffn_peers(nf, f)
    greet(peers)
    share = first_ref.shape[2]
    place = at(me * share, share)
    own = [
        pltpu.make_async_copy(block_ref.at[me], stage.at[me], own_sems.at[0]),
        pltpu.make_async_copy(small_ref.at[0], stage_small.at[me], own_sems.at[1]),
        pltpu.make_async_copy(small_ref.at[1], stage_small.at[n], own_sems.at[2]),
        pltpu.make_async_copy(x_ref, x_all.at[me], own_sems.at[3]),
        pltpu.make_async_copy(wout_ref, out_stage.at[me], own_sems.at[4]),
        pltpu.make_async_copy(first_ref.at[me], ffn_stage.at[0, :, place], own_sems.at[5]),
        pltpu.make_async_copy(second_ref.at[me], ffn_stage.at[1, :, place], own_sems.at[6]),
    ]
    start(own)
    meet(peers)
    urgent, rest = [], []
    for i, peer in enumerate(dp_peers(n, me), 1):
        urgent.append(send(block_ref.at[me ^ i], stage.at[me], d_sems, (i, 0), peer))
        urgent.append(send(small_ref.at[0], stage_small.at[me], d_sems, (i, 1), peer))
    for i, peer in enumerate(dp_peers(n, me), 1):
        rest.append(send(x_ref, x_all.at[me], x_sems, (i, 0), peer))
    for i, peer in enumerate(dp_peers(n, me), 1):
        rest.append(send(first_ref.at[me ^ i], ffn_stage.at[0, :, place], x_sems, (i, 1), peer))
        rest.append(send(second_ref.at[me ^ i], ffn_stage.at[1, :, place], x_sems, (i, 2), peer))
        rest.append(send(wout_ref, out_stage.at[me], x_sems, (i, 3), peer))
    start(urgent + rest)
    wait(urgent + own[:3])

    def shard(index, sems, side, peer):
        pieces = [stage, stage_small] if side is None else [w_all.at[:, side], small_all.at[side]]
        side = f if side is None else side
        places = [w_all.at[:, side], small_all.at[side]]
        return [send(pieces[k], places[k], sems, (index, k), peer) for k in range(2)]

    mine = [
        pltpu.make_async_copy(stage, w_all.at[:, f], own_sems.at[0]),
        pltpu.make_async_copy(stage_small, small_all.at[f], own_sems.at[1]),
    ]
    far = [shard(j, z_sems, None, {"ffn": f ^ (2 * j)}) for j in range(1, nz)]
    near = shard(0, z_sems, None, {"ffn": f ^ 1})
    start([copy for group in far for copy in group] + near + mine)
    forwards = []
    for j in range(1, nz):
        for copy in far[j - 1]:
            copy.wait_recv()
        group = shard(j, f_sems, f ^ (2 * j), {"ffn": f ^ 1})
        start(group)
        forwards += group
    for group in far:
        for copy in group:
            copy.wait_send()
    wait(near + forwards + rest + mine + own[3:])

    def lay_out(out_ref, index, begin, size):
        together = 128 // size
        for b in range(nf // together):
            total = small_all[b * together, index].astype(F32)
            for k in range(1, together):
                total = total + small_all[b * together + k, index].astype(F32)
            out_ref[:, begin + b * 128 : begin + (b + 1) * 128] = total

    count = wout_ref.shape[0]
    for d in range(n):
        lay_out(wide_ref, d, d * nf * count, count)
    lay_out(mid_ref, n, 0, part)


def spread(x, blocks, wout, small, first, second, n, nf):
    _, rows, wide = blocks.shape
    width = wout.shape[1]
    part = first.shape[1]
    tile = small.shape[1:]
    return pl.pallas_call(
        lambda *refs: spread_kernel(n, nf, part, *refs),
        name="spread",
        out_shape=(
            shape((n, *x.shape), LOW),
            shape((n, nf, rows, wide), LOW),
            shape((n, rows, width), LOW),
            shape((2, part, width), LOW),
            shape((16, width), F32),
            shape((16, nf * part), F32),
        ),
        in_specs=[VMEM] * 6,
        out_specs=(ANY,) * 4 + (VMEM,) * 2,
        scratch_shapes=[
            pltpu.VMEM((n, rows, wide), LOW),
            pltpu.VMEM((n + 1, *tile), LOW),
            pltpu.VMEM((nf, n + 1, *tile), LOW),
            DMA((2, n, 2)),
            DMA((2, n, 4)),
            DMA((2, nf // 2, 2)),
            DMA((2, nf // 2, 2)),
            DMA((7,)),
        ],
        compiler_params=pltpu.CompilerParams(
            collective_id=0, has_side_effects=True, vmem_limit_bytes=16 << 20
        ),
    )(x, blocks, wout, small, first, second)


def attend_kernel(
    n, nf, x_all, dy_ref, w_ref, stage_ref, wide_ref, lens_ref, scale_ref,
    dy_all, out_all, h_out, qkv_out, p_out, a_own,
    h_all, qkv_all, p_all, a_all, w_sems, f_sems, y_sems, a_sems, own_sems,
):
    me = lax.axis_index("dp")
    f = lax.axis_index("ffn")
    nz = nf // 2
    batch, tok, width = dy_ref.shape
    cols = a_all.shape[3]
    pairs = cols // 128
    peers = dp_peers(n, me) + ffn_peers(nf, f)
    greet(peers)
    meet(peers)
    place = at(me * cols, cols)
    band = at(me * tok, tok)
    far = [
        send(stage_ref, out_all.at[:, f], w_sems, (j,), {"ffn": f ^ (2 * j)}) for j in range(1, nz)
    ]
    near = send(stage_ref, out_all.at[:, f], w_sems, (0,), {"ffn": f ^ 1})
    rows = [
        send(dy_ref, dy_all.at[:, band, :], y_sems, (i,), peer)
        for i, peer in enumerate(dp_peers(n, me), 1)
    ]
    own = [
        pltpu.make_async_copy(stage_ref, out_all.at[:, f], own_sems.at[0]),
        pltpu.make_async_copy(dy_ref, dy_all.at[:, band, :], own_sems.at[1]),
    ]
    start(far + [near] + own)
    gain, shift = wide_ref[0:1, :], wide_ref[3:4, :]
    bias_q, bias_v = wide_ref[4:5, place], wide_ref[5:6, place]
    left = lax.broadcasted_iota(jnp.int32, (1, 128), 1) < HDIM

    def block_copies(micro):
        return [
            send(a_all.at[micro, me ^ i], a_own.at[micro, :, place], a_sems, (micro, i), peer)
            for i, peer in enumerate(dp_peers(n, me), 1)
        ]

    def keep_copies(micro):
        return [
            pltpu.make_async_copy(source.at[micro], out.at[micro], own_sems.at[2 + 3 * micro + k])
            for k, (source, out) in enumerate(
                [(h_all, h_out), (qkv_all, qkv_out), (p_all, p_out)]
            )
        ]

    def one(micro, _):
        def norm_rows(d, _):
            values, _ = normal(x_all[d, micro].astype(F32))
            h_all[micro, at(d * tok, tok), :] = (values * gain + shift).astype(LOW)
            return 0

        lax.fori_loop(0, n, norm_rows, 0)
        for part, bias in enumerate((bias_q, None, bias_v)):
            value = dot(h_all[micro], w_ref[:, part * cols : (part + 1) * cols])
            if bias is not None:
                value = value + bias
            qkv_all[micro, :, part * cols : (part + 1) * cols] = value.astype(LOW)
        length = lens_ref[micro, 0]

        def pair_of(pair, _):
            def column(part):
                return at(part * cols + pair * 128, 128)

            head = pair * 2
            scales = jnp.where(
                left, scale_ref[me * 2 * pairs + head], scale_ref[me * 2 * pairs + head + 1]
            )
            for block in range(n):
                end = (block + 1) * tok
                q = qkv_all[micro, block * tok : end, column(0)] * HDIM ** (-0.5)
                k = qkv_all[micro, :end, column(1)]
                v = qkv_all[micro, :end, column(2)]
                key = lax.broadcasted_iota(jnp.int32, (tok, end), 1)
                query = lax.broadcasted_iota(jnp.int32, (tok, end), 0) + block * tok
                mask = (key <= query) & (key < length)
                out = []
                for side in range(2):
                    mine = left if side == 0 else jnp.logical_not(left)
                    scores = dot_nt(jnp.where(mine, q, jnp.zeros_like(q)), k)
                    scores = jnp.where(mask, scores, -1e30)
                    expo = jnp.exp(scores - jnp.max(scores, axis=-1, keepdims=True))
                    probs = expo * (1.0 / jnp.sum(expo, axis=-1, keepdims=True))
                    probs = probs.astype(LOW)
                    p_all[micro, head + side, block * tok : end, :end] = probs
                    out.append(dot(probs, v))
                joined = jnp.where(left, out[0], out[1]) * scales
                a_all[micro, block, :, at(pair * 128, 128)] = joined.astype(LOW)
            return 0

        lax.fori_loop(0, pairs, pair_of, 0)
        start(block_copies(micro))
        start(keep_copies(micro))
        a_own[micro, :, place] = a_all[micro, me]
        return 0

    lax.fori_loop(0, batch - 1, one, 0)
    start(rows)
    forwards = []
    for j in range(1, nz):
        far[j - 1].wait_recv()
        side = out_all.at[:, f ^ (2 * j)]
        forwards.append(send(side, side, f_sems, (j,), {"ffn": f ^ 1}))
    start(forwards)
    one(batch - 1, 0)
    for copy in far:
        copy.wait_send()
    for micro in range(batch):
        wait(block_copies(micro) + keep_copies(micro))
    wait(forwards + [near] + rows + own)


def attend(x_all, dy, w_qkv, stage, wide, lens, scale, nf):
    n, batch, tok, width = x_all.shape
    rows = stage.shape[1]
    cols = nf * rows
    slot = n * tok
    heads = cols // HDIM
    return pl.pallas_call(
        lambda *refs: attend_kernel(n, nf, *refs),
        name="attend",
        out_shape=(
            shape((batch, slot, width), LOW),
            shape((n, nf, rows, width), LOW),
            shape((batch, slot, width), LOW),
            shape((batch, slot, 3 * cols), LOW),
            shape((batch, heads, slot, slot), LOW),
            shape((batch, tok, width), LOW),
        ),
        in_specs=[VMEM] * 5 + [SMEM] * 2,
        out_specs=(ANY,) * 5 + (VMEM,),
        scratch_shapes=[
            pltpu.VMEM((batch, slot, width), LOW),
            pltpu.VMEM((batch, slot, 3 * cols), LOW),
            pltpu.VMEM((batch, heads, slot, slot), LOW),
            pltpu.VMEM((batch, n, tok, cols), LOW),
            DMA((2, nf // 2)),
            DMA((2, nf // 2)),
            DMA((2, n)),
            DMA((2, batch, n)),
            DMA((2 + 3 * batch,)),
        ],
        compiler_params=pltpu.CompilerParams(
            collective_id=1, has_side_effects=True, vmem_limit_bytes=40 << 20
        ),
    )(x_all, dy, w_qkv, stage, wide, lens, scale)


def feed_kernel(
    n, ff, x_ref, a_ref, wout_hbm, wide_ref, mid_ref, dy_hbm, w1_hbm, w2_hbm,
    z_out, x1_out, y_out, g1_out, g2_out, dh2_out, vec_out,
    wout, w1, w2, dy_all, h2_own, h2_all, act, slope, dmix, mixed, du, sums, sums_all,
    dh2_all, dh2_got, h_sems, s_sems, r_sems, own_sems,
):
    me = lax.axis_index("dp")
    batch, tok, width = x_ref.shape
    slot = n * tok
    hid = w1.shape[0]
    step = 256
    peers = dp_peers(n, me)
    greet(peers)
    loads = [
        pltpu.make_async_copy(source, target, own_sems.at[k])
        for k, (source, target) in enumerate(
            [(wout_hbm, wout), (dy_hbm, dy_all), (w2_hbm, w2), (w1_hbm, w1)]
        )
    ]
    start(loads)
    band = at(me * tok, tok)
    wait(loads[:1])
    for micro in range(batch):
        z = dot(a_ref[micro], wout[...]) + wide_ref[6:7, :]
        z_out[micro] = z
        values, _ = normal(z)
        x1 = x_ref[micro].astype(F32) + values * wide_ref[1:2, :] + wide_ref[7:8, :]
        x1_out[micro] = x1
        values, _ = normal(x1)
        h2_own[micro] = (values * wide_ref[2:3, :] + wide_ref[8:9, :]).astype(LOW)
    meet(peers)

    def row_copies(micro):
        return [
            send(h2_own.at[micro], h2_all.at[micro, band, :], h_sems, (micro, i), peer)
            for i, peer in enumerate(peers, 1)
        ]

    for micro in range(batch):
        start(row_copies(micro))
        h2_all[micro, band, :] = h2_own[micro]
    wait(loads[1:])

    def sum_copies(micro):
        return [
            send(sums.at[micro], sums_all.at[micro, me], s_sems, (micro, i), peer)
            for i, peer in enumerate(peers, 1)
        ]

    def grad_copies(micro):
        return [
            send(
                dh2_all.at[micro, at((me ^ i) * tok, tok), :],
                dh2_got.at[micro, i - 1],
                r_sems,
                (micro, i),
                peer,
            )
            for i, peer in enumerate(peers, 1)
        ]

    def mix_back(c, _):
        rows = at(c * step, step)
        for micro in range(batch):
            dmix[micro, :, rows] = dot_nt(dy_all[micro], w2[rows, :])
        return 0

    lax.fori_loop(0, hid // step, mix_back, 0)

    def fold(values):
        total = values[:, :128]
        for k in range(1, step // 128):
            total = total + values[:, k * 128 : (k + 1) * 128]
        return total

    def first_pass(micro, _):
        wait(row_copies(micro))

        def chunk(c, totals):
            rows = at(c * step, step)
            u = dot_nt(h2_all[micro], w1[rows, :]) + mid_ref[0:1, rows]
            phi = 0.5 + 0.5 * lax.erf(u * (0.5**0.5))
            f = u * phi
            act[micro, :, rows] = f
            slope[micro, :, rows] = phi + u * jnp.exp(u * u * -0.5) * 0.3989422804014327
            dn = dmix[micro, :, rows] * mid_ref[1:2, rows]
            return (
                totals[0] + fold(f),
                totals[1] + fold(f * f),
                totals[2] + fold(dn),
                totals[3] + fold(dn * f),
            )

        zero = jnp.zeros((slot, 128), F32)
        totals = lax.fori_loop(0, hid // step, chunk, (zero,) * 4)
        for k in range(4):
            sums[micro, k : k + 1, :] = column_sum(totals[k].T)
        sums[micro, 4:8, :] = jnp.zeros((4, slot), F32)
        start(sum_copies(micro))
        return 0

    lax.fori_loop(0, batch, first_pass, 0)
    vec_out[...] = jnp.zeros_like(vec_out)

    def second_pass(micro, _):
        wait(sum_copies(micro))
        sums_all[micro, me] = sums[micro]
        total = sums_all[micro, 0]
        for d in range(1, n):
            total = total + sums_all[micro, d]
        total = total * (1.0 / ff)
        mean = total[0:1]
        inverse = lax.rsqrt(total[1:2] - mean * mean + EPS)
        back = total[2:3]
        cross = inverse * (total[3:4] - mean * back)
        table = jnp.concatenate([mean, inverse, back, cross] * 32, axis=0).T
        mean, inverse, back, cross = [table[:, k : k + 1] for k in range(4)]

        def chunk(c, _):
            rows = at(c * step, step)
            normed = (act[micro, :, rows] - mean) * inverse
            dm = dmix[micro, :, rows]
            gain = mid_ref[1:2, rows]
            band = at(micro * slot, slot)
            mixed[band, rows] = (normed * gain + mid_ref[2:3, rows]).astype(LOW)
            df = inverse * (dm * gain - back - normed * cross)
            low = (df * slope[micro, :, rows]).astype(LOW)
            du[band, rows] = low
            vec_out[0:1, rows] += column_sum(low.astype(F32))
            vec_out[1:2, rows] += column_sum(dm * normed)
            vec_out[2:3, rows] += column_sum(dm)
            return 0

        lax.fori_loop(0, hid // step, chunk, 0)
        band = at(micro * slot, slot)

        def back_rows(c, _):
            rows = at(c * step, step)
            dh2_all[micro, :, rows] = dot(du[band, :], w1[:, rows]).astype(LOW)
            return 0

        lax.fori_loop(0, width // step, back_rows, 0)
        start(grad_copies(micro))

        def out_rows(c, _):
            rows = at(c * step, step)
            y_out[micro, :, rows] = dot(mixed[band, :], w2[:, rows]).astype(LOW)
            return 0

        lax.fori_loop(0, width // step, out_rows, 0)
        return 0

    lax.fori_loop(0, batch, second_pass, 0)

    def weight_grads(c, _):
        rows = at(c * step, step)
        h2 = h2_all[...].reshape(batch * slot, width)
        dy = dy_all[...].reshape(batch * slot, width)
        g1_out[rows, :] = dot_tn(du[:, rows], h2).astype(LOW)
        g2_out[rows, :] = dot_tn(mixed[:, rows], dy).astype(LOW)
        return 0

    lax.fori_loop(0, hid // step, weight_grads, 0)
    for micro in range(batch):
        wait(grad_copies(micro))
        total = dh2_all[micro, band, :].astype(F32)
        for i in range(1, n):
            total = total + dh2_got[micro, i - 1].astype(F32)
        dh2_out[micro] = total


def feed(x, a_own, w_out, wide, mids, dy_all, w1, w2, n, ff):
    batch, tok, width = x.shape
    slot = n * tok
    hid = w1.shape[0]

    def big(*dims):
        return pltpu.VMEM(dims, LOW)

    return pl.pallas_call(
        lambda *refs: feed_kernel(n, ff, *refs),
        name="feed",
        out_shape=(
            shape((batch, tok, width), F32),
            shape((batch, tok, width), F32),
            shape((batch, slot, width), LOW),
            shape((hid, width), LOW),
            shape((hid, width), LOW),
            shape((batch, tok, width), F32),
            shape((8, hid), F32),
        ),
        in_specs=[VMEM, VMEM, ANY, VMEM, VMEM, ANY, ANY, ANY],
        out_specs=(VMEM,) * 7,
        scratch_shapes=[
            big(*w_out.shape),
            big(hid, width),
            big(hid, width),
            big(batch, slot, width),
            big(batch, tok, width),
            big(batch, slot, width),
            pltpu.VMEM((batch, slot, hid), F32),
            pltpu.VMEM((batch, slot, hid), F32),
            pltpu.VMEM((batch, slot, hid), F32),
            big(batch * slot, hid),
            big(batch * slot, hid),
            pltpu.VMEM((batch, 8, slot), F32),
            pltpu.VMEM((batch, n, 8, slot), F32),
            big(batch, slot, width),
            big(batch, n - 1, tok, width),
            DMA((2, batch, n)),
            DMA((2, batch, n)),
            DMA((2, batch, n)),
            DMA((4,)),
        ],
        compiler_params=pltpu.CompilerParams(
            collective_id=2, has_side_effects=True, vmem_limit_bytes=58 << 20
        ),
    )(x, a_own, w_out, wide, mids, dy_all, w1, w2)


def back_kernel(
    n, x_ref, dy_ref, x1_ref, z_ref, dh2_ref, a_ref, wide_ref, lens_ref, scale_ref,
    y_hbm, wout_hbm, w_hbm, h_hbm, qkv_hbm, p_hbm,
    out_ref, dx_ref, gq_out, go_out, vec_out,
    y_all, wout, w_qkv, h_all, qkv_all, p_all, dx1, dz, do_own, do_all, ds_all, dqkv,
    dh_all, go_all, y_got, dh_got, go_got, vec, y_sems, o_sems, h_sems, g_sems, own_sems,
):
    me = lax.axis_index("dp")
    batch, tok, width = x_ref.shape
    slot = n * tok
    cols = w_qkv.shape[1] // 3
    pairs = cols // 128
    step = 256
    peers = dp_peers(n, me)
    greet(peers)
    loads = [
        pltpu.make_async_copy(source, target, own_sems.at[k])
        for k, (source, target) in enumerate(
            [(wout_hbm, wout), (y_hbm, y_all), (qkv_hbm, qkv_all), (p_hbm, p_all),
             (w_hbm, w_qkv), (h_hbm, h_all)]
        )
    ]
    start(loads)
    vec[...] = jnp.zeros_like(vec)
    band = at(me * tok, tok)
    place = at(me * cols, cols)
    for micro in range(batch):
        normed, inverse = normal(x1_ref[micro])
        grad = dh2_ref[micro]
        vec[2:3, :] += column_sum(grad * normed)
        vec[8:9, :] += column_sum(grad)
        dy = dy_ref[micro].astype(F32)
        vec[9:10, :] += column_sum(dy)
        grad = dy + normal_back(grad * wide_ref[2:3, :], normed, inverse)
        dx1[micro] = grad
        normed, inverse = normal(z_ref[micro])
        vec[1:2, :] += column_sum(grad * normed)
        vec[7:8, :] += column_sum(grad)
        low = normal_back(grad * wide_ref[1:2, :], normed, inverse).astype(LOW)
        vec[6:7, :] += column_sum(low.astype(F32))
        dz[micro * tok : (micro + 1) * tok, :] = low
    wait(loads[:1])
    heads = cols // HDIM
    for d in range(n):
        grad = dot_nt(dz[...], wout[d * cols : (d + 1) * cols, :])
        lane = lax.broadcasted_iota(jnp.int32, (1, cols), 1) // HDIM
        scales = jnp.zeros((1, cols), F32)
        for head in range(heads):
            scales = jnp.where(lane == head, scale_ref[d * heads + head], scales)
        grad = (grad * scales).astype(LOW)
        for micro in range(batch):
            do_own[micro, d] = grad[micro * tok : (micro + 1) * tok]
    meet(peers)

    def head_copies(micro):
        return [
            send(do_own.at[micro, me ^ i], do_all.at[micro, band, :], o_sems, (micro, i), peer)
            for i, peer in enumerate(peers, 1)
        ]

    def blocks(source, target, sems, size):
        return lambda micro: [
            send(
                source.at[micro, at((me ^ i) * size, size), :],
                target.at[micro, i - 1],
                sems,
                (micro, i),
                peer,
            )
            for i, peer in enumerate(peers, 1)
        ]

    out_copies = blocks(y_all, y_got, y_sems, tok)
    row_copies = blocks(dh_all, dh_got, h_sems, tok)
    weight_copies = [
        send(go_all.at[at((me ^ i) * cols, cols), :], go_got.at[i - 1], g_sems, (i,), peer)
        for i, peer in enumerate(peers, 1)
    ]
    for micro in range(batch):
        start(head_copies(micro))
        do_all[micro, band, :] = do_own[micro, me]
    wait(loads[1:2])
    for micro in range(batch):
        start(out_copies(micro))

    def out_weight(d, _):
        rows = at(d * cols, cols)
        a = a_ref[:, :, rows].reshape(batch * tok, cols)
        go_all[rows, :] = dot_tn(a, dz[...]).astype(LOW)
        return 0

    lax.fori_loop(0, n, out_weight, 0)
    start(weight_copies)
    wait(loads[2:])
    left = lax.broadcasted_iota(jnp.int32, (1, 128), 1) < HDIM

    def one(micro, _):
        wait(head_copies(micro))

        def pair_of(pair, _):
            def column(part):
                return at(part * cols + pair * 128, 128)

            head = pair * 2
            own_cols = at(pair * 128, 128)
            sums = []
            k = qkv_all[micro, :, column(1)]
            v = qkv_all[micro, :, column(2)]
            for block in range(n):
                end = (block + 1) * tok
                rows = slice(block * tok, end)
                do = do_all[micro, rows, own_cols]
                out = []
                for side in range(2):
                    mine = left if side == 0 else jnp.logical_not(left)
                    probs = p_all[micro, head + side, rows, :end].astype(F32)
                    dp = dot_nt(jnp.where(mine, do, jnp.zeros_like(do)), v[:end])
                    delta = jnp.sum(probs * dp, axis=-1, keepdims=True)
                    ds = (probs * (dp - delta)).astype(LOW)
                    ds_all[side, rows, :end] = ds
                    out.append(dot(ds, k[:end]))
                    sums.append(jnp.sum(delta, axis=0, keepdims=True))
                dq = jnp.where(left, out[0], out[1]) * HDIM ** (-0.5)
                dqkv[micro, rows, column(0)] = dq.astype(LOW)
            q = qkv_all[micro, :, column(0)]
            do = do_all[micro, :, own_cols]
            for block in range(n):
                begin = block * tok
                keys = slice(begin, begin + tok)
                dk = [dot_tn(ds_all[side, begin:, keys], q[begin:]) for side in range(2)]
                dv = [
                    dot_tn(p_all[micro, head + side, begin:, keys], do[begin:])
                    for side in range(2)
                ]
                dk = jnp.where(left, dk[0], dk[1]) * HDIM ** (-0.5)
                dqkv[micro, keys, column(1)] = dk.astype(LOW)
                dqkv[micro, keys, column(2)] = jnp.where(left, dv[0], dv[1]).astype(LOW)
            first = sums[0] + sums[2] + sums[4] + sums[6] if n == 4 else sum(sums[0::2])
            second = sums[1] + sums[3] + sums[5] + sums[7] if n == 4 else sum(sums[1::2])
            spot = me * heads + head
            first = first * (1.0 / scale_ref[spot])
            second = second * (1.0 / scale_ref[spot + 1])
            vec[10:11, at(me * cols + pair * 128, 128)] += jnp.where(left, first, second)
            return 0

        lax.fori_loop(0, pairs, pair_of, 0)
        grads = dqkv[micro].astype(F32)
        vec[4:5, place] += column_sum(grads[:, :cols])
        vec[5:6, place] += column_sum(grads[:, 2 * cols :])

        def back_rows(c, _):
            rows = at(c * step, step)
            dh_all[micro, :, rows] = dot_nt(dqkv[micro], w_qkv[rows, :]).astype(LOW)
            return 0

        lax.fori_loop(0, width // step, back_rows, 0)
        start(row_copies(micro))
        return 0

    lax.fori_loop(0, batch, one, 0)

    def weight_grads(c, _):
        rows = at(c * step, step)
        h = h_all[:, :, rows].reshape(batch * slot, step)
        gq_out[rows, :] = dot_tn(h, dqkv[...].reshape(batch * slot, 3 * cols)).astype(LOW)
        return 0

    lax.fori_loop(0, width // step, weight_grads, 0)
    wait(weight_copies)
    total = go_all[place, :].astype(F32)
    for i in range(1, n):
        total = total + go_got[i - 1].astype(F32)
    go_out[...] = total.astype(LOW)

    def gathered(source, got, micro):
        total = source[micro, band, :].astype(F32)
        for i in range(1, n):
            total = total + got[micro, i - 1].astype(F32)
        return total

    for micro in range(batch):
        wait(out_copies(micro))
        total = x1_ref[micro] + gathered(y_all, y_got, micro) + wide_ref[9:10, :]
        out_ref[micro] = total.astype(LOW)
    for micro in range(batch):
        wait(row_copies(micro))
        grad = gathered(dh_all, dh_got, micro)
        normed, inverse = normal(x_ref[micro].astype(F32))
        vec[0:1, :] += column_sum(grad * normed)
        vec[3:4, :] += column_sum(grad)
        dx_ref[micro] = dx1[micro] + normal_back(grad * wide_ref[0:1, :], normed, inverse)
    share = vec_out.shape[2]
    row = lax.broadcasted_iota(jnp.int32, (16, 1), 0)
    own_scales = vec[10:11, place]
    for d in range(n):
        block = vec[:, d * share : (d + 1) * share]
        block = jnp.where(row >= 10, 0.0, block)
        vec_out[d] = jnp.where(row == 10 + me, own_scales, block)


def back(x, dy, x1, z, dh2, a_own, wide, lens, scale, y, w_out, w_qkv, h_all, qkv_all, p_all):
    batch, tok, width = x.shape
    slot = h_all.shape[1]
    n = slot // tok
    cols = w_qkv.shape[1] // 3

    def big(*dims):
        return pltpu.VMEM(dims, LOW)

    return pl.pallas_call(
        lambda *refs: back_kernel(n, *refs),
        name="back",
        out_shape=(
            shape((batch, tok, width), LOW),
            shape((batch, tok, width), F32),
            shape((width, 3 * cols), LOW),
            shape((cols, width), LOW),
            shape((n, 16, width // n), F32),
        ),
        in_specs=[VMEM] * 7 + [SMEM] * 2 + [ANY] * 6,
        out_specs=(VMEM,) * 5,
        scratch_shapes=[
            big(*y.shape),
            big(*w_out.shape),
            big(*w_qkv.shape),
            big(*h_all.shape),
            big(*qkv_all.shape),
            big(*p_all.shape),
            pltpu.VMEM((batch, tok, width), F32),
            big(batch * tok, width),
            big(batch, n, tok, cols),
            big(batch, slot, cols),
            big(2, slot, slot),
            big(batch, slot, 3 * cols),
            big(batch, slot, width),
            big(width, width),
            big(batch, n - 1, tok, width),
            big(batch, n - 1, tok, width),
            big(n - 1, cols, width),
            pltpu.VMEM((16, width), F32),
            DMA((2, batch, n)),
            DMA((2, batch, n)),
            DMA((2, batch, n)),
            DMA((2, n)),
            DMA((6,)),
        ],
        compiler_params=pltpu.CompilerParams(
            collective_id=3, has_side_effects=True, vmem_limit_bytes=56 << 20
        ),
    )(x, dy, x1, z, dh2, a_own, wide, lens, scale, y, w_out, w_qkv, h_all, qkv_all, p_all)


def settle_kernel(
    n, nf, gq_ref, go_ref, gv_ref, vec_ref, g1_ref, g2_ref, q_out, o_out, v_out, vec_out, ffn_out,
    pair_q, pair_o, pair_v, sum_q, sum_o, sum_v, far_q, far_o, far_v, last_q,
    vec_got, vec_sum, vec_far, vec_pair, p_sems, z_sems, d_sems, e_sems, own_sems,
):
    me = lax.axis_index("dp")
    f = lax.axis_index("ffn")
    nz = nf // 2
    core = lax.rem(f, 2)
    row = lax.div(f, 2)
    cols = q_out.shape[2] // n
    part, width = g1_ref.shape
    peers = dp_peers(n, me) + ffn_peers(nf, f)
    greet(peers)
    meet(peers)
    pair = {"ffn": f ^ 1}
    pairs = [
        send(source.at[..., 1 - core, :, :], target, p_sems, (k,), pair)
        for k, (source, target) in enumerate(
            [(gq_ref, pair_q), (go_ref, pair_o), (gv_ref, pair_v)]
        )
    ]
    start(pairs)
    shares, halves = [], []
    band = at(me * part, part, 8)
    for i, peer in enumerate(dp_peers(n, me), 1):
        shares.append(send(vec_ref.at[me ^ i], vec_got.at[i - 1], e_sems, (i, 0), peer))
    for i, peer in enumerate(dp_peers(n, me), 1):
        theirs = at((me ^ i) * (width // n), width // n)
        for k, source in enumerate([g1_ref, g2_ref]):
            halves.append(
                send(source.at[:, theirs], ffn_out.at[k, me], e_sems, (i, 1 + k), peer)
            )
    start(shares)
    start(halves)
    mine = at(me * (width // n), width // n)
    own = [
        pltpu.make_async_copy(source.at[:, mine], ffn_out.at[k, me], own_sems.at[3 + k])
        for k, source in enumerate([g1_ref, g2_ref])
    ]
    start(own)
    wait(pairs)

    def add_pair(k, _):
        for d in range(n):
            total = gq_ref[d, k, core].astype(F32) + pair_q[d, k].astype(F32)
            sum_q[d, k] = total.astype(LOW)
        total = go_ref[k, core].astype(F32) + pair_o[k].astype(F32)
        sum_o[k] = total.astype(LOW)
        sum_v[k] = gv_ref[k, core] + pair_v[k]
        return 0

    lax.fori_loop(0, nz, add_pair, 0)
    wait(shares)
    total = vec_ref[me]
    for i in range(1, n):
        total = total + vec_got[i - 1]
    vec_sum[...] = total
    far = []
    for j in range(1, nz):
        peer = {"ffn": f ^ (2 * j)}
        theirs = row ^ j
        for k, (piece, place) in enumerate(
            [
                (sum_q.at[:, theirs], far_q),
                (sum_o.at[theirs], far_o),
                (sum_v.at[theirs], far_v),
                (vec_sum, vec_far),
            ]
        ):
            far.append(send(piece, place.at[j - 1], z_sems, (j, k), peer))
    start(far)
    wait(far)
    total = vec_sum[...]
    for j in range(1, nz):
        total = total + vec_far[j - 1]
    vec_out[...] = total
    vec_sum[...] = total
    last = [send(vec_sum, vec_pair, p_sems, (3,), pair)]
    for d in range(n):
        total = sum_q[d, row].astype(F32)
        for j in range(1, nz):
            total = total + far_q[j - 1, d].astype(F32)
        last_q[d] = total
    total = sum_v[row]
    for j in range(1, nz):
        total = total + far_v[j - 1]
    v_out[me] = total
    place = at(me * cols, cols)
    for i, peer in enumerate(dp_peers(n, me), 1):
        for k in range(3):
            source = last_q.at[me ^ i, :, k * cols : (k + 1) * cols]
            last.append(send(source, q_out.at[k, :, place], d_sems, (i, k), peer))
        last.append(send(v_out.at[me], v_out.at[me], d_sems, (i, 3), peer))
    own += [
        pltpu.make_async_copy(
            last_q.at[me, :, k * cols : (k + 1) * cols], q_out.at[k, :, place], own_sems.at[k]
        )
        for k in range(3)
    ]
    start(last + own[2:])
    total = sum_o[row].astype(F32)
    for j in range(1, nz):
        total = total + far_o[j - 1].astype(F32)
    o_out[...] = total
    wait(last + own + halves)
    vec_out[...] += vec_pair[...]


def settle(gq, go, gv, vec, g1, g2):
    n, nz, _, rows, wide = gq.shape
    width = go.shape[3]
    part = g1.shape[0]
    tile = gv.shape[2:]
    block = vec.shape[1:]
    return pl.pallas_call(
        lambda *refs: settle_kernel(n, 2 * nz, *refs),
        name="settle",
        out_shape=(
            shape((3, rows, width), F32),
            shape((rows, width), F32),
            shape((n, *tile), F32),
            shape(block, F32),
            shape((2, n, part, width // n), LOW),
        ),
        in_specs=[VMEM] * 6,
        out_specs=(VMEM,) * 5,
        scratch_shapes=[
            pltpu.VMEM((n, nz, rows, wide), LOW),
            pltpu.VMEM((nz, rows, width), LOW),
            pltpu.VMEM((nz, *tile), F32),
            pltpu.VMEM((n, nz, rows, wide), LOW),
            pltpu.VMEM((nz, rows, width), LOW),
            pltpu.VMEM((nz, *tile), F32),
            pltpu.VMEM((nz - 1, n, rows, wide), LOW),
            pltpu.VMEM((nz - 1, rows, width), LOW),
            pltpu.VMEM((nz - 1, *tile), F32),
            pltpu.VMEM((n, rows, wide), F32),
            pltpu.VMEM((n - 1, *block), F32),
            pltpu.VMEM(block, F32),
            pltpu.VMEM((nz - 1, *block), F32),
            pltpu.VMEM(block, F32),
            DMA((2, 4)),
            DMA((2, nz, 4)),
            DMA((2, n, 4)),
            DMA((2, n, 3)),
            DMA((5,)),
        ],
        compiler_params=pltpu.CompilerParams(
            collective_id=4, has_side_effects=True, vmem_limit_bytes=24 << 20
        ),
    )(gq, go, gv, vec, g1, g2)


def on_device(
    tokens,
    seq_lens,
    qkv_weight,
    out_weight,
    head_scale,
    gains,
    biases,
    ffn_in,
    ffn_bias,
    mid_gain,
    mid_bias,
    ffn_out,
    out_cotangent,
):
    n = lax.axis_size("dp")
    nf = lax.axis_size("ffn")
    me = lax.axis_index("dp")
    f = lax.axis_index("ffn")
    batch, _, tok, width = tokens.shape
    heads = head_scale.shape[0]
    cols = width // n
    rows = qkv_weight.shape[1]
    hid = ffn_in.shape[1]
    part = hid // n
    ff = hid * nf

    def tiled(values):
        size = values.shape[1]
        spot = lax.rem(f, 128 // size) * size
        return lax.dynamic_update_slice(jnp.zeros((16, 128), LOW), values, (0, spot))

    vectors = lax.dynamic_index_in_dim(
        jnp.stack([ffn_bias, mid_gain, mid_bias]).reshape(3, n, part), me, 1, keepdims=False
    )
    x = tokens[:, 0]
    positions = me * tok + jnp.arange(tok, dtype=jnp.int32)
    valid = positions[None, :] < seq_lens
    dy = jnp.where(valid[:, :, None], out_cotangent[:, 0], jnp.zeros((), LOW))
    x_all, w_all, out_stage, ffn_stage, wide, mids = spread(
        x,
        qkv_weight.reshape(3, rows, n, cols).transpose(2, 1, 0, 3).reshape(n, rows, 3 * cols),
        out_weight,
        jnp.stack([tiled(jnp.concatenate([gains, biases])), tiled(vectors)]),
        ffn_in.T.reshape(n, part, cols),
        ffn_out.reshape(n, part, cols),
        n,
        nf,
    )
    w1 = lax.all_gather(ffn_stage[0], "ffn", axis=0, tiled=True)
    w2 = lax.all_gather(ffn_stage[1], "ffn", axis=0, tiled=True)
    w_qkv = w_all.reshape(width, 3 * cols)
    dy_all, out_all, h_all, qkv_all, p_all, a_own = attend(
        x_all, dy, w_qkv, out_stage, wide, seq_lens, head_scale, nf
    )
    w_out = out_all.reshape(width, width)
    z, x1, y, g1, g2, dh2, mid = feed(x, a_own, w_out, wide, mids, dy_all, w1, w2, n, ff)
    g1 = lax.psum_scatter(g1, "ffn", scatter_dimension=0, tiled=True)
    g2 = lax.psum_scatter(g2, "ffn", scatter_dimension=0, tiled=True)
    output, tokens_grad, gq, go, vec = back(
        x, dy, x1, z, dh2, a_own, wide, seq_lens, head_scale, y, w_out, w_qkv, h_all, qkv_all, p_all
    )
    nz = nf // 2
    qkv_grad, out_weight_grad, mid, vec, ffn = settle(
        gq.reshape(n, nz, 2, rows, 3 * cols),
        go.reshape(nz, 2, rows, width),
        mid.reshape(8, nz, 2, part).transpose(1, 2, 0, 3),
        vec,
        g1,
        g2,
    )
    mid = mid.transpose(1, 0, 2).reshape(8, hid)
    own = lax.dynamic_slice_in_dim(vec, f * rows, rows, 1)
    ffn = ffn.reshape(2, hid, cols)
    return (
        output[:, None],
        tokens_grad[:, None],
        qkv_grad,
        out_weight_grad,
        vec[10 : 10 + n, ::HDIM].reshape(heads),
        own[:3],
        own[3:10],
        ffn[0].T.astype(F32),
        mid[0],
        mid[1],
        mid[2],
        ffn[1].astype(F32),
    )


def solution(mesh):
    seqs = P(None, "ffn", "dp", None)
    wide = P(None, ("dp", "ffn"))
    hidden = P("ffn")
    return jax.shard_map(
        on_device,
        mesh=mesh,
        in_specs=(
            seqs,
            P(None, "ffn"),
            P(None, ("dp", "ffn"), None),
            P(("dp", "ffn"), None),
            P(),
            wide,
            wide,
            P("dp", "ffn"),
            hidden,
            hidden,
            hidden,
            P("ffn", "dp"),
            seqs,
        ),
        out_specs=(
            seqs,
            seqs,
            P(None, ("dp", "ffn"), None),
            P(("dp", "ffn"), None),
            P(),
            wide,
            wide,
            P("dp", "ffn"),
            hidden,
            hidden,
            hidden,
            P("ffn", "dp"),
        ),
        check_vma=False,
    )
```

```python
import jax
import jax.numpy as jnp
from jax import lax
from jax.experimental import pallas as pl
from jax.experimental.pallas import tpu as pltpu
from jax.sharding import PartitionSpec as P

HDIM = 64
EPS = 1e-05
LOW = jnp.bfloat16
F32 = jnp.float32
ANY = pl.BlockSpec(memory_space=pl.ANY)
VMEM = pl.BlockSpec(memory_space=pltpu.VMEM)
SMEM = pl.BlockSpec(memory_space=pltpu.SMEM)
MESH = pl.DeviceIdType.MESH
DMA = pltpu.SemaphoreType.DMA


def dot(left, right):
    return jnp.dot(left, right, preferred_element_type=F32)


def dot_nt(left, right):
    return lax.dot_general(left, right, (((1,), (1,)), ((), ())), preferred_element_type=F32)


def dot_tn(left, right):
    return lax.dot_general(left, right, (((0,), (0,)), ((), ())), preferred_element_type=F32)


def shape(dims, kind):
    return jax.ShapeDtypeStruct(tuple(dims), kind)


def at(start, size, unit=128):
    return pl.ds(pl.multiple_of(start, unit), size)


def send(src, dst, sems, index, where):
    return pltpu.make_async_remote_copy(
        src_ref=src,
        dst_ref=dst,
        send_sem=sems.at[(0, *index)],
        recv_sem=sems.at[(1, *index)],
        device_id=where,
        device_id_type=MESH,
    )


def greet(peers):
    barrier = pltpu.get_barrier_semaphore()
    for peer in peers:
        pl.semaphore_signal(barrier, inc=1, device_id=peer, device_id_type=MESH)


def meet(peers):
    pl.semaphore_wait(pltpu.get_barrier_semaphore(), len(peers))


def dp_peers(n, me):
    return [{"dp": me ^ i} for i in range(1, n)]


def ffn_peers(nf, f):
    return [{"ffn": f ^ (2 * j)} for j in range(1, nf // 2)] + [{"ffn": f ^ 1}]


def start(copies):
    for copy in copies:
        copy.start()


def wait(copies):
    for copy in copies:
        copy.wait()


class Line:
    def __init__(self, nf, f, items, hop_sems, side_sems):
        self.nz, self.core, self.q, self.f = nf // 2, lax.rem(f, 2), lax.div(f, 2), f
        self.items, self.hop_sems, self.side_sems = items, hop_sems, side_sems

    def hop(self, k, t, way):
        source, place = self.items[k]
        spot = place(2 * (self.q - t * way) + self.core)
        side = 0 if way > 0 else 1
        return pltpu.make_async_remote_copy(
            src_ref=spot if source is None else source,
            dst_ref=spot,
            send_sem=self.hop_sems.at[0, side, k, t],
            recv_sem=self.hop_sems.at[1, side, k, t + 1],
            device_id={"ffn": self.f + 2 * way},
            device_id_type=MESH,
        )

    def arrival(self, k, t, way):
        spot = self.items[k][1](2 * (self.q - t * way) + self.core)
        side = 0 if way > 0 else 1
        return pltpu.make_async_remote_copy(
            src_ref=spot,
            dst_ref=spot,
            send_sem=self.hop_sems.at[0, side, k, t],
            recv_sem=self.hop_sems.at[1, side, k, t],
            device_id={"ffn": self.f + 2 * way},
            device_id_type=MESH,
        )

    def over(self, k, t, way):
        source, place = self.items[k]
        index = self.f if t is None else 2 * (self.q - t * way) + self.core
        spot = place(index)
        t = 0 if t is None else t
        side = 0 if way > 0 else 1
        return pltpu.make_async_remote_copy(
            src_ref=spot if source is None else source,
            dst_ref=spot,
            send_sem=self.side_sems.at[0, side, k, t],
            recv_sem=self.side_sems.at[1, side, k, t],
            device_id={"ffn": self.f ^ 1},
            device_id_type=MESH,
        )

    def onward(self, way):
        return self.q < self.nz - 1 if way > 0 else self.q > 0

    def has(self, t, way):
        return self.q - t >= 0 if way > 0 else self.q + t <= self.nz - 1

    def begin(self, k):
        for way in (1, -1):

            @pl.when(self.onward(way))
            def _():
                self.hop(k, 0, way).start()

        self.over(k, None, 1).start()

    def step(self, k, t):
        keep = self.items[k]
        self.items[k] = (None, keep[1])
        for way in (1, -1):

            @pl.when(self.has(t, way))
            def _():
                self.arrival(k, t, way).wait_recv()
                self.over(k, t, way).start()

            @pl.when(self.has(t, way) & self.onward(way))
            def _():
                self.hop(k, t, way).start()

        self.items[k] = keep

    def finish(self, k):
        self.over(k, None, 1).wait()
        for way in (1, -1):

            @pl.when(self.onward(way))
            def _():
                self.hop(k, 0, way).wait_send()

        keep = self.items[k]
        self.items[k] = (None, keep[1])

        def close(t, _):
            for way in (1, -1):

                @pl.when(self.has(t, way))
                def _():
                    self.over(k, t, way).wait()

                @pl.when(self.has(t, way) & self.onward(way))
                def _():
                    self.hop(k, t, way).wait_send()

            return 0

        lax.fori_loop(1, self.nz, close, 0)
        self.items[k] = keep


def line_meet(n, nf, me, f):
    barrier = pltpu.get_barrier_semaphore()
    q, nz = lax.div(f, 2), nf // 2
    greet(dp_peers(n, me) + [{"ffn": f ^ 1}])

    @pl.when(q < nz - 1)
    def _():
        greet([{"ffn": f + 2}])

    @pl.when(q > 0)
    def _():
        greet([{"ffn": f - 2}])

    count = n + jnp.where(q < nz - 1, 1, 0) + jnp.where(q > 0, 1, 0)
    pl.semaphore_wait(barrier, count)


def normal(values):
    center = values - jnp.mean(values, axis=-1, keepdims=True)
    inverse = lax.rsqrt(jnp.mean(center * center, axis=-1, keepdims=True) + EPS)
    return center * inverse, inverse


def normal_back(grad, normed, inverse):
    return inverse * (
        grad
        - jnp.mean(grad, axis=-1, keepdims=True)
        - normed * jnp.mean(grad * normed, axis=-1, keepdims=True)
    )


def column_sum(values):
    return jnp.sum(values, axis=0, keepdims=True)


def spread_kernel(
    n, nf, part, x_ref, block_ref, wout_ref, small_ref, first_ref, second_ref,
    x_all, w_all, out_stage, first_stage, w2_all, wide_ref, mid_ref,
    stage, stage_small, second_stage, small_all, d_sems, x_sems, z_sems, f_sems, own_sems,
):
    me = lax.axis_index("dp")
    f = lax.axis_index("ffn")
    nz = nf // 2
    share = first_ref.shape[2]
    place = at(me * share, share)
    own = [
        pltpu.make_async_copy(block_ref.at[me], stage.at[me], own_sems.at[0]),
        pltpu.make_async_copy(small_ref.at[0], stage_small.at[me], own_sems.at[1]),
        pltpu.make_async_copy(small_ref.at[1], stage_small.at[n], own_sems.at[2]),
        pltpu.make_async_copy(second_ref.at[me], second_stage.at[:, place], own_sems.at[3]),
        pltpu.make_async_copy(x_ref, x_all.at[me], own_sems.at[4]),
        pltpu.make_async_copy(wout_ref, out_stage.at[me], own_sems.at[5]),
        pltpu.make_async_copy(first_ref.at[me], first_stage.at[:, place], own_sems.at[6]),
    ]
    start(own)
    line_meet(n, nf, me, f)
    urgent, soon, rest = [], [], []
    for i, peer in enumerate(dp_peers(n, me), 1):
        urgent.append(send(block_ref.at[me ^ i], stage.at[me], d_sems, (i, 0), peer))
        urgent.append(send(small_ref.at[0], stage_small.at[me], d_sems, (i, 1), peer))
        soon.append(send(second_ref.at[me ^ i], second_stage.at[:, place], x_sems, (i, 2), peer))
    for i, peer in enumerate(dp_peers(n, me), 1):
        rest.append(send(x_ref, x_all.at[me], x_sems, (i, 0), peer))
    for i, peer in enumerate(dp_peers(n, me), 1):
        rest.append(send(first_ref.at[me ^ i], first_stage.at[:, place], x_sems, (i, 1), peer))
        rest.append(send(wout_ref, out_stage.at[me], x_sems, (i, 3), peer))
    start(urgent + soon + rest)
    line = Line(
        nf,
        f,
        [
            (stage, lambda index: w_all.at[:, index]),
            (stage_small, lambda index: small_all.at[index]),
            (second_stage, lambda index: w2_all.at[index]),
        ],
        z_sems,
        f_sems,
    )
    wait(urgent + own[:3])
    line.begin(0)
    line.begin(1)
    wait(soon + own[3:4])
    line.begin(2)
    mine = [
        pltpu.make_async_copy(source, place(f), own_sems.at[k])
        for k, (source, place) in enumerate(line.items)
    ]
    start(mine)

    def step(t, _):
        for k in range(3):
            line.step(k, t)
        return 0

    lax.fori_loop(1, nz, step, 0)
    for k in range(3):
        line.finish(k)
    wait(rest + mine + own[4:])

    def lay_out(out_ref, index, begin, size):
        together = 128 // size
        for b in range(nf // together):
            total = small_all[b * together, index].astype(F32)
            for k in range(1, together):
                total = total + small_all[b * together + k, index].astype(F32)
            out_ref[:, begin + b * 128 : begin + (b + 1) * 128] = total

    count = wout_ref.shape[0]
    for d in range(n):
        lay_out(wide_ref, d, d * nf * count, count)
    lay_out(mid_ref, n, 0, part)


def spread(x, blocks, wout, small, first, second, n, nf):
    _, rows, wide = blocks.shape
    width = wout.shape[1]
    part = first.shape[1]
    tile = small.shape[1:]
    return pl.pallas_call(
        lambda *refs: spread_kernel(n, nf, part, *refs),
        name="spread",
        out_shape=(
            shape((n, *x.shape), LOW),
            shape((n, nf, rows, wide), LOW),
            shape((n, rows, width), LOW),
            shape((part, width), LOW),
            shape((nf, part, width), LOW),
            shape((16, width), F32),
            shape((16, nf * part), F32),
        ),
        in_specs=[VMEM] * 6,
        out_specs=(ANY,) * 5 + (VMEM,) * 2,
        scratch_shapes=[
            pltpu.VMEM((n, rows, wide), LOW),
            pltpu.VMEM((n + 1, *tile), LOW),
            pltpu.VMEM((part, width), LOW),
            pltpu.VMEM((nf, n + 1, *tile), LOW),
            DMA((2, n, 2)),
            DMA((2, n, 4)),
            DMA((2, 2, 3, nf // 2)),
            DMA((2, 2, 3, nf // 2)),
            DMA((7,)),
        ],
        compiler_params=pltpu.CompilerParams(
            collective_id=0, has_side_effects=True, vmem_limit_bytes=16 << 20
        ),
    )(x, blocks, wout, small, first, second)


def attend_kernel(
    n, nf, x_all, dy_ref, w_ref, stage_ref, first_ref, wide_ref, lens_ref, scale_ref,
    dy_all, out_all, w1_all, h_out, qkv_out, p_out, a_own,
    h_all, qkv_all, p_all, a_all, w_sems, f_sems, y_sems, a_sems, own_sems,
):
    me = lax.axis_index("dp")
    f = lax.axis_index("ffn")
    nz = nf // 2
    batch, tok, width = dy_ref.shape
    cols = a_all.shape[3]
    pairs = cols // 128
    line_meet(n, nf, me, f)
    place = at(me * cols, cols)
    band = at(me * tok, tok)
    line = Line(
        nf,
        f,
        [
            (stage_ref, lambda index: out_all.at[:, index]),
            (first_ref, lambda index: w1_all.at[index]),
        ],
        w_sems,
        f_sems,
    )
    rows = [
        send(dy_ref, dy_all.at[:, band, :], y_sems, (i,), peer)
        for i, peer in enumerate(dp_peers(n, me), 1)
    ]
    own = [
        pltpu.make_async_copy(stage_ref, out_all.at[:, f], own_sems.at[0]),
        pltpu.make_async_copy(dy_ref, dy_all.at[:, band, :], own_sems.at[1]),
        pltpu.make_async_copy(first_ref, w1_all.at[f], own_sems.at[2]),
    ]
    line.begin(0)
    line.begin(1)
    start(rows + own)
    gain, shift = wide_ref[0:1, :], wide_ref[3:4, :]
    bias_q, bias_v = wide_ref[4:5, place], wide_ref[5:6, place]
    left = lax.broadcasted_iota(jnp.int32, (1, 128), 1) < HDIM

    def block_copies(micro):
        return [
            send(a_all.at[micro, me ^ i], a_own.at[micro, :, place], a_sems, (micro, i), peer)
            for i, peer in enumerate(dp_peers(n, me), 1)
        ]

    def keep_copies(micro):
        return [
            pltpu.make_async_copy(source.at[micro], out.at[micro], own_sems.at[3 + 3 * micro + k])
            for k, (source, out) in enumerate(
                [(h_all, h_out), (qkv_all, qkv_out), (p_all, p_out)]
            )
        ]

    def one(micro, _):
        def norm_rows(d, _):
            values, _ = normal(x_all[d, micro].astype(F32))
            h_all[micro, at(d * tok, tok), :] = (values * gain + shift).astype(LOW)
            return 0

        lax.fori_loop(0, n, norm_rows, 0)
        for part, bias in enumerate((bias_q, None, bias_v)):
            value = dot(h_all[micro], w_ref[:, part * cols : (part + 1) * cols])
            if bias is not None:
                value = value + bias
            qkv_all[micro, :, part * cols : (part + 1) * cols] = value.astype(LOW)
        length = lens_ref[micro, 0]

        def pair_of(pair, _):
            def column(part):
                return at(part * cols + pair * 128, 128)

            head = pair * 2
            scales = jnp.where(
                left, scale_ref[me * 2 * pairs + head], scale_ref[me * 2 * pairs + head + 1]
            )
            for block in range(n):
                end = (block + 1) * tok
                q = qkv_all[micro, block * tok : end, column(0)] * HDIM ** (-0.5)
                k = qkv_all[micro, :end, column(1)]
                v = qkv_all[micro, :end, column(2)]
                key = lax.broadcasted_iota(jnp.int32, (tok, end), 1)
                query = lax.broadcasted_iota(jnp.int32, (tok, end), 0) + block * tok
                mask = (key <= query) & (key < length)
                out = []
                for side in range(2):
                    mine = left if side == 0 else jnp.logical_not(left)
                    scores = dot_nt(jnp.where(mine, q, jnp.zeros_like(q)), k)
                    scores = jnp.where(mask, scores, -1e30)
                    expo = jnp.exp(scores - jnp.max(scores, axis=-1, keepdims=True))
                    probs = expo * (1.0 / jnp.sum(expo, axis=-1, keepdims=True))
                    probs = probs.astype(LOW)
                    p_all[micro, head + side, block * tok : end, :end] = probs
                    out.append(dot(probs, v))
                joined = jnp.where(left, out[0], out[1]) * scales
                a_all[micro, block, :, at(pair * 128, 128)] = joined.astype(LOW)
            return 0

        lax.fori_loop(0, pairs, pair_of, 0)
        start(block_copies(micro))
        start(keep_copies(micro))
        a_own[micro, :, place] = a_all[micro, me]
        return 0

    def step(t, _):
        line.step(0, t)
        line.step(1, t)
        return 0

    def one_and_step(micro, _):
        one(micro, 0)

        @pl.when(micro + 1 < nz)
        def _():
            step(micro + 1, 0)

        return 0

    lax.fori_loop(0, batch, one_and_step, 0)
    lax.fori_loop(batch + 1, nz, step, 0)
    for micro in range(batch):
        wait(block_copies(micro) + keep_copies(micro))
    line.finish(0)
    line.finish(1)
    wait(rows + own)


def attend(x_all, dy, w_qkv, stage, first, wide, lens, scale, nf):
    n, batch, tok, width = x_all.shape
    rows = stage.shape[1]
    cols = nf * rows
    slot = n * tok
    heads = cols // HDIM
    return pl.pallas_call(
        lambda *refs: attend_kernel(n, nf, *refs),
        name="attend",
        out_shape=(
            shape((batch, slot, width), LOW),
            shape((n, nf, rows, width), LOW),
            shape((nf, *first.shape), LOW),
            shape((batch, slot, width), LOW),
            shape((batch, slot, 3 * cols), LOW),
            shape((batch, heads, slot, slot), LOW),
            shape((batch, tok, width), LOW),
        ),
        in_specs=[VMEM] * 6 + [SMEM] * 2,
        out_specs=(ANY,) * 6 + (VMEM,),
        scratch_shapes=[
            pltpu.VMEM((batch, slot, width), LOW),
            pltpu.VMEM((batch, slot, 3 * cols), LOW),
            pltpu.VMEM((batch, heads, slot, slot), LOW),
            pltpu.VMEM((batch, n, tok, cols), LOW),
            DMA((2, 2, 2, nf // 2)),
            DMA((2, 2, 2, nf // 2)),
            DMA((2, n)),
            DMA((2, batch, n)),
            DMA((3 + 3 * batch,)),
        ],
        compiler_params=pltpu.CompilerParams(
            collective_id=1, has_side_effects=True, vmem_limit_bytes=40 << 20
        ),
    )(x_all, dy, w_qkv, stage, first, wide, lens, scale)


def feed_kernel(
    n, ff, x_ref, a_ref, wide_ref, mid_ref, lens_ref, wout_hbm, dy_hbm, w1_hbm, w2_hbm,
    z_hbm, x1_hbm, y_hbm, g_hbm, dh2_out, vec_out,
    wout, w1, w2, dy_all, z_out, x1_out, h2_own, h2_all, act, slope, dmix, mixed, du, sums,
    sums_all, dh2_all, dh2_got, y_out, grads, pair_got, h_sems, s_sems, r_sems, p_sems, own_sems,
):
    me = lax.axis_index("dp")
    f = lax.axis_index("ffn")
    core = lax.rem(f, 2)
    part = grads.shape[2]
    batch, tok, width = x_ref.shape
    slot = n * tok
    hid = w1.shape[0]
    step = 256
    peers = dp_peers(n, me)
    pair = {"ffn": f ^ 1}
    greet(peers + [pair])
    loads = [
        pltpu.make_async_copy(source, target, own_sems.at[k])
        for k, (source, target) in enumerate(
            [(wout_hbm, wout), (dy_hbm, dy_all), (w2_hbm, w2), (w1_hbm, w1)]
        )
    ]
    start(loads)
    band = at(me * tok, tok)
    wait(loads[:1])
    for micro in range(batch):
        z = dot(a_ref[micro], wout[...]) + wide_ref[6:7, :]
        z_out[micro] = z
        values, _ = normal(z)
        x1 = x_ref[micro].astype(F32) + values * wide_ref[1:2, :] + wide_ref[7:8, :]
        x1_out[micro] = x1
        values, _ = normal(x1)
        h2_own[micro] = (values * wide_ref[2:3, :] + wide_ref[8:9, :]).astype(LOW)
    meet(peers + [pair])
    kept = [
        pltpu.make_async_copy(z_out, z_hbm, own_sems.at[4]),
        pltpu.make_async_copy(x1_out, x1_hbm, own_sems.at[5]),
    ]

    def row_copies(micro):
        return [
            send(h2_own.at[micro], h2_all.at[micro, band, :], h_sems, (micro, i), peer)
            for i, peer in enumerate(peers, 1)
        ]

    for micro in range(batch):
        start(row_copies(micro))
        h2_all[micro, band, :] = h2_own[micro]
    start(kept)
    wait(loads[1:])
    for micro in range(batch):
        valid = lax.broadcasted_iota(jnp.int32, (slot, 1), 0) < lens_ref[micro, 0]
        rows = dy_all[micro]
        dy_all[micro] = jnp.where(valid, rows, jnp.zeros_like(rows))

    def sum_copies(micro):
        return [
            send(sums.at[micro], sums_all.at[micro, me], s_sems, (micro, i), peer)
            for i, peer in enumerate(peers, 1)
        ]

    def grad_copies(micro):
        return [
            send(
                dh2_all.at[micro, at((me ^ i) * tok, tok), :],
                dh2_got.at[micro, i - 1],
                r_sems,
                (micro, i),
                peer,
            )
            for i, peer in enumerate(peers, 1)
        ]

    def mix_back(c, _):
        rows = at(c * step, step)
        for micro in range(batch):
            dmix[micro, :, rows] = dot_nt(dy_all[micro], w2[rows, :])
        return 0

    lax.fori_loop(0, hid // step, mix_back, 0)

    def fold(values):
        total = values[:, :128]
        for k in range(1, step // 128):
            total = total + values[:, k * 128 : (k + 1) * 128]
        return total

    def first_pass(micro, _):
        wait(row_copies(micro))

        def chunk(c, totals):
            rows = at(c * step, step)
            u = dot_nt(h2_all[micro], w1[rows, :]) + mid_ref[0:1, rows]
            phi = 0.5 + 0.5 * lax.erf(u * (0.5**0.5))
            f = u * phi
            act[micro, :, rows] = f
            slope[micro, :, rows] = phi + u * jnp.exp(u * u * -0.5) * 0.3989422804014327
            dn = dmix[micro, :, rows] * mid_ref[1:2, rows]
            return (
                totals[0] + fold(f),
                totals[1] + fold(f * f),
                totals[2] + fold(dn),
                totals[3] + fold(dn * f),
            )

        zero = jnp.zeros((slot, 128), F32)
        totals = lax.fori_loop(0, hid // step, chunk, (zero,) * 4)
        for k in range(4):
            sums[micro, k : k + 1, :] = column_sum(totals[k].T)
        sums[micro, 4:8, :] = jnp.zeros((4, slot), F32)
        start(sum_copies(micro))
        return 0

    lax.fori_loop(0, batch, first_pass, 0)
    vec_out[...] = jnp.zeros_like(vec_out)

    def second_pass(micro, _):
        wait(sum_copies(micro))
        sums_all[micro, me] = sums[micro]
        total = sums_all[micro, 0]
        for d in range(1, n):
            total = total + sums_all[micro, d]
        total = total * (1.0 / ff)
        mean = total[0:1]
        inverse = lax.rsqrt(total[1:2] - mean * mean + EPS)
        back = total[2:3]
        cross = inverse * (total[3:4] - mean * back)
        table = jnp.concatenate([mean, inverse, back, cross] * 32, axis=0).T
        mean, inverse, back, cross = [table[:, k : k + 1] for k in range(4)]

        def chunk(c, _):
            rows = at(c * step, step)
            normed = (act[micro, :, rows] - mean) * inverse
            dm = dmix[micro, :, rows]
            gain = mid_ref[1:2, rows]
            band = at(micro * slot, slot)
            mixed[band, rows] = (normed * gain + mid_ref[2:3, rows]).astype(LOW)
            df = inverse * (dm * gain - back - normed * cross)
            low = (df * slope[micro, :, rows]).astype(LOW)
            du[band, rows] = low
            vec_out[0:1, rows] += column_sum(low.astype(F32))
            vec_out[1:2, rows] += column_sum(dm * normed)
            vec_out[2:3, rows] += column_sum(dm)
            return 0

        lax.fori_loop(0, hid // step, chunk, 0)
        band = at(micro * slot, slot)

        def back_rows(c, _):
            rows = at(c * step, step)
            dh2_all[micro, :, rows] = dot(du[band, :], w1[:, rows]).astype(LOW)
            return 0

        lax.fori_loop(0, width // step, back_rows, 0)
        start(grad_copies(micro))
        return 0

    lax.fori_loop(0, batch, second_pass, 0)
    each = step // part // 2

    def pair_copies(c):
        copies = []
        for k in range(each):
            index = c * (2 * each) + 2 * k
            for w in range(2):
                copies.append(
                    send(
                        grads.at[w, index + 1 - core],
                        pair_got.at[w, c * each + k],
                        p_sems,
                        (c, k, w),
                        pair,
                    )
                )
        return copies

    def weight_grads(c, _):
        rows = at(c * step, step)
        h2 = h2_all[...].reshape(batch * slot, width)
        dy = dy_all[...].reshape(batch * slot, width)
        first = dot_tn(du[:, rows], h2).astype(LOW)
        second = dot_tn(mixed[:, rows], dy).astype(LOW)
        for k in range(step // part):
            grads[0, c * (step // part) + k] = first[k * part : (k + 1) * part]
            grads[1, c * (step // part) + k] = second[k * part : (k + 1) * part]
        start(pair_copies(c))
        return 0

    lax.fori_loop(0, hid // step, weight_grads, 0)

    def out_rows(c, _):
        rows = at(c * step, step)
        for micro in range(batch):
            band = at(micro * slot, slot)
            y_out[micro, :, rows] = dot(mixed[band, :], w2[:, rows]).astype(LOW)
        return 0

    lax.fori_loop(0, width // step, out_rows, 0)
    y_copy = pltpu.make_async_copy(y_out, y_hbm, own_sems.at[6])
    y_copy.start()

    def pair_sum(c, _):
        wait(pair_copies(c))
        for k in range(each):
            for w in range(2):
                total = grads[w, c * (2 * each) + 2 * k + core].astype(F32)
                total = total + pair_got[w, c * each + k].astype(F32)
                pair_got[w, c * each + k] = total.astype(LOW)
        return 0

    lax.fori_loop(0, hid // step, pair_sum, 0)
    g_copy = pltpu.make_async_copy(pair_got, g_hbm, own_sems.at[7])
    g_copy.start()
    for micro in range(batch):
        wait(grad_copies(micro))
        total = dh2_all[micro, band, :].astype(F32)
        for i in range(1, n):
            total = total + dh2_got[micro, i - 1].astype(F32)
        dh2_out[micro] = total
    wait(kept + [y_copy, g_copy])


def feed(x, a_own, wide, mids, lens, w_out, dy_all, w1, w2, n, ff, part):
    batch, tok, width = x.shape
    slot = n * tok
    hid = w1.shape[0]
    nf = hid // part

    def big(*dims):
        return pltpu.VMEM(dims, LOW)

    return pl.pallas_call(
        lambda *refs: feed_kernel(n, ff, *refs),
        name="feed",
        out_shape=(
            shape((batch, tok, width), F32),
            shape((batch, tok, width), F32),
            shape((batch, slot, width), LOW),
            shape((2, nf // 2, part, width), LOW),
            shape((batch, tok, width), F32),
            shape((8, hid), F32),
        ),
        in_specs=[VMEM] * 4 + [SMEM] + [ANY] * 4,
        out_specs=(ANY,) * 4 + (VMEM,) * 2,
        scratch_shapes=[
            big(*w_out.shape),
            big(hid, width),
            big(hid, width),
            big(batch, slot, width),
            pltpu.VMEM((batch, tok, width), F32),
            pltpu.VMEM((batch, tok, width), F32),
            big(batch, tok, width),
            big(batch, slot, width),
            pltpu.VMEM((batch, slot, hid), F32),
            pltpu.VMEM((batch, slot, hid), F32),
            pltpu.VMEM((batch, slot, hid), F32),
            big(batch * slot, hid),
            big(batch * slot, hid),
            pltpu.VMEM((batch, 8, slot), F32),
            pltpu.VMEM((batch, n, 8, slot), F32),
            big(batch, slot, width),
            big(batch, n - 1, tok, width),
            big(batch, slot, width),
            big(2, nf, part, width),
            big(2, nf // 2, part, width),
            DMA((2, batch, n)),
            DMA((2, batch, n)),
            DMA((2, batch, n)),
            DMA((2, hid // 256, 128 // part, 2)),
            DMA((8,)),
        ],
        compiler_params=pltpu.CompilerParams(
            collective_id=2, has_side_effects=True, vmem_limit_bytes=58 << 20
        ),
    )(x, a_own, wide, mids, lens, w_out, dy_all, w1, w2)


def back_kernel(
    n, nf, x_hbm, dy_hbm, x1_hbm, z_hbm, dh2_hbm, a_hbm, wide_ref, lens_ref, scale_ref,
    g_hbm, wout_hbm, w_hbm, h_hbm, qkv_hbm, p_hbm,
    dx_ref, gq_out, go_out, vec_out, g_out,
    x_ref, dy_ref, x1_ref, z_ref, dh2_ref, a_ref,
    wout, w_qkv, h_all, qkv_all, p_all, dx1, dz, do_own, do_all, ds_all, dqkv,
    dh_all, go_all, go_pair, go_got, go_half, dh_got, g_own, g_got, vec,
    o_sems, h_sems, g_sems, p_sems, z_sems, own_sems,
):
    me = lax.axis_index("dp")
    f = lax.axis_index("ffn")
    core, q_me = lax.rem(f, 2), lax.div(f, 2)
    nz = nf // 2
    batch, tok, width = x_ref.shape
    slot = n * tok
    cols = w_qkv.shape[1] // 3
    half = cols // 2
    pairs = cols // 128
    step = 256
    peers = dp_peers(n, me)
    pair = {"ffn": f ^ 1}
    everyone = peers + ffn_peers(nf, f)
    greet(everyone)
    loads = [
        pltpu.make_async_copy(source, target, own_sems.at[k])
        for k, (source, target) in enumerate(
            [(x1_hbm, x1_ref), (dh2_hbm, dh2_ref), (dy_hbm, dy_ref), (z_hbm, z_ref),
             (wout_hbm, wout), (a_hbm, a_ref), (qkv_hbm, qkv_all), (p_hbm, p_all),
             (w_hbm, w_qkv), (h_hbm, h_all), (x_hbm, x_ref), (g_hbm.at[:, q_me], g_own)]
        )
    ]
    start(loads)
    vec[...] = jnp.zeros_like(vec)
    band = at(me * tok, tok)
    place = at(me * cols, cols)
    wait(loads[:4])
    for micro in range(batch):
        normed, inverse = normal(x1_ref[micro])
        grad = dh2_ref[micro]
        vec[2:3, :] += column_sum(grad * normed)
        vec[8:9, :] += column_sum(grad)
        valid = lax.broadcasted_iota(jnp.int32, (tok, 1), 0) + me * tok < lens_ref[micro, 0]
        dy = jnp.where(valid, dy_ref[micro].astype(F32), 0.0)
        vec[9:10, :] += column_sum(dy)
        grad = dy + normal_back(grad * wide_ref[2:3, :], normed, inverse)
        dx1[micro] = grad
        normed, inverse = normal(z_ref[micro])
        vec[1:2, :] += column_sum(grad * normed)
        vec[7:8, :] += column_sum(grad)
        low = normal_back(grad * wide_ref[1:2, :], normed, inverse).astype(LOW)
        vec[6:7, :] += column_sum(low.astype(F32))
        dz[micro * tok : (micro + 1) * tok, :] = low
    wait(loads[4:5])
    heads = cols // HDIM
    for d in range(n):
        grad = dot_nt(dz[...], wout[d * cols : (d + 1) * cols, :])
        lane = lax.broadcasted_iota(jnp.int32, (1, cols), 1) // HDIM
        scales = jnp.zeros((1, cols), F32)
        for head in range(heads):
            scales = jnp.where(lane == head, scale_ref[d * heads + head], scales)
        grad = (grad * scales).astype(LOW)
        for micro in range(batch):
            do_own[micro, d] = grad[micro * tok : (micro + 1) * tok]
    meet(everyone)

    def head_copies(micro):
        return [
            send(do_own.at[micro, me ^ i], do_all.at[micro, band, :], o_sems, (micro, i), peer)
            for i, peer in enumerate(peers, 1)
        ]

    def row_copies(micro):
        return [
            send(
                dh_all.at[micro, at((me ^ i) * tok, tok), :],
                dh_got.at[micro, i - 1],
                h_sems,
                (micro, i),
                peer,
            )
            for i, peer in enumerate(peers, 1)
        ]

    pair_copy = send(go_all.at[:, 1 - core], go_pair, p_sems, (0,), pair)
    weight_copies = [
        send(go_half.at[me ^ i], go_got.at[i - 1], g_sems, (i,), peer)
        for i, peer in enumerate(peers, 1)
    ]
    last_copy = send(go_out.at[core], go_out.at[core], p_sems, (1,), pair)
    ffn_copies = [
        send(g_hbm.at[:, q_me ^ j], g_got.at[j - 1], z_sems, (j,), {"ffn": f ^ (2 * j)})
        for j in range(1, nz)
    ]
    for micro in range(batch):
        start(head_copies(micro))
        do_all[micro, band, :] = do_own[micro, me]
    start(ffn_copies)
    wait(loads[5:6])

    def out_weight(d, _):
        a = a_ref[:, :, at(d * cols, cols)].reshape(batch * tok, cols)
        grad = dot_tn(a, dz[...]).astype(LOW)
        go_all[d, 0] = grad[:half]
        go_all[d, 1] = grad[half:]
        return 0

    lax.fori_loop(0, n, out_weight, 0)
    pair_copy.start()
    wait(loads[6:])
    left = lax.broadcasted_iota(jnp.int32, (1, 128), 1) < HDIM

    def one(micro, _):
        wait(head_copies(micro))

        def pair_of(pair, _):
            def column(part):
                return at(part * cols + pair * 128, 128)

            head = pair * 2
            own_cols = at(pair * 128, 128)
            sums = []
            k = qkv_all[micro, :, column(1)]
            v = qkv_all[micro, :, column(2)]
            for block in range(n):
                end = (block + 1) * tok
                rows = slice(block * tok, end)
                do = do_all[micro, rows, own_cols]
                out = []
                for side in range(2):
                    mine = left if side == 0 else jnp.logical_not(left)
                    probs = p_all[micro, head + side, rows, :end].astype(F32)
                    dp = dot_nt(jnp.where(mine, do, jnp.zeros_like(do)), v[:end])
                    delta = jnp.sum(probs * dp, axis=-1, keepdims=True)
                    ds = (probs * (dp - delta)).astype(LOW)
                    ds_all[side, rows, :end] = ds
                    out.append(dot(ds, k[:end]))
                    sums.append(jnp.sum(delta, axis=0, keepdims=True))
                dq = jnp.where(left, out[0], out[1]) * HDIM ** (-0.5)
                dqkv[micro, rows, column(0)] = dq.astype(LOW)
            q = qkv_all[micro, :, column(0)]
            do = do_all[micro, :, own_cols]
            for block in range(n):
                begin = block * tok
                keys = slice(begin, begin + tok)
                dk = [dot_tn(ds_all[side, begin:, keys], q[begin:]) for side in range(2)]
                dv = [
                    dot_tn(p_all[micro, head + side, begin:, keys], do[begin:])
                    for side in range(2)
                ]
                dk = jnp.where(left, dk[0], dk[1]) * HDIM ** (-0.5)
                dqkv[micro, keys, column(1)] = dk.astype(LOW)
                dqkv[micro, keys, column(2)] = jnp.where(left, dv[0], dv[1]).astype(LOW)
            first = sums[0] + sums[2] + sums[4] + sums[6] if n == 4 else sum(sums[0::2])
            second = sums[1] + sums[3] + sums[5] + sums[7] if n == 4 else sum(sums[1::2])
            spot = me * heads + head
            first = first * (1.0 / scale_ref[spot])
            second = second * (1.0 / scale_ref[spot + 1])
            vec[10:11, at(me * cols + pair * 128, 128)] += jnp.where(left, first, second)
            return 0

        lax.fori_loop(0, pairs, pair_of, 0)
        grads = dqkv[micro].astype(F32)
        vec[4:5, place] += column_sum(grads[:, :cols])
        vec[5:6, place] += column_sum(grads[:, 2 * cols :])

        def back_rows(c, _):
            rows = at(c * step, step)
            dh_all[micro, :, rows] = dot_nt(dqkv[micro], w_qkv[rows, :]).astype(LOW)
            return 0

        lax.fori_loop(0, width // step, back_rows, 0)
        start(row_copies(micro))

        @pl.when(micro == 0)
        def _():
            pair_copy.wait()
            for d in range(n):
                total = go_all[d, core].astype(F32) + go_pair[d].astype(F32)
                go_half[d] = total.astype(LOW)
            start(weight_copies)

        return 0

    lax.fori_loop(0, batch, one, 0)

    def weight_grads(c, _):
        rows = at(c * step, step)
        h = h_all[:, :, rows].reshape(batch * slot, step)
        gq_out[rows, :] = dot_tn(h, dqkv[...].reshape(batch * slot, 3 * cols)).astype(LOW)
        return 0

    lax.fori_loop(0, width // step, weight_grads, 0)
    wait(weight_copies)
    total = go_half[me].astype(F32)
    for i in range(1, n):
        total = total + go_got[i - 1].astype(F32)
    go_out[core] = total.astype(LOW)
    last_copy.start()

    def gathered(source, got, micro):
        total = source[micro, band, :].astype(F32)
        for i in range(1, n):
            total = total + got[micro, i - 1].astype(F32)
        return total

    for micro in range(batch):
        wait(row_copies(micro))
        grad = gathered(dh_all, dh_got, micro)
        normed, inverse = normal(x_ref[micro].astype(F32))
        vec[0:1, :] += column_sum(grad * normed)
        vec[3:4, :] += column_sum(grad)
        dx_ref[micro] = dx1[micro] + normal_back(grad * wide_ref[0:1, :], normed, inverse)
    share = vec_out.shape[2]
    row = lax.broadcasted_iota(jnp.int32, (16, 1), 0)
    own_scales = vec[10:11, place]
    for d in range(n):
        block = vec[:, d * share : (d + 1) * share]
        block = jnp.where(row >= 10, 0.0, block)
        vec_out[d] = jnp.where(row == 10 + me, own_scales, block)
    wait(ffn_copies)
    for w in range(2):
        total = g_own[w].astype(F32)
        for j in range(1, nz):
            total = total + g_got[j - 1, w].astype(F32)
        g_out[w] = total.astype(LOW)
    last_copy.wait()


def back(x, dy, x1, z, dh2, a_own, wide, lens, scale, g, w_out, w_qkv, h_all, qkv_all, p_all):
    batch, tok, width = x.shape
    slot = h_all.shape[1]
    n = slot // tok
    cols = w_qkv.shape[1] // 3
    _, nz, part, _ = g.shape

    def big(*dims):
        return pltpu.VMEM(dims, LOW)

    return pl.pallas_call(
        lambda *refs: back_kernel(n, 2 * nz, *refs),
        name="back",
        out_shape=(
            shape((batch, tok, width), F32),
            shape((width, 3 * cols), LOW),
            shape((2, cols // 2, width), LOW),
            shape((n, 16, width // n), F32),
            shape((2, part, width), LOW),
        ),
        in_specs=[ANY] * 6 + [VMEM] + [SMEM] * 2 + [ANY] * 6,
        out_specs=(VMEM,) * 5,
        scratch_shapes=[
            big(batch, tok, width),
            big(batch, tok, width),
            pltpu.VMEM((batch, tok, width), F32),
            pltpu.VMEM((batch, tok, width), F32),
            pltpu.VMEM((batch, tok, width), F32),
            big(batch, tok, width),
            big(*w_out.shape),
            big(*w_qkv.shape),
            big(*h_all.shape),
            big(*qkv_all.shape),
            big(*p_all.shape),
            pltpu.VMEM((batch, tok, width), F32),
            big(batch * tok, width),
            big(batch, n, tok, cols),
            big(batch, slot, cols),
            big(2, slot, slot),
            big(batch, slot, 3 * cols),
            big(batch, slot, width),
            big(n, 2, cols // 2, width),
            big(n, cols // 2, width),
            big(n - 1, cols // 2, width),
            big(n, cols // 2, width),
            big(batch, n - 1, tok, width),
            big(2, part, width),
            big(nz - 1, 2, part, width),
            pltpu.VMEM((16, width), F32),
            DMA((2, batch, n)),
            DMA((2, batch, n)),
            DMA((2, n)),
            DMA((2, 2)),
            DMA((2, nz)),
            DMA((12,)),
        ],
        compiler_params=pltpu.CompilerParams(
            collective_id=3, has_side_effects=True, vmem_limit_bytes=56 << 20
        ),
    )(x, dy, x1, z, dh2, a_own, wide, lens, scale, g, w_out, w_qkv, h_all, qkv_all, p_all)


def settle_kernel(
    n, nf, gq_ref, go_ref, gv_ref, vec_ref, g_ref, wide_ref, x1_hbm, y_hbm,
    q_out, o_out, v_out, vec_out, ffn_out, out_ref,
    pair_q, pair_v, sum_q, sum_v, far_q, far_o, far_v, last_q,
    vec_got, vec_sum, vec_far, vec_pair, x1_ref, y_own, y_got,
    p_sems, z_sems, d_sems, e_sems, y_sems, own_sems,
):
    me = lax.axis_index("dp")
    f = lax.axis_index("ffn")
    nz = nf // 2
    core = lax.rem(f, 2)
    row = lax.div(f, 2)
    cols = q_out.shape[2] // n
    _, part, width = g_ref.shape
    batch, tok = out_ref.shape[:2]
    peers = dp_peers(n, me) + ffn_peers(nf, f)
    greet(peers)
    band = at(me * tok, tok)
    loads = [
        pltpu.make_async_copy(x1_hbm, x1_ref, own_sems.at[5]),
        pltpu.make_async_copy(y_hbm.at[:, band, :], y_own, own_sems.at[6]),
    ]
    start(loads)
    meet(peers)
    pair = {"ffn": f ^ 1}
    pairs = [
        send(gq_ref.at[:, :, 1 - core], pair_q, p_sems, (0,), pair),
        send(gv_ref.at[:, 1 - core], pair_v, p_sems, (1,), pair),
    ]
    start(pairs)
    far = []
    for j in range(1, nz):
        source = go_ref.at[row ^ j, core]
        far.append(send(source, far_o.at[j - 1], z_sems, (j, 1), {"ffn": f ^ (2 * j)}))
    start(far)
    shares, halves = [], []
    for i, peer in enumerate(dp_peers(n, me), 1):
        shares.append(send(vec_ref.at[me ^ i], vec_got.at[i - 1], e_sems, (i, 0), peer))
    for i, peer in enumerate(dp_peers(n, me), 1):
        theirs = at((me ^ i) * (width // n), width // n)
        for k in range(2):
            source = g_ref.at[k, :, theirs]
            halves.append(send(source, ffn_out.at[k, me], e_sems, (i, 1 + k), peer))
    outs = [
        send(
            y_hbm.at[:, at((me ^ i) * tok, tok), :], y_got.at[i - 1], y_sems, (i,), peer
        )
        for i, peer in enumerate(dp_peers(n, me), 1)
    ]
    start(shares)
    start(halves)
    start(outs)
    mine = at(me * (width // n), width // n)
    own = [
        pltpu.make_async_copy(g_ref.at[k, :, mine], ffn_out.at[k, me], own_sems.at[3 + k])
        for k in range(2)
    ]
    start(own)
    wait(pairs)

    def add_pair(k, _):
        for d in range(n):
            total = gq_ref[d, k, core].astype(F32) + pair_q[d, k].astype(F32)
            sum_q[d, k] = total.astype(LOW)
        sum_v[k] = gv_ref[k, core] + pair_v[k]
        return 0

    lax.fori_loop(0, nz, add_pair, 0)
    wait(shares)
    total = vec_ref[me]
    for i in range(1, n):
        total = total + vec_got[i - 1]
    vec_sum[...] = total
    later = []
    for j in range(1, nz):
        peer = {"ffn": f ^ (2 * j)}
        theirs = row ^ j
        for k, piece, place in [
            (0, sum_q.at[:, theirs], far_q),
            (2, sum_v.at[theirs], far_v),
            (3, vec_sum, vec_far),
        ]:
            later.append(send(piece, place.at[j - 1], z_sems, (j, k), peer))
    start(later)
    wait(far + later)
    total = vec_sum[...]
    for j in range(1, nz):
        total = total + vec_far[j - 1]
    vec_out[...] = total
    vec_sum[...] = total
    last = [send(vec_sum, vec_pair, p_sems, (2,), pair)]
    for d in range(n):
        total = sum_q[d, row].astype(F32)
        for j in range(1, nz):
            total = total + far_q[j - 1, d].astype(F32)
        last_q[d] = total
    total = sum_v[row]
    for j in range(1, nz):
        total = total + far_v[j - 1]
    v_out[me] = total
    place = at(me * cols, cols)
    for i, peer in enumerate(dp_peers(n, me), 1):
        for k in range(3):
            source = last_q.at[me ^ i, :, k * cols : (k + 1) * cols]
            last.append(send(source, q_out.at[k, :, place], d_sems, (i, k), peer))
        last.append(send(v_out.at[me], v_out.at[me], d_sems, (i, 3), peer))
    own += [
        pltpu.make_async_copy(
            last_q.at[me, :, k * cols : (k + 1) * cols], q_out.at[k, :, place], own_sems.at[k]
        )
        for k in range(3)
    ]
    start(last + own[2:])
    total = go_ref[row, core].astype(F32)
    for j in range(1, nz):
        total = total + far_o[j - 1].astype(F32)
    o_out[...] = total
    wait(loads + outs)
    for micro in range(batch):
        total = x1_ref[micro] + y_own[micro].astype(F32) + wide_ref[9:10, :]
        for i in range(1, n):
            total = total + y_got[i - 1, micro].astype(F32)
        out_ref[micro] = total.astype(LOW)
    wait(last + own + halves)
    vec_out[...] += vec_pair[...]


def settle(gq, go, gv, vec, g, wide_rows, x1, y):
    n, nz, _, rows, wide = gq.shape
    width = go.shape[3]
    part = g.shape[1]
    tile = gv.shape[2:]
    block = vec.shape[1:]
    batch, tok, _ = x1.shape
    return pl.pallas_call(
        lambda *refs: settle_kernel(n, 2 * nz, *refs),
        name="settle",
        out_shape=(
            shape((3, rows, width), F32),
            shape((rows, width), F32),
            shape((n, *tile), F32),
            shape(block, F32),
            shape((2, n, part, width // n), LOW),
            shape(x1.shape, LOW),
        ),
        in_specs=[VMEM] * 6 + [ANY] * 2,
        out_specs=(VMEM,) * 6,
        scratch_shapes=[
            pltpu.VMEM((n, nz, rows, wide), LOW),
            pltpu.VMEM((nz, *tile), F32),
            pltpu.VMEM((n, nz, rows, wide), LOW),
            pltpu.VMEM((nz, *tile), F32),
            pltpu.VMEM((nz - 1, n, rows, wide), LOW),
            pltpu.VMEM((nz - 1, rows, width), LOW),
            pltpu.VMEM((nz - 1, *tile), F32),
            pltpu.VMEM((n, rows, wide), F32),
            pltpu.VMEM((n - 1, *block), F32),
            pltpu.VMEM(block, F32),
            pltpu.VMEM((nz - 1, *block), F32),
            pltpu.VMEM(block, F32),
            pltpu.VMEM(x1.shape, F32),
            pltpu.VMEM(x1.shape, LOW),
            pltpu.VMEM((n - 1, *x1.shape), LOW),
            DMA((2, 3)),
            DMA((2, nz, 4)),
            DMA((2, n, 4)),
            DMA((2, n, 3)),
            DMA((2, n)),
            DMA((7,)),
        ],
        compiler_params=pltpu.CompilerParams(
            collective_id=4, has_side_effects=True, vmem_limit_bytes=24 << 20
        ),
    )(gq, go, gv, vec, g, wide_rows, x1, y)


def on_device(
    tokens,
    seq_lens,
    qkv_weight,
    out_weight,
    head_scale,
    gains,
    biases,
    ffn_in,
    ffn_bias,
    mid_gain,
    mid_bias,
    ffn_out,
    out_cotangent,
):
    n = lax.axis_size("dp")
    nf = lax.axis_size("ffn")
    me = lax.axis_index("dp")
    f = lax.axis_index("ffn")
    batch, _, tok, width = tokens.shape
    heads = head_scale.shape[0]
    cols = width // n
    rows = qkv_weight.shape[1]
    hid = ffn_in.shape[1]
    part = hid // n
    ff = hid * nf

    def tiled(values):
        size = values.shape[1]
        spot = lax.rem(f, 128 // size) * size
        return lax.dynamic_update_slice(jnp.zeros((16, 128), LOW), values, (0, spot))

    vectors = lax.dynamic_index_in_dim(
        jnp.stack([ffn_bias, mid_gain, mid_bias]).reshape(3, n, part), me, 1, keepdims=False
    )
    x, dy = tokens[:, 0], out_cotangent[:, 0]
    x_all, w_all, out_stage, first_stage, w2, wide, mids = spread(
        x,
        qkv_weight.reshape(3, rows, n, cols).transpose(2, 1, 0, 3).reshape(n, rows, 3 * cols),
        out_weight,
        jnp.stack([tiled(jnp.concatenate([gains, biases])), tiled(vectors)]),
        ffn_in.T.reshape(n, part, cols),
        ffn_out.reshape(n, part, cols),
        n,
        nf,
    )
    w_qkv = w_all.reshape(width, 3 * cols)
    dy_all, out_all, w1, h_all, qkv_all, p_all, a_own = attend(
        x_all, dy, w_qkv, out_stage, first_stage, wide, seq_lens, head_scale, nf
    )
    w_out = out_all.reshape(width, width)
    w1, w2 = w1.reshape(nf * part, width), w2.reshape(nf * part, width)
    z, x1, y, g, dh2, mid = feed(
        x, a_own, wide, mids, seq_lens, w_out, dy_all, w1, w2, n, ff, part
    )
    tokens_grad, gq, go, vec, g = back(
        x, dy, x1, z, dh2, a_own, wide, seq_lens, head_scale, g, w_out, w_qkv, h_all, qkv_all, p_all
    )
    nz = nf // 2
    qkv_grad, out_weight_grad, mid, vec, ffn, output = settle(
        gq.reshape(n, nz, 2, rows, 3 * cols),
        go.reshape(nz, 2, rows, width),
        mid.reshape(8, nz, 2, part).transpose(1, 2, 0, 3),
        vec,
        g,
        wide,
        x1,
        y,
    )
    mid = mid.transpose(1, 0, 2).reshape(8, hid)
    own = lax.dynamic_slice_in_dim(vec, f * rows, rows, 1)
    ffn = ffn.reshape(2, hid, cols)
    return (
        output[:, None],
        tokens_grad[:, None],
        qkv_grad,
        out_weight_grad,
        vec[10 : 10 + n, ::HDIM].reshape(heads),
        own[:3],
        own[3:10],
        ffn[0].T.astype(F32),
        mid[0],
        mid[1],
        mid[2],
        ffn[1].astype(F32),
    )


def solution(mesh):
    seqs = P(None, "ffn", "dp", None)
    wide = P(None, ("dp", "ffn"))
    hidden = P("ffn")
    return jax.shard_map(
        on_device,
        mesh=mesh,
        in_specs=(
            seqs,
            P(None, "ffn"),
            P(None, ("dp", "ffn"), None),
            P(("dp", "ffn"), None),
            P(),
            wide,
            wide,
            P("dp", "ffn"),
            hidden,
            hidden,
            hidden,
            P("ffn", "dp"),
            seqs,
        ),
        out_specs=(
            seqs,
            seqs,
            P(None, ("dp", "ffn"), None),
            P(("dp", "ffn"), None),
            P(),
            wide,
            wide,
            P("dp", "ffn"),
            hidden,
            hidden,
            hidden,
            P("ffn", "dp"),
        ),
        check_vma=False,
    )
```

```python
from types import SimpleNamespace

import jax
import jax.numpy as jnp
from jax import lax
from jax.experimental import pallas as pl
from jax.experimental.pallas import tpu as pltpu
from jax.sharding import PartitionSpec as P

HDIM = 64
EPS = 1e-05
LOW = jnp.bfloat16
F32 = jnp.float32
ANY = pl.BlockSpec(memory_space=pl.ANY)
VMEM = pl.BlockSpec(memory_space=pltpu.VMEM)
SMEM = pl.BlockSpec(memory_space=pltpu.SMEM)
MESH = pl.DeviceIdType.MESH
DMA = pltpu.SemaphoreType.DMA


def dot(left, right):
    return jnp.dot(left, right, preferred_element_type=F32)


def dot_nt(left, right):
    return lax.dot_general(left, right, (((1,), (1,)), ((), ())), preferred_element_type=F32)


def dot_tn(left, right):
    return lax.dot_general(left, right, (((0,), (0,)), ((), ())), preferred_element_type=F32)


def shape(dims, kind):
    return jax.ShapeDtypeStruct(tuple(dims), kind)


def at(start, size, unit=128):
    return pl.ds(pl.multiple_of(start, unit), size)


def send(src, dst, sems, index, where):
    return pltpu.make_async_remote_copy(
        src_ref=src,
        dst_ref=dst,
        send_sem=sems.at[(0, *index)],
        recv_sem=sems.at[(1, *index)],
        device_id=where,
        device_id_type=MESH,
    )


def greet(peers):
    barrier = pltpu.get_barrier_semaphore()
    for peer in peers:
        pl.semaphore_signal(barrier, inc=1, device_id=peer, device_id_type=MESH)


def meet(peers):
    pl.semaphore_wait(pltpu.get_barrier_semaphore(), len(peers))


def dp_peers(n, me):
    return [{"dp": me ^ i} for i in range(1, n)]


def ffn_peers(nf, f):
    return [{"ffn": f ^ (2 * j)} for j in range(1, nf // 2)] + [{"ffn": f ^ 1}]


def start(copies):
    for copy in copies:
        copy.start()


def wait(copies):
    for copy in copies:
        copy.wait()


class Line:
    def __init__(self, nf, f, items, hop_sems, side_sems):
        self.nz, self.core, self.q, self.f = nf // 2, lax.rem(f, 2), lax.div(f, 2), f
        self.items, self.hop_sems, self.side_sems = items, hop_sems, side_sems
        self.next = [1] * len(items)

    def copy(self, sems, k, t, came, way, first, target):
        source, place = self.items[k]
        index = self.f if first else 2 * (self.q - t * way) + self.core
        spot = place(index)
        side = 0 if way > 0 else 1
        return pltpu.make_async_remote_copy(
            src_ref=source if first else spot,
            dst_ref=spot,
            send_sem=sems.at[0, side, k, t],
            recv_sem=sems.at[1, side, k, came],
            device_id={"ffn": target},
            device_id_type=MESH,
        )

    def hop(self, k, t, way, first=False):
        return self.copy(self.hop_sems, k, t, t + 1, way, first, self.f + 2 * way)

    def arrival(self, k, t, way):
        return self.copy(self.hop_sems, k, t, t, way, False, self.f + 2 * way)

    def over(self, k, t, way, first=False):
        return self.copy(self.side_sems, k, t, t, way, first, self.f ^ 1)

    def onward(self, way):
        return self.q < self.nz - 1 if way > 0 else self.q > 0

    def has(self, t, way):
        return self.q - t >= 0 if way > 0 else self.q + t <= self.nz - 1

    def begin(self, *items):
        for k in items:
            for way in (1, -1):

                @pl.when(self.onward(way))
                def _():
                    self.hop(k, 0, way, True).start()

        for k in items:
            self.over(k, 0, 1, True).start()

    def step(self, k, t):
        for way in (1, -1):

            @pl.when(self.has(t, way) & self.onward(way))
            def _():
                self.arrival(k, t, way).wait_recv()
                self.hop(k, t, way).start()

        for way in (1, -1):

            @pl.when(self.has(t, way))
            def _():
                @pl.when(jnp.logical_not(self.onward(way)))
                def _():
                    self.arrival(k, t, way).wait_recv()

                self.over(k, t, way).start()

    def advance(self, *items):
        for k in items:
            if self.next[k] < self.nz:
                self.step(k, self.next[k])
                self.next[k] += 1

    def arrive(self, *items):
        begin = self.next[items[0]]

        def rest(t, _):
            for k in items:
                self.step(k, t)
            return 0

        lax.fori_loop(begin, self.nz, rest, 0)

        def close(t, _):
            for k in items:
                for way in (1, -1):

                    @pl.when(self.has(t, way))
                    def _():
                        self.over(k, t, way).wait_recv()

            return 0

        for k in items:
            self.over(k, 0, 1, True).wait_recv()
        lax.fori_loop(1, self.nz, close, 0)

    def finish(self, *items):
        for k in items:
            self.over(k, 0, 1, True).wait_send()
            for way in (1, -1):

                @pl.when(self.onward(way))
                def _():
                    self.hop(k, 0, way, True).wait_send()

        def close(t, _):
            for k in items:
                for way in (1, -1):

                    @pl.when(self.has(t, way))
                    def _():
                        self.over(k, t, way).wait_send()

                    @pl.when(self.has(t, way) & self.onward(way))
                    def _():
                        self.hop(k, t, way).wait_send()

            return 0

        lax.fori_loop(1, self.nz, close, 0)


def line_meet(n, nf, me, f):
    barrier = pltpu.get_barrier_semaphore()
    q, nz = lax.div(f, 2), nf // 2
    greet(dp_peers(n, me) + [{"ffn": f ^ 1}])

    @pl.when(q < nz - 1)
    def _():
        greet([{"ffn": f + 2}])

    @pl.when(q > 0)
    def _():
        greet([{"ffn": f - 2}])

    count = n + jnp.where(q < nz - 1, 1, 0) + jnp.where(q > 0, 1, 0)
    pl.semaphore_wait(barrier, count)


def normal(values):
    center = values - jnp.mean(values, axis=-1, keepdims=True)
    inverse = lax.rsqrt(jnp.mean(center * center, axis=-1, keepdims=True) + EPS)
    return center * inverse, inverse


def normal_back(grad, normed, inverse):
    return inverse * (
        grad
        - jnp.mean(grad, axis=-1, keepdims=True)
        - normed * jnp.mean(grad * normed, axis=-1, keepdims=True)
    )


def column_sum(values):
    return jnp.sum(values, axis=0, keepdims=True)


def launch(body, name, inputs, outputs, scratch, number, limit):
    names = [*inputs, *outputs, *scratch]
    results = pl.pallas_call(
        lambda *refs: body(SimpleNamespace(**dict(zip(names, refs)))),
        name=name,
        out_shape=tuple(kind for kind, _ in outputs.values()),
        in_specs=[spec for _, spec in inputs.values()],
        out_specs=tuple(spec for _, spec in outputs.values()),
        scratch_shapes=list(scratch.values()),
        compiler_params=pltpu.CompilerParams(
            collective_id=number, has_side_effects=True, vmem_limit_bytes=limit << 20
        ),
    )(*[value for value, _ in inputs.values()])
    return dict(zip(outputs, results))


def forward_kernel(n, nf, part, r):
    me = lax.axis_index("dp")
    f = lax.axis_index("ffn")
    core, nz = lax.rem(f, 2), nf // 2
    batch, tok, width = r.x.shape
    rows_each = r.wout.shape[0]
    cols = width // n
    pairs = cols // 128
    slot = n * tok
    hid = nf * part
    ff = n * hid
    step = 256
    peers = dp_peers(n, me)
    pair = {"ffn": f ^ 1}
    place = at(me * cols, cols)
    band = at(me * tok, tok)

    own = [
        pltpu.make_async_copy(r.qkv.at[:, :, place], r.stage.at[me], r.own_sems.at[0]),
        pltpu.make_async_copy(r.small.at[0], r.small_stage.at[me], r.own_sems.at[1]),
        pltpu.make_async_copy(r.small.at[1], r.small_stage.at[n], r.own_sems.at[2]),
        pltpu.make_async_copy(r.wout, r.out_stage.at[me], r.own_sems.at[3]),
        pltpu.make_async_copy(r.first.at[me], r.first_stage.at[:, place], r.own_sems.at[4]),
        pltpu.make_async_copy(r.second.at[me], r.second_stage.at[:, place], r.own_sems.at[5]),
        pltpu.make_async_copy(r.x, r.x_all.at[me], r.own_sems.at[6]),
        pltpu.make_async_copy(r.dy, r.dy_all.at[:, band, :], r.own_sems.at[7]),
    ]
    start(own)
    line_meet(n, nf, me, f)

    def to_peers(make):
        return [make(i, peer) for i, peer in enumerate(peers, 1)]

    blocks = to_peers(
        lambda i, peer: send(
            r.qkv.at[:, :, at((me ^ i) * cols, cols)], r.stage.at[me], r.w_sems, (i, 0), peer
        )
    )
    smalls = to_peers(
        lambda i, peer: send(r.small.at[0], r.small_stage.at[me], r.w_sems, (i, 1), peer)
    )
    outs = to_peers(lambda i, peer: send(r.wout, r.out_stage.at[me], r.w_sems, (i, 2), peer))
    firsts = to_peers(
        lambda i, peer: send(
            r.first.at[me ^ i], r.first_stage.at[:, place], r.w_sems, (i, 3), peer
        )
    )
    seconds = to_peers(
        lambda i, peer: send(
            r.second.at[me ^ i], r.second_stage.at[:, place], r.w_sems, (i, 4), peer
        )
    )

    def x_copies(micro):
        return to_peers(
            lambda i, peer: send(r.x.at[micro], r.x_all.at[me, micro], r.x_sems, (micro, i), peer)
        )

    def y_copies(micro):
        return to_peers(
            lambda i, peer: send(
                r.dy.at[micro], r.dy_all.at[micro, band, :], r.y_sems, (micro, i), peer
            )
        )

    start(blocks + smalls)
    start(x_copies(0))
    start(outs + firsts)
    start(x_copies(1))
    start(seconds)
    start(y_copies(0))
    line = Line(
        nf,
        f,
        [
            (r.stage, lambda index: r.w_all.at[:, index]),
            (r.small_stage, lambda index: r.small_all.at[index]),
            (r.out_stage, lambda index: r.out_all.at[:, index]),
            (r.first_stage, lambda index: r.w1.at[index]),
            (r.second_stage, lambda index: r.w2.at[index]),
        ],
        r.hop_sems,
        r.side_sems,
    )
    mine = [
        pltpu.make_async_copy(source, spot(f), r.own_sems.at[8 + k])
        for k, (source, spot) in enumerate(line.items)
    ]
    wait(blocks + smalls + own[:3])
    line.begin(0, 1)
    start(mine[:2])
    line.advance(0, 1)
    line.advance(0, 1)
    wait(outs + own[3:4])
    line.begin(2)
    start(mine[2:3])
    line.arrive(0, 1)
    wait(firsts + own[4:5])
    line.begin(3)
    start(mine[3:4])
    wait(mine[:2] + own[6:7])

    def lay_out(out_ref, index, begin, size):
        together = 128 // size
        for b in range(nf // together):
            total = r.small_all[b * together, index].astype(F32)
            for k in range(1, together):
                total = total + r.small_all[b * together + k, index].astype(F32)
            out_ref[:, begin + b * 128 : begin + (b + 1) * 128] = total

    for d in range(n):
        lay_out(r.wide, d, d * nf * rows_each, rows_each)
    lay_out(r.mids, n, 0, part)

    gain, shift = r.wide[0:1, :], r.wide[3:4, :]
    bias_q, bias_v = r.wide[4:5, place], r.wide[5:6, place]
    left = lax.broadcasted_iota(jnp.int32, (1, 128), 1) < HDIM

    def block_copies(micro):
        return to_peers(
            lambda i, peer: send(
                r.a_all.at[micro, me ^ i], r.a_own.at[micro, :, place], r.a_sems, (micro, i), peer
            )
        )

    def keep_copies(micro):
        return [
            pltpu.make_async_copy(source.at[micro], out.at[micro], r.keep_sems.at[micro, k])
            for k, (source, out) in enumerate(
                [(r.h_all, r.h_hbm), (r.qkv_all, r.qkv_hbm), (r.p_all, r.p_hbm)]
            )
        ]

    def after_first():
        line.advance(2)

    def after_second():
        line.advance(3)

    def after_third():
        line.advance(2)
        wait(seconds + own[5:6])
        line.begin(4)
        start(mine[4:5])

    def after_last():
        start(y_copies(1))
        line.advance(3)

    def attend(index, _):
        micro, two = lax.div(index, pairs), lax.rem(index, pairs)

        @pl.when(two == 0)
        def _():
            wait(x_copies(micro))

            def norm_rows(d, _):
                values, _ = normal(r.x_all[d, micro].astype(F32))
                r.h_all[micro, at(d * tok, tok), :] = (values * gain + shift).astype(LOW)
                return 0

            lax.fori_loop(0, n, norm_rows, 0)
            for k, bias in enumerate((bias_q, None, bias_v)):
                weight = r.w_all[:, :, k].reshape(width, cols)
                value = dot(r.h_all[micro], weight)
                if bias is not None:
                    value = value + bias
                r.qkv_all[micro, :, k * cols : (k + 1) * cols] = value.astype(LOW)

        length = r.lens[micro, 0]

        def column(k):
            return at(k * cols + two * 128, 128)

        head = two * 2
        scales = jnp.where(
            left, r.scale[me * 2 * pairs + head], r.scale[me * 2 * pairs + head + 1]
        )
        for block in range(n):
            end = (block + 1) * tok
            q = r.qkv_all[micro, block * tok : end, column(0)] * HDIM ** (-0.5)
            k = r.qkv_all[micro, :end, column(1)]
            v = r.qkv_all[micro, :end, column(2)]
            key = lax.broadcasted_iota(jnp.int32, (tok, end), 1)
            query = lax.broadcasted_iota(jnp.int32, (tok, end), 0) + block * tok
            mask = (key <= query) & (key < length)
            out = []
            for side in range(2):
                mine_ = left if side == 0 else jnp.logical_not(left)
                scores = dot_nt(jnp.where(mine_, q, jnp.zeros_like(q)), k)
                scores = jnp.where(mask, scores, -1e30)
                expo = jnp.exp(scores - jnp.max(scores, axis=-1, keepdims=True))
                probs = expo * (1.0 / jnp.sum(expo, axis=-1, keepdims=True))
                probs = probs.astype(LOW)
                r.p_all[micro, head + side, block * tok : end, :end] = probs
                out.append(dot(probs, v))
            joined = jnp.where(left, out[0], out[1]) * scales
            r.a_all[micro, block, :, at(two * 128, 128)] = joined.astype(LOW)

        @pl.when(two == pairs - 1)
        def _():
            start(block_copies(micro))
            start(keep_copies(micro))
            r.a_own[micro, :, place] = r.a_all[micro, me]

        work = [after_first, after_second, after_third, after_last]
        for k, act in enumerate(work[: batch * pairs]):
            pl.when(index == k)(act)
        return 0

    lax.fori_loop(0, batch * pairs, attend, 0)

    line.arrive(2)
    wait(mine[2:3])
    late = [
        pltpu.make_async_copy(source, target, r.own_sems.at[13 + k])
        for k, (source, target) in enumerate(
            [(r.w_all, r.w_hbm), (r.out_all, r.out_hbm), (r.z, r.z_hbm), (r.x1, r.x1_hbm),
             (r.a_own, r.a_hbm), (r.y, r.y_hbm), (r.pair_got, r.g_hbm)]
        )
    ]
    start(late[:2])

    def row_copies(micro):
        return to_peers(
            lambda i, peer: send(
                r.h2_own.at[micro], r.h2_all.at[micro, band, :], r.h_sems, (micro, i), peer
            )
        )

    for micro in range(batch):
        wait(block_copies(micro))
        z = dot(r.a_own[micro], r.out_all[...].reshape(width, width)) + r.wide[6:7, :]
        r.z[micro] = z
        values, _ = normal(z)
        x1 = r.x[micro].astype(F32) + values * r.wide[1:2, :] + r.wide[7:8, :]
        r.x1[micro] = x1
        values, _ = normal(x1)
        r.h2_own[micro] = (values * r.wide[2:3, :] + r.wide[8:9, :]).astype(LOW)
        start(row_copies(micro))
        r.h2_all[micro, band, :] = r.h2_own[micro]
    start(late[2:5])
    line.advance(4)
    line.arrive(3)
    wait(mine[3:4])

    def weights(ref, c):
        count = step // part
        return ref[pl.ds(c * count, count)].reshape(step, width)

    def w_columns(ref, columns):
        return ref[:, :, columns].reshape(hid, step)

    def sum_copies(micro):
        return to_peers(
            lambda i, peer: send(
                r.sums.at[micro], r.sums_all.at[micro, me], r.s_sems, (micro, i), peer
            )
        )

    def grad_copies(micro):
        return to_peers(
            lambda i, peer: send(
                r.dh2_all.at[micro, at((me ^ i) * tok, tok), :],
                r.dh2_got.at[micro, i - 1],
                r.r_sems,
                (micro, i),
                peer,
            )
        )

    def fold(values):
        total = values[:, :128]
        for k in range(1, step // 128):
            total = total + values[:, k * 128 : (k + 1) * 128]
        return total

    def units(micro):
        wait(row_copies(micro))

        def chunk(c, totals):
            rows = at(c * step, step)
            u = dot_nt(r.h2_all[micro], weights(r.w1, c)) + r.mids[0:1, rows]
            phi = 0.5 + 0.5 * lax.erf(u * (0.5**0.5))
            value = u * phi
            r.act[micro, :, rows] = value
            r.slope[micro, :, rows] = phi + u * jnp.exp(u * u * -0.5) * 0.3989422804014327
            return totals[0] + fold(value), totals[1] + fold(value * value)

        zero = jnp.zeros((slot, 128), F32)
        totals = lax.fori_loop(0, hid // step, chunk, (zero,) * 2)
        for k in range(2):
            r.sums[micro, k : k + 1, :] = column_sum(totals[k].T)

    def cotangents(micro):
        wait(y_copies(micro))
        valid = lax.broadcasted_iota(jnp.int32, (slot, 1), 0) < r.lens[micro, 0]
        rows = r.dy_all[micro]
        r.dy_all[micro] = jnp.where(valid, rows, jnp.zeros_like(rows))

        def chunk(c, totals):
            rows = at(c * step, step)
            dm = dot_nt(r.dy_all[micro], weights(r.w2, c))
            r.dmix[micro, :, rows] = dm
            dn = dm * r.mids[1:2, rows]
            return totals[0] + fold(dn), totals[1] + fold(dn * r.act[micro, :, rows])

        zero = jnp.zeros((slot, 128), F32)
        totals = lax.fori_loop(0, hid // step, chunk, (zero,) * 2)
        for k in range(2):
            r.sums[micro, 2 + k : 3 + k, :] = column_sum(totals[k].T)
        r.sums[micro, 4:8, :] = jnp.zeros((4, slot), F32)
        start(sum_copies(micro))

    def passes(micro, _):
        units(micro)

        @pl.when(micro == 0)
        def _():
            line.arrive(4)
            wait(mine[4:5] + own[7:8])

        cotangents(micro)
        return 0

    lax.fori_loop(0, batch, passes, 0)
    r.vec_out[...] = jnp.zeros_like(r.vec_out)

    def second_pass(micro, _):
        wait(sum_copies(micro))
        r.sums_all[micro, me] = r.sums[micro]
        total = r.sums_all[micro, 0]
        for d in range(1, n):
            total = total + r.sums_all[micro, d]
        total = total * (1.0 / ff)
        mean = total[0:1]
        inverse = lax.rsqrt(total[1:2] - mean * mean + EPS)
        back = total[2:3]
        cross = inverse * (total[3:4] - mean * back)
        table = jnp.concatenate([mean, inverse, back, cross] * 32, axis=0).T
        mean, inverse, back, cross = [table[:, k : k + 1] for k in range(4)]
        rows_of = at(micro * slot, slot)

        def chunk(c, _):
            rows = at(c * step, step)
            normed = (r.act[micro, :, rows] - mean) * inverse
            dm = r.dmix[micro, :, rows]
            gain = r.mids[1:2, rows]
            r.mixed[rows_of, rows] = (normed * gain + r.mids[2:3, rows]).astype(LOW)
            df = inverse * (dm * gain - back - normed * cross)
            low = (df * r.slope[micro, :, rows]).astype(LOW)
            r.du[rows_of, rows] = low
            r.vec_out[0:1, rows] += column_sum(low.astype(F32))
            r.vec_out[1:2, rows] += column_sum(dm * normed)
            r.vec_out[2:3, rows] += column_sum(dm)
            return 0

        lax.fori_loop(0, hid // step, chunk, 0)

        def back_rows(c, _):
            columns = at(c * step, step)
            value = dot(r.du[rows_of, :], w_columns(r.w1, columns))
            r.dh2_all[micro, :, columns] = value.astype(LOW)
            return 0

        lax.fori_loop(0, width // step, back_rows, 0)
        start(grad_copies(micro))
        return 0

    lax.fori_loop(0, batch, second_pass, 0)
    each = step // part // 2

    def pair_copies(c):
        copies = []
        for k in range(each):
            index = c * (2 * each) + 2 * k
            for w in range(2):
                copies.append(
                    send(
                        r.grads.at[w, index + 1 - core],
                        r.pair_got.at[w, c * each + k],
                        r.p_sems,
                        (c, k, w),
                        pair,
                    )
                )
        return copies

    def weight_grads(c, _):
        rows = at(c * step, step)
        h2 = r.h2_all[...].reshape(batch * slot, width)
        dy = r.dy_all[...].reshape(batch * slot, width)
        first = dot_tn(r.du[:, rows], h2).astype(LOW)
        second = dot_tn(r.mixed[:, rows], dy).astype(LOW)
        for k in range(step // part):
            r.grads[0, c * (step // part) + k] = first[k * part : (k + 1) * part]
            r.grads[1, c * (step // part) + k] = second[k * part : (k + 1) * part]
        start(pair_copies(c))
        return 0

    lax.fori_loop(0, hid // step, weight_grads, 0)

    def out_rows(c, _):
        columns = at(c * step, step)
        for micro in range(batch):
            value = dot(r.mixed[micro * slot : (micro + 1) * slot, :], w_columns(r.w2, columns))
            r.y[micro, :, columns] = value.astype(LOW)
        return 0

    lax.fori_loop(0, width // step, out_rows, 0)
    start(late[5:6])

    def pair_sum(c, _):
        wait(pair_copies(c))
        for k in range(each):
            for w in range(2):
                total = r.grads[w, c * (2 * each) + 2 * k + core].astype(F32)
                total = total + r.pair_got[w, c * each + k].astype(F32)
                r.pair_got[w, c * each + k] = total.astype(LOW)
        return 0

    lax.fori_loop(0, hid // step, pair_sum, 0)
    start(late[6:])
    line.finish(0, 1, 2, 3, 4)
    for micro in range(batch):
        wait(keep_copies(micro))
    for micro in range(batch):
        wait(grad_copies(micro))
        total = r.dh2_all[micro, band, :].astype(F32)
        for i in range(1, n):
            total = total + r.dh2_got[micro, i - 1].astype(F32)
        r.dh2_out[micro] = total
    wait(late)


def forward(x, qkv, wout, small, first, second, dy, lens, scale, n, nf):
    batch, tok, width = x.shape
    rows = wout.shape[0]
    part = first.shape[1]
    cols = width // n
    slot, hid = n * tok, nf * part
    heads = cols // HDIM

    def low(*dims):
        return pltpu.VMEM(dims, LOW)

    def full(*dims):
        return pltpu.VMEM(dims, F32)

    inputs = {
        name: (value, VMEM)
        for name, value in zip(
            ("x", "qkv", "wout", "small", "first", "second", "dy"),
            (x, qkv, wout, small, first, second, dy),
        )
    }
    inputs["lens"] = (lens, SMEM)
    inputs["scale"] = (scale, SMEM)
    outputs = {
        "wide": (shape((16, width), F32), VMEM),
        "w_hbm": (shape((n, nf, 3, rows, cols), LOW), ANY),
        "out_hbm": (shape((n, nf, rows, width), LOW), ANY),
        "h_hbm": (shape((batch, slot, width), LOW), ANY),
        "qkv_hbm": (shape((batch, slot, 3 * cols), LOW), ANY),
        "p_hbm": (shape((batch, heads, slot, slot), LOW), ANY),
        "a_hbm": (shape((batch, tok, width), LOW), ANY),
        "z_hbm": (shape((batch, tok, width), F32), ANY),
        "x1_hbm": (shape((batch, tok, width), F32), ANY),
        "y_hbm": (shape((batch, slot, width), LOW), ANY),
        "g_hbm": (shape((2, nf // 2, part, width), LOW), ANY),
        "dh2_out": (shape((batch, tok, width), F32), VMEM),
        "vec_out": (shape((8, hid), F32), VMEM),
    }
    scratch = {
        "mids": full(16, hid),
        "stage": low(n, 3, rows, cols),
        "small_stage": low(n + 1, *small.shape[1:]),
        "out_stage": low(n, rows, width),
        "first_stage": low(part, width),
        "second_stage": low(part, width),
        "small_all": low(nf, n + 1, *small.shape[1:]),
        "w_all": low(n, nf, 3, rows, cols),
        "out_all": low(n, nf, rows, width),
        "w1": low(nf, part, width),
        "w2": low(nf, part, width),
        "x_all": low(n, batch, tok, width),
        "dy_all": low(batch, slot, width),
        "h_all": low(batch, slot, width),
        "qkv_all": low(batch, slot, 3 * cols),
        "p_all": low(batch, heads, slot, slot),
        "a_all": low(batch, n, tok, cols),
        "a_own": low(batch, tok, width),
        "z": full(batch, tok, width),
        "x1": full(batch, tok, width),
        "h2_own": low(batch, tok, width),
        "h2_all": low(batch, slot, width),
        "act": full(batch, slot, hid),
        "slope": full(batch, slot, hid),
        "dmix": full(batch, slot, hid),
        "mixed": low(batch * slot, hid),
        "du": low(batch * slot, hid),
        "sums": full(batch, 8, slot),
        "sums_all": full(batch, n, 8, slot),
        "dh2_all": low(batch, slot, width),
        "dh2_got": low(batch, n - 1, tok, width),
        "y": low(batch, slot, width),
        "grads": low(2, nf, part, width),
        "pair_got": low(2, nf // 2, part, width),
        "w_sems": DMA((2, n, 5)),
        "x_sems": DMA((2, batch, n)),
        "y_sems": DMA((2, batch, n)),
        "a_sems": DMA((2, batch, n)),
        "h_sems": DMA((2, batch, n)),
        "s_sems": DMA((2, batch, n)),
        "r_sems": DMA((2, batch, n)),
        "p_sems": DMA((2, hid // 256, 128 // part, 2)),
        "hop_sems": DMA((2, 2, 5, nf // 2)),
        "side_sems": DMA((2, 2, 5, nf // 2)),
        "keep_sems": DMA((batch, 3)),
        "own_sems": DMA((20,)),
    }
    return launch(
        lambda r: forward_kernel(n, nf, part, r), "forward", inputs, outputs, scratch, 0, 63
    )


def back_kernel(
    n, nf, x_hbm, dy_hbm, x1_hbm, z_hbm, dh2_hbm, a_hbm, wide_ref, lens_ref, scale_ref,
    g_hbm, wout_hbm, w_hbm, h_hbm, qkv_hbm, p_hbm,
    dx_ref, gq_out, go_out, vec_out, g_out,
    x_ref, dy_ref, x1_ref, z_ref, dh2_ref, a_ref,
    wout, w_qkv, h_all, qkv_all, p_all, dx1, dz, do_own, do_all, ds_all, dqkv,
    dh_all, go_all, go_pair, go_got, go_half, dh_got, g_own, g_got, vec,
    o_sems, h_sems, g_sems, p_sems, z_sems, own_sems,
):
    me = lax.axis_index("dp")
    f = lax.axis_index("ffn")
    core, q_me = lax.rem(f, 2), lax.div(f, 2)
    nz = nf // 2
    batch, tok, width = x_ref.shape
    slot = n * tok
    cols = w_qkv.shape[1] // 3
    half = cols // 2
    pairs = cols // 128
    step = 256
    peers = dp_peers(n, me)
    pair = {"ffn": f ^ 1}
    everyone = peers + ffn_peers(nf, f)
    greet(everyone)
    loads = [
        pltpu.make_async_copy(source, target, own_sems.at[k])
        for k, (source, target) in enumerate(
            [(x1_hbm, x1_ref), (dh2_hbm, dh2_ref), (dy_hbm, dy_ref), (z_hbm, z_ref),
             (wout_hbm, wout), (a_hbm, a_ref), (qkv_hbm, qkv_all), (p_hbm, p_all),
             (w_hbm, w_qkv), (h_hbm, h_all), (x_hbm, x_ref), (g_hbm.at[:, q_me], g_own)]
        )
    ]
    start(loads)
    vec[...] = jnp.zeros_like(vec)
    band = at(me * tok, tok)
    place = at(me * cols, cols)
    wait(loads[:4])
    for micro in range(batch):
        normed, inverse = normal(x1_ref[micro])
        grad = dh2_ref[micro]
        vec[2:3, :] += column_sum(grad * normed)
        vec[8:9, :] += column_sum(grad)
        valid = lax.broadcasted_iota(jnp.int32, (tok, 1), 0) + me * tok < lens_ref[micro, 0]
        dy = jnp.where(valid, dy_ref[micro].astype(F32), 0.0)
        vec[9:10, :] += column_sum(dy)
        grad = dy + normal_back(grad * wide_ref[2:3, :], normed, inverse)
        dx1[micro] = grad
        normed, inverse = normal(z_ref[micro])
        vec[1:2, :] += column_sum(grad * normed)
        vec[7:8, :] += column_sum(grad)
        low = normal_back(grad * wide_ref[1:2, :], normed, inverse).astype(LOW)
        vec[6:7, :] += column_sum(low.astype(F32))
        dz[micro * tok : (micro + 1) * tok, :] = low
    wait(loads[4:5])
    heads = cols // HDIM
    for d in range(n):
        grad = dot_nt(dz[...], wout[d * cols : (d + 1) * cols, :])
        lane = lax.broadcasted_iota(jnp.int32, (1, cols), 1) // HDIM
        scales = jnp.zeros((1, cols), F32)
        for head in range(heads):
            scales = jnp.where(lane == head, scale_ref[d * heads + head], scales)
        grad = (grad * scales).astype(LOW)
        for micro in range(batch):
            do_own[micro, d] = grad[micro * tok : (micro + 1) * tok]
    meet(everyone)

    def head_copies(micro):
        return [
            send(do_own.at[micro, me ^ i], do_all.at[micro, band, :], o_sems, (micro, i), peer)
            for i, peer in enumerate(peers, 1)
        ]

    def row_copies(micro):
        return [
            send(
                dh_all.at[micro, at((me ^ i) * tok, tok), :],
                dh_got.at[micro, i - 1],
                h_sems,
                (micro, i),
                peer,
            )
            for i, peer in enumerate(peers, 1)
        ]

    pair_copy = send(go_all.at[:, 1 - core], go_pair, p_sems, (0,), pair)
    weight_copies = [
        send(go_half.at[me ^ i], go_got.at[i - 1], g_sems, (i,), peer)
        for i, peer in enumerate(peers, 1)
    ]
    last_copy = send(go_out.at[core], go_out.at[core], p_sems, (1,), pair)
    ffn_copies = [
        send(g_hbm.at[:, q_me ^ j], g_got.at[j - 1], z_sems, (j,), {"ffn": f ^ (2 * j)})
        for j in range(1, nz)
    ]
    for micro in range(batch):
        start(head_copies(micro))
        do_all[micro, band, :] = do_own[micro, me]
    start(ffn_copies)
    wait(loads[5:6])

    def out_weight(d, _):
        a = a_ref[:, :, at(d * cols, cols)].reshape(batch * tok, cols)
        grad = dot_tn(a, dz[...]).astype(LOW)
        go_all[d, 0] = grad[:half]
        go_all[d, 1] = grad[half:]
        return 0

    lax.fori_loop(0, n, out_weight, 0)
    pair_copy.start()
    wait(loads[6:])
    left = lax.broadcasted_iota(jnp.int32, (1, 128), 1) < HDIM

    def one(micro, _):
        wait(head_copies(micro))

        def pair_of(pair, _):
            def column(part):
                return at(part * cols + pair * 128, 128)

            head = pair * 2
            own_cols = at(pair * 128, 128)
            sums = []
            k = qkv_all[micro, :, column(1)]
            v = qkv_all[micro, :, column(2)]
            for block in range(n):
                end = (block + 1) * tok
                rows = slice(block * tok, end)
                do = do_all[micro, rows, own_cols]
                out = []
                for side in range(2):
                    mine = left if side == 0 else jnp.logical_not(left)
                    probs = p_all[micro, head + side, rows, :end].astype(F32)
                    dp = dot_nt(jnp.where(mine, do, jnp.zeros_like(do)), v[:end])
                    delta = jnp.sum(probs * dp, axis=-1, keepdims=True)
                    ds = (probs * (dp - delta)).astype(LOW)
                    ds_all[side, rows, :end] = ds
                    out.append(dot(ds, k[:end]))
                    sums.append(jnp.sum(delta, axis=0, keepdims=True))
                dq = jnp.where(left, out[0], out[1]) * HDIM ** (-0.5)
                dqkv[micro, rows, column(0)] = dq.astype(LOW)
            q = qkv_all[micro, :, column(0)]
            do = do_all[micro, :, own_cols]
            for block in range(n):
                begin = block * tok
                keys = slice(begin, begin + tok)
                dk = [dot_tn(ds_all[side, begin:, keys], q[begin:]) for side in range(2)]
                dv = [
                    dot_tn(p_all[micro, head + side, begin:, keys], do[begin:])
                    for side in range(2)
                ]
                dk = jnp.where(left, dk[0], dk[1]) * HDIM ** (-0.5)
                dqkv[micro, keys, column(1)] = dk.astype(LOW)
                dqkv[micro, keys, column(2)] = jnp.where(left, dv[0], dv[1]).astype(LOW)
            first = sums[0] + sums[2] + sums[4] + sums[6] if n == 4 else sum(sums[0::2])
            second = sums[1] + sums[3] + sums[5] + sums[7] if n == 4 else sum(sums[1::2])
            spot = me * heads + head
            first = first * (1.0 / scale_ref[spot])
            second = second * (1.0 / scale_ref[spot + 1])
            vec[10:11, at(me * cols + pair * 128, 128)] += jnp.where(left, first, second)
            return 0

        lax.fori_loop(0, pairs, pair_of, 0)
        grads = dqkv[micro].astype(F32)
        vec[4:5, place] += column_sum(grads[:, :cols])
        vec[5:6, place] += column_sum(grads[:, 2 * cols :])

        def back_rows(c, _):
            rows = at(c * step, step)
            dh_all[micro, :, rows] = dot_nt(dqkv[micro], w_qkv[rows, :]).astype(LOW)
            return 0

        lax.fori_loop(0, width // step, back_rows, 0)
        start(row_copies(micro))

        @pl.when(micro == 0)
        def _():
            pair_copy.wait()
            for d in range(n):
                total = go_all[d, core].astype(F32) + go_pair[d].astype(F32)
                go_half[d] = total.astype(LOW)
            start(weight_copies)

        return 0

    lax.fori_loop(0, batch, one, 0)

    def weight_grads(c, _):
        rows = at(c * step, step)
        h = h_all[:, :, rows].reshape(batch * slot, step)
        gq_out[rows, :] = dot_tn(h, dqkv[...].reshape(batch * slot, 3 * cols)).astype(LOW)
        return 0

    lax.fori_loop(0, width // step, weight_grads, 0)
    wait(weight_copies)
    total = go_half[me].astype(F32)
    for i in range(1, n):
        total = total + go_got[i - 1].astype(F32)
    go_out[core] = total.astype(LOW)
    last_copy.start()

    def gathered(source, got, micro):
        total = source[micro, band, :].astype(F32)
        for i in range(1, n):
            total = total + got[micro, i - 1].astype(F32)
        return total

    for micro in range(batch):
        wait(row_copies(micro))
        grad = gathered(dh_all, dh_got, micro)
        normed, inverse = normal(x_ref[micro].astype(F32))
        vec[0:1, :] += column_sum(grad * normed)
        vec[3:4, :] += column_sum(grad)
        dx_ref[micro] = dx1[micro] + normal_back(grad * wide_ref[0:1, :], normed, inverse)
    share = vec_out.shape[2]
    row = lax.broadcasted_iota(jnp.int32, (16, 1), 0)
    own_scales = vec[10:11, place]
    for d in range(n):
        block = vec[:, d * share : (d + 1) * share]
        block = jnp.where(row >= 10, 0.0, block)
        vec_out[d] = jnp.where(row == 10 + me, own_scales, block)
    wait(ffn_copies)
    for w in range(2):
        total = g_own[w].astype(F32)
        for j in range(1, nz):
            total = total + g_got[j - 1, w].astype(F32)
        g_out[w] = total.astype(LOW)
    last_copy.wait()


def back(x, dy, x1, z, dh2, a_own, wide, lens, scale, g, w_out, w_qkv, h_all, qkv_all, p_all):
    batch, tok, width = x.shape
    slot = h_all.shape[1]
    n = slot // tok
    cols = w_qkv.shape[1] // 3
    _, nz, part, _ = g.shape

    def big(*dims):
        return pltpu.VMEM(dims, LOW)

    return pl.pallas_call(
        lambda *refs: back_kernel(n, 2 * nz, *refs),
        name="back",
        out_shape=(
            shape((batch, tok, width), F32),
            shape((width, 3 * cols), LOW),
            shape((2, cols // 2, width), LOW),
            shape((n, 16, width // n), F32),
            shape((2, part, width), LOW),
        ),
        in_specs=[ANY] * 6 + [VMEM] + [SMEM] * 2 + [ANY] * 6,
        out_specs=(VMEM,) * 5,
        scratch_shapes=[
            big(batch, tok, width),
            big(batch, tok, width),
            pltpu.VMEM((batch, tok, width), F32),
            pltpu.VMEM((batch, tok, width), F32),
            pltpu.VMEM((batch, tok, width), F32),
            big(batch, tok, width),
            big(*w_out.shape),
            big(*w_qkv.shape),
            big(*h_all.shape),
            big(*qkv_all.shape),
            big(*p_all.shape),
            pltpu.VMEM((batch, tok, width), F32),
            big(batch * tok, width),
            big(batch, n, tok, cols),
            big(batch, slot, cols),
            big(2, slot, slot),
            big(batch, slot, 3 * cols),
            big(batch, slot, width),
            big(n, 2, cols // 2, width),
            big(n, cols // 2, width),
            big(n - 1, cols // 2, width),
            big(n, cols // 2, width),
            big(batch, n - 1, tok, width),
            big(2, part, width),
            big(nz - 1, 2, part, width),
            pltpu.VMEM((16, width), F32),
            DMA((2, batch, n)),
            DMA((2, batch, n)),
            DMA((2, n)),
            DMA((2, 2)),
            DMA((2, nz)),
            DMA((12,)),
        ],
        compiler_params=pltpu.CompilerParams(
            collective_id=3, has_side_effects=True, vmem_limit_bytes=56 << 20
        ),
    )(x, dy, x1, z, dh2, a_own, wide, lens, scale, g, w_out, w_qkv, h_all, qkv_all, p_all)


def settle_kernel(
    n, nf, gq_ref, go_ref, gv_ref, vec_ref, g_ref, wide_ref, x1_hbm, y_hbm,
    q_out, o_out, v_out, vec_out, ffn_out, out_ref,
    pair_q, pair_v, sum_q, sum_v, far_q, far_o, far_v, last_q,
    vec_got, vec_sum, vec_far, vec_pair, x1_ref, y_own, y_got,
    p_sems, z_sems, d_sems, e_sems, y_sems, own_sems,
):
    me = lax.axis_index("dp")
    f = lax.axis_index("ffn")
    nz = nf // 2
    core = lax.rem(f, 2)
    row = lax.div(f, 2)
    cols = q_out.shape[2] // n
    _, part, width = g_ref.shape
    batch, tok = out_ref.shape[:2]
    peers = dp_peers(n, me) + ffn_peers(nf, f)
    greet(peers)
    band = at(me * tok, tok)
    loads = [
        pltpu.make_async_copy(x1_hbm, x1_ref, own_sems.at[5]),
        pltpu.make_async_copy(y_hbm.at[:, band, :], y_own, own_sems.at[6]),
    ]
    start(loads)
    meet(peers)
    pair = {"ffn": f ^ 1}
    pairs = [
        send(gq_ref.at[:, :, 1 - core], pair_q, p_sems, (0,), pair),
        send(gv_ref.at[:, 1 - core], pair_v, p_sems, (1,), pair),
    ]
    start(pairs)
    far = []
    for j in range(1, nz):
        source = go_ref.at[row ^ j, core]
        far.append(send(source, far_o.at[j - 1], z_sems, (j, 1), {"ffn": f ^ (2 * j)}))
    start(far)
    shares, halves = [], []
    for i, peer in enumerate(dp_peers(n, me), 1):
        shares.append(send(vec_ref.at[me ^ i], vec_got.at[i - 1], e_sems, (i, 0), peer))
    for i, peer in enumerate(dp_peers(n, me), 1):
        theirs = at((me ^ i) * (width // n), width // n)
        for k in range(2):
            source = g_ref.at[k, :, theirs]
            halves.append(send(source, ffn_out.at[k, me], e_sems, (i, 1 + k), peer))
    outs = [
        send(
            y_hbm.at[:, at((me ^ i) * tok, tok), :], y_got.at[i - 1], y_sems, (i,), peer
        )
        for i, peer in enumerate(dp_peers(n, me), 1)
    ]
    start(shares)
    start(halves)
    start(outs)
    mine = at(me * (width // n), width // n)
    own = [
        pltpu.make_async_copy(g_ref.at[k, :, mine], ffn_out.at[k, me], own_sems.at[3 + k])
        for k in range(2)
    ]
    start(own)
    wait(pairs)

    def add_pair(k, _):
        for d in range(n):
            total = gq_ref[d, k, core].astype(F32) + pair_q[d, k].astype(F32)
            sum_q[d, k] = total.astype(LOW)
        sum_v[k] = gv_ref[k, core] + pair_v[k]
        return 0

    lax.fori_loop(0, nz, add_pair, 0)
    wait(shares)
    total = vec_ref[me]
    for i in range(1, n):
        total = total + vec_got[i - 1]
    vec_sum[...] = total
    later = []
    for j in range(1, nz):
        peer = {"ffn": f ^ (2 * j)}
        theirs = row ^ j
        for k, piece, place in [
            (0, sum_q.at[:, theirs], far_q),
            (2, sum_v.at[theirs], far_v),
            (3, vec_sum, vec_far),
        ]:
            later.append(send(piece, place.at[j - 1], z_sems, (j, k), peer))
    start(later)
    wait(far + later)
    total = vec_sum[...]
    for j in range(1, nz):
        total = total + vec_far[j - 1]
    vec_out[...] = total
    vec_sum[...] = total
    last = [send(vec_sum, vec_pair, p_sems, (2,), pair)]
    for d in range(n):
        total = sum_q[d, row].astype(F32)
        for j in range(1, nz):
            total = total + far_q[j - 1, d].astype(F32)
        last_q[d] = total
    total = sum_v[row]
    for j in range(1, nz):
        total = total + far_v[j - 1]
    v_out[me] = total
    place = at(me * cols, cols)
    for i, peer in enumerate(dp_peers(n, me), 1):
        for k in range(3):
            source = last_q.at[me ^ i, :, k * cols : (k + 1) * cols]
            last.append(send(source, q_out.at[k, :, place], d_sems, (i, k), peer))
        last.append(send(v_out.at[me], v_out.at[me], d_sems, (i, 3), peer))
    own += [
        pltpu.make_async_copy(
            last_q.at[me, :, k * cols : (k + 1) * cols], q_out.at[k, :, place], own_sems.at[k]
        )
        for k in range(3)
    ]
    start(last + own[2:])
    total = go_ref[row, core].astype(F32)
    for j in range(1, nz):
        total = total + far_o[j - 1].astype(F32)
    o_out[...] = total
    wait(loads + outs)
    for micro in range(batch):
        total = x1_ref[micro] + y_own[micro].astype(F32) + wide_ref[9:10, :]
        for i in range(1, n):
            total = total + y_got[i - 1, micro].astype(F32)
        out_ref[micro] = total.astype(LOW)
    wait(last + own + halves)
    vec_out[...] += vec_pair[...]


def settle(gq, go, gv, vec, g, wide_rows, x1, y):
    n, nz, _, rows, wide = gq.shape
    width = go.shape[3]
    part = g.shape[1]
    tile = gv.shape[2:]
    block = vec.shape[1:]
    batch, tok, _ = x1.shape
    return pl.pallas_call(
        lambda *refs: settle_kernel(n, 2 * nz, *refs),
        name="settle",
        out_shape=(
            shape((3, rows, width), F32),
            shape((rows, width), F32),
            shape((n, *tile), F32),
            shape(block, F32),
            shape((2, n, part, width // n), LOW),
            shape(x1.shape, LOW),
        ),
        in_specs=[VMEM] * 6 + [ANY] * 2,
        out_specs=(VMEM,) * 6,
        scratch_shapes=[
            pltpu.VMEM((n, nz, rows, wide), LOW),
            pltpu.VMEM((nz, *tile), F32),
            pltpu.VMEM((n, nz, rows, wide), LOW),
            pltpu.VMEM((nz, *tile), F32),
            pltpu.VMEM((nz - 1, n, rows, wide), LOW),
            pltpu.VMEM((nz - 1, rows, width), LOW),
            pltpu.VMEM((nz - 1, *tile), F32),
            pltpu.VMEM((n, rows, wide), F32),
            pltpu.VMEM((n - 1, *block), F32),
            pltpu.VMEM(block, F32),
            pltpu.VMEM((nz - 1, *block), F32),
            pltpu.VMEM(block, F32),
            pltpu.VMEM(x1.shape, F32),
            pltpu.VMEM(x1.shape, LOW),
            pltpu.VMEM((n - 1, *x1.shape), LOW),
            DMA((2, 3)),
            DMA((2, nz, 4)),
            DMA((2, n, 4)),
            DMA((2, n, 3)),
            DMA((2, n)),
            DMA((7,)),
        ],
        compiler_params=pltpu.CompilerParams(
            collective_id=4, has_side_effects=True, vmem_limit_bytes=24 << 20
        ),
    )(gq, go, gv, vec, g, wide_rows, x1, y)


def on_device(
    tokens,
    seq_lens,
    qkv_weight,
    out_weight,
    head_scale,
    gains,
    biases,
    ffn_in,
    ffn_bias,
    mid_gain,
    mid_bias,
    ffn_out,
    out_cotangent,
):
    n = lax.axis_size("dp")
    nf = lax.axis_size("ffn")
    me = lax.axis_index("dp")
    f = lax.axis_index("ffn")
    batch, _, tok, width = tokens.shape
    heads = head_scale.shape[0]
    cols = width // n
    rows = qkv_weight.shape[1]
    hid = ffn_in.shape[1]
    part = hid // n
    ff = hid * nf

    def tiled(values):
        size = values.shape[1]
        spot = lax.rem(f, 128 // size) * size
        return lax.dynamic_update_slice(jnp.zeros((16, 128), LOW), values, (0, spot))

    vectors = lax.dynamic_index_in_dim(
        jnp.stack([ffn_bias, mid_gain, mid_bias]).reshape(3, n, part), me, 1, keepdims=False
    )
    x, dy = tokens[:, 0], out_cotangent[:, 0]
    kept = forward(
        x,
        qkv_weight,
        out_weight,
        jnp.stack([tiled(jnp.concatenate([gains, biases])), tiled(vectors)]),
        ffn_in.T.reshape(n, part, cols),
        ffn_out.reshape(n, part, cols),
        dy,
        seq_lens,
        head_scale,
        n,
        nf,
    )
    w_qkv = kept["w_hbm"].transpose(0, 1, 3, 2, 4).reshape(width, 3 * cols)
    w_out = kept["out_hbm"].reshape(width, width)
    h_all, qkv_all, p_all, a_own = kept["h_hbm"], kept["qkv_hbm"], kept["p_hbm"], kept["a_hbm"]
    z, x1, y, g, dh2, mid, wide = [
        kept[name] for name in ("z_hbm", "x1_hbm", "y_hbm", "g_hbm", "dh2_out", "vec_out", "wide")
    ]
    tokens_grad, gq, go, vec, g = back(
        x, dy, x1, z, dh2, a_own, wide, seq_lens, head_scale, g, w_out, w_qkv, h_all, qkv_all, p_all
    )
    nz = nf // 2
    qkv_grad, out_weight_grad, mid, vec, ffn, output = settle(
        gq.reshape(n, nz, 2, rows, 3 * cols),
        go.reshape(nz, 2, rows, width),
        mid.reshape(8, nz, 2, part).transpose(1, 2, 0, 3),
        vec,
        g,
        wide,
        x1,
        y,
    )
    mid = mid.transpose(1, 0, 2).reshape(8, hid)
    own = lax.dynamic_slice_in_dim(vec, f * rows, rows, 1)
    ffn = ffn.reshape(2, hid, cols)
    return (
        output[:, None],
        tokens_grad[:, None],
        qkv_grad,
        out_weight_grad,
        vec[10 : 10 + n, ::HDIM].reshape(heads),
        own[:3],
        own[3:10],
        ffn[0].T.astype(F32),
        mid[0],
        mid[1],
        mid[2],
        ffn[1].astype(F32),
    )


def solution(mesh):
    seqs = P(None, "ffn", "dp", None)
    wide = P(None, ("dp", "ffn"))
    hidden = P("ffn")
    return jax.shard_map(
        on_device,
        mesh=mesh,
        in_specs=(
            seqs,
            P(None, "ffn"),
            P(None, ("dp", "ffn"), None),
            P(("dp", "ffn"), None),
            P(),
            wide,
            wide,
            P("dp", "ffn"),
            hidden,
            hidden,
            hidden,
            P("ffn", "dp"),
            seqs,
        ),
        out_specs=(
            seqs,
            seqs,
            P(None, ("dp", "ffn"), None),
            P(("dp", "ffn"), None),
            P(),
            wide,
            wide,
            P("dp", "ffn"),
            hidden,
            hidden,
            hidden,
            P("ffn", "dp"),
        ),
        check_vma=False,
    )
```

```python
from types import SimpleNamespace

import jax
import jax.numpy as jnp
from jax import lax
from jax.experimental import pallas as pl
from jax.experimental.pallas import tpu as pltpu
from jax.sharding import PartitionSpec as P

HDIM = 64
EPS = 1e-05
LOW = jnp.bfloat16
F32 = jnp.float32
ANY = pl.BlockSpec(memory_space=pl.ANY)
VMEM = pl.BlockSpec(memory_space=pltpu.VMEM)
SMEM = pl.BlockSpec(memory_space=pltpu.SMEM)
MESH = pl.DeviceIdType.MESH
DMA = pltpu.SemaphoreType.DMA


def dot(left, right):
    return jnp.dot(left, right, preferred_element_type=F32)


def dot_nt(left, right):
    return lax.dot_general(left, right, (((1,), (1,)), ((), ())), preferred_element_type=F32)


def dot_tn(left, right):
    return lax.dot_general(left, right, (((0,), (0,)), ((), ())), preferred_element_type=F32)


def shape(dims, kind):
    return jax.ShapeDtypeStruct(tuple(dims), kind)


def at(start, size, unit=128):
    return pl.ds(pl.multiple_of(start, unit), size)


def send(src, dst, sems, index, where):
    return pltpu.make_async_remote_copy(
        src_ref=src,
        dst_ref=dst,
        send_sem=sems.at[(0, *index)],
        recv_sem=sems.at[(1, *index)],
        device_id=where,
        device_id_type=MESH,
    )


def greet(peers):
    barrier = pltpu.get_barrier_semaphore()
    for peer in peers:
        pl.semaphore_signal(barrier, inc=1, device_id=peer, device_id_type=MESH)


def meet(peers):
    pl.semaphore_wait(pltpu.get_barrier_semaphore(), len(peers))


def dp_peers(n, me):
    return [{"dp": me ^ i} for i in range(1, n)]


def ffn_peers(nf, f):
    return [{"ffn": f ^ (2 * j)} for j in range(1, nf // 2)] + [{"ffn": f ^ 1}]


def start(copies):
    for copy in copies:
        copy.start()


def wait(copies):
    for copy in copies:
        copy.wait()


class Line:
    def __init__(self, nf, f, items, hop_sems, side_sems):
        self.nz, self.core, self.q, self.f = nf // 2, lax.rem(f, 2), lax.div(f, 2), f
        self.items, self.hop_sems, self.side_sems = items, hop_sems, side_sems
        self.next = [1] * len(items)

    def copy(self, sems, k, t, came, way, first, target):
        source, place = self.items[k]
        index = self.f if first else 2 * (self.q - t * way) + self.core
        spot = place(index)
        side = 0 if way > 0 else 1
        return pltpu.make_async_remote_copy(
            src_ref=source if first else spot,
            dst_ref=spot,
            send_sem=sems.at[0, side, k, t],
            recv_sem=sems.at[1, side, k, came],
            device_id={"ffn": target},
            device_id_type=MESH,
        )

    def hop(self, k, t, way, first=False):
        return self.copy(self.hop_sems, k, t, t + 1, way, first, self.f + 2 * way)

    def arrival(self, k, t, way):
        return self.copy(self.hop_sems, k, t, t, way, False, self.f + 2 * way)

    def over(self, k, t, way, first=False):
        return self.copy(self.side_sems, k, t, t, way, first, self.f ^ 1)

    def onward(self, way):
        return self.q < self.nz - 1 if way > 0 else self.q > 0

    def has(self, t, way):
        return self.q - t >= 0 if way > 0 else self.q + t <= self.nz - 1

    def begin(self, *items):
        for k in items:
            for way in (1, -1):

                @pl.when(self.onward(way))
                def _():
                    self.hop(k, 0, way, True).start()

        for k in items:
            self.over(k, 0, 1, True).start()

    def step(self, k, t):
        for way in (1, -1):

            @pl.when(self.has(t, way) & self.onward(way))
            def _():
                self.arrival(k, t, way).wait_recv()
                self.hop(k, t, way).start()

        for way in (1, -1):

            @pl.when(self.has(t, way))
            def _():
                @pl.when(jnp.logical_not(self.onward(way)))
                def _():
                    self.arrival(k, t, way).wait_recv()

                self.over(k, t, way).start()

    def advance(self, *items):
        for k in items:
            if self.next[k] < self.nz:
                self.step(k, self.next[k])
                self.next[k] += 1

    def arrive(self, *items):
        begin = self.next[items[0]]

        def rest(t, _):
            for k in items:
                self.step(k, t)
            return 0

        lax.fori_loop(begin, self.nz, rest, 0)

        def close(t, _):
            for k in items:
                for way in (1, -1):

                    @pl.when(self.has(t, way))
                    def _():
                        self.over(k, t, way).wait_recv()

            return 0

        for k in items:
            self.over(k, 0, 1, True).wait_recv()
        lax.fori_loop(1, self.nz, close, 0)

    def finish(self, *items):
        for k in items:
            self.over(k, 0, 1, True).wait_send()
            for way in (1, -1):

                @pl.when(self.onward(way))
                def _():
                    self.hop(k, 0, way, True).wait_send()

        def close(t, _):
            for k in items:
                for way in (1, -1):

                    @pl.when(self.has(t, way))
                    def _():
                        self.over(k, t, way).wait_send()

                    @pl.when(self.has(t, way) & self.onward(way))
                    def _():
                        self.hop(k, t, way).wait_send()

            return 0

        lax.fori_loop(1, self.nz, close, 0)


def line_meet(n, nf, me, f):
    barrier = pltpu.get_barrier_semaphore()
    q, nz = lax.div(f, 2), nf // 2
    greet(dp_peers(n, me) + [{"ffn": f ^ 1}])

    @pl.when(q < nz - 1)
    def _():
        greet([{"ffn": f + 2}])

    @pl.when(q > 0)
    def _():
        greet([{"ffn": f - 2}])

    count = n + jnp.where(q < nz - 1, 1, 0) + jnp.where(q > 0, 1, 0)
    pl.semaphore_wait(barrier, count)


def normal(values):
    center = values - jnp.mean(values, axis=-1, keepdims=True)
    inverse = lax.rsqrt(jnp.mean(center * center, axis=-1, keepdims=True) + EPS)
    return center * inverse, inverse


def normal_back(grad, normed, inverse):
    return inverse * (
        grad
        - jnp.mean(grad, axis=-1, keepdims=True)
        - normed * jnp.mean(grad * normed, axis=-1, keepdims=True)
    )


def column_sum(values):
    return jnp.sum(values, axis=0, keepdims=True)


def launch(body, name, inputs, outputs, scratch, number, limit):
    names = [*inputs, *outputs, *scratch]
    results = pl.pallas_call(
        lambda *refs: body(SimpleNamespace(**dict(zip(names, refs)))),
        name=name,
        out_shape=tuple(kind for kind, _ in outputs.values()),
        in_specs=[spec for _, spec in inputs.values()],
        out_specs=tuple(spec for _, spec in outputs.values()),
        scratch_shapes=list(scratch.values()),
        compiler_params=pltpu.CompilerParams(
            collective_id=number, has_side_effects=True, vmem_limit_bytes=limit << 20
        ),
    )(*[value for value, _ in inputs.values()])
    return dict(zip(outputs, results))


def forward_kernel(n, nf, part, r):
    me = lax.axis_index("dp")
    f = lax.axis_index("ffn")
    core, nz = lax.rem(f, 2), nf // 2
    batch, tok, width = r.x.shape
    rows_each = r.wout.shape[0]
    cols = width // n
    pairs = cols // 128
    slot = n * tok
    hid = nf * part
    ff = n * hid
    step = 256
    peers = dp_peers(n, me)
    pair = {"ffn": f ^ 1}
    place = at(me * cols, cols)
    band = at(me * tok, tok)

    own = [
        pltpu.make_async_copy(r.qkv.at[:, :, place], r.stage.at[:, me], r.own_sems.at[0]),
        pltpu.make_async_copy(r.small.at[0], r.small_stage.at[me], r.own_sems.at[1]),
        pltpu.make_async_copy(r.small.at[1], r.small_stage.at[n], r.own_sems.at[2]),
        pltpu.make_async_copy(r.wout, r.out_stage.at[me], r.own_sems.at[3]),
        pltpu.make_async_copy(r.first.at[me], r.first_stage.at[:, place], r.own_sems.at[4]),
        pltpu.make_async_copy(r.second.at[me], r.second_stage.at[:, place], r.own_sems.at[5]),
        pltpu.make_async_copy(r.x, r.x_all.at[me], r.own_sems.at[6]),
        pltpu.make_async_copy(r.dy, r.dy_all.at[:, band, :], r.own_sems.at[7]),
    ]
    start(own)
    line_meet(n, nf, me, f)

    def to_peers(make):
        return [make(i, peer) for i, peer in enumerate(peers, 1)]

    blocks = to_peers(
        lambda i, peer: send(
            r.qkv.at[:, :, at((me ^ i) * cols, cols)], r.stage.at[:, me], r.w_sems, (i, 0), peer
        )
    )
    smalls = to_peers(
        lambda i, peer: send(r.small.at[0], r.small_stage.at[me], r.w_sems, (i, 1), peer)
    )
    outs = to_peers(lambda i, peer: send(r.wout, r.out_stage.at[me], r.w_sems, (i, 2), peer))
    firsts = to_peers(
        lambda i, peer: send(
            r.first.at[me ^ i], r.first_stage.at[:, place], r.w_sems, (i, 3), peer
        )
    )
    seconds = to_peers(
        lambda i, peer: send(
            r.second.at[me ^ i], r.second_stage.at[:, place], r.w_sems, (i, 4), peer
        )
    )

    def x_copies(micro):
        return to_peers(
            lambda i, peer: send(r.x.at[micro], r.x_all.at[me, micro], r.x_sems, (micro, i), peer)
        )

    def y_copies(micro):
        return to_peers(
            lambda i, peer: send(
                r.dy.at[micro], r.dy_all.at[micro, band, :], r.y_sems, (micro, i), peer
            )
        )

    start(blocks + smalls)
    start(x_copies(0))
    start(outs + firsts)
    start(x_copies(1))
    start(seconds)
    start(y_copies(0))
    line = Line(
        nf,
        f,
        [
            (r.stage, lambda index: r.w_all.at[:, :, index]),
            (r.small_stage, lambda index: r.small_all.at[index]),
            (r.out_stage, lambda index: r.out_all.at[:, index]),
            (r.first_stage, lambda index: r.w1.at[index]),
            (r.second_stage, lambda index: r.w2.at[index]),
        ],
        r.hop_sems,
        r.side_sems,
    )
    mine = [
        pltpu.make_async_copy(source, spot(f), r.own_sems.at[8 + k])
        for k, (source, spot) in enumerate(line.items)
    ]
    wait(blocks + smalls + own[:3])
    line.begin(0, 1)
    start(mine[:2])
    line.advance(0, 1)
    line.advance(0, 1)
    wait(outs + own[3:4])
    line.begin(2)
    start(mine[2:3])
    line.arrive(0, 1)
    wait(firsts + own[4:5])
    line.begin(3)
    start(mine[3:4])
    wait(mine[:2] + own[6:7])

    def lay_out(out_ref, index, begin, size):
        together = 128 // size
        for b in range(nf // together):
            total = r.small_all[b * together, index].astype(F32)
            for k in range(1, together):
                total = total + r.small_all[b * together + k, index].astype(F32)
            out_ref[:, begin + b * 128 : begin + (b + 1) * 128] = total

    for d in range(n):
        lay_out(r.wide, d, d * nf * rows_each, rows_each)
    lay_out(r.mids, n, 0, part)

    gain, shift = r.wide[0:1, :], r.wide[3:4, :]
    bias_q, bias_v = r.wide[4:5, place], r.wide[5:6, place]
    left = lax.broadcasted_iota(jnp.int32, (1, 128), 1) < HDIM

    def block_copies(micro):
        return to_peers(
            lambda i, peer: send(
                r.a_all.at[micro, me ^ i], r.a_own.at[micro, :, place], r.a_sems, (micro, i), peer
            )
        )

    def keep_copies(micro):
        return [
            pltpu.make_async_copy(source.at[micro], out.at[micro], r.keep_sems.at[micro, k])
            for k, (source, out) in enumerate(
                [(r.h_all, r.h_hbm), (r.qkv_all, r.qkv_hbm), (r.p_all, r.p_hbm)]
            )
        ]

    def after_first():
        line.advance(2)

    def after_second():
        line.advance(3)

    def after_third():
        line.advance(2)
        wait(seconds + own[5:6])
        line.begin(4)
        start(mine[4:5])

    def after_last():
        start(y_copies(1))
        line.advance(3)

    def attend(index, _):
        micro, two = lax.div(index, pairs), lax.rem(index, pairs)

        @pl.when(two == 0)
        def _():
            wait(x_copies(micro))

            def norm_rows(d, _):
                values, _ = normal(r.x_all[d, micro].astype(F32))
                r.h_all[micro, at(d * tok, tok), :] = (values * gain + shift).astype(LOW)
                return 0

            lax.fori_loop(0, n, norm_rows, 0)
            for k, bias in enumerate((bias_q, None, bias_v)):
                weight = r.w_all[k].reshape(width, cols)
                value = dot(r.h_all[micro], weight)
                if bias is not None:
                    value = value + bias
                r.qkv_all[micro, :, k * cols : (k + 1) * cols] = value.astype(LOW)

        length = r.lens[micro, 0]

        def column(k):
            return at(k * cols + two * 128, 128)

        head = two * 2
        scales = jnp.where(
            left, r.scale[me * 2 * pairs + head], r.scale[me * 2 * pairs + head + 1]
        )
        for block in range(n):
            end = (block + 1) * tok
            q = r.qkv_all[micro, block * tok : end, column(0)] * HDIM ** (-0.5)
            k = r.qkv_all[micro, :end, column(1)]
            v = r.qkv_all[micro, :end, column(2)]
            key = lax.broadcasted_iota(jnp.int32, (tok, end), 1)
            query = lax.broadcasted_iota(jnp.int32, (tok, end), 0) + block * tok
            mask = (key <= query) & (key < length)
            out = []
            for side in range(2):
                mine_ = left if side == 0 else jnp.logical_not(left)
                scores = dot_nt(jnp.where(mine_, q, jnp.zeros_like(q)), k)
                scores = jnp.where(mask, scores, -1e30)
                expo = jnp.exp(scores - jnp.max(scores, axis=-1, keepdims=True))
                probs = expo * (1.0 / jnp.sum(expo, axis=-1, keepdims=True))
                probs = probs.astype(LOW)
                r.p_all[micro, head + side, block * tok : end, :end] = probs
                out.append(dot(probs, v))
            joined = jnp.where(left, out[0], out[1]) * scales
            r.a_all[micro, block, :, at(two * 128, 128)] = joined.astype(LOW)

        @pl.when(two == pairs - 1)
        def _():
            start(block_copies(micro))
            start(keep_copies(micro))
            r.a_own[micro, :, place] = r.a_all[micro, me]

        work = [after_first, after_second, after_third, after_last]
        for k, act in enumerate(work[: batch * pairs]):
            pl.when(index == k)(act)
        return 0

    lax.fori_loop(0, batch * pairs, attend, 0)

    line.arrive(2)
    wait(mine[2:3])
    late = [
        pltpu.make_async_copy(source, target, r.own_sems.at[13 + k])
        for k, (source, target) in enumerate(
            [(r.w_all, r.w_hbm), (r.out_all, r.out_hbm), (r.z, r.z_hbm), (r.x1, r.x1_hbm),
             (r.a_own, r.a_hbm), (r.y, r.y_hbm), (r.pair_got, r.g_hbm), (r.dh2, r.dh2_hbm)]
        )
    ]
    start(late[:2])

    def row_copies(micro):
        return to_peers(
            lambda i, peer: send(
                r.h2_own.at[micro], r.h2_all.at[micro, band, :], r.h_sems, (micro, i), peer
            )
        )

    for micro in range(batch):
        wait(block_copies(micro))
        z = dot(r.a_own[micro], r.out_all[...].reshape(width, width)) + r.wide[6:7, :]
        r.z[micro] = z
        values, _ = normal(z)
        x1 = r.x_all[me, micro].astype(F32) + values * r.wide[1:2, :] + r.wide[7:8, :]
        r.x1[micro] = x1
        values, _ = normal(x1)
        r.h2_own[micro] = (values * r.wide[2:3, :] + r.wide[8:9, :]).astype(LOW)
        start(row_copies(micro))
        r.h2_all[micro, band, :] = r.h2_own[micro]
    start(late[2:5])
    line.advance(4)
    line.arrive(3)
    wait(mine[3:4])

    def weights(ref, c):
        count = step // part
        return ref[pl.ds(c * count, count)].reshape(step, width)

    def w_columns(ref, columns):
        return ref[:, :, columns].reshape(hid, step)

    def sum_copies(micro):
        return to_peers(
            lambda i, peer: send(
                r.sums.at[micro], r.sums_all.at[micro, me], r.s_sems, (micro, i), peer
            )
        )

    def grad_copies(micro):
        return to_peers(
            lambda i, peer: send(
                r.dh2_all.at[micro, at((me ^ i) * tok, tok), :],
                r.dh2_got.at[micro, i - 1],
                r.r_sems,
                (micro, i),
                peer,
            )
        )

    def fold(values):
        total = values[:, :128]
        for k in range(1, step // 128):
            total = total + values[:, k * 128 : (k + 1) * 128]
        return total

    def units(micro):
        wait(row_copies(micro))

        def chunk(c, totals):
            rows = at(c * step, step)
            u = dot_nt(r.h2_all[micro], weights(r.w1, c)) + r.mids[0:1, rows]
            phi = 0.5 + 0.5 * lax.erf(u * (0.5**0.5))
            value = u * phi
            r.act[micro, :, rows] = value
            r.slope[micro, :, rows] = phi + u * jnp.exp(u * u * -0.5) * 0.3989422804014327
            return totals[0] + fold(value), totals[1] + fold(value * value)

        zero = jnp.zeros((slot, 128), F32)
        totals = lax.fori_loop(0, hid // step, chunk, (zero,) * 2)
        for k in range(2):
            r.sums[micro, k : k + 1, :] = column_sum(totals[k].T)

    def cotangents(micro):
        wait(y_copies(micro))
        valid = lax.broadcasted_iota(jnp.int32, (slot, 1), 0) < r.lens[micro, 0]
        rows = r.dy_all[micro]
        r.dy_all[micro] = jnp.where(valid, rows, jnp.zeros_like(rows))

        def chunk(c, totals):
            rows = at(c * step, step)
            dm = dot_nt(r.dy_all[micro], weights(r.w2, c))
            r.dmix[micro, :, rows] = dm
            dn = dm * r.mids[1:2, rows]
            return totals[0] + fold(dn), totals[1] + fold(dn * r.act[micro, :, rows])

        zero = jnp.zeros((slot, 128), F32)
        totals = lax.fori_loop(0, hid // step, chunk, (zero,) * 2)
        for k in range(2):
            r.sums[micro, 2 + k : 3 + k, :] = column_sum(totals[k].T)
        r.sums[micro, 4:8, :] = jnp.zeros((4, slot), F32)
        start(sum_copies(micro))

    def passes(micro, _):
        units(micro)

        @pl.when(micro == 0)
        def _():
            line.arrive(4)
            wait(mine[4:5] + own[7:8])

        cotangents(micro)
        return 0

    lax.fori_loop(0, batch, passes, 0)
    r.vec[...] = jnp.zeros_like(r.vec)

    def second_pass(micro, _):
        wait(sum_copies(micro))
        r.sums_all[micro, me] = r.sums[micro]
        total = r.sums_all[micro, 0]
        for d in range(1, n):
            total = total + r.sums_all[micro, d]
        total = total * (1.0 / ff)
        mean = total[0:1]
        inverse = lax.rsqrt(total[1:2] - mean * mean + EPS)
        back = total[2:3]
        cross = inverse * (total[3:4] - mean * back)
        table = jnp.concatenate([mean, inverse, back, cross] * 32, axis=0).T
        mean, inverse, back, cross = [table[:, k : k + 1] for k in range(4)]
        rows_of = at(micro * slot, slot)

        def chunk(c, _):
            rows = at(c * step, step)
            normed = (r.act[micro, :, rows] - mean) * inverse
            dm = r.dmix[micro, :, rows]
            gain = r.mids[1:2, rows]
            r.mixed[rows_of, rows] = (normed * gain + r.mids[2:3, rows]).astype(LOW)
            df = inverse * (dm * gain - back - normed * cross)
            low = (df * r.slope[micro, :, rows]).astype(LOW)
            r.du[rows_of, rows] = low
            r.vec[0:1, rows] += column_sum(low.astype(F32))
            r.vec[1:2, rows] += column_sum(dm * normed)
            r.vec[2:3, rows] += column_sum(dm)
            return 0

        lax.fori_loop(0, hid // step, chunk, 0)

        def back_rows(c, _):
            columns = at(c * step, step)
            value = dot(r.du[rows_of, :], w_columns(r.w1, columns))
            r.dh2_all[micro, :, columns] = value.astype(LOW)
            return 0

        lax.fori_loop(0, width // step, back_rows, 0)
        start(grad_copies(micro))
        return 0

    lax.fori_loop(0, batch, second_pass, 0)
    each = step // part // 2

    def pair_copies(c):
        copies = []
        for k in range(each):
            index = c * (2 * each) + 2 * k
            for w in range(2):
                copies.append(
                    send(
                        r.grads.at[w, index + 1 - core],
                        r.pair_got.at[w, c * each + k],
                        r.p_sems,
                        (c, k, w),
                        pair,
                    )
                )
        return copies

    def weight_grads(c, _):
        rows = at(c * step, step)
        h2 = r.h2_all[...].reshape(batch * slot, width)
        dy = r.dy_all[...].reshape(batch * slot, width)
        first = dot_tn(r.du[:, rows], h2).astype(LOW)
        second = dot_tn(r.mixed[:, rows], dy).astype(LOW)
        for k in range(step // part):
            r.grads[0, c * (step // part) + k] = first[k * part : (k + 1) * part]
            r.grads[1, c * (step // part) + k] = second[k * part : (k + 1) * part]
        start(pair_copies(c))
        return 0

    lax.fori_loop(0, hid // step, weight_grads, 0)

    def out_rows(c, _):
        columns = at(c * step, step)
        for micro in range(batch):
            value = dot(r.mixed[micro * slot : (micro + 1) * slot, :], w_columns(r.w2, columns))
            r.y[micro, :, columns] = value.astype(LOW)
        return 0

    lax.fori_loop(0, width // step, out_rows, 0)
    start(late[5:6])

    def pair_sum(c, _):
        wait(pair_copies(c))
        for k in range(each):
            for w in range(2):
                total = r.grads[w, c * (2 * each) + 2 * k + core].astype(F32)
                total = total + r.pair_got[w, c * each + k].astype(F32)
                r.pair_got[w, c * each + k] = total.astype(LOW)
        return 0

    lax.fori_loop(0, hid // step, pair_sum, 0)
    start(late[6:7])
    for k in range(nf):
        r.mid[k // 2, k % 2] = r.vec[:, k * part : (k + 1) * part]
    line.finish(0, 1, 2, 3, 4)
    for micro in range(batch):
        wait(keep_copies(micro))
    for micro in range(batch):
        wait(grad_copies(micro))
        total = r.dh2_all[micro, band, :].astype(F32)
        for i in range(1, n):
            total = total + r.dh2_got[micro, i - 1].astype(F32)
        r.dh2[micro] = total
    start(late[7:])
    wait(late)


def forward(x, qkv, wout, small, first, second, dy, lens, scale, n, nf):
    batch, tok, width = x.shape
    rows = wout.shape[0]
    part = first.shape[1]
    cols = width // n
    slot, hid = n * tok, nf * part
    heads = cols // HDIM

    def low(*dims):
        return pltpu.VMEM(dims, LOW)

    def full(*dims):
        return pltpu.VMEM(dims, F32)

    inputs = {
        name: (value, ANY)
        for name, value in zip(
            ("x", "qkv", "wout", "small", "first", "second", "dy"),
            (x, qkv, wout, small, first, second, dy),
        )
    }
    inputs["lens"] = (lens, SMEM)
    inputs["scale"] = (scale, SMEM)
    outputs = {
        "wide": (shape((16, width), F32), VMEM),
        "w_hbm": (shape((3, n, nf, rows, cols), LOW), ANY),
        "out_hbm": (shape((n, nf, rows, width), LOW), ANY),
        "h_hbm": (shape((batch, slot, width), LOW), ANY),
        "qkv_hbm": (shape((batch, slot, 3 * cols), LOW), ANY),
        "p_hbm": (shape((batch, heads, slot, slot), LOW), ANY),
        "a_hbm": (shape((batch, tok, width), LOW), ANY),
        "z_hbm": (shape((batch, tok, width), F32), ANY),
        "x1_hbm": (shape((batch, tok, width), F32), ANY),
        "y_hbm": (shape((batch, slot, width), LOW), ANY),
        "g_hbm": (shape((2, nf // 2, part, width), LOW), ANY),
        "dh2_hbm": (shape((batch, tok, width), F32), ANY),
        "mid": (shape((nf // 2, 2, 8, part), F32), VMEM),
    }
    scratch = {
        "mids": full(16, hid),
        "dh2": full(batch, tok, width),
        "vec": full(8, hid),
        "stage": low(3, n, rows, cols),
        "small_stage": low(n + 1, *small.shape[1:]),
        "out_stage": low(n, rows, width),
        "first_stage": low(part, width),
        "second_stage": low(part, width),
        "small_all": low(nf, n + 1, *small.shape[1:]),
        "w_all": low(3, n, nf, rows, cols),
        "out_all": low(n, nf, rows, width),
        "w1": low(nf, part, width),
        "w2": low(nf, part, width),
        "x_all": low(n, batch, tok, width),
        "dy_all": low(batch, slot, width),
        "h_all": low(batch, slot, width),
        "qkv_all": low(batch, slot, 3 * cols),
        "p_all": low(batch, heads, slot, slot),
        "a_all": low(batch, n, tok, cols),
        "a_own": low(batch, tok, width),
        "z": full(batch, tok, width),
        "x1": full(batch, tok, width),
        "h2_own": low(batch, tok, width),
        "h2_all": low(batch, slot, width),
        "act": full(batch, slot, hid),
        "slope": full(batch, slot, hid),
        "dmix": full(batch, slot, hid),
        "mixed": low(batch * slot, hid),
        "du": low(batch * slot, hid),
        "sums": full(batch, 8, slot),
        "sums_all": full(batch, n, 8, slot),
        "dh2_all": low(batch, slot, width),
        "dh2_got": low(batch, n - 1, tok, width),
        "y": low(batch, slot, width),
        "grads": low(2, nf, part, width),
        "pair_got": low(2, nf // 2, part, width),
        "w_sems": DMA((2, n, 5)),
        "x_sems": DMA((2, batch, n)),
        "y_sems": DMA((2, batch, n)),
        "a_sems": DMA((2, batch, n)),
        "h_sems": DMA((2, batch, n)),
        "s_sems": DMA((2, batch, n)),
        "r_sems": DMA((2, batch, n)),
        "p_sems": DMA((2, hid // 256, 128 // part, 2)),
        "hop_sems": DMA((2, 2, 5, nf // 2)),
        "side_sems": DMA((2, 2, 5, nf // 2)),
        "keep_sems": DMA((batch, 3)),
        "own_sems": DMA((21,)),
    }
    return launch(
        lambda r: forward_kernel(n, nf, part, r), "forward", inputs, outputs, scratch, 0, 63
    )


def backward_kernel(n, nf, r):
    me = lax.axis_index("dp")
    f = lax.axis_index("ffn")
    core, row, nz = lax.rem(f, 2), lax.div(f, 2), nf // 2
    batch, tok, width = r.dx.shape
    slot = n * tok
    cols = width // n
    rows_each = r.o_out.shape[0]
    pairs = cols // 128
    heads = cols // HDIM
    share = width // n
    step = 256
    peers = dp_peers(n, me)
    pair = {"ffn": f ^ 1}
    everyone = peers + ffn_peers(nf, f)
    greet(everyone)
    band = at(me * tok, tok)
    place = at(me * cols, cols)
    loads = [
        pltpu.make_async_copy(source, target, r.own_sems.at[k])
        for k, (source, target) in enumerate(
            [(r.x1_hbm, r.x1), (r.dh2_hbm, r.dh2), (r.dy_hbm, r.dy), (r.z_hbm, r.z),
             (r.out_hbm, r.wout), (r.a_hbm, r.a), (r.qkv_hbm, r.qkv_all), (r.p_hbm, r.p_all),
             (r.w_hbm, r.w_qkv), (r.h_hbm, r.h_all), (r.x_hbm, r.x), (r.g_hbm.at[:, row], r.g_own),
             (r.y_hbm.at[:, band, :], r.y_own)]
        )
    ]
    start(loads)
    r.vec[...] = jnp.zeros_like(r.vec)
    wait(loads[:4])
    for micro in range(batch):
        normed, inverse = normal(r.x1[micro])
        grad = r.dh2[micro]
        r.vec[2:3, :] += column_sum(grad * normed)
        r.vec[8:9, :] += column_sum(grad)
        valid = lax.broadcasted_iota(jnp.int32, (tok, 1), 0) + me * tok < r.lens[micro, 0]
        dy = jnp.where(valid, r.dy[micro].astype(F32), 0.0)
        r.vec[9:10, :] += column_sum(dy)
        grad = dy + normal_back(grad * r.wide[2:3, :], normed, inverse)
        r.dx1[micro] = grad
        normed, inverse = normal(r.z[micro])
        r.vec[1:2, :] += column_sum(grad * normed)
        r.vec[7:8, :] += column_sum(grad)
        low = normal_back(grad * r.wide[1:2, :], normed, inverse).astype(LOW)
        r.vec[6:7, :] += column_sum(low.astype(F32))
        r.dz[micro * tok : (micro + 1) * tok, :] = low
    wait(loads[4:5])
    for d in range(n):
        grad = dot_nt(r.dz[...], r.wout[d].reshape(cols, width))
        lane = lax.broadcasted_iota(jnp.int32, (1, cols), 1) // HDIM
        scales = jnp.zeros((1, cols), F32)
        for head in range(heads):
            scales = jnp.where(lane == head, r.scale[d * heads + head], scales)
        grad = (grad * scales).astype(LOW)
        for micro in range(batch):
            r.do_own[micro, d] = grad[micro * tok : (micro + 1) * tok]
    meet(everyone)

    def to_peers(make):
        return [make(i, peer) for i, peer in enumerate(peers, 1)]

    def along(make):
        return [make(j, {"ffn": f ^ (2 * j)}) for j in range(1, nz)]

    def head_copies(micro):
        return to_peers(
            lambda i, peer: send(
                r.do_own.at[micro, me ^ i], r.do_all.at[micro, band, :], r.o_sems, (micro, i), peer
            )
        )

    def row_copies(micro):
        return to_peers(
            lambda i, peer: send(
                r.dh_all.at[micro, at((me ^ i) * tok, tok), :],
                r.dh_got.at[micro, i - 1],
                r.h_sems,
                (micro, i),
                peer,
            )
        )

    def out_copies(micro):
        return to_peers(
            lambda i, peer: send(
                r.y_hbm.at[micro, at((me ^ i) * tok, tok), :],
                r.y_got.at[micro, i - 1],
                r.y_sems,
                (micro, i),
                peer,
            )
        )

    pair_o = send(r.go_all.at[:, 1 - core], r.go_pair, r.p_sems, (0,), pair)
    pair_v = send(r.mid.at[:, 1 - core], r.mid_pair, r.p_sems, (1,), pair)
    pair_vec = send(r.vec_sum, r.vec_pair, r.p_sems, (2,), pair)

    def pair_q(d):
        return send(r.gq_all.at[d, 1 - core], r.gq_pair.at[d], r.q_sems, (d,), pair)

    weight_copies = to_peers(
        lambda i, peer: send(r.go_half.at[me ^ i], r.go_got.at[i - 1], r.e_sems, (i, 0), peer)
    )
    shares = to_peers(
        lambda i, peer: send(r.vec_part.at[me ^ i], r.vec_got.at[i - 1], r.e_sems, (i, 1), peer)
    )
    ffn_copies = along(
        lambda j, peer: send(r.g_hbm.at[:, row ^ j], r.g_got.at[j - 1], r.z_sems, (j, 0), peer)
    )
    far_o = along(
        lambda j, peer: send(r.go_sum.at[row ^ j], r.o_far.at[j - 1], r.z_sems, (j, 1), peer)
    )
    far_q = along(
        lambda j, peer: send(r.gq_sum.at[:, row ^ j], r.q_far.at[j - 1], r.z_sems, (j, 2), peer)
    )
    far_v = along(
        lambda j, peer: send(r.mid_sum.at[row ^ j], r.v_far.at[j - 1], r.z_sems, (j, 3), peer)
    )
    far_vec = along(lambda j, peer: send(r.vec_mine, r.vec_far.at[j - 1], r.z_sems, (j, 4), peer))
    for micro in range(batch):
        start(head_copies(micro))
        r.do_all[micro, band, :] = r.do_own[micro, me]
    pair_v.start()
    start(ffn_copies)
    start(out_copies(0))
    wait(loads[5:6])

    def out_weight(d, _):
        a = r.a[:, :, at(d * cols, cols)].reshape(batch * tok, cols)
        grad = dot_tn(a, r.dz[...]).astype(LOW)
        for k in range(nf):
            r.go_all[d, k % 2, k // 2] = grad[k * rows_each : (k + 1) * rows_each]
        return 0

    lax.fori_loop(0, n, out_weight, 0)
    pair_o.start()
    wait(loads[6:10])
    left = lax.broadcasted_iota(jnp.int32, (1, 128), 1) < HDIM

    def one(micro, _):
        wait(head_copies(micro))

        def pair_of(two, _):
            def column(k):
                return at(k * cols + two * 128, 128)

            head = two * 2
            own_cols = at(two * 128, 128)
            sums = []
            k = r.qkv_all[micro, :, column(1)]
            v = r.qkv_all[micro, :, column(2)]
            for block in range(n):
                end = (block + 1) * tok
                rows = slice(block * tok, end)
                do = r.do_all[micro, rows, own_cols]
                out = []
                for side in range(2):
                    mine = left if side == 0 else jnp.logical_not(left)
                    probs = r.p_all[micro, head + side, rows, :end].astype(F32)
                    dp = dot_nt(jnp.where(mine, do, jnp.zeros_like(do)), v[:end])
                    delta = jnp.sum(probs * dp, axis=-1, keepdims=True)
                    ds = (probs * (dp - delta)).astype(LOW)
                    r.ds_all[side, rows, :end] = ds
                    out.append(dot(ds, k[:end]))
                    sums.append(jnp.sum(delta, axis=0, keepdims=True))
                dq = jnp.where(left, out[0], out[1]) * HDIM ** (-0.5)
                r.dqkv[micro, rows, column(0)] = dq.astype(LOW)
            q = r.qkv_all[micro, :, column(0)]
            do = r.do_all[micro, :, own_cols]
            for block in range(n):
                begin = block * tok
                keys = slice(begin, begin + tok)
                dk = [dot_tn(r.ds_all[side, begin:, keys], q[begin:]) for side in range(2)]
                dv = [
                    dot_tn(r.p_all[micro, head + side, begin:, keys], do[begin:])
                    for side in range(2)
                ]
                dk = jnp.where(left, dk[0], dk[1]) * HDIM ** (-0.5)
                r.dqkv[micro, keys, column(1)] = dk.astype(LOW)
                r.dqkv[micro, keys, column(2)] = jnp.where(left, dv[0], dv[1]).astype(LOW)
            spot = me * heads + head
            first = sum(sums[2::2], sums[0]) * (1.0 / r.scale[spot])
            second = sum(sums[3::2], sums[1]) * (1.0 / r.scale[spot + 1])
            r.vec[10:11, at(me * cols + two * 128, 128)] += jnp.where(left, first, second)
            return 0

        lax.fori_loop(0, pairs, pair_of, 0)

        @pl.when(micro == 0)
        def _():
            pair_o.wait()
            for d in range(n):
                total = r.go_all[d, core].astype(F32) + r.go_pair[d].astype(F32)
                r.go_half[d] = total.astype(LOW)
            start(weight_copies)

        def back_rows(d, _):
            total = dot_nt(r.dqkv[micro, :, :cols], r.w_qkv[0, d].reshape(cols, cols))
            for k in (1, 2):
                total = total + dot_nt(
                    r.dqkv[micro, :, k * cols : (k + 1) * cols],
                    r.w_qkv[k, d].reshape(cols, cols),
                )
            r.dh_all[micro, :, at(d * cols, cols)] = total.astype(LOW)
            return 0

        lax.fori_loop(0, n, back_rows, 0)
        start(row_copies(micro))
        grads = r.dqkv[micro].astype(F32)
        r.vec[4:5, place] += column_sum(grads[:, :cols])
        r.vec[5:6, place] += column_sum(grads[:, 2 * cols :])
        return 0

    lax.fori_loop(0, batch, one, 0)
    for micro in range(1, batch):
        start(out_copies(micro))

    def weight_grads(d, _):
        h = r.h_all[:, :, at(d * cols, cols)].reshape(batch * slot, cols)
        grad = dot_tn(h, r.dqkv[...].reshape(batch * slot, 3 * cols)).astype(LOW)
        for k in range(nf):
            r.gq_all[d, k % 2, k // 2] = grad[k * rows_each : (k + 1) * rows_each]
        pair_q(d).start()
        return 0

    lax.fori_loop(0, n, weight_grads, 0)
    wait(weight_copies)
    for k in range(nz):
        total = r.go_half[me, k].astype(F32)
        for i in range(1, n):
            total = total + r.go_got[i - 1, k].astype(F32)
        r.go_sum[k] = total.astype(LOW)
    start(far_o)
    pair_v.wait()
    for k in range(nz):
        r.mid_sum[k] = r.mid[k, core] + r.mid_pair[k]
    start(far_v)

    def add_pair(d, _):
        pair_q(d).wait()
        total = r.gq_all[d, core].astype(F32) + r.gq_pair[d].astype(F32)
        r.gq_sum[d] = total.astype(LOW)
        return 0

    lax.fori_loop(0, n, add_pair, 0)
    start(far_q)
    wait(loads[10:])
    for micro in range(batch):
        wait(row_copies(micro))
        grad = r.dh_all[micro, band, :].astype(F32)
        for i in range(1, n):
            grad = grad + r.dh_got[micro, i - 1].astype(F32)
        normed, inverse = normal(r.x[micro].astype(F32))
        r.vec[0:1, :] += column_sum(grad * normed)
        r.vec[3:4, :] += column_sum(grad)
        r.dx[micro] = r.dx1[micro] + normal_back(grad * r.wide[0:1, :], normed, inverse)
    spot = lax.broadcasted_iota(jnp.int32, (16, 1), 0)
    own_scales = r.vec[10:11, place]
    for d in range(n):
        block = jnp.where(spot >= 10, 0.0, r.vec[:, d * share : (d + 1) * share])
        r.vec_part[d] = jnp.where(spot == 10 + me, own_scales, block)
    start(shares)
    for micro in range(batch):
        wait(out_copies(micro))
        total = r.x1[micro] + r.y_own[micro].astype(F32) + r.wide[9:10, :]
        for i in range(1, n):
            total = total + r.y_got[micro, i - 1].astype(F32)
        r.out[micro] = total.astype(LOW)
    wait(shares)
    total = r.vec_part[me]
    for i in range(1, n):
        total = total + r.vec_got[i - 1]
    r.vec_mine[...] = total
    start(far_vec)
    wait(ffn_copies)
    halves = []
    for w in range(2):
        total = r.g_own[w].astype(F32)
        for j in range(1, nz):
            total = total + r.g_got[j - 1, w].astype(F32)
        r.g_sum[w] = total.astype(LOW)
        for i, peer in enumerate(peers, 1):
            source = r.g_sum.at[w, :, at((me ^ i) * cols, cols)]
            halves.append(send(source, r.ffn_out.at[w, me], r.d_sems, (i, 4 + w), peer))
    own = [
        pltpu.make_async_copy(r.g_sum.at[w, :, place], r.ffn_out.at[w, me], r.own_sems.at[13 + w])
        for w in range(2)
    ]
    start(halves + own)
    wait(far_o)
    total = r.go_sum[row].astype(F32)
    for j in range(1, nz):
        total = total + r.o_far[j - 1].astype(F32)
    r.o_out[...] = total
    wait(far_v)
    total = r.mid_sum[row]
    for j in range(1, nz):
        total = total + r.v_far[j - 1]
    r.v_out[me] = total
    last = to_peers(
        lambda i, peer: send(r.v_out.at[me], r.v_out.at[me], r.d_sems, (i, 3), peer)
    )
    start(last)
    wait(far_vec)
    total = r.vec_mine[...]
    for j in range(1, nz):
        total = total + r.vec_far[j - 1]
    r.vec_out[...] = total
    r.vec_sum[...] = total
    pair_vec.start()
    wait(far_q)
    for d in range(n):
        total = r.gq_sum[d, row].astype(F32)
        for j in range(1, nz):
            total = total + r.q_far[j - 1, d].astype(F32)
        r.q_last[d] = total
    more = []
    for i, peer in enumerate(peers, 1):
        for k in range(3):
            source = r.q_last.at[me ^ i, :, k * cols : (k + 1) * cols]
            more.append(send(source, r.q_out.at[k, :, place], r.d_sems, (i, k), peer))
    own += [
        pltpu.make_async_copy(
            r.q_last.at[me, :, k * cols : (k + 1) * cols],
            r.q_out.at[k, :, place],
            r.own_sems.at[15 + k],
        )
        for k in range(3)
    ]
    start(more + own[2:])
    wait(last + more + own + halves + [pair_vec])
    r.vec_out[...] += r.vec_pair[...]


def backward(x, dy, kept, lens, scale, n, nf):
    batch, tok, width = x.shape
    _, _, _, rows, cols = kept["w_hbm"].shape
    part = kept["mid"].shape[3]
    slot, nz = n * tok, nf // 2
    share = width // n
    heads = cols // HDIM

    def low(*dims):
        return pltpu.VMEM(dims, LOW)

    def full(*dims):
        return pltpu.VMEM(dims, F32)

    names = ("x1_hbm", "z_hbm", "dh2_hbm", "a_hbm", "g_hbm", "out_hbm", "w_hbm", "h_hbm")
    names += ("qkv_hbm", "p_hbm", "y_hbm")
    inputs = {name: (kept[name], ANY) for name in names}
    inputs["x_hbm"] = (x, ANY)
    inputs["dy_hbm"] = (dy, ANY)
    inputs["wide"] = (kept["wide"], VMEM)
    inputs["mid"] = (kept["mid"], VMEM)
    inputs["lens"] = (lens, SMEM)
    inputs["scale"] = (scale, SMEM)
    outputs = {
        "out": (shape((batch, tok, width), LOW), VMEM),
        "dx": (shape((batch, tok, width), F32), VMEM),
        "q_out": (shape((3, rows, width), F32), VMEM),
        "o_out": (shape((rows, width), F32), VMEM),
        "v_out": (shape((n, 8, part), F32), VMEM),
        "vec_out": (shape((16, share), F32), VMEM),
        "ffn_out": (shape((2, n, part, cols), LOW), VMEM),
    }
    scratch = {
        "x": low(batch, tok, width),
        "dy": low(batch, tok, width),
        "x1": full(batch, tok, width),
        "z": full(batch, tok, width),
        "dh2": full(batch, tok, width),
        "a": low(batch, tok, width),
        "wout": low(n, nf, rows, width),
        "w_qkv": low(3, n, nf, rows, cols),
        "h_all": low(batch, slot, width),
        "qkv_all": low(batch, slot, 3 * cols),
        "p_all": low(batch, heads, slot, slot),
        "y_own": low(batch, tok, width),
        "y_got": low(batch, n - 1, tok, width),
        "dx1": full(batch, tok, width),
        "dz": low(batch * tok, width),
        "do_own": low(batch, n, tok, cols),
        "do_all": low(batch, slot, cols),
        "ds_all": low(2, slot, slot),
        "dqkv": low(batch, slot, 3 * cols),
        "dh_all": low(batch, slot, width),
        "dh_got": low(batch, n - 1, tok, width),
        "go_all": low(n, 2, nz, rows, width),
        "go_pair": low(n, nz, rows, width),
        "go_half": low(n, nz, rows, width),
        "go_got": low(n - 1, nz, rows, width),
        "go_sum": low(nz, rows, width),
        "o_far": low(nz - 1, rows, width),
        "gq_all": low(n, 2, nz, rows, 3 * cols),
        "gq_pair": low(n, nz, rows, 3 * cols),
        "gq_sum": low(n, nz, rows, 3 * cols),
        "q_far": low(nz - 1, n, rows, 3 * cols),
        "q_last": full(n, rows, 3 * cols),
        "g_own": low(2, part, width),
        "g_got": low(nz - 1, 2, part, width),
        "g_sum": low(2, part, width),
        "mid_pair": full(nz, 8, part),
        "mid_sum": full(nz, 8, part),
        "v_far": full(nz - 1, 8, part),
        "vec": full(16, width),
        "vec_part": full(n, 16, share),
        "vec_got": full(n - 1, 16, share),
        "vec_mine": full(16, share),
        "vec_far": full(nz - 1, 16, share),
        "vec_sum": full(16, share),
        "vec_pair": full(16, share),
        "o_sems": DMA((2, batch, n)),
        "h_sems": DMA((2, batch, n)),
        "y_sems": DMA((2, batch, n)),
        "p_sems": DMA((2, 3)),
        "q_sems": DMA((2, n)),
        "e_sems": DMA((2, n, 2)),
        "z_sems": DMA((2, nz, 5)),
        "d_sems": DMA((2, n, 6)),
        "own_sems": DMA((18,)),
    }
    return launch(
        lambda r: backward_kernel(n, nf, r), "backward", inputs, outputs, scratch, 1, 60
    )


def on_device(
    tokens,
    seq_lens,
    qkv_weight,
    out_weight,
    head_scale,
    gains,
    biases,
    ffn_in,
    ffn_bias,
    mid_gain,
    mid_bias,
    ffn_out,
    out_cotangent,
):
    n = lax.axis_size("dp")
    nf = lax.axis_size("ffn")
    me = lax.axis_index("dp")
    f = lax.axis_index("ffn")
    batch, _, tok, width = tokens.shape
    heads = head_scale.shape[0]
    cols = width // n
    rows = qkv_weight.shape[1]
    hid = ffn_in.shape[1]
    part = hid // n

    def tiled(values):
        size = values.shape[1]
        spot = lax.rem(f, 128 // size) * size
        return lax.dynamic_update_slice(jnp.zeros((16, 128), LOW), values, (0, spot))

    vectors = lax.dynamic_index_in_dim(
        jnp.stack([ffn_bias, mid_gain, mid_bias]).reshape(3, n, part), me, 1, keepdims=False
    )
    x, dy = tokens[:, 0], out_cotangent[:, 0]
    kept = forward(
        x,
        qkv_weight,
        out_weight,
        jnp.stack([tiled(jnp.concatenate([gains, biases])), tiled(vectors)]),
        ffn_in.T.reshape(n, part, cols),
        ffn_out.reshape(n, part, cols),
        dy,
        seq_lens,
        head_scale,
        n,
        nf,
    )
    done = backward(x, dy, kept, seq_lens, head_scale, n, nf)
    vec, ffn, output, tokens_grad = done["vec_out"], done["ffn_out"], done["out"], done["dx"]
    qkv_grad, out_weight_grad = done["q_out"], done["o_out"]
    mid = done["v_out"].transpose(1, 0, 2).reshape(8, hid)
    own = lax.dynamic_slice_in_dim(vec, f * rows, rows, 1)
    ffn = ffn.reshape(2, hid, cols)
    return (
        output[:, None],
        tokens_grad[:, None],
        qkv_grad,
        out_weight_grad,
        vec[10 : 10 + n, ::HDIM].reshape(heads),
        own[:3],
        own[3:10],
        ffn[0].T.astype(F32),
        mid[0],
        mid[1],
        mid[2],
        ffn[1].astype(F32),
    )


def solution(mesh):
    seqs = P(None, "ffn", "dp", None)
    wide = P(None, ("dp", "ffn"))
    hidden = P("ffn")
    return jax.shard_map(
        on_device,
        mesh=mesh,
        in_specs=(
            seqs,
            P(None, "ffn"),
            P(None, ("dp", "ffn"), None),
            P(("dp", "ffn"), None),
            P(),
            wide,
            wide,
            P("dp", "ffn"),
            hidden,
            hidden,
            hidden,
            P("ffn", "dp"),
            seqs,
        ),
        out_specs=(
            seqs,
            seqs,
            P(None, ("dp", "ffn"), None),
            P(("dp", "ffn"), None),
            P(),
            wide,
            wide,
            P("dp", "ffn"),
            hidden,
            hidden,
            hidden,
            P("ffn", "dp"),
        ),
        check_vma=False,
    )
```

```python
from types import SimpleNamespace

import jax
import jax.numpy as jnp
from jax import lax
from jax.experimental import pallas as pl
from jax.experimental.pallas import tpu as pltpu
from jax.sharding import PartitionSpec as P

HDIM = 64
EPS = 1e-05
LOW = jnp.bfloat16
F32 = jnp.float32
ANY = pl.BlockSpec(memory_space=pl.ANY)
VMEM = pl.BlockSpec(memory_space=pltpu.VMEM)
SMEM = pl.BlockSpec(memory_space=pltpu.SMEM)
MESH = pl.DeviceIdType.MESH
DMA = pltpu.SemaphoreType.DMA


def dot(left, right):
    return jnp.dot(left, right, preferred_element_type=F32)


def dot_nt(left, right):
    return lax.dot_general(left, right, (((1,), (1,)), ((), ())), preferred_element_type=F32)


def dot_tn(left, right):
    return lax.dot_general(left, right, (((0,), (0,)), ((), ())), preferred_element_type=F32)


def shape(dims, kind):
    return jax.ShapeDtypeStruct(tuple(dims), kind)


def at(start, size, unit=128):
    return pl.ds(pl.multiple_of(start, unit), size)


def send(src, dst, sems, index, where):
    return pltpu.make_async_remote_copy(
        src_ref=src,
        dst_ref=dst,
        send_sem=sems.at[(0, *index)],
        recv_sem=sems.at[(1, *index)],
        device_id=where,
        device_id_type=MESH,
    )


def greet(peers):
    barrier = pltpu.get_barrier_semaphore()
    for peer in peers:
        pl.semaphore_signal(barrier, inc=1, device_id=peer, device_id_type=MESH)


def meet(peers):
    pl.semaphore_wait(pltpu.get_barrier_semaphore(), len(peers))


def dp_peers(n, me):
    return [{"dp": me ^ i} for i in range(1, n)]


def ffn_peers(nf, f):
    return [{"ffn": f ^ (2 * j)} for j in range(1, nf // 2)] + [{"ffn": f ^ 1}]


def start(copies):
    for copy in copies:
        copy.start()


def wait(copies):
    for copy in copies:
        copy.wait()


class Line:
    def __init__(self, nf, f, items, hop_sems, side_sems):
        self.nz, self.core, self.q, self.f = nf // 2, lax.rem(f, 2), lax.div(f, 2), f
        self.items, self.hop_sems, self.side_sems = items, hop_sems, side_sems
        self.next = [1] * len(items)

    def copy(self, sems, k, t, came, way, first, target):
        source, place = self.items[k]
        index = self.f if first else 2 * (self.q - t * way) + self.core
        spot = place(index)
        side = 0 if way > 0 else 1
        return pltpu.make_async_remote_copy(
            src_ref=source if first else spot,
            dst_ref=spot,
            send_sem=sems.at[0, side, k, t],
            recv_sem=sems.at[1, side, k, came],
            device_id={"ffn": target},
            device_id_type=MESH,
        )

    def hop(self, k, t, way, first=False):
        return self.copy(self.hop_sems, k, t, t + 1, way, first, self.f + 2 * way)

    def arrival(self, k, t, way):
        return self.copy(self.hop_sems, k, t, t, way, False, self.f + 2 * way)

    def over(self, k, t, way, first=False):
        return self.copy(self.side_sems, k, t, t, way, first, self.f ^ 1)

    def onward(self, way):
        return self.q < self.nz - 1 if way > 0 else self.q > 0

    def has(self, t, way):
        return self.q - t >= 0 if way > 0 else self.q + t <= self.nz - 1

    def begin(self, *items):
        for k in items:
            for way in (1, -1):

                @pl.when(self.onward(way))
                def _():
                    self.hop(k, 0, way, True).start()

        for k in items:
            self.over(k, 0, 1, True).start()

    def step(self, k, t):
        for way in (1, -1):

            @pl.when(self.has(t, way) & self.onward(way))
            def _():
                self.arrival(k, t, way).wait_recv()
                self.hop(k, t, way).start()

        for way in (1, -1):

            @pl.when(self.has(t, way))
            def _():
                @pl.when(jnp.logical_not(self.onward(way)))
                def _():
                    self.arrival(k, t, way).wait_recv()

                self.over(k, t, way).start()

    def advance(self, *items):
        for k in items:
            if self.next[k] < self.nz:
                self.step(k, self.next[k])
                self.next[k] += 1

    def arrive(self, *items):
        begin = self.next[items[0]]

        def rest(t, _):
            for k in items:
                self.step(k, t)
            return 0

        lax.fori_loop(begin, self.nz, rest, 0)

        def close(t, _):
            for k in items:
                for way in (1, -1):

                    @pl.when(self.has(t, way))
                    def _():
                        self.over(k, t, way).wait_recv()

            return 0

        for k in items:
            self.over(k, 0, 1, True).wait_recv()
        lax.fori_loop(1, self.nz, close, 0)

    def finish(self, *items):
        for k in items:
            self.over(k, 0, 1, True).wait_send()
            for way in (1, -1):

                @pl.when(self.onward(way))
                def _():
                    self.hop(k, 0, way, True).wait_send()

        def close(t, _):
            for k in items:
                for way in (1, -1):

                    @pl.when(self.has(t, way))
                    def _():
                        self.over(k, t, way).wait_send()

                    @pl.when(self.has(t, way) & self.onward(way))
                    def _():
                        self.hop(k, t, way).wait_send()

            return 0

        lax.fori_loop(1, self.nz, close, 0)


def line_meet(n, nf, me, f):
    barrier = pltpu.get_barrier_semaphore()
    q, nz = lax.div(f, 2), nf // 2
    greet(dp_peers(n, me) + [{"ffn": f ^ 1}])

    @pl.when(q < nz - 1)
    def _():
        greet([{"ffn": f + 2}])

    @pl.when(q > 0)
    def _():
        greet([{"ffn": f - 2}])

    count = n + jnp.where(q < nz - 1, 1, 0) + jnp.where(q > 0, 1, 0)
    pl.semaphore_wait(barrier, count)


class Gather:
    def __init__(self, me, source, place, size, sems, index):
        self.me, self.source, self.place, self.half = me, source, place, size // 2
        self.sems, self.index = sems, index

    def straight(self, k):
        spot = self.place(self.me, 0, 2 * self.half)
        return send(self.source, spot, self.sems, (*self.index, k), {"dp": self.me ^ (k + 1)})

    def relay(self, k):
        spot = self.place(self.me ^ (k + 1), k * self.half, self.half)
        return send(spot, spot, self.sems, (*self.index, 2 + k), {"dp": self.me ^ (2 - k)})

    def begin(self):
        for k in range(2):
            self.straight(k).start()

    def turn(self):
        for k in range(2):
            self.straight(k).wait()
            self.relay(k).start()

    def finish(self):
        for k in range(2):
            self.relay(k).wait()


class Reduce:
    def __init__(self, me, block, got, passed, last, sems, index):
        self.me, self.block, self.passed = me, block, passed
        self.got, self.last, self.sems, self.index = got, last, sems, index

    def first(self, side, far):
        step = side + 1
        owner = self.me ^ (3 if far else step)
        target = self.got.at[(*self.index, side, far)]
        spot = (*self.index, side, far)
        return send(self.block(owner, side), target, self.sems, spot, {"dp": self.me ^ step})

    def second(self, side):
        where = (*self.index, side)
        target = {"dp": self.me ^ (2 - side)}
        return send(self.passed.at[where], self.last.at[where], self.sems, (*where, 2), target)

    def begin(self):
        for far in (1, 0):
            for side in range(2):
                self.first(side, far).start()

    def turn(self):
        for side in range(2):
            self.first(side, 1).wait()
            total = self.block(self.me ^ (2 - side), side)[...].astype(F32)
            total = total + self.got[(*self.index, side, 1)].astype(F32)
            self.passed[(*self.index, side)] = total.astype(LOW)
            self.second(side).start()

    def finish(self):
        halves = []
        for side in range(2):
            self.first(side, 0).wait()
            self.second(side).wait()
            total = self.block(self.me, side)[...].astype(F32)
            total = total + self.got[(*self.index, side, 0)].astype(F32)
            halves.append(total + self.last[(*self.index, side)].astype(F32))
        return jnp.concatenate(halves, axis=-1)


def normal(values):
    center = values - jnp.mean(values, axis=-1, keepdims=True)
    inverse = lax.rsqrt(jnp.mean(center * center, axis=-1, keepdims=True) + EPS)
    return center * inverse, inverse


def normal_back(grad, normed, inverse):
    return inverse * (
        grad
        - jnp.mean(grad, axis=-1, keepdims=True)
        - normed * jnp.mean(grad * normed, axis=-1, keepdims=True)
    )


def column_sum(values):
    return jnp.sum(values, axis=0, keepdims=True)


def launch(body, name, inputs, outputs, scratch, number, limit):
    names = [*inputs, *outputs, *scratch]
    results = pl.pallas_call(
        lambda *refs: body(SimpleNamespace(**dict(zip(names, refs)))),
        name=name,
        out_shape=tuple(kind for kind, _ in outputs.values()),
        in_specs=[spec for _, spec in inputs.values()],
        out_specs=tuple(spec for _, spec in outputs.values()),
        scratch_shapes=list(scratch.values()),
        compiler_params=pltpu.CompilerParams(
            collective_id=number, has_side_effects=True, vmem_limit_bytes=limit << 20
        ),
    )(*[value for value, _ in inputs.values()])
    return dict(zip(outputs, results))


def forward_kernel(n, nf, part, r):
    me = lax.axis_index("dp")
    f = lax.axis_index("ffn")
    core, nz = lax.rem(f, 2), nf // 2
    batch, tok, width = r.x.shape
    rows_each = r.wout.shape[0]
    cols = width // n
    pairs = cols // 128
    slot = n * tok
    hid = nf * part
    ff = n * hid
    step = 256
    peers = dp_peers(n, me)
    pair = {"ffn": f ^ 1}
    place = at(me * cols, cols)
    band = at(me * tok, tok)

    own = [
        pltpu.make_async_copy(r.qkv.at[:, :, place], r.stage.at[:, me], r.own_sems.at[0]),
        pltpu.make_async_copy(r.small.at[0], r.small_stage.at[me], r.own_sems.at[1]),
        pltpu.make_async_copy(r.small.at[1], r.small_stage.at[n], r.own_sems.at[2]),
        pltpu.make_async_copy(r.wout, r.out_stage.at[me], r.own_sems.at[3]),
        pltpu.make_async_copy(r.first.at[me], r.first_stage.at[:, place], r.own_sems.at[4]),
        pltpu.make_async_copy(r.second.at[me], r.second_stage.at[:, place], r.own_sems.at[5]),
        pltpu.make_async_copy(r.x, r.x_all.at[me], r.own_sems.at[6]),
        pltpu.make_async_copy(r.dy, r.dy_all.at[:, band, :], r.own_sems.at[7]),
    ]
    start(own)
    line_meet(n, nf, me, f)

    def to_peers(make):
        return [make(i, peer) for i, peer in enumerate(peers, 1)]

    blocks = to_peers(
        lambda i, peer: send(
            r.qkv.at[:, :, at((me ^ i) * cols, cols)], r.stage.at[:, me], r.w_sems, (i, 0), peer
        )
    )
    smalls = to_peers(
        lambda i, peer: send(r.small.at[0], r.small_stage.at[me], r.w_sems, (i, 1), peer)
    )
    outs = to_peers(lambda i, peer: send(r.wout, r.out_stage.at[me], r.w_sems, (i, 2), peer))
    firsts = to_peers(
        lambda i, peer: send(
            r.first.at[me ^ i], r.first_stage.at[:, place], r.w_sems, (i, 3), peer
        )
    )
    seconds = to_peers(
        lambda i, peer: send(
            r.second.at[me ^ i], r.second_stage.at[:, place], r.w_sems, (i, 4), peer
        )
    )

    def x_rows(micro):
        def spot(owner, start, size):
            return r.x_all.at[owner, micro, start : start + size]

        return Gather(me, r.x.at[micro], spot, tok, r.x_sems, (micro,))

    def y_rows(micro):
        def spot(owner, start, size):
            return r.dy_all.at[micro, at(owner * tok + start, size, 64), :]

        return Gather(me, r.dy.at[micro], spot, tok, r.y_sems, (micro,))

    start(blocks + smalls)
    x_rows(0).begin()
    start(outs + firsts)
    line = Line(
        nf,
        f,
        [
            (r.stage, lambda index: r.w_all.at[:, :, index]),
            (r.small_stage, lambda index: r.small_all.at[index]),
            (r.out_stage, lambda index: r.out_all.at[:, index]),
            (r.first_stage, lambda index: r.w1.at[index]),
            (r.second_stage, lambda index: r.w2.at[index]),
        ],
        r.hop_sems,
        r.side_sems,
    )
    mine = [
        pltpu.make_async_copy(source, spot(f), r.own_sems.at[8 + k])
        for k, (source, spot) in enumerate(line.items)
    ]
    wait(blocks + smalls + own[:3])
    line.begin(0, 1)
    start(mine[:2])
    line.advance(0, 1)
    x_rows(0).turn()
    x_rows(1).begin()
    line.advance(0, 1)
    wait(outs + own[3:4])
    line.begin(2)
    start(mine[2:3])
    line.arrive(0, 1)
    wait(firsts + own[4:5])
    line.begin(3)
    start(mine[3:4])
    wait(mine[:2] + own[6:7])

    def lay_out(out_ref, index, begin, size):
        together = 128 // size
        for b in range(nf // together):
            total = r.small_all[b * together, index].astype(F32)
            for k in range(1, together):
                total = total + r.small_all[b * together + k, index].astype(F32)
            out_ref[:, begin + b * 128 : begin + (b + 1) * 128] = total

    for d in range(n):
        lay_out(r.wide, d, d * nf * rows_each, rows_each)
    lay_out(r.mids, n, 0, part)

    gain, shift = r.wide[0:1, :], r.wide[3:4, :]
    bias_q, bias_v = r.wide[4:5, place], r.wide[5:6, place]
    left = lax.broadcasted_iota(jnp.int32, (1, 128), 1) < HDIM

    def block_copies(micro):
        return to_peers(
            lambda i, peer: send(
                r.a_all.at[micro, me ^ i], r.a_own.at[micro, :, place], r.a_sems, (micro, i), peer
            )
        )

    def keep_copies(micro):
        return [
            pltpu.make_async_copy(source.at[micro], out.at[micro], r.keep_sems.at[micro, k])
            for k, (source, out) in enumerate(
                [(r.h_all, r.h_hbm), (r.qkv_all, r.qkv_hbm), (r.p_all, r.p_hbm)]
            )
        ]

    def after_first():
        line.advance(2)
        x_rows(1).turn()
        start(seconds)
        y_rows(0).begin()

    def after_second():
        line.advance(3)

    def after_third():
        line.advance(2)
        wait(seconds + own[5:6])
        line.begin(4)
        start(mine[4:5])

    def after_last():
        y_rows(0).turn()
        y_rows(1).begin()
        line.advance(3)

    def attend(index, _):
        micro, two = lax.div(index, pairs), lax.rem(index, pairs)

        @pl.when(two == 0)
        def _():
            x_rows(micro).finish()

            def norm_rows(d, _):
                values, _ = normal(r.x_all[d, micro].astype(F32))
                r.h_all[micro, at(d * tok, tok), :] = (values * gain + shift).astype(LOW)
                return 0

            lax.fori_loop(0, n, norm_rows, 0)
            for k, bias in enumerate((bias_q, None, bias_v)):
                weight = r.w_all[k].reshape(width, cols)
                value = dot(r.h_all[micro], weight)
                if bias is not None:
                    value = value + bias
                r.qkv_all[micro, :, k * cols : (k + 1) * cols] = value.astype(LOW)

        length = r.lens[micro, 0]

        def column(k):
            return at(k * cols + two * 128, 128)

        head = two * 2
        scales = jnp.where(
            left, r.scale[me * 2 * pairs + head], r.scale[me * 2 * pairs + head + 1]
        )
        for block in range(n):
            end = (block + 1) * tok
            q = r.qkv_all[micro, block * tok : end, column(0)] * HDIM ** (-0.5)
            k = r.qkv_all[micro, :end, column(1)]
            v = r.qkv_all[micro, :end, column(2)]
            key = lax.broadcasted_iota(jnp.int32, (tok, end), 1)
            query = lax.broadcasted_iota(jnp.int32, (tok, end), 0) + block * tok
            mask = (key <= query) & (key < length)
            out = []
            for side in range(2):
                mine_ = left if side == 0 else jnp.logical_not(left)
                scores = dot_nt(jnp.where(mine_, q, jnp.zeros_like(q)), k)
                scores = jnp.where(mask, scores, -1e30)
                expo = jnp.exp(scores - jnp.max(scores, axis=-1, keepdims=True))
                probs = expo * (1.0 / jnp.sum(expo, axis=-1, keepdims=True))
                probs = probs.astype(LOW)
                r.p_all[micro, head + side, block * tok : end, :end] = probs
                out.append(dot(probs, v))
            joined = jnp.where(left, out[0], out[1]) * scales
            r.a_all[micro, block, :, at(two * 128, 128)] = joined.astype(LOW)

        @pl.when(two == pairs - 1)
        def _():
            start(block_copies(micro))
            start(keep_copies(micro))
            r.a_own[micro, :, place] = r.a_all[micro, me]

        work = [after_first, after_second, after_third, after_last]
        for k, act in enumerate(work[: batch * pairs]):
            pl.when(index == k)(act)
        return 0

    lax.fori_loop(0, batch * pairs, attend, 0)

    line.arrive(2)
    wait(mine[2:3])
    late = [
        pltpu.make_async_copy(source, target, r.own_sems.at[13 + k])
        for k, (source, target) in enumerate(
            [(r.w_all, r.w_hbm), (r.out_all, r.out_hbm), (r.z, r.z_hbm), (r.x1, r.x1_hbm),
             (r.a_own, r.a_hbm), (r.y, r.y_hbm), (r.pair_got, r.g_hbm), (r.dh2, r.dh2_hbm)]
        )
    ]
    start(late[:2])

    def h2_rows(micro):
        def spot(owner, start, size):
            return r.h2_all.at[micro, at(owner * tok + start, size, 64), :]

        return Gather(me, r.h2_own.at[micro], spot, tok, r.h_sems, (micro,))

    for micro in range(batch):
        wait(block_copies(micro))
        z = dot(r.a_own[micro], r.out_all[...].reshape(width, width)) + r.wide[6:7, :]
        r.z[micro] = z
        values, _ = normal(z)
        x1 = r.x_all[me, micro].astype(F32) + values * r.wide[1:2, :] + r.wide[7:8, :]
        r.x1[micro] = x1
        values, _ = normal(x1)
        r.h2_own[micro] = (values * r.wide[2:3, :] + r.wide[8:9, :]).astype(LOW)
        h2_rows(micro).begin()
        r.h2_all[micro, band, :] = r.h2_own[micro]
    start(late[2:5])
    line.advance(4)
    h2_rows(0).turn()
    y_rows(1).turn()
    for micro in range(1, batch):
        h2_rows(micro).turn()
    line.arrive(3)
    wait(mine[3:4])

    def weights(ref, c):
        count = step // part
        return ref[pl.ds(c * count, count)].reshape(step, width)

    def w_columns(ref, columns):
        return ref[:, :, columns].reshape(hid, step)

    def sum_copies(micro):
        return to_peers(
            lambda i, peer: send(
                r.sums.at[micro], r.sums_all.at[micro, me], r.s_sems, (micro, i), peer
            )
        )

    def dh2_rows(micro):
        def block(owner, side):
            columns = slice(side * (width // 2), (side + 1) * (width // 2))
            return r.dh2_all.at[micro, at(owner * tok, tok), columns]

        return Reduce(me, block, r.dh2_got, r.dh2_passed, r.dh2_last, r.r_sems, (micro,))

    def fold(values):
        total = values[:, :128]
        for k in range(1, step // 128):
            total = total + values[:, k * 128 : (k + 1) * 128]
        return total

    def units(micro):
        h2_rows(micro).finish()

        def chunk(c, totals):
            rows = at(c * step, step)
            u = dot_nt(r.h2_all[micro], weights(r.w1, c)) + r.mids[0:1, rows]
            phi = 0.5 + 0.5 * lax.erf(u * (0.5**0.5))
            value = u * phi
            r.act[micro, :, rows] = value
            r.slope[micro, :, rows] = phi + u * jnp.exp(u * u * -0.5) * 0.3989422804014327
            return totals[0] + fold(value), totals[1] + fold(value * value)

        zero = jnp.zeros((slot, 128), F32)
        totals = lax.fori_loop(0, hid // step, chunk, (zero,) * 2)
        for k in range(2):
            r.sums[micro, k : k + 1, :] = column_sum(totals[k].T)

    def cotangents(micro):
        y_rows(micro).finish()
        valid = lax.broadcasted_iota(jnp.int32, (slot, 1), 0) < r.lens[micro, 0]
        rows = r.dy_all[micro]
        r.dy_all[micro] = jnp.where(valid, rows, jnp.zeros_like(rows))

        def chunk(c, totals):
            rows = at(c * step, step)
            dm = dot_nt(r.dy_all[micro], weights(r.w2, c))
            r.dmix[micro, :, rows] = dm
            dn = dm * r.mids[1:2, rows]
            return totals[0] + fold(dn), totals[1] + fold(dn * r.act[micro, :, rows])

        zero = jnp.zeros((slot, 128), F32)
        totals = lax.fori_loop(0, hid // step, chunk, (zero,) * 2)
        for k in range(2):
            r.sums[micro, 2 + k : 3 + k, :] = column_sum(totals[k].T)
        r.sums[micro, 4:8, :] = jnp.zeros((4, slot), F32)
        start(sum_copies(micro))

    r.vec[...] = jnp.zeros_like(r.vec)

    def second_pass(micro, _):
        wait(sum_copies(micro))
        r.sums_all[micro, me] = r.sums[micro]
        total = r.sums_all[micro, 0]
        for d in range(1, n):
            total = total + r.sums_all[micro, d]
        total = total * (1.0 / ff)
        mean = total[0:1]
        inverse = lax.rsqrt(total[1:2] - mean * mean + EPS)
        back = total[2:3]
        cross = inverse * (total[3:4] - mean * back)
        table = jnp.concatenate([mean, inverse, back, cross] * 32, axis=0).T
        mean, inverse, back, cross = [table[:, k : k + 1] for k in range(4)]
        rows_of = at(micro * slot, slot)

        def chunk(c, _):
            rows = at(c * step, step)
            normed = (r.act[micro, :, rows] - mean) * inverse
            dm = r.dmix[micro, :, rows]
            gain = r.mids[1:2, rows]
            r.mixed[rows_of, rows] = (normed * gain + r.mids[2:3, rows]).astype(LOW)
            df = inverse * (dm * gain - back - normed * cross)
            low = (df * r.slope[micro, :, rows]).astype(LOW)
            r.du[rows_of, rows] = low
            r.vec[0:1, rows] += column_sum(low.astype(F32))
            r.vec[1:2, rows] += column_sum(dm * normed)
            r.vec[2:3, rows] += column_sum(dm)
            return 0

        lax.fori_loop(0, hid // step, chunk, 0)

        def back_rows(c, _):
            columns = at(c * step, step)
            value = dot(r.du[rows_of, :], w_columns(r.w1, columns))
            r.dh2_all[micro, :, columns] = value.astype(LOW)
            return 0

        lax.fori_loop(0, width // step, back_rows, 0)
        dh2_rows(micro).begin()
        return 0

    def passes(micro, _):
        units(micro)

        @pl.when(micro == 0)
        def _():
            line.arrive(4)
            wait(mine[4:5] + own[7:8])

        cotangents(micro)

        @pl.when(micro > 0)
        def _():
            dh2_rows(micro - 1).turn()

        second_pass(micro, 0)
        return 0

    lax.fori_loop(0, batch, passes, 0)
    each = step // part // 2

    def halved(index):
        return lax.div(index, 2), lax.rem(index, 2)

    def pair_copies(c):
        copies = []
        for k in range(each):
            index = c * (2 * each) + 2 * k
            for w in range(2):
                copies.append(
                    send(
                        r.grads.at[w, index + 1 - core],
                        r.pair_got.at[(w, *halved(c * each + k))],
                        r.p_sems,
                        (c, k, w),
                        pair,
                    )
                )
        return copies

    def weight_grads(c, _):
        rows = at(c * step, step)
        h2 = r.h2_all[...].reshape(batch * slot, width)
        dy = r.dy_all[...].reshape(batch * slot, width)
        first = dot_tn(r.du[:, rows], h2).astype(LOW)
        second = dot_tn(r.mixed[:, rows], dy).astype(LOW)
        for k in range(step // part):
            r.grads[0, c * (step // part) + k] = first[k * part : (k + 1) * part]
            r.grads[1, c * (step // part) + k] = second[k * part : (k + 1) * part]
        start(pair_copies(c))
        return 0

    lax.fori_loop(0, hid // step, weight_grads, 0)
    dh2_rows(batch - 1).turn()

    def out_rows(c, _):
        columns = at(c * step, step)
        for micro in range(batch):
            value = dot(r.mixed[micro * slot : (micro + 1) * slot, :], w_columns(r.w2, columns))
            r.y[micro, :, columns] = value.astype(LOW)
        return 0

    lax.fori_loop(0, width // step, out_rows, 0)
    start(late[5:6])

    def pair_sum(c, _):
        wait(pair_copies(c))
        for k in range(each):
            for w in range(2):
                total = r.grads[w, c * (2 * each) + 2 * k + core].astype(F32)
                spot = (w, *halved(c * each + k))
                total = total + r.pair_got[spot].astype(F32)
                r.pair_got[spot] = total.astype(LOW)
        return 0

    lax.fori_loop(0, hid // step, pair_sum, 0)
    start(late[6:7])
    for k in range(nf):
        r.mid[k // 2, k % 2] = r.vec[:, k * part : (k + 1) * part]
    line.finish(0, 1, 2, 3, 4)
    for micro in range(batch):
        wait(keep_copies(micro))
    for micro in range(batch):
        r.dh2[micro] = dh2_rows(micro).finish()
    start(late[7:])
    wait(late)


def forward(x, qkv, wout, small, first, second, dy, lens, scale, n, nf):
    batch, tok, width = x.shape
    rows = wout.shape[0]
    part = first.shape[1]
    cols = width // n
    slot, hid = n * tok, nf * part
    heads = cols // HDIM

    def low(*dims):
        return pltpu.VMEM(dims, LOW)

    def full(*dims):
        return pltpu.VMEM(dims, F32)

    inputs = {
        name: (value, ANY)
        for name, value in zip(
            ("x", "qkv", "wout", "small", "first", "second", "dy"),
            (x, qkv, wout, small, first, second, dy),
        )
    }
    inputs["lens"] = (lens, SMEM)
    inputs["scale"] = (scale, SMEM)
    outputs = {
        "wide": (shape((16, width), F32), VMEM),
        "w_hbm": (shape((3, n, nf, rows, cols), LOW), ANY),
        "out_hbm": (shape((n, nf, rows, width), LOW), ANY),
        "h_hbm": (shape((batch, slot, width), LOW), ANY),
        "qkv_hbm": (shape((batch, slot, 3 * cols), LOW), ANY),
        "p_hbm": (shape((batch, heads, slot, slot), LOW), ANY),
        "a_hbm": (shape((batch, tok, width), LOW), ANY),
        "z_hbm": (shape((batch, tok, width), F32), ANY),
        "x1_hbm": (shape((batch, tok, width), F32), ANY),
        "y_hbm": (shape((batch, slot, width), LOW), ANY),
        "g_hbm": (shape((2, nf // 4, 2, part, width), LOW), ANY),
        "dh2_hbm": (shape((batch, tok, width), F32), ANY),
        "mid": (shape((nf // 2, 2, 8, part), F32), VMEM),
    }
    scratch = {
        "mids": full(16, hid),
        "dh2": full(batch, tok, width),
        "vec": full(8, hid),
        "stage": low(3, n, rows, cols),
        "small_stage": low(n + 1, *small.shape[1:]),
        "out_stage": low(n, rows, width),
        "first_stage": low(part, width),
        "second_stage": low(part, width),
        "small_all": low(nf, n + 1, *small.shape[1:]),
        "w_all": low(3, n, nf, rows, cols),
        "out_all": low(n, nf, rows, width),
        "w1": low(nf, part, width),
        "w2": low(nf, part, width),
        "x_all": low(n, batch, tok, width),
        "dy_all": low(batch, slot, width),
        "h_all": low(batch, slot, width),
        "qkv_all": low(batch, slot, 3 * cols),
        "p_all": low(batch, heads, slot, slot),
        "a_all": low(batch, n, tok, cols),
        "a_own": low(batch, tok, width),
        "z": full(batch, tok, width),
        "x1": full(batch, tok, width),
        "h2_own": low(batch, tok, width),
        "h2_all": low(batch, slot, width),
        "act": full(batch, slot, hid),
        "slope": full(batch, slot, hid),
        "dmix": full(batch, slot, hid),
        "mixed": low(batch * slot, hid),
        "du": low(batch * slot, hid),
        "sums": full(batch, 8, slot),
        "sums_all": full(batch, n, 8, slot),
        "dh2_all": low(batch, slot, width),
        "dh2_got": low(batch, 2, 2, tok, width // 2),
        "dh2_passed": low(batch, 2, tok, width // 2),
        "dh2_last": low(batch, 2, tok, width // 2),
        "y": low(batch, slot, width),
        "grads": low(2, nf, part, width),
        "pair_got": low(2, nf // 4, 2, part, width),
        "w_sems": DMA((2, n, 5)),
        "x_sems": DMA((2, batch, 4)),
        "y_sems": DMA((2, batch, 4)),
        "a_sems": DMA((2, batch, n)),
        "h_sems": DMA((2, batch, 4)),
        "s_sems": DMA((2, batch, n)),
        "r_sems": DMA((2, batch, 2, 3)),
        "p_sems": DMA((2, hid // 256, 128 // part, 2)),
        "hop_sems": DMA((2, 2, 5, nf // 2)),
        "side_sems": DMA((2, 2, 5, nf // 2)),
        "keep_sems": DMA((batch, 3)),
        "own_sems": DMA((21,)),
    }
    return launch(
        lambda r: forward_kernel(n, nf, part, r), "forward", inputs, outputs, scratch, 0, 63
    )


def backward_kernel(n, nf, r):
    me = lax.axis_index("dp")
    f = lax.axis_index("ffn")
    core, row, nz = lax.rem(f, 2), lax.div(f, 2), nf // 2
    even, two_row = lax.rem(row, 2), lax.div(row, 2)
    batch, tok, width = r.dx.shape
    slot = n * tok
    cols = width // n
    rows_each = r.o_out.shape[0]
    pairs = cols // 128
    heads = cols // HDIM
    share = width // n
    step = 256
    peers = dp_peers(n, me)
    pair = {"ffn": f ^ 1}
    everyone = peers + ffn_peers(nf, f)
    greet(everyone)
    band = at(me * tok, tok)
    place = at(me * cols, cols)
    loads = [
        pltpu.make_async_copy(source, target, r.own_sems.at[k])
        for k, (source, target) in enumerate(
            [(r.x1_hbm, r.x1), (r.dh2_hbm, r.dh2), (r.dy_hbm, r.dy), (r.z_hbm, r.z),
             (r.out_hbm, r.wout), (r.a_hbm, r.a), (r.qkv_hbm, r.qkv_all), (r.p_hbm, r.p_all),
             (r.w_hbm, r.w_qkv), (r.h_hbm, r.h_all), (r.x_hbm, r.x), (r.g_hbm.at[:, :, even], r.g_own),
             (r.y_hbm, r.y_all)]
        )
    ]
    start(loads)
    r.vec[...] = jnp.zeros_like(r.vec)

    def to_peers(make):
        return [make(i, peer) for i, peer in enumerate(peers, 1)]

    def along(make):
        return [make(j, {"ffn": f ^ (2 * j)}) for j in range(1, nz)]

    def columns_of(side):
        return slice(side * (width // 2), (side + 1) * (width // 2))

    def y_rows(micro):
        def block(owner, side):
            return r.y_all.at[micro, at(owner * tok, tok), columns_of(side)]

        return Reduce(me, block, r.y_got, r.y_passed, r.y_last, r.y_sems, (micro,))

    def dh_rows(micro):
        def block(owner, side):
            return r.dh_all.at[micro, at(owner * tok, tok), columns_of(side)]

        return Reduce(me, block, r.dh_got, r.dh_passed, r.dh_last, r.h_sems, (micro,))

    def go_block(owner, side):
        return r.go_half.at[owner, :, :, columns_of(side)]

    go = Reduce(me, go_block, r.go_got, r.go_passed, r.go_last, r.e_sems, ())

    def g_first(w):
        return send(
            r.g_hbm.at[w, :, 1 - even], r.g_pair.at[w], r.g_sems, (0, w), {"ffn": f ^ 2}
        )

    def g_second(w):
        return [
            send(r.g_mid.at[w, two_row ^ j], r.g_far.at[j - 1, w], r.g_sems, (j, w), {"ffn": f ^ (4 * j)})
            for j in range(1, nz // 2)
        ]

    def g_turn(w):
        g_first(w).wait()
        for k in range(nz // 2):
            total = r.g_own[w, k].astype(F32) + r.g_pair[w, k].astype(F32)
            r.g_mid[w, k] = total.astype(LOW)
        start(g_second(w))

    pair_v = send(r.mid.at[:, 1 - core], r.mid_pair, r.p_sems, (1,), pair)
    wait(loads[:4] + loads[12:])
    meet(everyone)
    for w in range(2):
        g_first(w).start()
    pair_v.start()
    y_rows(0).begin()
    for micro in range(batch):
        normed, inverse = normal(r.x1[micro])
        grad = r.dh2[micro]
        r.vec[2:3, :] += column_sum(grad * normed)
        r.vec[8:9, :] += column_sum(grad)
        valid = lax.broadcasted_iota(jnp.int32, (tok, 1), 0) + me * tok < r.lens[micro, 0]
        dy = jnp.where(valid, r.dy[micro].astype(F32), 0.0)
        r.vec[9:10, :] += column_sum(dy)
        grad = dy + normal_back(grad * r.wide[2:3, :], normed, inverse)
        r.dx1[micro] = grad
        normed, inverse = normal(r.z[micro])
        r.vec[1:2, :] += column_sum(grad * normed)
        r.vec[7:8, :] += column_sum(grad)
        low = normal_back(grad * r.wide[1:2, :], normed, inverse).astype(LOW)
        r.vec[6:7, :] += column_sum(low.astype(F32))
        r.dz[micro * tok : (micro + 1) * tok, :] = low
    wait(loads[4:5])
    for d in range(n):
        grad = dot_nt(r.dz[...], r.wout[d].reshape(cols, width))
        lane = lax.broadcasted_iota(jnp.int32, (1, cols), 1) // HDIM
        scales = jnp.zeros((1, cols), F32)
        for head in range(heads):
            scales = jnp.where(lane == head, r.scale[d * heads + head], scales)
        grad = (grad * scales).astype(LOW)
        for micro in range(batch):
            r.do_own[micro, d] = grad[micro * tok : (micro + 1) * tok]

    def head_copies(micro):
        return to_peers(
            lambda i, peer: send(
                r.do_own.at[micro, me ^ i], r.do_all.at[micro, band, :], r.o_sems, (micro, i), peer
            )
        )

    pair_o = send(r.go_all.at[:, 1 - core], r.go_pair, r.p_sems, (0,), pair)
    pair_vec = send(r.vec_sum, r.vec_pair, r.p_sems, (2,), pair)

    def pair_q(d):
        return send(r.gq_all.at[d, 1 - core], r.gq_pair.at[d], r.q_sems, (d,), pair)

    shares = to_peers(
        lambda i, peer: send(r.vec_part.at[me ^ i], r.vec_got.at[i - 1], r.d_sems, (i, 6), peer)
    )
    far_o = along(
        lambda j, peer: send(r.go_sum.at[row ^ j], r.o_far.at[j - 1], r.z_sems, (j, 1), peer)
    )
    far_q = along(
        lambda j, peer: send(r.gq_sum.at[:, row ^ j], r.q_far.at[j - 1], r.z_sems, (j, 2), peer)
    )
    far_v = along(
        lambda j, peer: send(r.mid_sum.at[row ^ j], r.v_far.at[j - 1], r.z_sems, (j, 3), peer)
    )
    far_vec = along(lambda j, peer: send(r.vec_mine, r.vec_far.at[j - 1], r.z_sems, (j, 4), peer))
    for micro in range(batch):
        start(head_copies(micro))
        r.do_all[micro, band, :] = r.do_own[micro, me]
    wait(loads[5:6])

    def out_weight(d, _):
        a = r.a[:, :, at(d * cols, cols)].reshape(batch * tok, cols)
        grad = dot_tn(a, r.dz[...]).astype(LOW)
        for k in range(nf):
            r.go_all[d, k % 2, k // 2] = grad[k * rows_each : (k + 1) * rows_each]
        return 0

    lax.fori_loop(0, n, out_weight, 0)
    pair_o.start()
    y_rows(0).turn()
    wait(loads[6:12])
    left = lax.broadcasted_iota(jnp.int32, (1, 128), 1) < HDIM

    def one(micro, _):
        wait(head_copies(micro))

        def pair_of(two, _):
            def column(k):
                return at(k * cols + two * 128, 128)

            head = two * 2
            own_cols = at(two * 128, 128)
            sums = []
            k = r.qkv_all[micro, :, column(1)]
            v = r.qkv_all[micro, :, column(2)]
            for block in range(n):
                end = (block + 1) * tok
                rows = slice(block * tok, end)
                do = r.do_all[micro, rows, own_cols]
                out = []
                for side in range(2):
                    mine = left if side == 0 else jnp.logical_not(left)
                    probs = r.p_all[micro, head + side, rows, :end].astype(F32)
                    dp = dot_nt(jnp.where(mine, do, jnp.zeros_like(do)), v[:end])
                    delta = jnp.sum(probs * dp, axis=-1, keepdims=True)
                    ds = (probs * (dp - delta)).astype(LOW)
                    r.ds_all[side, rows, :end] = ds
                    out.append(dot(ds, k[:end]))
                    sums.append(jnp.sum(delta, axis=0, keepdims=True))
                dq = jnp.where(left, out[0], out[1]) * HDIM ** (-0.5)
                r.dqkv[micro, rows, column(0)] = dq.astype(LOW)
            q = r.qkv_all[micro, :, column(0)]
            do = r.do_all[micro, :, own_cols]
            for block in range(n):
                begin = block * tok
                keys = slice(begin, begin + tok)
                dk = [dot_tn(r.ds_all[side, begin:, keys], q[begin:]) for side in range(2)]
                dv = [
                    dot_tn(r.p_all[micro, head + side, begin:, keys], do[begin:])
                    for side in range(2)
                ]
                dk = jnp.where(left, dk[0], dk[1]) * HDIM ** (-0.5)
                r.dqkv[micro, keys, column(1)] = dk.astype(LOW)
                r.dqkv[micro, keys, column(2)] = jnp.where(left, dv[0], dv[1]).astype(LOW)
            spot = me * heads + head
            first = sum(sums[2::2], sums[0]) * (1.0 / r.scale[spot])
            second = sum(sums[3::2], sums[1]) * (1.0 / r.scale[spot + 1])
            r.vec[10:11, at(me * cols + two * 128, 128)] += jnp.where(left, first, second)
            return 0

        lax.fori_loop(0, pairs, pair_of, 0)

        @pl.when(micro == 0)
        def _():
            g_turn(0)
            pair_o.wait()
            for d in range(n):
                total = r.go_all[d, core].astype(F32) + r.go_pair[d].astype(F32)
                r.go_half[d] = total.astype(LOW)
            go.begin()

        @pl.when(micro == 1)
        def _():
            g_turn(1)
            go.turn()
            dh_rows(0).turn()

        def back_rows(d, _):
            total = dot_nt(r.dqkv[micro, :, :cols], r.w_qkv[0, d].reshape(cols, cols))
            for k in (1, 2):
                total = total + dot_nt(
                    r.dqkv[micro, :, k * cols : (k + 1) * cols],
                    r.w_qkv[k, d].reshape(cols, cols),
                )
            r.dh_all[micro, :, at(d * cols, cols)] = total.astype(LOW)
            return 0

        lax.fori_loop(0, n, back_rows, 0)
        dh_rows(micro).begin()
        grads = r.dqkv[micro].astype(F32)
        r.vec[4:5, place] += column_sum(grads[:, :cols])
        r.vec[5:6, place] += column_sum(grads[:, 2 * cols :])
        return 0

    lax.fori_loop(0, batch, one, 0)
    for micro in range(1, batch):
        y_rows(micro).begin()

    def weight_grads(d, _):
        h = r.h_all[:, :, at(d * cols, cols)].reshape(batch * slot, cols)
        grad = dot_tn(h, r.dqkv[...].reshape(batch * slot, 3 * cols)).astype(LOW)
        for k in range(nf):
            r.gq_all[d, k % 2, k // 2] = grad[k * rows_each : (k + 1) * rows_each]
        pair_q(d).start()
        return 0

    lax.fori_loop(0, n, weight_grads, 0)
    r.go_sum[...] = go.finish().astype(LOW)
    start(far_o)
    pair_v.wait()
    for k in range(nz):
        r.mid_sum[k] = r.mid[k, core] + r.mid_pair[k]
    start(far_v)

    def add_pair(d, _):
        pair_q(d).wait()
        total = r.gq_all[d, core].astype(F32) + r.gq_pair[d].astype(F32)
        r.gq_sum[d] = total.astype(LOW)
        return 0

    lax.fori_loop(0, n, add_pair, 0)
    start(far_q)
    for micro in range(1, batch):
        dh_rows(micro).turn()
    for micro in range(batch):
        grad = dh_rows(micro).finish()
        normed, inverse = normal(r.x[micro].astype(F32))
        r.vec[0:1, :] += column_sum(grad * normed)
        r.vec[3:4, :] += column_sum(grad)
        r.dx[micro] = r.dx1[micro] + normal_back(grad * r.wide[0:1, :], normed, inverse)
    spot = lax.broadcasted_iota(jnp.int32, (16, 1), 0)
    own_scales = r.vec[10:11, place]
    for d in range(n):
        block = jnp.where(spot >= 10, 0.0, r.vec[:, d * share : (d + 1) * share])
        r.vec_part[d] = jnp.where(spot == 10 + me, own_scales, block)
    start(shares)
    for micro in range(1, batch):
        y_rows(micro).turn()
    for micro in range(batch):
        total = r.x1[micro] + y_rows(micro).finish() + r.wide[9:10, :]
        r.out[micro] = total.astype(LOW)
    wait(shares)
    total = r.vec_part[me]
    for i in range(1, n):
        total = total + r.vec_got[i - 1]
    r.vec_mine[...] = total
    start(far_vec)
    halves = []
    for w in range(2):
        wait(g_second(w))
        total = r.g_mid[w, two_row].astype(F32)
        for j in range(1, nz // 2):
            total = total + r.g_far[j - 1, w].astype(F32)
        r.g_sum[w] = total.astype(LOW)
        for i, peer in enumerate(peers, 1):
            source = r.g_sum.at[w, :, at((me ^ i) * cols, cols)]
            halves.append(send(source, r.ffn_out.at[w, me], r.d_sems, (i, 4 + w), peer))
    own = [
        pltpu.make_async_copy(r.g_sum.at[w, :, place], r.ffn_out.at[w, me], r.own_sems.at[13 + w])
        for w in range(2)
    ]
    start(halves + own)
    wait(far_o)
    total = r.go_sum[row].astype(F32)
    for j in range(1, nz):
        total = total + r.o_far[j - 1].astype(F32)
    r.o_out[...] = total
    wait(far_v)
    total = r.mid_sum[row]
    for j in range(1, nz):
        total = total + r.v_far[j - 1]
    r.v_out[me] = total
    last = to_peers(
        lambda i, peer: send(r.v_out.at[me], r.v_out.at[me], r.d_sems, (i, 3), peer)
    )
    start(last)
    wait(far_vec)
    total = r.vec_mine[...]
    for j in range(1, nz):
        total = total + r.vec_far[j - 1]
    r.vec_out[...] = total
    r.vec_sum[...] = total
    pair_vec.start()
    wait(far_q)
    for d in range(n):
        total = r.gq_sum[d, row].astype(F32)
        for j in range(1, nz):
            total = total + r.q_far[j - 1, d].astype(F32)
        r.q_last[d] = total
    more = []
    for i, peer in enumerate(peers, 1):
        for k in range(3):
            source = r.q_last.at[me ^ i, :, k * cols : (k + 1) * cols]
            more.append(send(source, r.q_out.at[k, :, place], r.d_sems, (i, k), peer))
    own += [
        pltpu.make_async_copy(
            r.q_last.at[me, :, k * cols : (k + 1) * cols],
            r.q_out.at[k, :, place],
            r.own_sems.at[15 + k],
        )
        for k in range(3)
    ]
    start(more + own[2:])
    wait(last + more + own + halves + [pair_vec])
    r.vec_out[...] += r.vec_pair[...]


def backward(x, dy, kept, lens, scale, n, nf):
    batch, tok, width = x.shape
    _, _, _, rows, cols = kept["w_hbm"].shape
    part = kept["mid"].shape[3]
    slot, nz = n * tok, nf // 2
    share = width // n
    heads = cols // HDIM

    def low(*dims):
        return pltpu.VMEM(dims, LOW)

    def full(*dims):
        return pltpu.VMEM(dims, F32)

    names = ("x1_hbm", "z_hbm", "dh2_hbm", "a_hbm", "g_hbm", "out_hbm", "w_hbm", "h_hbm")
    names += ("qkv_hbm", "p_hbm", "y_hbm")
    inputs = {name: (kept[name], ANY) for name in names}
    inputs["x_hbm"] = (x, ANY)
    inputs["dy_hbm"] = (dy, ANY)
    inputs["wide"] = (kept["wide"], VMEM)
    inputs["mid"] = (kept["mid"], VMEM)
    inputs["lens"] = (lens, SMEM)
    inputs["scale"] = (scale, SMEM)
    outputs = {
        "out": (shape((batch, tok, width), LOW), VMEM),
        "dx": (shape((batch, tok, width), F32), VMEM),
        "q_out": (shape((3, rows, width), F32), VMEM),
        "o_out": (shape((rows, width), F32), VMEM),
        "v_out": (shape((n, 8, part), F32), VMEM),
        "vec_out": (shape((16, share), F32), VMEM),
        "ffn_out": (shape((2, n, part, cols), LOW), VMEM),
    }
    scratch = {
        "x": low(batch, tok, width),
        "dy": low(batch, tok, width),
        "x1": full(batch, tok, width),
        "z": full(batch, tok, width),
        "dh2": full(batch, tok, width),
        "a": low(batch, tok, width),
        "wout": low(n, nf, rows, width),
        "w_qkv": low(3, n, nf, rows, cols),
        "h_all": low(batch, slot, width),
        "qkv_all": low(batch, slot, 3 * cols),
        "p_all": low(batch, heads, slot, slot),
        "y_all": low(batch, slot, width),
        "y_got": low(batch, 2, 2, tok, width // 2),
        "y_passed": low(batch, 2, tok, width // 2),
        "y_last": low(batch, 2, tok, width // 2),
        "dx1": full(batch, tok, width),
        "dz": low(batch * tok, width),
        "do_own": low(batch, n, tok, cols),
        "do_all": low(batch, slot, cols),
        "ds_all": low(2, slot, slot),
        "dqkv": low(batch, slot, 3 * cols),
        "dh_all": low(batch, slot, width),
        "dh_got": low(batch, 2, 2, tok, width // 2),
        "dh_passed": low(batch, 2, tok, width // 2),
        "dh_last": low(batch, 2, tok, width // 2),
        "go_all": low(n, 2, nz, rows, width),
        "go_pair": low(n, nz, rows, width),
        "go_half": low(n, nz, rows, width),
        "go_got": low(2, 2, nz, rows, width // 2),
        "go_passed": low(2, nz, rows, width // 2),
        "go_last": low(2, nz, rows, width // 2),
        "go_sum": low(nz, rows, width),
        "o_far": low(nz - 1, rows, width),
        "gq_all": low(n, 2, nz, rows, 3 * cols),
        "gq_pair": low(n, nz, rows, 3 * cols),
        "gq_sum": low(n, nz, rows, 3 * cols),
        "q_far": low(nz - 1, n, rows, 3 * cols),
        "q_last": full(n, rows, 3 * cols),
        "g_own": low(2, nz // 2, part, width),
        "g_pair": low(2, nz // 2, part, width),
        "g_mid": low(2, nz // 2, part, width),
        "g_far": low(nz // 2 - 1, 2, part, width),
        "g_sum": low(2, part, width),
        "mid_pair": full(nz, 8, part),
        "mid_sum": full(nz, 8, part),
        "v_far": full(nz - 1, 8, part),
        "vec": full(16, width),
        "vec_part": full(n, 16, share),
        "vec_got": full(n - 1, 16, share),
        "vec_mine": full(16, share),
        "vec_far": full(nz - 1, 16, share),
        "vec_sum": full(16, share),
        "vec_pair": full(16, share),
        "o_sems": DMA((2, batch, n)),
        "h_sems": DMA((2, batch, 2, 3)),
        "y_sems": DMA((2, batch, 2, 3)),
        "p_sems": DMA((2, 3)),
        "q_sems": DMA((2, n)),
        "e_sems": DMA((2, 2, 3)),
        "g_sems": DMA((2, nz // 2, 2)),
        "z_sems": DMA((2, nz, 5)),
        "d_sems": DMA((2, n, 7)),
        "own_sems": DMA((18,)),
    }
    return launch(
        lambda r: backward_kernel(n, nf, r), "backward", inputs, outputs, scratch, 1, 60
    )


def on_device(
    tokens,
    seq_lens,
    qkv_weight,
    out_weight,
    head_scale,
    gains,
    biases,
    ffn_in,
    ffn_bias,
    mid_gain,
    mid_bias,
    ffn_out,
    out_cotangent,
):
    n = lax.axis_size("dp")
    nf = lax.axis_size("ffn")
    me = lax.axis_index("dp")
    f = lax.axis_index("ffn")
    batch, _, tok, width = tokens.shape
    heads = head_scale.shape[0]
    cols = width // n
    rows = qkv_weight.shape[1]
    hid = ffn_in.shape[1]
    part = hid // n

    def tiled(values):
        size = values.shape[1]
        spot = lax.rem(f, 128 // size) * size
        return lax.dynamic_update_slice(jnp.zeros((16, 128), LOW), values, (0, spot))

    vectors = lax.dynamic_index_in_dim(
        jnp.stack([ffn_bias, mid_gain, mid_bias]).reshape(3, n, part), me, 1, keepdims=False
    )
    x, dy = tokens[:, 0], out_cotangent[:, 0]
    kept = forward(
        x,
        qkv_weight,
        out_weight,
        jnp.stack([tiled(jnp.concatenate([gains, biases])), tiled(vectors)]),
        ffn_in.T.reshape(n, part, cols),
        ffn_out.reshape(n, part, cols),
        dy,
        seq_lens,
        head_scale,
        n,
        nf,
    )
    done = backward(x, dy, kept, seq_lens, head_scale, n, nf)
    vec, ffn, output, tokens_grad = done["vec_out"], done["ffn_out"], done["out"], done["dx"]
    qkv_grad, out_weight_grad = done["q_out"], done["o_out"]
    mid = done["v_out"].transpose(1, 0, 2).reshape(8, hid)
    own = lax.dynamic_slice_in_dim(vec, f * rows, rows, 1)
    ffn = ffn.reshape(2, hid, cols)
    return (
        output[:, None],
        tokens_grad[:, None],
        qkv_grad,
        out_weight_grad,
        vec[10 : 10 + n, ::HDIM].reshape(heads),
        own[:3],
        own[3:10],
        ffn[0].T.astype(F32),
        mid[0],
        mid[1],
        mid[2],
        ffn[1].astype(F32),
    )


def solution(mesh):
    seqs = P(None, "ffn", "dp", None)
    wide = P(None, ("dp", "ffn"))
    hidden = P("ffn")
    return jax.shard_map(
        on_device,
        mesh=mesh,
        in_specs=(
            seqs,
            P(None, "ffn"),
            P(None, ("dp", "ffn"), None),
            P(("dp", "ffn"), None),
            P(),
            wide,
            wide,
            P("dp", "ffn"),
            hidden,
            hidden,
            hidden,
            P("ffn", "dp"),
            seqs,
        ),
        out_specs=(
            seqs,
            seqs,
            P(None, ("dp", "ffn"), None),
            P(("dp", "ffn"), None),
            P(),
            wide,
            wide,
            P("dp", "ffn"),
            hidden,
            hidden,
            hidden,
            P("ffn", "dp"),
        ),
        check_vma=False,
    )
```

```python
from types import SimpleNamespace

import jax
import jax.numpy as jnp
from jax import lax
from jax.experimental import pallas as pl
from jax.experimental.pallas import tpu as pltpu
from jax.sharding import PartitionSpec as P

HDIM = 64
EPS = 1e-05
LOW = jnp.bfloat16
F32 = jnp.float32
ANY = pl.BlockSpec(memory_space=pl.ANY)
VMEM = pl.BlockSpec(memory_space=pltpu.VMEM)
SMEM = pl.BlockSpec(memory_space=pltpu.SMEM)
MESH = pl.DeviceIdType.MESH
DMA = pltpu.SemaphoreType.DMA


def dot(left, right):
    return jnp.dot(left, right, preferred_element_type=F32)


def dot_nt(left, right):
    return lax.dot_general(left, right, (((1,), (1,)), ((), ())), preferred_element_type=F32)


def dot_tn(left, right):
    return lax.dot_general(left, right, (((0,), (0,)), ((), ())), preferred_element_type=F32)


def shape(dims, kind):
    return jax.ShapeDtypeStruct(tuple(dims), kind)


def at(start, size, unit=128):
    return pl.ds(pl.multiple_of(start, unit), size)


def send(src, dst, sems, index, where):
    return pltpu.make_async_remote_copy(
        src_ref=src,
        dst_ref=dst,
        send_sem=sems.at[(0, *index)],
        recv_sem=sems.at[(1, *index)],
        device_id=where,
        device_id_type=MESH,
    )


def greet(peers):
    barrier = pltpu.get_barrier_semaphore()
    for peer in peers:
        pl.semaphore_signal(barrier, inc=1, device_id=peer, device_id_type=MESH)


def meet(peers):
    pl.semaphore_wait(pltpu.get_barrier_semaphore(), len(peers))


def dp_peers(n, me):
    return [{"dp": me ^ i} for i in range(1, n)]


def ffn_peers(nf, f):
    return [{"ffn": f ^ (2 * j)} for j in range(1, nf // 2)] + [{"ffn": f ^ 1}]


def start(copies):
    for copy in copies:
        copy.start()


def wait(copies):
    for copy in copies:
        copy.wait()


class Line:
    def __init__(self, nf, f, items, hop_sems, side_sems):
        self.nz, self.core, self.q, self.f = nf // 2, lax.rem(f, 2), lax.div(f, 2), f
        self.items, self.hop_sems, self.side_sems = items, hop_sems, side_sems
        self.next = [1] * len(items)

    def copy(self, sems, k, t, came, way, first, target):
        source, place = self.items[k]
        index = self.f if first else 2 * (self.q - t * way) + self.core
        spot = place(index)
        side = 0 if way > 0 else 1
        return pltpu.make_async_remote_copy(
            src_ref=source if first else spot,
            dst_ref=spot,
            send_sem=sems.at[0, side, k, t],
            recv_sem=sems.at[1, side, k, came],
            device_id={"ffn": target},
            device_id_type=MESH,
        )

    def hop(self, k, t, way, first=False):
        return self.copy(self.hop_sems, k, t, t + 1, way, first, self.f + 2 * way)

    def arrival(self, k, t, way):
        return self.copy(self.hop_sems, k, t, t, way, False, self.f + 2 * way)

    def over(self, k, t, way, first=False):
        return self.copy(self.side_sems, k, t, t, way, first, self.f ^ 1)

    def onward(self, way):
        return self.q < self.nz - 1 if way > 0 else self.q > 0

    def has(self, t, way):
        return self.q - t >= 0 if way > 0 else self.q + t <= self.nz - 1

    def begin(self, *items):
        for k in items:
            for way in (1, -1):

                @pl.when(self.onward(way))
                def _():
                    self.hop(k, 0, way, True).start()

        for k in items:
            self.over(k, 0, 1, True).start()

    def step(self, k, t):
        for way in (1, -1):

            @pl.when(self.has(t, way) & self.onward(way))
            def _():
                self.arrival(k, t, way).wait_recv()
                self.hop(k, t, way).start()

        for way in (1, -1):

            @pl.when(self.has(t, way))
            def _():
                @pl.when(jnp.logical_not(self.onward(way)))
                def _():
                    self.arrival(k, t, way).wait_recv()

                self.over(k, t, way).start()

    def advance(self, *items):
        for k in items:
            if self.next[k] < self.nz:
                self.step(k, self.next[k])
                self.next[k] += 1

    def arrive(self, *items):
        begin = self.next[items[0]]

        def rest(t, _):
            for k in items:
                self.step(k, t)
            return 0

        lax.fori_loop(begin, self.nz, rest, 0)

        def close(t, _):
            for k in items:
                for way in (1, -1):

                    @pl.when(self.has(t, way))
                    def _():
                        self.over(k, t, way).wait_recv()

            return 0

        for k in items:
            self.over(k, 0, 1, True).wait_recv()
        lax.fori_loop(1, self.nz, close, 0)

    def finish(self, *items):
        for k in items:
            self.over(k, 0, 1, True).wait_send()
            for way in (1, -1):

                @pl.when(self.onward(way))
                def _():
                    self.hop(k, 0, way, True).wait_send()

        def close(t, _):
            for k in items:
                for way in (1, -1):

                    @pl.when(self.has(t, way))
                    def _():
                        self.over(k, t, way).wait_send()

                    @pl.when(self.has(t, way) & self.onward(way))
                    def _():
                        self.hop(k, t, way).wait_send()

            return 0

        lax.fori_loop(1, self.nz, close, 0)


def line_meet(n, nf, me, f):
    barrier = pltpu.get_barrier_semaphore()
    q, nz = lax.div(f, 2), nf // 2
    greet(dp_peers(n, me) + [{"ffn": f ^ 1}])

    @pl.when(q < nz - 1)
    def _():
        greet([{"ffn": f + 2}])

    @pl.when(q > 0)
    def _():
        greet([{"ffn": f - 2}])

    count = n + jnp.where(q < nz - 1, 1, 0) + jnp.where(q > 0, 1, 0)
    pl.semaphore_wait(barrier, count)


class Gather:
    def __init__(self, me, source, place, size, sems, index):
        self.me, self.source, self.place, self.half = me, source, place, size // 2
        self.sems, self.index = sems, index

    def straight(self, k):
        spot = self.place(self.me, 0, 2 * self.half)
        return send(self.source, spot, self.sems, (*self.index, k), {"dp": self.me ^ (k + 1)})

    def relay(self, k):
        spot = self.place(self.me ^ (k + 1), k * self.half, self.half)
        return send(spot, spot, self.sems, (*self.index, 2 + k), {"dp": self.me ^ (2 - k)})

    def begin(self):
        for k in range(2):
            self.straight(k).start()

    def turn(self):
        for k in range(2):
            self.straight(k).wait()
            self.relay(k).start()

    def finish(self):
        for k in range(2):
            self.relay(k).wait()


class Reduce:
    def __init__(self, me, block, got, passed, last, sems, index):
        self.me, self.block, self.passed = me, block, passed
        self.got, self.last, self.sems, self.index = got, last, sems, index

    def first(self, side, far):
        step = side + 1
        owner = self.me ^ (3 if far else step)
        target = self.got.at[(*self.index, side, far)]
        spot = (*self.index, side, far)
        return send(self.block(owner, side), target, self.sems, spot, {"dp": self.me ^ step})

    def second(self, side):
        where = (*self.index, side)
        target = {"dp": self.me ^ (2 - side)}
        return send(self.passed.at[where], self.last.at[where], self.sems, (*where, 2), target)

    def begin(self):
        for far in (1, 0):
            for side in range(2):
                self.first(side, far).start()

    def turn(self):
        for side in range(2):
            self.first(side, 1).wait()
            total = self.block(self.me ^ (2 - side), side)[...].astype(F32)
            total = total + self.got[(*self.index, side, 1)].astype(F32)
            self.passed[(*self.index, side)] = total.astype(LOW)
            self.second(side).start()

    def finish(self):
        halves = []
        for side in range(2):
            self.first(side, 0).wait()
            self.second(side).wait()
            total = self.block(self.me, side)[...].astype(F32)
            total = total + self.got[(*self.index, side, 0)].astype(F32)
            halves.append(total + self.last[(*self.index, side)].astype(F32))
        return jnp.concatenate(halves, axis=-1)


def normal(values):
    center = values - jnp.mean(values, axis=-1, keepdims=True)
    inverse = lax.rsqrt(jnp.mean(center * center, axis=-1, keepdims=True) + EPS)
    return center * inverse, inverse


def normal_back(grad, normed, inverse):
    return inverse * (
        grad
        - jnp.mean(grad, axis=-1, keepdims=True)
        - normed * jnp.mean(grad * normed, axis=-1, keepdims=True)
    )


def column_sum(values):
    return jnp.sum(values, axis=0, keepdims=True)


def launch(body, name, inputs, outputs, scratch, number, limit):
    names = [*inputs, *outputs, *scratch]
    results = pl.pallas_call(
        lambda *refs: body(SimpleNamespace(**dict(zip(names, refs)))),
        name=name,
        out_shape=tuple(kind for kind, _ in outputs.values()),
        in_specs=[spec for _, spec in inputs.values()],
        out_specs=tuple(spec for _, spec in outputs.values()),
        scratch_shapes=list(scratch.values()),
        compiler_params=pltpu.CompilerParams(
            collective_id=number, has_side_effects=True, vmem_limit_bytes=limit << 20
        ),
    )(*[value for value, _ in inputs.values()])
    return dict(zip(outputs, results))


def forward_kernel(n, nf, part, r):
    me = lax.axis_index("dp")
    f = lax.axis_index("ffn")
    core, nz = lax.rem(f, 2), nf // 2
    batch, tok, width = r.x.shape
    rows_each = r.wout.shape[0]
    cols = width // n
    pairs = cols // 128
    slot = n * tok
    hid = nf * part
    ff = n * hid
    step = 256
    peers = dp_peers(n, me)
    pair = {"ffn": f ^ 1}
    place = at(me * cols, cols)
    band = at(me * tok, tok)

    own = [
        pltpu.make_async_copy(r.qkv.at[:, :, place], r.stage.at[:, me], r.own_sems.at[0]),
        pltpu.make_async_copy(r.small.at[0], r.small_stage.at[me], r.own_sems.at[1]),
        pltpu.make_async_copy(r.small.at[1], r.small_stage.at[n], r.own_sems.at[2]),
        pltpu.make_async_copy(r.wout, r.out_stage.at[me], r.own_sems.at[3]),
        pltpu.make_async_copy(r.first, r.first_in, r.own_sems.at[4]),
        pltpu.make_async_copy(r.second.at[me], r.second_stage.at[:, place], r.own_sems.at[5]),
        pltpu.make_async_copy(r.x, r.x_all.at[me], r.own_sems.at[6]),
        pltpu.make_async_copy(r.dy, r.dy_all.at[:, band, :], r.own_sems.at[7]),
    ]
    start(own)
    line_meet(n, nf, me, f)

    def to_peers(make):
        return [make(i, peer) for i, peer in enumerate(peers, 1)]

    blocks = to_peers(
        lambda i, peer: send(
            r.qkv.at[:, :, at((me ^ i) * cols, cols)], r.stage.at[:, me], r.w_sems, (i, 0), peer
        )
    )
    smalls = to_peers(
        lambda i, peer: send(r.small.at[0], r.small_stage.at[me], r.w_sems, (i, 1), peer)
    )
    outs = to_peers(lambda i, peer: send(r.wout, r.out_stage.at[me], r.w_sems, (i, 2), peer))
    firsts = to_peers(
        lambda i, peer: send(
            r.first_all.at[me ^ i], r.first_stage.at[:, place], r.w_sems, (i, 3), peer
        )
    )
    seconds = to_peers(
        lambda i, peer: send(
            r.second.at[me ^ i], r.second_stage.at[:, place], r.w_sems, (i, 4), peer
        )
    )

    def x_rows(micro):
        def spot(owner, start, size):
            return r.x_all.at[owner, micro, start : start + size]

        return Gather(me, r.x.at[micro], spot, tok, r.x_sems, (micro,))

    def y_rows(micro):
        def spot(owner, start, size):
            return r.dy_all.at[micro, at(owner * tok + start, size, 64), :]

        return Gather(me, r.dy.at[micro], spot, tok, r.y_sems, (micro,))

    start(blocks + smalls)
    x_rows(0).begin()
    wait(own[4:5])
    r.first_all[...] = r.first_in[...].T.reshape(r.first_all.shape)
    own[4] = pltpu.make_async_copy(
        r.first_all.at[me], r.first_stage.at[:, place], r.own_sems.at[4]
    )
    start(own[4:5])
    start(outs + firsts)
    line = Line(
        nf,
        f,
        [
            (r.stage, lambda index: r.w_all.at[:, :, index]),
            (r.small_stage, lambda index: r.small_all.at[index]),
            (r.out_stage, lambda index: r.out_all.at[:, index]),
            (r.first_stage, lambda index: r.w1.at[index]),
            (r.second_stage, lambda index: r.w2.at[index]),
        ],
        r.hop_sems,
        r.side_sems,
    )
    mine = [
        pltpu.make_async_copy(source, spot(f), r.own_sems.at[8 + k])
        for k, (source, spot) in enumerate(line.items)
    ]
    wait(blocks + smalls + own[:3])
    line.begin(0, 1)
    start(mine[:2])
    line.advance(0, 1)
    x_rows(0).turn()
    x_rows(1).begin()
    line.advance(0, 1)
    wait(outs + own[3:4])
    line.begin(2)
    start(mine[2:3])
    line.arrive(0, 1)
    wait(firsts + own[4:5])
    line.begin(3)
    start(mine[3:4])
    wait(mine[:2] + own[6:7])

    def lay_out(out_ref, index, begin, size):
        together = 128 // size
        for b in range(nf // together):
            total = r.small_all[b * together, index].astype(F32)
            for k in range(1, together):
                total = total + r.small_all[b * together + k, index].astype(F32)
            out_ref[:, begin + b * 128 : begin + (b + 1) * 128] = total

    for d in range(n):
        lay_out(r.wide, d, d * nf * rows_each, rows_each)
    lay_out(r.mids, n, 0, part)

    gain, shift = r.wide[0:1, :], r.wide[3:4, :]
    bias_q, bias_v = r.wide[4:5, place], r.wide[5:6, place]
    left = lax.broadcasted_iota(jnp.int32, (1, 128), 1) < HDIM

    def block_copies(micro):
        return to_peers(
            lambda i, peer: send(
                r.a_all.at[micro, me ^ i], r.a_own.at[micro, :, place], r.a_sems, (micro, i), peer
            )
        )

    def keep_copies(micro):
        return [
            pltpu.make_async_copy(source.at[micro], out.at[micro], r.keep_sems.at[micro, k])
            for k, (source, out) in enumerate(
                [(r.h_all, r.h_hbm), (r.qkv_all, r.qkv_hbm), (r.p_all, r.p_hbm)]
            )
        ]

    def after_first():
        line.advance(2)
        x_rows(1).turn()
        start(seconds)
        y_rows(0).begin()

    def after_second():
        line.advance(3)

    def after_third():
        line.advance(2)
        wait(seconds + own[5:6])
        line.begin(4)
        start(mine[4:5])

    def after_last():
        y_rows(0).turn()
        y_rows(1).begin()
        line.advance(3)

    def attend(index, _):
        micro, two = lax.div(index, pairs), lax.rem(index, pairs)

        @pl.when(two == 0)
        def _():
            x_rows(micro).finish()

            def norm_rows(d, _):
                values, _ = normal(r.x_all[d, micro].astype(F32))
                r.h_all[micro, at(d * tok, tok), :] = (values * gain + shift).astype(LOW)
                return 0

            lax.fori_loop(0, n, norm_rows, 0)
            for k, bias in enumerate((bias_q, None, bias_v)):
                weight = r.w_all[k].reshape(width, cols)
                value = dot(r.h_all[micro], weight)
                if bias is not None:
                    value = value + bias
                r.qkv_all[micro, :, k * cols : (k + 1) * cols] = value.astype(LOW)

        length = r.lens[micro]

        def column(k):
            return at(k * cols + two * 128, 128)

        head = two * 2
        scales = jnp.where(
            left, r.scale[me * 2 * pairs + head], r.scale[me * 2 * pairs + head + 1]
        )
        for block in range(n):
            end = (block + 1) * tok
            q = r.qkv_all[micro, block * tok : end, column(0)] * HDIM ** (-0.5)
            k = r.qkv_all[micro, :end, column(1)]
            v = r.qkv_all[micro, :end, column(2)]
            key = lax.broadcasted_iota(jnp.int32, (tok, end), 1)
            query = lax.broadcasted_iota(jnp.int32, (tok, end), 0) + block * tok
            mask = (key <= query) & (key < length)
            out = []
            for side in range(2):
                mine_ = left if side == 0 else jnp.logical_not(left)
                scores = dot_nt(jnp.where(mine_, q, jnp.zeros_like(q)), k)
                scores = jnp.where(mask, scores, -1e30)
                expo = jnp.exp(scores - jnp.max(scores, axis=-1, keepdims=True))
                probs = expo * (1.0 / jnp.sum(expo, axis=-1, keepdims=True))
                probs = probs.astype(LOW)
                r.p_all[micro, head + side, block * tok : end, :end] = probs
                out.append(dot(probs, v))
            joined = jnp.where(left, out[0], out[1]) * scales
            r.a_all[micro, block, :, at(two * 128, 128)] = joined.astype(LOW)

        @pl.when(two == pairs - 1)
        def _():
            start(block_copies(micro))
            start(keep_copies(micro))
            r.a_own[micro, :, place] = r.a_all[micro, me]

        work = [after_first, after_second, after_third, after_last]
        for k, act in enumerate(work[: batch * pairs]):
            pl.when(index == k)(act)
        return 0

    lax.fori_loop(0, batch * pairs, attend, 0)

    line.arrive(2)
    wait(mine[2:3])
    late = [
        pltpu.make_async_copy(source, target, r.own_sems.at[13 + k])
        for k, (source, target) in enumerate(
            [(r.w_all, r.w_hbm), (r.out_all, r.out_hbm), (r.z, r.z_hbm), (r.x1, r.x1_hbm),
             (r.a_own, r.a_hbm), (r.y, r.y_hbm), (r.pair_got, r.g_hbm), (r.dh2, r.dh2_hbm)]
        )
    ]
    start(late[:2])

    def h2_rows(micro):
        def spot(owner, start, size):
            return r.h2_all.at[micro, at(owner * tok + start, size, 64), :]

        return Gather(me, r.h2_own.at[micro], spot, tok, r.h_sems, (micro,))

    for micro in range(batch):
        wait(block_copies(micro))
        z = dot(r.a_own[micro], r.out_all[...].reshape(width, width)) + r.wide[6:7, :]
        r.z[micro] = z
        values, _ = normal(z)
        x1 = r.x_all[me, micro].astype(F32) + values * r.wide[1:2, :] + r.wide[7:8, :]
        r.x1[micro] = x1
        values, _ = normal(x1)
        r.h2_own[micro] = (values * r.wide[2:3, :] + r.wide[8:9, :]).astype(LOW)
        h2_rows(micro).begin()
        r.h2_all[micro, band, :] = r.h2_own[micro]
    start(late[2:5])
    line.advance(4)
    h2_rows(0).turn()
    y_rows(1).turn()
    for micro in range(1, batch):
        h2_rows(micro).turn()
    line.arrive(3)
    wait(mine[3:4])

    def weights(ref, c):
        count = step // part
        return ref[pl.ds(c * count, count)].reshape(step, width)

    def w_columns(ref, columns):
        return ref[:, :, columns].reshape(hid, step)

    def sum_copies(micro):
        return to_peers(
            lambda i, peer: send(
                r.sums.at[micro], r.sums_all.at[micro, me], r.s_sems, (micro, i), peer
            )
        )

    def dh2_rows(micro):
        def block(owner, side):
            columns = slice(side * (width // 2), (side + 1) * (width // 2))
            return r.dh2_all.at[micro, at(owner * tok, tok), columns]

        return Reduce(me, block, r.dh2_got, r.dh2_passed, r.dh2_last, r.r_sems, (micro,))

    def fold(values):
        total = values[:, :128]
        for k in range(1, step // 128):
            total = total + values[:, k * 128 : (k + 1) * 128]
        return total

    def units(micro):
        h2_rows(micro).finish()

        def chunk(c, totals):
            rows = at(c * step, step)
            u = dot_nt(r.h2_all[micro], weights(r.w1, c)) + r.mids[0:1, rows]
            phi = 0.5 + 0.5 * lax.erf(u * (0.5**0.5))
            value = u * phi
            r.act[micro, :, rows] = value
            r.slope[micro, :, rows] = phi + u * jnp.exp(u * u * -0.5) * 0.3989422804014327
            return totals[0] + fold(value), totals[1] + fold(value * value)

        zero = jnp.zeros((slot, 128), F32)
        totals = lax.fori_loop(0, hid // step, chunk, (zero,) * 2)
        for k in range(2):
            r.sums[micro, k : k + 1, :] = column_sum(totals[k].T)

    def cotangents(micro):
        y_rows(micro).finish()
        valid = lax.broadcasted_iota(jnp.int32, (slot, 1), 0) < r.lens[micro]
        rows = r.dy_all[micro]
        r.dy_all[micro] = jnp.where(valid, rows, jnp.zeros_like(rows))

        def chunk(c, totals):
            rows = at(c * step, step)
            dm = dot_nt(r.dy_all[micro], weights(r.w2, c))
            r.dmix[micro, :, rows] = dm
            dn = dm * r.mids[1:2, rows]
            return totals[0] + fold(dn), totals[1] + fold(dn * r.act[micro, :, rows])

        zero = jnp.zeros((slot, 128), F32)
        totals = lax.fori_loop(0, hid // step, chunk, (zero,) * 2)
        for k in range(2):
            r.sums[micro, 2 + k : 3 + k, :] = column_sum(totals[k].T)
        r.sums[micro, 4:8, :] = jnp.zeros((4, slot), F32)
        start(sum_copies(micro))

    r.vec[...] = jnp.zeros_like(r.vec)

    def second_pass(micro, _):
        wait(sum_copies(micro))
        r.sums_all[micro, me] = r.sums[micro]
        total = r.sums_all[micro, 0]
        for d in range(1, n):
            total = total + r.sums_all[micro, d]
        total = total * (1.0 / ff)
        mean = total[0:1]
        inverse = lax.rsqrt(total[1:2] - mean * mean + EPS)
        back = total[2:3]
        cross = inverse * (total[3:4] - mean * back)
        table = jnp.concatenate([mean, inverse, back, cross] * 32, axis=0).T
        mean, inverse, back, cross = [table[:, k : k + 1] for k in range(4)]
        rows_of = at(micro * slot, slot)

        def chunk(c, _):
            rows = at(c * step, step)
            normed = (r.act[micro, :, rows] - mean) * inverse
            dm = r.dmix[micro, :, rows]
            gain = r.mids[1:2, rows]
            r.mixed[rows_of, rows] = (normed * gain + r.mids[2:3, rows]).astype(LOW)
            df = inverse * (dm * gain - back - normed * cross)
            low = (df * r.slope[micro, :, rows]).astype(LOW)
            r.du[rows_of, rows] = low
            r.vec[0:1, rows] += column_sum(low.astype(F32))
            r.vec[1:2, rows] += column_sum(dm * normed)
            r.vec[2:3, rows] += column_sum(dm)
            return 0

        lax.fori_loop(0, hid // step, chunk, 0)

        def back_rows(c, _):
            columns = at(c * step, step)
            value = dot(r.du[rows_of, :], w_columns(r.w1, columns))
            r.dh2_all[micro, :, columns] = value.astype(LOW)
            return 0

        lax.fori_loop(0, width // step, back_rows, 0)
        dh2_rows(micro).begin()
        return 0

    def passes(micro, _):
        units(micro)

        @pl.when(micro == 0)
        def _():
            line.arrive(4)
            wait(mine[4:5] + own[7:8])

        cotangents(micro)

        @pl.when(micro > 0)
        def _():
            dh2_rows(micro - 1).turn()

        second_pass(micro, 0)
        return 0

    lax.fori_loop(0, batch, passes, 0)
    each = step // part // 2

    def halved(index):
        return lax.div(index, 2), lax.rem(index, 2)

    def pair_copies(c):
        copies = []
        for k in range(each):
            index = c * (2 * each) + 2 * k
            for w in range(2):
                copies.append(
                    send(
                        r.grads.at[w, index + 1 - core],
                        r.pair_got.at[(w, *halved(c * each + k))],
                        r.p_sems,
                        (c, k, w),
                        pair,
                    )
                )
        return copies

    def weight_grads(c, _):
        rows = at(c * step, step)
        h2 = r.h2_all[...].reshape(batch * slot, width)
        dy = r.dy_all[...].reshape(batch * slot, width)
        first = dot_tn(r.du[:, rows], h2).astype(LOW)
        second = dot_tn(r.mixed[:, rows], dy).astype(LOW)
        for k in range(step // part):
            r.grads[0, c * (step // part) + k] = first[k * part : (k + 1) * part]
            r.grads[1, c * (step // part) + k] = second[k * part : (k + 1) * part]
        start(pair_copies(c))
        return 0

    lax.fori_loop(0, hid // step, weight_grads, 0)
    dh2_rows(batch - 1).turn()

    def out_rows(c, _):
        columns = at(c * step, step)
        for micro in range(batch):
            value = dot(r.mixed[micro * slot : (micro + 1) * slot, :], w_columns(r.w2, columns))
            r.y[micro, :, columns] = value.astype(LOW)
        return 0

    lax.fori_loop(0, width // step, out_rows, 0)
    start(late[5:6])

    def pair_sum(c, _):
        wait(pair_copies(c))
        for k in range(each):
            for w in range(2):
                total = r.grads[w, c * (2 * each) + 2 * k + core].astype(F32)
                spot = (w, *halved(c * each + k))
                total = total + r.pair_got[spot].astype(F32)
                r.pair_got[spot] = total.astype(LOW)
        return 0

    lax.fori_loop(0, hid // step, pair_sum, 0)
    start(late[6:7])
    for k in range(nf):
        r.mid[k // 2, k % 2] = r.vec[:, k * part : (k + 1) * part]
    line.finish(0, 1, 2, 3, 4)
    for micro in range(batch):
        wait(keep_copies(micro))
    for micro in range(batch):
        r.dh2[micro] = dh2_rows(micro).finish()
    start(late[7:])
    wait(late)


def forward(x, qkv, wout, small, first, second, dy, lens, scale, n, nf):
    batch, tok, width = x.shape
    rows = wout.shape[0]
    part = second.shape[1]
    cols = width // n
    slot, hid = n * tok, nf * part
    heads = cols // HDIM

    def low(*dims):
        return pltpu.VMEM(dims, LOW)

    def full(*dims):
        return pltpu.VMEM(dims, F32)

    inputs = {
        name: (value, ANY)
        for name, value in zip(
            ("x", "qkv", "wout", "small", "first", "second", "dy"),
            (x, qkv, wout, small, first, second, dy),
        )
    }
    inputs["lens"] = (lens, SMEM)
    inputs["scale"] = (scale, SMEM)
    outputs = {
        "wide": (shape((16, width), F32), VMEM),
        "w_hbm": (shape((3, n, nf, rows, cols), LOW), ANY),
        "out_hbm": (shape((n, nf, rows, width), LOW), ANY),
        "h_hbm": (shape((batch, slot, width), LOW), ANY),
        "qkv_hbm": (shape((batch, slot, 3 * cols), LOW), ANY),
        "p_hbm": (shape((batch, heads, slot, slot), LOW), ANY),
        "a_hbm": (shape((batch, tok, width), LOW), ANY),
        "z_hbm": (shape((batch, tok, width), F32), ANY),
        "x1_hbm": (shape((batch, tok, width), F32), ANY),
        "y_hbm": (shape((batch, slot, width), LOW), ANY),
        "g_hbm": (shape((2, nf // 4, 2, part, width), LOW), ANY),
        "dh2_hbm": (shape((batch, tok, width), F32), ANY),
        "mid": (shape((nf // 2, 2, 8, part), F32), VMEM),
    }
    scratch = {
        "mids": full(16, hid),
        "dh2": full(batch, tok, width),
        "vec": full(8, hid),
        "stage": low(3, n, rows, cols),
        "small_stage": low(n + 1, *small.shape[1:]),
        "out_stage": low(n, rows, width),
        "first_in": low(*first.shape),
        "first_all": low(*second.shape),
        "first_stage": low(part, width),
        "second_stage": low(part, width),
        "small_all": low(nf, n + 1, *small.shape[1:]),
        "w_all": low(3, n, nf, rows, cols),
        "out_all": low(n, nf, rows, width),
        "w1": low(nf, part, width),
        "w2": low(nf, part, width),
        "x_all": low(n, batch, tok, width),
        "dy_all": low(batch, slot, width),
        "h_all": low(batch, slot, width),
        "qkv_all": low(batch, slot, 3 * cols),
        "p_all": low(batch, heads, slot, slot),
        "a_all": low(batch, n, tok, cols),
        "a_own": low(batch, tok, width),
        "z": full(batch, tok, width),
        "x1": full(batch, tok, width),
        "h2_own": low(batch, tok, width),
        "h2_all": low(batch, slot, width),
        "act": full(batch, slot, hid),
        "slope": full(batch, slot, hid),
        "dmix": full(batch, slot, hid),
        "mixed": low(batch * slot, hid),
        "du": low(batch * slot, hid),
        "sums": full(batch, 8, slot),
        "sums_all": full(batch, n, 8, slot),
        "dh2_all": low(batch, slot, width),
        "dh2_got": low(batch, 2, 2, tok, width // 2),
        "dh2_passed": low(batch, 2, tok, width // 2),
        "dh2_last": low(batch, 2, tok, width // 2),
        "y": low(batch, slot, width),
        "grads": low(2, nf, part, width),
        "pair_got": low(2, nf // 4, 2, part, width),
        "w_sems": DMA((2, n, 5)),
        "x_sems": DMA((2, batch, 4)),
        "y_sems": DMA((2, batch, 4)),
        "a_sems": DMA((2, batch, n)),
        "h_sems": DMA((2, batch, 4)),
        "s_sems": DMA((2, batch, n)),
        "r_sems": DMA((2, batch, 2, 3)),
        "p_sems": DMA((2, hid // 256, 128 // part, 2)),
        "hop_sems": DMA((2, 2, 5, nf // 2)),
        "side_sems": DMA((2, 2, 5, nf // 2)),
        "keep_sems": DMA((batch, 3)),
        "own_sems": DMA((21,)),
    }
    return launch(
        lambda r: forward_kernel(n, nf, part, r), "forward", inputs, outputs, scratch, 0, 63
    )


def backward_kernel(n, nf, r):
    me = lax.axis_index("dp")
    f = lax.axis_index("ffn")
    core, row, nz = lax.rem(f, 2), lax.div(f, 2), nf // 2
    even, two_row = lax.rem(row, 2), lax.div(row, 2)
    batch, tok, width = r.dx.shape
    slot = n * tok
    cols = width // n
    rows_each = r.o_out.shape[0]
    pairs = cols // 128
    heads = cols // HDIM
    share = width // n
    step = 256
    peers = dp_peers(n, me)
    pair = {"ffn": f ^ 1}
    everyone = peers + ffn_peers(nf, f)
    greet(everyone)
    band = at(me * tok, tok)
    place = at(me * cols, cols)
    loads = [
        pltpu.make_async_copy(source, target, r.own_sems.at[k])
        for k, (source, target) in enumerate(
            [(r.x1_hbm, r.x1), (r.dh2_hbm, r.dh2), (r.dy_hbm, r.dy), (r.z_hbm, r.z),
             (r.out_hbm, r.wout), (r.a_hbm, r.a), (r.qkv_hbm, r.qkv_all), (r.p_hbm, r.p_all),
             (r.w_hbm, r.w_qkv), (r.h_hbm, r.h_all), (r.x_hbm, r.x), (r.g_hbm.at[:, :, even], r.g_own),
             (r.y_hbm, r.y_all)]
        )
    ]
    start(loads)
    r.vec[...] = jnp.zeros_like(r.vec)

    def to_peers(make):
        return [make(i, peer) for i, peer in enumerate(peers, 1)]

    def along(make):
        return [make(j, {"ffn": f ^ (2 * j)}) for j in range(1, nz)]

    def columns_of(side):
        return slice(side * (width // 2), (side + 1) * (width // 2))

    def y_rows(micro):
        def block(owner, side):
            return r.y_all.at[micro, at(owner * tok, tok), columns_of(side)]

        return Reduce(me, block, r.y_got, r.y_passed, r.y_last, r.y_sems, (micro,))

    def dh_rows(micro):
        def block(owner, side):
            return r.dh_all.at[micro, at(owner * tok, tok), columns_of(side)]

        return Reduce(me, block, r.dh_got, r.dh_passed, r.dh_last, r.h_sems, (micro,))

    def go_block(owner, side):
        return r.go_half.at[owner, :, :, columns_of(side)]

    go = Reduce(me, go_block, r.go_got, r.go_passed, r.go_last, r.e_sems, ())

    def g_first(w):
        return send(
            r.g_hbm.at[w, :, 1 - even], r.g_pair.at[w], r.g_sems, (0, w), {"ffn": f ^ 2}
        )

    def g_second(w):
        return [
            send(r.g_mid.at[w, two_row ^ j], r.g_far.at[j - 1, w], r.g_sems, (j, w), {"ffn": f ^ (4 * j)})
            for j in range(1, nz // 2)
        ]

    def g_turn(w):
        g_first(w).wait()
        for k in range(nz // 2):
            total = r.g_own[w, k].astype(F32) + r.g_pair[w, k].astype(F32)
            r.g_mid[w, k] = total.astype(LOW)
        start(g_second(w))

    pair_v = send(r.mid.at[:, 1 - core], r.mid_pair, r.p_sems, (1,), pair)
    wait(loads[:4] + loads[12:])
    meet(everyone)
    for w in range(2):
        g_first(w).start()
    pair_v.start()
    y_rows(0).begin()
    for micro in range(batch):
        normed, inverse = normal(r.x1[micro])
        grad = r.dh2[micro]
        r.vec[2:3, :] += column_sum(grad * normed)
        r.vec[8:9, :] += column_sum(grad)
        valid = lax.broadcasted_iota(jnp.int32, (tok, 1), 0) + me * tok < r.lens[micro]
        dy = jnp.where(valid, r.dy[micro].astype(F32), 0.0)
        r.vec[9:10, :] += column_sum(dy)
        grad = dy + normal_back(grad * r.wide[2:3, :], normed, inverse)
        r.dx1[micro] = grad
        normed, inverse = normal(r.z[micro])
        r.vec[1:2, :] += column_sum(grad * normed)
        r.vec[7:8, :] += column_sum(grad)
        low = normal_back(grad * r.wide[1:2, :], normed, inverse).astype(LOW)
        r.vec[6:7, :] += column_sum(low.astype(F32))
        r.dz[micro * tok : (micro + 1) * tok, :] = low
    wait(loads[4:5])
    for d in range(n):
        grad = dot_nt(r.dz[...], r.wout[d].reshape(cols, width))
        lane = lax.broadcasted_iota(jnp.int32, (1, cols), 1) // HDIM
        scales = jnp.zeros((1, cols), F32)
        for head in range(heads):
            scales = jnp.where(lane == head, r.scale[d * heads + head], scales)
        grad = (grad * scales).astype(LOW)
        for micro in range(batch):
            r.do_own[micro, d] = grad[micro * tok : (micro + 1) * tok]

    def head_copies(micro):
        return to_peers(
            lambda i, peer: send(
                r.do_own.at[micro, me ^ i], r.do_all.at[micro, band, :], r.o_sems, (micro, i), peer
            )
        )

    pair_o = send(r.go_all.at[:, 1 - core], r.go_pair, r.p_sems, (0,), pair)
    pair_vec = send(r.vec_sum, r.vec_pair, r.p_sems, (2,), pair)

    def pair_q(d):
        return send(r.gq_all.at[d, 1 - core], r.gq_pair.at[d], r.q_sems, (d,), pair)

    shares = to_peers(
        lambda i, peer: send(r.vec_part.at[me ^ i], r.vec_got.at[i - 1], r.d_sems, (i, 6), peer)
    )
    far_o = along(
        lambda j, peer: send(r.go_sum.at[row ^ j], r.o_far.at[j - 1], r.z_sems, (j, 1), peer)
    )
    far_q = along(
        lambda j, peer: send(r.gq_sum.at[:, row ^ j], r.q_far.at[j - 1], r.z_sems, (j, 2), peer)
    )
    far_v = along(
        lambda j, peer: send(r.mid_sum.at[row ^ j], r.v_far.at[j - 1], r.z_sems, (j, 3), peer)
    )
    far_vec = along(lambda j, peer: send(r.vec_mine, r.vec_far.at[j - 1], r.z_sems, (j, 4), peer))
    for micro in range(batch):
        start(head_copies(micro))
        r.do_all[micro, band, :] = r.do_own[micro, me]
    wait(loads[5:6])

    def out_weight(d, _):
        a = r.a[:, :, at(d * cols, cols)].reshape(batch * tok, cols)
        grad = dot_tn(a, r.dz[...]).astype(LOW)
        for k in range(nf):
            r.go_all[d, k % 2, k // 2] = grad[k * rows_each : (k + 1) * rows_each]
        return 0

    lax.fori_loop(0, n, out_weight, 0)
    pair_o.start()
    y_rows(0).turn()
    wait(loads[6:12])
    left = lax.broadcasted_iota(jnp.int32, (1, 128), 1) < HDIM

    def one(micro, _):
        wait(head_copies(micro))

        def pair_of(two, _):
            def column(k):
                return at(k * cols + two * 128, 128)

            head = two * 2
            own_cols = at(two * 128, 128)
            sums = []
            k = r.qkv_all[micro, :, column(1)]
            v = r.qkv_all[micro, :, column(2)]
            for block in range(n):
                end = (block + 1) * tok
                rows = slice(block * tok, end)
                do = r.do_all[micro, rows, own_cols]
                out = []
                for side in range(2):
                    mine = left if side == 0 else jnp.logical_not(left)
                    probs = r.p_all[micro, head + side, rows, :end].astype(F32)
                    dp = dot_nt(jnp.where(mine, do, jnp.zeros_like(do)), v[:end])
                    delta = jnp.sum(probs * dp, axis=-1, keepdims=True)
                    ds = (probs * (dp - delta)).astype(LOW)
                    r.ds_all[side, rows, :end] = ds
                    out.append(dot(ds, k[:end]))
                    sums.append(jnp.sum(delta, axis=0, keepdims=True))
                dq = jnp.where(left, out[0], out[1]) * HDIM ** (-0.5)
                r.dqkv[micro, rows, column(0)] = dq.astype(LOW)
            q = r.qkv_all[micro, :, column(0)]
            do = r.do_all[micro, :, own_cols]
            for block in range(n):
                begin = block * tok
                keys = slice(begin, begin + tok)
                dk = [dot_tn(r.ds_all[side, begin:, keys], q[begin:]) for side in range(2)]
                dv = [
                    dot_tn(r.p_all[micro, head + side, begin:, keys], do[begin:])
                    for side in range(2)
                ]
                dk = jnp.where(left, dk[0], dk[1]) * HDIM ** (-0.5)
                r.dqkv[micro, keys, column(1)] = dk.astype(LOW)
                r.dqkv[micro, keys, column(2)] = jnp.where(left, dv[0], dv[1]).astype(LOW)
            spot = me * heads + head
            first = sum(sums[2::2], sums[0]) * (1.0 / r.scale[spot])
            second = sum(sums[3::2], sums[1]) * (1.0 / r.scale[spot + 1])
            r.vec[10:11, at(me * cols + two * 128, 128)] += jnp.where(left, first, second)

            @pl.when((micro == 0) & (two == 0))
            def _():
                g_turn(0)

            return 0

        lax.fori_loop(0, pairs, pair_of, 0)

        @pl.when(micro == 0)
        def _():
            pair_o.wait()
            for d in range(n):
                total = r.go_all[d, core].astype(F32) + r.go_pair[d].astype(F32)
                r.go_half[d] = total.astype(LOW)
            go.begin()

        @pl.when(micro == 1)
        def _():
            g_turn(1)
            go.turn()
            dh_rows(0).turn()

        def back_rows(d, _):
            total = dot_nt(r.dqkv[micro, :, :cols], r.w_qkv[0, d].reshape(cols, cols))
            for k in (1, 2):
                total = total + dot_nt(
                    r.dqkv[micro, :, k * cols : (k + 1) * cols],
                    r.w_qkv[k, d].reshape(cols, cols),
                )
            r.dh_all[micro, :, at(d * cols, cols)] = total.astype(LOW)
            return 0

        lax.fori_loop(0, n, back_rows, 0)
        dh_rows(micro).begin()
        grads = r.dqkv[micro].astype(F32)
        r.vec[4:5, place] += column_sum(grads[:, :cols])
        r.vec[5:6, place] += column_sum(grads[:, 2 * cols :])
        return 0

    lax.fori_loop(0, batch, one, 0)
    for micro in range(1, batch):
        y_rows(micro).begin()

    def weight_grads(d, _):
        h = r.h_all[:, :, at(d * cols, cols)].reshape(batch * slot, cols)
        grad = dot_tn(h, r.dqkv[...].reshape(batch * slot, 3 * cols)).astype(LOW)
        for k in range(nf):
            r.gq_all[d, k % 2, k // 2] = grad[k * rows_each : (k + 1) * rows_each]
        pair_q(d).start()
        return 0

    lax.fori_loop(0, n, weight_grads, 0)
    r.go_sum[...] = go.finish().astype(LOW)
    start(far_o)
    pair_v.wait()
    for k in range(nz):
        r.mid_sum[k] = r.mid[k, core] + r.mid_pair[k]
    start(far_v)

    def add_pair(d, _):
        pair_q(d).wait()
        total = r.gq_all[d, core].astype(F32) + r.gq_pair[d].astype(F32)
        r.gq_sum[d] = total.astype(LOW)
        return 0

    lax.fori_loop(0, n, add_pair, 0)
    start(far_q)
    for micro in range(1, batch):
        dh_rows(micro).turn()
    for micro in range(batch):
        grad = dh_rows(micro).finish()
        normed, inverse = normal(r.x[micro].astype(F32))
        r.vec[0:1, :] += column_sum(grad * normed)
        r.vec[3:4, :] += column_sum(grad)
        r.dx[micro] = r.dx1[micro] + normal_back(grad * r.wide[0:1, :], normed, inverse)
    spot = lax.broadcasted_iota(jnp.int32, (16, 1), 0)
    own_scales = r.vec[10:11, place]
    for d in range(n):
        block = jnp.where(spot >= 10, 0.0, r.vec[:, d * share : (d + 1) * share])
        r.vec_part[d] = jnp.where(spot == 10 + me, own_scales, block)
    start(shares)
    for micro in range(1, batch):
        y_rows(micro).turn()
    for micro in range(batch):
        total = r.x1[micro] + y_rows(micro).finish() + r.wide[9:10, :]
        r.out[micro] = total.astype(LOW)
    wait(shares)
    total = r.vec_part[me]
    for i in range(1, n):
        total = total + r.vec_got[i - 1]
    r.vec_mine[...] = total
    start(far_vec)
    halves = []
    for w in range(2):
        wait(g_second(w))
        total = r.g_mid[w, two_row].astype(F32)
        for j in range(1, nz // 2):
            total = total + r.g_far[j - 1, w].astype(F32)
        r.g_sum[w] = total.astype(LOW)
        for i, peer in enumerate(peers, 1):
            source = r.g_sum.at[w, :, at((me ^ i) * cols, cols)]
            halves.append(send(source, r.ffn_out.at[w, me], r.d_sems, (i, 4 + w), peer))
    own = [
        pltpu.make_async_copy(r.g_sum.at[w, :, place], r.ffn_out.at[w, me], r.own_sems.at[13 + w])
        for w in range(2)
    ]
    start(halves + own)
    wait(far_o)
    total = r.go_sum[row].astype(F32)
    for j in range(1, nz):
        total = total + r.o_far[j - 1].astype(F32)
    r.o_out[...] = total
    wait(far_v)
    total = r.mid_sum[row]
    for j in range(1, nz):
        total = total + r.v_far[j - 1]
    r.v_out[me] = total
    last = to_peers(
        lambda i, peer: send(r.v_out.at[me], r.v_out.at[me], r.d_sems, (i, 3), peer)
    )
    start(last)
    wait(far_vec)
    total = r.vec_mine[...]
    for j in range(1, nz):
        total = total + r.vec_far[j - 1]
    r.vec_out[...] = total
    r.vec_sum[...] = total
    pair_vec.start()
    wait(far_q)
    for d in range(n):
        total = r.gq_sum[d, row].astype(F32)
        for j in range(1, nz):
            total = total + r.q_far[j - 1, d].astype(F32)
        r.q_last[d] = total
    more = []
    for i, peer in enumerate(peers, 1):
        for k in range(3):
            source = r.q_last.at[me ^ i, :, k * cols : (k + 1) * cols]
            more.append(send(source, r.q_out.at[k, :, place], r.d_sems, (i, k), peer))
    own += [
        pltpu.make_async_copy(
            r.q_last.at[me, :, k * cols : (k + 1) * cols],
            r.q_out.at[k, :, place],
            r.own_sems.at[15 + k],
        )
        for k in range(3)
    ]
    start(more + own[2:])
    wait(last + more + own + halves + [pair_vec])
    r.vec_out[...] += r.vec_pair[...]


def backward(x, dy, kept, lens, scale, n, nf):
    batch, tok, width = x.shape
    _, _, _, rows, cols = kept["w_hbm"].shape
    part = kept["mid"].shape[3]
    slot, nz = n * tok, nf // 2
    share = width // n
    heads = cols // HDIM

    def low(*dims):
        return pltpu.VMEM(dims, LOW)

    def full(*dims):
        return pltpu.VMEM(dims, F32)

    names = ("x1_hbm", "z_hbm", "dh2_hbm", "a_hbm", "g_hbm", "out_hbm", "w_hbm", "h_hbm")
    names += ("qkv_hbm", "p_hbm", "y_hbm")
    inputs = {name: (kept[name], ANY) for name in names}
    inputs["x_hbm"] = (x, ANY)
    inputs["dy_hbm"] = (dy, ANY)
    inputs["wide"] = (kept["wide"], VMEM)
    inputs["mid"] = (kept["mid"], VMEM)
    inputs["lens"] = (lens, SMEM)
    inputs["scale"] = (scale, SMEM)
    outputs = {
        "out": (shape((batch, tok, width), LOW), VMEM),
        "dx": (shape((batch, tok, width), F32), VMEM),
        "q_out": (shape((3, rows, width), F32), VMEM),
        "o_out": (shape((rows, width), F32), VMEM),
        "v_out": (shape((n, 8, part), F32), VMEM),
        "vec_out": (shape((16, share), F32), VMEM),
        "ffn_out": (shape((2, n, part, cols), LOW), VMEM),
    }
    scratch = {
        "x": low(batch, tok, width),
        "dy": low(batch, tok, width),
        "x1": full(batch, tok, width),
        "z": full(batch, tok, width),
        "dh2": full(batch, tok, width),
        "a": low(batch, tok, width),
        "wout": low(n, nf, rows, width),
        "w_qkv": low(3, n, nf, rows, cols),
        "h_all": low(batch, slot, width),
        "qkv_all": low(batch, slot, 3 * cols),
        "p_all": low(batch, heads, slot, slot),
        "y_all": low(batch, slot, width),
        "y_got": low(batch, 2, 2, tok, width // 2),
        "y_passed": low(batch, 2, tok, width // 2),
        "y_last": low(batch, 2, tok, width // 2),
        "dx1": full(batch, tok, width),
        "dz": low(batch * tok, width),
        "do_own": low(batch, n, tok, cols),
        "do_all": low(batch, slot, cols),
        "ds_all": low(2, slot, slot),
        "dqkv": low(batch, slot, 3 * cols),
        "dh_all": low(batch, slot, width),
        "dh_got": low(batch, 2, 2, tok, width // 2),
        "dh_passed": low(batch, 2, tok, width // 2),
        "dh_last": low(batch, 2, tok, width // 2),
        "go_all": low(n, 2, nz, rows, width),
        "go_pair": low(n, nz, rows, width),
        "go_half": low(n, nz, rows, width),
        "go_got": low(2, 2, nz, rows, width // 2),
        "go_passed": low(2, nz, rows, width // 2),
        "go_last": low(2, nz, rows, width // 2),
        "go_sum": low(nz, rows, width),
        "o_far": low(nz - 1, rows, width),
        "gq_all": low(n, 2, nz, rows, 3 * cols),
        "gq_pair": low(n, nz, rows, 3 * cols),
        "gq_sum": low(n, nz, rows, 3 * cols),
        "q_far": low(nz - 1, n, rows, 3 * cols),
        "q_last": full(n, rows, 3 * cols),
        "g_own": low(2, nz // 2, part, width),
        "g_pair": low(2, nz // 2, part, width),
        "g_mid": low(2, nz // 2, part, width),
        "g_far": low(nz // 2 - 1, 2, part, width),
        "g_sum": low(2, part, width),
        "mid_pair": full(nz, 8, part),
        "mid_sum": full(nz, 8, part),
        "v_far": full(nz - 1, 8, part),
        "vec": full(16, width),
        "vec_part": full(n, 16, share),
        "vec_got": full(n - 1, 16, share),
        "vec_mine": full(16, share),
        "vec_far": full(nz - 1, 16, share),
        "vec_sum": full(16, share),
        "vec_pair": full(16, share),
        "o_sems": DMA((2, batch, n)),
        "h_sems": DMA((2, batch, 2, 3)),
        "y_sems": DMA((2, batch, 2, 3)),
        "p_sems": DMA((2, 3)),
        "q_sems": DMA((2, n)),
        "e_sems": DMA((2, 2, 3)),
        "g_sems": DMA((2, nz // 2, 2)),
        "z_sems": DMA((2, nz, 5)),
        "d_sems": DMA((2, n, 7)),
        "own_sems": DMA((18,)),
    }
    return launch(
        lambda r: backward_kernel(n, nf, r), "backward", inputs, outputs, scratch, 1, 60
    )


def finish_kernel(n, nf, r):
    f = lax.axis_index("ffn")
    rows_each = r.gains.shape[1]
    part = r.mid.shape[2]
    cols, hid = r.w_in.shape
    r.out_to[...] = r.out[...]
    r.dx_to[...] = r.dx[...]
    r.q_to[...] = r.q_out[...]
    r.o_to[...] = r.o_out[...]
    r.w_in[...] = r.ffn[0].reshape(hid, cols).astype(F32).T
    r.w_out[...] = r.ffn[1].reshape(hid, cols).astype(F32)
    own = jnp.zeros((16, rows_each), F32)
    for k in range(nf):
        own = own + jnp.where(f == k, r.vec[:, k * rows_each : (k + 1) * rows_each], 0.0)
    r.gains[...] = own[:3]
    r.biases[...] = own[3:10]
    heads = r.heads.shape[1]
    lane = lax.broadcasted_iota(jnp.int32, (1, heads), 1)
    total = jnp.zeros((1, heads), F32)
    for head in range(heads):
        d, c = divmod(head, heads // n)
        value = r.vec[10 + d : 11 + d, c * HDIM : c * HDIM + 1]
        total = total + jnp.where(lane == head, value, 0.0)
    r.heads[...] = total
    for k, target in enumerate((r.mid_0, r.mid_1, r.mid_2)):
        for d in range(n):
            target[:, d * part : (d + 1) * part] = r.mid[d, k : k + 1]


def finish(done, heads, n, nf):
    out, dx, q_out, o_out = [done[name] for name in ("out", "dx", "q_out", "o_out")]
    vec, mid, ffn = done["vec_out"], done["v_out"], done["ffn_out"]
    _, _, part, cols = ffn.shape
    rows = o_out.shape[0]
    hid = n * part
    inputs = dict(out=out, dx=dx, q_out=q_out, o_out=o_out, vec=vec, mid=mid, ffn=ffn)
    outputs = dict(
        out_to=shape(out.shape, LOW),
        dx_to=shape(dx.shape, F32),
        q_to=shape(q_out.shape, F32),
        o_to=shape(o_out.shape, F32),
        heads=shape((1, heads), F32),
        gains=shape((3, rows), F32),
        biases=shape((7, rows), F32),
        w_in=shape((cols, hid), F32),
        mid_0=shape((1, hid), F32),
        mid_1=shape((1, hid), F32),
        mid_2=shape((1, hid), F32),
        w_out=shape((hid, cols), F32),
    )
    names = [*inputs, *outputs]
    return pl.pallas_call(
        lambda *refs: finish_kernel(n, nf, SimpleNamespace(**dict(zip(names, refs)))),
        name="finish",
        out_shape=tuple(outputs.values()),
        in_specs=[VMEM] * len(inputs),
        out_specs=(VMEM,) * len(outputs),
        compiler_params=pltpu.CompilerParams(vmem_limit_bytes=62 << 20),
    )(*inputs.values())


def on_device(
    tokens,
    seq_lens,
    qkv_weight,
    out_weight,
    head_scale,
    gains,
    biases,
    ffn_in,
    ffn_bias,
    mid_gain,
    mid_bias,
    ffn_out,
    out_cotangent,
):
    n = lax.axis_size("dp")
    nf = lax.axis_size("ffn")
    me = lax.axis_index("dp")
    f = lax.axis_index("ffn")
    batch, _, tok, width = tokens.shape
    heads = head_scale.shape[0]
    cols = width // n
    rows = qkv_weight.shape[1]
    hid = ffn_in.shape[1]
    part = hid // n

    def tiled(values):
        size = values.shape[1]
        spot = lax.rem(f, 128 // size) * size
        return lax.dynamic_update_slice(jnp.zeros((16, 128), LOW), values, (0, spot))

    vectors = lax.dynamic_index_in_dim(
        jnp.stack([ffn_bias, mid_gain, mid_bias]).reshape(3, n, part), me, 1, keepdims=False
    )
    x, dy = tokens[:, 0], out_cotangent[:, 0]
    lens = seq_lens.reshape(-1)
    kept = forward(
        x,
        qkv_weight,
        out_weight,
        jnp.stack([tiled(jnp.concatenate([gains, biases])), tiled(vectors)]),
        ffn_in,
        ffn_out.reshape(n, part, cols),
        dy,
        lens,
        head_scale,
        n,
        nf,
    )
    done = backward(x, dy, kept, lens, head_scale, n, nf)
    out, dx, q_grad, o_grad, head_grad, gain_grad, bias_grad, in_grad, *mids, last_grad = finish(
        done, heads, n, nf
    )
    return (
        out[:, None],
        dx[:, None],
        q_grad,
        o_grad,
        head_grad.reshape(heads),
        gain_grad,
        bias_grad,
        in_grad,
        *[mid.reshape(hid) for mid in mids],
        last_grad,
    )


def solution(mesh):
    seqs = P(None, "ffn", "dp", None)
    wide = P(None, ("dp", "ffn"))
    hidden = P("ffn")
    return jax.shard_map(
        on_device,
        mesh=mesh,
        in_specs=(
            seqs,
            P(None, "ffn"),
            P(None, ("dp", "ffn"), None),
            P(("dp", "ffn"), None),
            P(),
            wide,
            wide,
            P("dp", "ffn"),
            hidden,
            hidden,
            hidden,
            P("ffn", "dp"),
            seqs,
        ),
        out_specs=(
            seqs,
            seqs,
            P(None, ("dp", "ffn"), None),
            P(("dp", "ffn"), None),
            P(),
            wide,
            wide,
            P("dp", "ffn"),
            hidden,
            hidden,
            hidden,
            P("ffn", "dp"),
        ),
        check_vma=False,
    )
```

```python
from types import SimpleNamespace

import jax
import jax.numpy as jnp
from jax import lax
from jax.experimental import pallas as pl
from jax.experimental.pallas import tpu as pltpu
from jax.sharding import PartitionSpec as P

HDIM = 64
EPS = 1e-05
LOW = jnp.bfloat16
F32 = jnp.float32
ANY = pl.BlockSpec(memory_space=pl.ANY)
VMEM = pl.BlockSpec(memory_space=pltpu.VMEM)
SMEM = pl.BlockSpec(memory_space=pltpu.SMEM)
MESH = pl.DeviceIdType.MESH
DMA = pltpu.SemaphoreType.DMA


def dot(left, right):
    return jnp.dot(left, right, preferred_element_type=F32)


def dot_nt(left, right):
    return lax.dot_general(left, right, (((1,), (1,)), ((), ())), preferred_element_type=F32)


def dot_tn(left, right):
    return lax.dot_general(left, right, (((0,), (0,)), ((), ())), preferred_element_type=F32)


def shape(dims, kind):
    return jax.ShapeDtypeStruct(tuple(dims), kind)


def at(start, size, unit=128):
    return pl.ds(pl.multiple_of(start, unit), size)


def send(src, dst, sems, index, where):
    return pltpu.make_async_remote_copy(
        src_ref=src,
        dst_ref=dst,
        send_sem=sems.at[(0, *index)],
        recv_sem=sems.at[(1, *index)],
        device_id=where,
        device_id_type=MESH,
    )


def greet(peers):
    barrier = pltpu.get_barrier_semaphore()
    for peer in peers:
        pl.semaphore_signal(barrier, inc=1, device_id=peer, device_id_type=MESH)


def meet(peers):
    pl.semaphore_wait(pltpu.get_barrier_semaphore(), len(peers))


def dp_peers(n, me):
    return [{"dp": me ^ i} for i in range(1, n)]


def ffn_peers(nf, f):
    return [{"ffn": f ^ (2 * j)} for j in range(1, nf // 2)] + [{"ffn": f ^ 1}]


def start(copies):
    for copy in copies:
        copy.start()


def wait(copies):
    for copy in copies:
        copy.wait()


class Line:
    def __init__(self, nf, f, items, hop_sems, side_sems):
        self.nz, self.core, self.q, self.f = nf // 2, lax.rem(f, 2), lax.div(f, 2), f
        self.items, self.hop_sems, self.side_sems = items, hop_sems, side_sems
        self.next = [1] * len(items)

    def copy(self, sems, k, t, came, way, first, target):
        source, place = self.items[k]
        index = self.f if first else 2 * (self.q - t * way) + self.core
        spot = place(index)
        side = 0 if way > 0 else 1
        return pltpu.make_async_remote_copy(
            src_ref=source if first else spot,
            dst_ref=spot,
            send_sem=sems.at[0, side, k, t],
            recv_sem=sems.at[1, side, k, came],
            device_id={"ffn": target},
            device_id_type=MESH,
        )

    def hop(self, k, t, way, first=False):
        return self.copy(self.hop_sems, k, t, t + 1, way, first, self.f + 2 * way)

    def arrival(self, k, t, way):
        return self.copy(self.hop_sems, k, t, t, way, False, self.f + 2 * way)

    def over(self, k, t, way, first=False):
        return self.copy(self.side_sems, k, t, t, way, first, self.f ^ 1)

    def onward(self, way):
        return self.q < self.nz - 1 if way > 0 else self.q > 0

    def has(self, t, way):
        return self.q - t >= 0 if way > 0 else self.q + t <= self.nz - 1

    def begin(self, *items):
        for k in items:
            for way in (1, -1):

                @pl.when(self.onward(way))
                def _():
                    self.hop(k, 0, way, True).start()

        for k in items:
            self.over(k, 0, 1, True).start()

    def step(self, k, t):
        for way in (1, -1):

            @pl.when(self.has(t, way) & self.onward(way))
            def _():
                self.arrival(k, t, way).wait_recv()
                self.hop(k, t, way).start()

        for way in (1, -1):

            @pl.when(self.has(t, way))
            def _():
                @pl.when(jnp.logical_not(self.onward(way)))
                def _():
                    self.arrival(k, t, way).wait_recv()

                self.over(k, t, way).start()

    def advance(self, *items):
        for k in items:
            if self.next[k] < self.nz:
                self.step(k, self.next[k])
                self.next[k] += 1

    def arrive(self, *items):
        begin = self.next[items[0]]

        def rest(t, _):
            for k in items:
                self.step(k, t)
            return 0

        lax.fori_loop(begin, self.nz, rest, 0)

        def close(t, _):
            for k in items:
                for way in (1, -1):

                    @pl.when(self.has(t, way))
                    def _():
                        self.over(k, t, way).wait_recv()

            return 0

        for k in items:
            self.over(k, 0, 1, True).wait_recv()
        lax.fori_loop(1, self.nz, close, 0)

    def finish(self, *items):
        for k in items:
            self.over(k, 0, 1, True).wait_send()
            for way in (1, -1):

                @pl.when(self.onward(way))
                def _():
                    self.hop(k, 0, way, True).wait_send()

        def close(t, _):
            for k in items:
                for way in (1, -1):

                    @pl.when(self.has(t, way))
                    def _():
                        self.over(k, t, way).wait_send()

                    @pl.when(self.has(t, way) & self.onward(way))
                    def _():
                        self.hop(k, t, way).wait_send()

            return 0

        lax.fori_loop(1, self.nz, close, 0)


def line_meet(n, nf, me, f):
    barrier = pltpu.get_barrier_semaphore()
    q, nz = lax.div(f, 2), nf // 2
    greet(dp_peers(n, me) + [{"ffn": f ^ 1}])

    @pl.when(q < nz - 1)
    def _():
        greet([{"ffn": f + 2}])

    @pl.when(q > 0)
    def _():
        greet([{"ffn": f - 2}])

    count = n + jnp.where(q < nz - 1, 1, 0) + jnp.where(q > 0, 1, 0)
    pl.semaphore_wait(barrier, count)


class Gather:
    def __init__(self, me, source, place, size, sems, index):
        self.me, self.source, self.place, self.half = me, source, place, size // 2
        self.sems, self.index = sems, index

    def straight(self, k):
        spot = self.place(self.me, 0, 2 * self.half)
        return send(self.source, spot, self.sems, (*self.index, k), {"dp": self.me ^ (k + 1)})

    def relay(self, k):
        spot = self.place(self.me ^ (k + 1), k * self.half, self.half)
        return send(spot, spot, self.sems, (*self.index, 2 + k), {"dp": self.me ^ (2 - k)})

    def begin(self):
        for k in range(2):
            self.straight(k).start()

    def turn(self):
        for k in range(2):
            self.straight(k).wait()
            self.relay(k).start()

    def finish(self):
        for k in range(2):
            self.relay(k).wait()


class Reduce:
    def __init__(self, me, block, got, passed, last, sems, index):
        self.me, self.block, self.passed = me, block, passed
        self.got, self.last, self.sems, self.index = got, last, sems, index

    def first(self, side, far):
        step = side + 1
        owner = self.me ^ (3 if far else step)
        target = self.got.at[(*self.index, side, far)]
        spot = (*self.index, side, far)
        return send(self.block(owner, side), target, self.sems, spot, {"dp": self.me ^ step})

    def second(self, side):
        where = (*self.index, side)
        target = {"dp": self.me ^ (2 - side)}
        return send(self.passed.at[where], self.last.at[where], self.sems, (*where, 2), target)

    def begin(self):
        for far in (1, 0):
            for side in range(2):
                self.first(side, far).start()

    def turn(self):
        for side in range(2):
            self.first(side, 1).wait()
            total = self.block(self.me ^ (2 - side), side)[...].astype(F32)
            total = total + self.got[(*self.index, side, 1)].astype(F32)
            self.passed[(*self.index, side)] = total.astype(LOW)
            self.second(side).start()

    def finish(self):
        halves = []
        for side in range(2):
            self.first(side, 0).wait()
            self.second(side).wait()
            total = self.block(self.me, side)[...].astype(F32)
            total = total + self.got[(*self.index, side, 0)].astype(F32)
            halves.append(total + self.last[(*self.index, side)].astype(F32))
        return jnp.concatenate(halves, axis=-1)


def normal(values):
    center = values - jnp.mean(values, axis=-1, keepdims=True)
    inverse = lax.rsqrt(jnp.mean(center * center, axis=-1, keepdims=True) + EPS)
    return center * inverse, inverse


def normal_back(grad, normed, inverse):
    return inverse * (
        grad
        - jnp.mean(grad, axis=-1, keepdims=True)
        - normed * jnp.mean(grad * normed, axis=-1, keepdims=True)
    )


def column_sum(values):
    return jnp.sum(values, axis=0, keepdims=True)


def launch(body, name, inputs, outputs, scratch, number, limit):
    names = [*inputs, *outputs, *scratch]
    results = pl.pallas_call(
        lambda *refs: body(SimpleNamespace(**dict(zip(names, refs)))),
        name=name,
        out_shape=tuple(kind for kind, _ in outputs.values()),
        in_specs=[spec for _, spec in inputs.values()],
        out_specs=tuple(spec for _, spec in outputs.values()),
        scratch_shapes=list(scratch.values()),
        compiler_params=pltpu.CompilerParams(
            collective_id=number, has_side_effects=True, vmem_limit_bytes=limit << 20
        ),
    )(*[value for value, _ in inputs.values()])
    return dict(zip(outputs, results))


def forward_kernel(n, nf, part, r):
    me = lax.axis_index("dp")
    f = lax.axis_index("ffn")
    core, nz = lax.rem(f, 2), nf // 2
    batch, tok, width = r.x.shape
    rows_each = r.wout.shape[0]
    cols = width // n
    pairs = cols // 128
    slot = n * tok
    hid = nf * part
    ff = n * hid
    step = 256
    peers = dp_peers(n, me)
    pair = {"ffn": f ^ 1}
    place = at(me * cols, cols)
    band = at(me * tok, tok)

    own = [
        pltpu.make_async_copy(r.qkv.at[:, :, place], r.stage.at[:, me], r.own_sems.at[0]),
        pltpu.make_async_copy(r.small.at[0], r.small_stage.at[me], r.own_sems.at[1]),
        pltpu.make_async_copy(r.small.at[1], r.small_stage.at[n], r.own_sems.at[2]),
        pltpu.make_async_copy(r.wout, r.out_stage.at[me], r.own_sems.at[3]),
        pltpu.make_async_copy(r.first, r.first_in, r.own_sems.at[4]),
        pltpu.make_async_copy(r.second.at[me], r.second_stage.at[:, place], r.own_sems.at[5]),
        pltpu.make_async_copy(r.x, r.x_all.at[me], r.own_sems.at[6]),
        pltpu.make_async_copy(r.dy, r.dy_all.at[:, band, :], r.own_sems.at[7]),
    ]
    start(own[:1] + own[3:])
    line_meet(n, nf, me, f)

    def to_peers(make):
        return [make(i, peer) for i, peer in enumerate(peers, 1)]

    blocks = to_peers(
        lambda i, peer: send(
            r.qkv.at[:, :, at((me ^ i) * cols, cols)], r.stage.at[:, me], r.w_sems, (i, 0), peer
        )
    )
    smalls = to_peers(
        lambda i, peer: send(r.small.at[0], r.small_stage.at[me], r.w_sems, (i, 1), peer)
    )
    outs = to_peers(lambda i, peer: send(r.wout, r.out_stage.at[me], r.w_sems, (i, 2), peer))
    firsts = to_peers(
        lambda i, peer: send(
            r.first_all.at[me ^ i], r.first_stage.at[:, place], r.w_sems, (i, 3), peer
        )
    )
    seconds = to_peers(
        lambda i, peer: send(
            r.second.at[me ^ i], r.second_stage.at[:, place], r.w_sems, (i, 4), peer
        )
    )

    def x_rows(micro):
        def spot(owner, start, size):
            return r.x_all.at[owner, micro, start : start + size]

        return Gather(me, r.x.at[micro], spot, tok, r.x_sems, (micro,))

    def y_rows(micro):
        def spot(owner, start, size):
            return r.dy_all.at[micro, at(owner * tok + start, size, 64), :]

        return Gather(me, r.dy.at[micro], spot, tok, r.y_sems, (micro,))

    start(blocks)
    size = r.gains.shape[1]
    lanes = lax.broadcasted_iota(jnp.int32, (16, 128), 1)
    r.tile[...] = jnp.zeros_like(r.tile)
    for k in range(128 // size):
        r.tile[0, 0:3, k * size : (k + 1) * size] = r.gains[...].astype(F32)
        r.tile[0, 3:10, k * size : (k + 1) * size] = r.biases[...].astype(F32)
    for k in range(128 // part):
        r.tile[1, 0:3, k * part : (k + 1) * part] = r.hidden[...].astype(F32)
    for k, each_ in enumerate((size, part)):
        mine_ = lanes // each_ == lax.rem(f, 128 // each_)
        r.small[k] = jnp.where(mine_, r.tile[k], 0.0).astype(LOW)
    start(own[1:3] + smalls)
    x_rows(0).begin()
    wait(own[4:5])
    r.first_all[...] = r.first_in[...].T.reshape(r.first_all.shape)
    own[4] = pltpu.make_async_copy(
        r.first_all.at[me], r.first_stage.at[:, place], r.own_sems.at[4]
    )
    start(own[4:5])
    start(outs + firsts)
    line = Line(
        nf,
        f,
        [
            (r.stage, lambda index: r.w_all.at[:, :, index]),
            (r.small_stage, lambda index: r.small_all.at[index]),
            (r.out_stage, lambda index: r.out_all.at[:, index]),
            (r.first_stage, lambda index: r.w1.at[index]),
            (r.second_stage, lambda index: r.w2.at[index]),
        ],
        r.hop_sems,
        r.side_sems,
    )
    mine = [
        pltpu.make_async_copy(source, spot(f), r.own_sems.at[8 + k])
        for k, (source, spot) in enumerate(line.items)
    ]
    wait(blocks + smalls + own[:3])
    line.begin(0, 1)
    start(mine[:2])
    line.advance(0, 1)
    x_rows(0).turn()
    x_rows(1).begin()
    line.advance(0, 1)
    wait(outs + own[3:4])
    line.begin(2)
    start(mine[2:3])
    line.arrive(0, 1)
    wait(firsts + own[4:5])
    line.begin(3)
    start(mine[3:4])
    wait(mine[:2] + own[6:7])

    def lay_out(out_ref, index, begin, size):
        together = 128 // size
        for b in range(nf // together):
            total = r.small_all[b * together, index].astype(F32)
            for k in range(1, together):
                total = total + r.small_all[b * together + k, index].astype(F32)
            out_ref[:, begin + b * 128 : begin + (b + 1) * 128] = total

    for d in range(n):
        lay_out(r.wide, d, d * nf * rows_each, rows_each)
    lay_out(r.mids, n, 0, part)

    gain, shift = r.wide[0:1, :], r.wide[3:4, :]
    bias_q, bias_v = r.wide[4:5, place], r.wide[5:6, place]
    left = lax.broadcasted_iota(jnp.int32, (1, 128), 1) < HDIM

    def block_copies(micro):
        return to_peers(
            lambda i, peer: send(
                r.a_all.at[micro, me ^ i], r.a_own.at[micro, :, place], r.a_sems, (micro, i), peer
            )
        )

    def keep_copies(micro):
        return [
            pltpu.make_async_copy(source.at[micro], out.at[micro], r.keep_sems.at[micro, k])
            for k, (source, out) in enumerate(
                [(r.h_all, r.h_hbm), (r.qkv_all, r.qkv_hbm), (r.p_all, r.p_hbm)]
            )
        ]

    def after_first():
        line.advance(2)
        x_rows(1).turn()
        start(seconds)
        y_rows(0).begin()

    def after_second():
        line.advance(3)

    def after_third():
        line.advance(2)
        wait(seconds + own[5:6])
        line.begin(4)
        start(mine[4:5])

    def after_last():
        y_rows(0).turn()
        y_rows(1).begin()
        line.advance(3)

    def attend(index, _):
        micro, two = lax.div(index, pairs), lax.rem(index, pairs)

        @pl.when(two == 0)
        def _():
            x_rows(micro).finish()

            def norm_rows(d, _):
                values, _ = normal(r.x_all[d, micro].astype(F32))
                r.h_all[micro, at(d * tok, tok), :] = (values * gain + shift).astype(LOW)
                return 0

            lax.fori_loop(0, n, norm_rows, 0)
            for k, bias in enumerate((bias_q, None, bias_v)):
                weight = r.w_all[k].reshape(width, cols)
                value = dot(r.h_all[micro], weight)
                if bias is not None:
                    value = value + bias
                r.qkv_all[micro, :, k * cols : (k + 1) * cols] = value.astype(LOW)

        length = r.lens[micro]

        def column(k):
            return at(k * cols + two * 128, 128)

        head = two * 2
        scales = jnp.where(
            left, r.scale[me * 2 * pairs + head], r.scale[me * 2 * pairs + head + 1]
        )
        for block in range(n):
            end = (block + 1) * tok
            q = r.qkv_all[micro, block * tok : end, column(0)] * HDIM ** (-0.5)
            k = r.qkv_all[micro, :end, column(1)]
            v = r.qkv_all[micro, :end, column(2)]
            key = lax.broadcasted_iota(jnp.int32, (tok, end), 1)
            query = lax.broadcasted_iota(jnp.int32, (tok, end), 0) + block * tok
            mask = (key <= query) & (key < length)
            out = []
            for side in range(2):
                mine_ = left if side == 0 else jnp.logical_not(left)
                scores = dot_nt(jnp.where(mine_, q, jnp.zeros_like(q)), k)
                scores = jnp.where(mask, scores, -1e30)
                expo = jnp.exp(scores - jnp.max(scores, axis=-1, keepdims=True))
                probs = expo * (1.0 / jnp.sum(expo, axis=-1, keepdims=True))
                probs = probs.astype(LOW)
                r.p_all[micro, head + side, block * tok : end, :end] = probs
                out.append(dot(probs, v))
            joined = jnp.where(left, out[0], out[1]) * scales
            r.a_all[micro, block, :, at(two * 128, 128)] = joined.astype(LOW)

        @pl.when(two == pairs - 1)
        def _():
            start(block_copies(micro))
            start(keep_copies(micro))
            r.a_own[micro, :, place] = r.a_all[micro, me]

        work = [after_first, after_second, after_third, after_last]
        for k, act in enumerate(work[: batch * pairs]):
            pl.when(index == k)(act)
        return 0

    lax.fori_loop(0, batch * pairs, attend, 0)

    line.arrive(2)
    wait(mine[2:3])
    late = [
        pltpu.make_async_copy(source, target, r.own_sems.at[13 + k])
        for k, (source, target) in enumerate(
            [(r.w_all, r.w_hbm), (r.out_all, r.out_hbm), (r.z, r.z_hbm), (r.x1, r.x1_hbm),
             (r.a_own, r.a_hbm), (r.mixed, r.mixed_hbm), (r.pair_got, r.g_hbm), (r.dh2, r.dh2_hbm),
             (r.w2, r.w2_hbm)]
        )
    ]
    start(late[:2])

    def h2_rows(micro):
        def spot(owner, start, size):
            return r.h2_all.at[micro, at(owner * tok + start, size, 64), :]

        return Gather(me, r.h2_own.at[micro], spot, tok, r.h_sems, (micro,))

    for micro in range(batch):
        wait(block_copies(micro))
        z = dot(r.a_own[micro], r.out_all[...].reshape(width, width)) + r.wide[6:7, :]
        r.z[micro] = z
        values, _ = normal(z)
        x1 = r.x_all[me, micro].astype(F32) + values * r.wide[1:2, :] + r.wide[7:8, :]
        r.x1[micro] = x1
        values, _ = normal(x1)
        r.h2_own[micro] = (values * r.wide[2:3, :] + r.wide[8:9, :]).astype(LOW)
        h2_rows(micro).begin()
        r.h2_all[micro, band, :] = r.h2_own[micro]
    start(late[2:5])
    line.advance(4)
    h2_rows(0).turn()
    y_rows(1).turn()
    for micro in range(1, batch):
        h2_rows(micro).turn()
    line.arrive(3)
    wait(mine[3:4])

    def weights(ref, c):
        count = step // part
        return ref[pl.ds(c * count, count)].reshape(step, width)

    def w_columns(ref, columns):
        return ref[:, :, columns].reshape(hid, step)

    def sum_copies(micro):
        return to_peers(
            lambda i, peer: send(
                r.sums.at[micro], r.sums_all.at[micro, me], r.s_sems, (micro, i), peer
            )
        )

    def dh2_rows(micro):
        def block(owner, side):
            columns = slice(side * (width // 2), (side + 1) * (width // 2))
            return r.dh2_all.at[micro, at(owner * tok, tok), columns]

        return Reduce(me, block, r.dh2_got, r.dh2_passed, r.dh2_last, r.r_sems, (micro,))

    def fold(values):
        total = values[:, :128]
        for k in range(1, step // 128):
            total = total + values[:, k * 128 : (k + 1) * 128]
        return total

    def units(micro):
        h2_rows(micro).finish()

        def chunk(c, totals):
            rows = at(c * step, step)
            u = dot_nt(r.h2_all[micro], weights(r.w1, c)) + r.mids[0:1, rows]
            phi = 0.5 + 0.5 * lax.erf(u * (0.5**0.5))
            value = u * phi
            r.act[micro, :, rows] = value
            r.slope[micro, :, rows] = phi + u * jnp.exp(u * u * -0.5) * 0.3989422804014327
            return totals[0] + fold(value), totals[1] + fold(value * value)

        zero = jnp.zeros((slot, 128), F32)
        totals = lax.fori_loop(0, hid // step, chunk, (zero,) * 2)
        for k in range(2):
            r.sums[micro, k : k + 1, :] = column_sum(totals[k].T)

    def cotangents(micro):
        y_rows(micro).finish()
        valid = lax.broadcasted_iota(jnp.int32, (slot, 1), 0) < r.lens[micro]
        rows = r.dy_all[micro]
        r.dy_all[micro] = jnp.where(valid, rows, jnp.zeros_like(rows))

        def chunk(c, totals):
            rows = at(c * step, step)
            dm = dot_nt(r.dy_all[micro], weights(r.w2, c))
            r.dmix[micro, :, rows] = dm
            dn = dm * r.mids[1:2, rows]
            return totals[0] + fold(dn), totals[1] + fold(dn * r.act[micro, :, rows])

        zero = jnp.zeros((slot, 128), F32)
        totals = lax.fori_loop(0, hid // step, chunk, (zero,) * 2)
        for k in range(2):
            r.sums[micro, 2 + k : 3 + k, :] = column_sum(totals[k].T)
        r.sums[micro, 4:8, :] = jnp.zeros((4, slot), F32)
        start(sum_copies(micro))

    r.vec[...] = jnp.zeros_like(r.vec)

    def second_pass(micro, _):
        wait(sum_copies(micro))
        r.sums_all[micro, me] = r.sums[micro]
        total = r.sums_all[micro, 0]
        for d in range(1, n):
            total = total + r.sums_all[micro, d]
        total = total * (1.0 / ff)
        mean = total[0:1]
        inverse = lax.rsqrt(total[1:2] - mean * mean + EPS)
        back = total[2:3]
        cross = inverse * (total[3:4] - mean * back)
        table = jnp.concatenate([mean, inverse, back, cross] * 32, axis=0).T
        mean, inverse, back, cross = [table[:, k : k + 1] for k in range(4)]
        rows_of = at(micro * slot, slot)

        def chunk(c, _):
            rows = at(c * step, step)
            normed = (r.act[micro, :, rows] - mean) * inverse
            dm = r.dmix[micro, :, rows]
            gain = r.mids[1:2, rows]
            r.mixed[rows_of, rows] = (normed * gain + r.mids[2:3, rows]).astype(LOW)
            df = inverse * (dm * gain - back - normed * cross)
            low = (df * r.slope[micro, :, rows]).astype(LOW)
            r.du[rows_of, rows] = low
            r.vec[0:1, rows] += column_sum(low.astype(F32))
            r.vec[1:2, rows] += column_sum(dm * normed)
            r.vec[2:3, rows] += column_sum(dm)
            return 0

        lax.fori_loop(0, hid // step, chunk, 0)

        def back_rows(c, _):
            columns = at(c * step, step)
            value = dot(r.du[rows_of, :], w_columns(r.w1, columns))
            r.dh2_all[micro, :, columns] = value.astype(LOW)
            return 0

        lax.fori_loop(0, width // step, back_rows, 0)
        dh2_rows(micro).begin()
        return 0

    def passes(micro, _):
        units(micro)

        @pl.when(micro == 0)
        def _():
            line.arrive(4)
            wait(mine[4:5] + own[7:8])

        cotangents(micro)

        @pl.when(micro > 0)
        def _():
            dh2_rows(micro - 1).turn()

        second_pass(micro, 0)
        return 0

    lax.fori_loop(0, batch, passes, 0)
    start(late[5:6] + late[8:])
    each = step // part // 2

    def halved(index):
        return lax.div(index, 2), lax.rem(index, 2)

    def pair_copies(c):
        copies = []
        for k in range(each):
            index = c * (2 * each) + 2 * k
            for w in range(2):
                copies.append(
                    send(
                        r.grads.at[w, index + 1 - core],
                        r.pair_got.at[(w, *halved(c * each + k))],
                        r.p_sems,
                        (c, k, w),
                        pair,
                    )
                )
        return copies

    def weight_grads(c, _):
        rows = at(c * step, step)
        h2 = r.h2_all[...].reshape(batch * slot, width)
        dy = r.dy_all[...].reshape(batch * slot, width)
        first = dot_tn(r.du[:, rows], h2).astype(LOW)
        second = dot_tn(r.mixed[:, rows], dy).astype(LOW)
        for k in range(step // part):
            r.grads[0, c * (step // part) + k] = first[k * part : (k + 1) * part]
            r.grads[1, c * (step // part) + k] = second[k * part : (k + 1) * part]
        start(pair_copies(c))
        return 0

    lax.fori_loop(0, hid // step, weight_grads, 0)
    dh2_rows(batch - 1).turn()

    def pair_sum(c, _):
        wait(pair_copies(c))
        for k in range(each):
            for w in range(2):
                total = r.grads[w, c * (2 * each) + 2 * k + core].astype(F32)
                spot = (w, *halved(c * each + k))
                total = total + r.pair_got[spot].astype(F32)
                r.pair_got[spot] = total.astype(LOW)
        return 0

    lax.fori_loop(0, hid // step, pair_sum, 0)
    start(late[6:7])
    for k in range(nf):
        r.mid[k // 2, k % 2] = r.vec[:, k * part : (k + 1) * part]
    line.finish(0, 1, 2, 3, 4)
    for micro in range(batch):
        wait(keep_copies(micro))
    for micro in range(batch):
        r.dh2[micro] = dh2_rows(micro).finish()
    start(late[7:8])
    wait(late)


def forward(x, qkv, wout, small, first, second, dy, lens, scale, n, nf):
    batch, tok, width = x.shape
    rows = wout.shape[0]
    part = second.shape[1]
    cols = width // n
    slot, hid = n * tok, nf * part
    heads = cols // HDIM

    def low(*dims):
        return pltpu.VMEM(dims, LOW)

    def full(*dims):
        return pltpu.VMEM(dims, F32)

    inputs = {
        name: (value, ANY)
        for name, value in zip(
            ("x", "qkv", "wout", "first", "second", "dy"),
            (x, qkv, wout, first, second, dy),
        )
    }
    for name, value in zip(("gains", "biases", "hidden"), small):
        inputs[name] = (value, VMEM)
    inputs["lens"] = (lens, SMEM)
    inputs["scale"] = (scale, SMEM)
    outputs = {
        "wide": (shape((16, width), F32), VMEM),
        "w_hbm": (shape((3, n, nf, rows, cols), LOW), ANY),
        "out_hbm": (shape((n, nf, rows, width), LOW), ANY),
        "h_hbm": (shape((batch, slot, width), LOW), ANY),
        "qkv_hbm": (shape((batch, slot, 3 * cols), LOW), ANY),
        "p_hbm": (shape((batch, heads, slot, slot), LOW), ANY),
        "a_hbm": (shape((batch, tok, width), LOW), ANY),
        "z_hbm": (shape((batch, tok, width), F32), ANY),
        "x1_hbm": (shape((batch, tok, width), F32), ANY),
        "mixed_hbm": (shape((batch * slot, hid), LOW), ANY),
        "w2_hbm": (shape((nf, part, width), LOW), ANY),
        "g_hbm": (shape((2, nf // 4, 2, part, width), LOW), ANY),
        "dh2_hbm": (shape((batch, tok, width), F32), ANY),
        "mid": (shape((nf // 2, 2, 8, part), F32), VMEM),
    }
    scratch = {
        "mids": full(16, hid),
        "dh2": full(batch, tok, width),
        "vec": full(8, hid),
        "stage": low(3, n, rows, cols),
        "tile": full(2, 16, 128),
        "small": low(2, 16, 128),
        "small_stage": low(n + 1, 16, 128),
        "out_stage": low(n, rows, width),
        "first_in": low(*first.shape),
        "first_all": low(*second.shape),
        "first_stage": low(part, width),
        "second_stage": low(part, width),
        "small_all": low(nf, n + 1, 16, 128),
        "w_all": low(3, n, nf, rows, cols),
        "out_all": low(n, nf, rows, width),
        "w1": low(nf, part, width),
        "w2": low(nf, part, width),
        "x_all": low(n, batch, tok, width),
        "dy_all": low(batch, slot, width),
        "h_all": low(batch, slot, width),
        "qkv_all": low(batch, slot, 3 * cols),
        "p_all": low(batch, heads, slot, slot),
        "a_all": low(batch, n, tok, cols),
        "a_own": low(batch, tok, width),
        "z": full(batch, tok, width),
        "x1": full(batch, tok, width),
        "h2_own": low(batch, tok, width),
        "h2_all": low(batch, slot, width),
        "act": full(batch, slot, hid),
        "slope": full(batch, slot, hid),
        "dmix": full(batch, slot, hid),
        "mixed": low(batch * slot, hid),
        "du": low(batch * slot, hid),
        "sums": full(batch, 8, slot),
        "sums_all": full(batch, n, 8, slot),
        "dh2_all": low(batch, slot, width),
        "dh2_got": low(batch, 2, 2, tok, width // 2),
        "dh2_passed": low(batch, 2, tok, width // 2),
        "dh2_last": low(batch, 2, tok, width // 2),
        "grads": low(2, nf, part, width),
        "pair_got": low(2, nf // 4, 2, part, width),
        "w_sems": DMA((2, n, 5)),
        "x_sems": DMA((2, batch, 4)),
        "y_sems": DMA((2, batch, 4)),
        "a_sems": DMA((2, batch, n)),
        "h_sems": DMA((2, batch, 4)),
        "s_sems": DMA((2, batch, n)),
        "r_sems": DMA((2, batch, 2, 3)),
        "p_sems": DMA((2, hid // 256, 128 // part, 2)),
        "hop_sems": DMA((2, 2, 5, nf // 2)),
        "side_sems": DMA((2, 2, 5, nf // 2)),
        "keep_sems": DMA((batch, 3)),
        "own_sems": DMA((22,)),
    }
    return launch(
        lambda r: forward_kernel(n, nf, part, r), "forward", inputs, outputs, scratch, 0, 63
    )


def backward_kernel(n, nf, r):
    me = lax.axis_index("dp")
    f = lax.axis_index("ffn")
    core, row, nz = lax.rem(f, 2), lax.div(f, 2), nf // 2
    even, two_row = lax.rem(row, 2), lax.div(row, 2)
    batch, tok, width = r.dx.shape
    slot = n * tok
    cols = width // n
    rows_each = r.o_out.shape[0]
    pairs = cols // 128
    heads = cols // HDIM
    share = width // n
    step = 256
    peers = dp_peers(n, me)
    pair = {"ffn": f ^ 1}
    everyone = peers + ffn_peers(nf, f)
    greet(everyone)
    band = at(me * tok, tok)
    place = at(me * cols, cols)
    loads = [
        pltpu.make_async_copy(source, target, r.own_sems.at[k])
        for k, (source, target) in enumerate(
            [(r.x1_hbm, r.x1), (r.dh2_hbm, r.dh2), (r.dy_hbm, r.dy), (r.z_hbm, r.z),
             (r.out_hbm, r.wout), (r.a_hbm, r.a), (r.qkv_hbm, r.qkv_all), (r.p_hbm, r.p_all),
             (r.w_hbm, r.w_qkv), (r.h_hbm, r.h_all), (r.x_hbm, r.x), (r.g_hbm.at[:, :, even], r.g_own),
             (r.mixed_hbm, r.mixed), (r.w2_hbm, r.w2)]
        )
    ]
    start(loads)
    r.vec[...] = jnp.zeros_like(r.vec)

    def to_peers(make):
        return [make(i, peer) for i, peer in enumerate(peers, 1)]

    def along(make):
        return [make(j, {"ffn": f ^ (2 * j)}) for j in range(1, nz)]

    def columns_of(side):
        return slice(side * (width // 2), (side + 1) * (width // 2))

    def y_rows(micro):
        def block(owner, side):
            return r.y_all.at[micro, at(owner * tok, tok), columns_of(side)]

        return Reduce(me, block, r.y_got, r.y_passed, r.y_last, r.y_sems, (micro,))

    def dh_rows(micro):
        def block(owner, side):
            return r.dh_all.at[micro, at(owner * tok, tok), columns_of(side)]

        return Reduce(me, block, r.dh_got, r.dh_passed, r.dh_last, r.h_sems, (micro,))

    def go_block(owner, side):
        return r.go_half.at[owner, :, :, columns_of(side)]

    go = Reduce(me, go_block, r.go_got, r.go_passed, r.go_last, r.e_sems, ())

    def g_first(w):
        return send(
            r.g_hbm.at[w, :, 1 - even], r.g_pair.at[w], r.g_sems, (0, w), {"ffn": f ^ 2}
        )

    def g_second(w):
        return [
            send(r.g_mid.at[w, two_row ^ j], r.g_far.at[j - 1, w], r.g_sems, (j, w), {"ffn": f ^ (4 * j)})
            for j in range(1, nz // 2)
        ]

    def g_turn(w):
        g_first(w).wait()
        for k in range(nz // 2):
            total = r.g_own[w, k].astype(F32) + r.g_pair[w, k].astype(F32)
            r.g_mid[w, k] = total.astype(LOW)
        start(g_second(w))

    pair_v = send(r.mid.at[:, 1 - core], r.mid_pair, r.p_sems, (1,), pair)
    wait(loads[:4])
    meet(everyone)
    for w in range(2):
        g_first(w).start()
    pair_v.start()
    for micro in range(batch):
        normed, inverse = normal(r.x1[micro])
        grad = r.dh2[micro]
        r.vec[2:3, :] += column_sum(grad * normed)
        r.vec[8:9, :] += column_sum(grad)
        valid = lax.broadcasted_iota(jnp.int32, (tok, 1), 0) + me * tok < r.lens[micro]
        dy = jnp.where(valid, r.dy[micro].astype(F32), 0.0)
        r.vec[9:10, :] += column_sum(dy)
        grad = dy + normal_back(grad * r.wide[2:3, :], normed, inverse)
        r.dx1[micro] = grad
        normed, inverse = normal(r.z[micro])
        r.vec[1:2, :] += column_sum(grad * normed)
        r.vec[7:8, :] += column_sum(grad)
        low = normal_back(grad * r.wide[1:2, :], normed, inverse).astype(LOW)
        r.vec[6:7, :] += column_sum(low.astype(F32))
        r.dz[micro * tok : (micro + 1) * tok, :] = low
    wait(loads[4:5])
    for d in range(n):
        grad = dot_nt(r.dz[...], r.wout[d].reshape(cols, width))
        lane = lax.broadcasted_iota(jnp.int32, (1, cols), 1) // HDIM
        scales = jnp.zeros((1, cols), F32)
        for head in range(heads):
            scales = jnp.where(lane == head, r.scale[d * heads + head], scales)
        grad = (grad * scales).astype(LOW)
        for micro in range(batch):
            r.do_own[micro, d] = grad[micro * tok : (micro + 1) * tok]

    def head_copies(micro):
        return to_peers(
            lambda i, peer: send(
                r.do_own.at[micro, me ^ i], r.do_all.at[micro, band, :], r.o_sems, (micro, i), peer
            )
        )

    pair_o = send(r.go_all.at[:, 1 - core], r.go_pair, r.p_sems, (0,), pair)
    pair_vec = send(r.vec_sum, r.vec_pair, r.p_sems, (2,), pair)

    def pair_q(d):
        return send(r.gq_all.at[d, 1 - core], r.gq_pair.at[d], r.q_sems, (d,), pair)

    shares = to_peers(
        lambda i, peer: send(r.vec_part.at[me ^ i], r.vec_got.at[i - 1], r.d_sems, (i, 6), peer)
    )
    far_o = along(
        lambda j, peer: send(r.go_sum.at[row ^ j], r.o_far.at[j - 1], r.z_sems, (j, 1), peer)
    )
    far_q = along(
        lambda j, peer: send(r.gq_sum.at[:, row ^ j], r.q_far.at[j - 1], r.z_sems, (j, 2), peer)
    )
    far_v = along(
        lambda j, peer: send(r.mid_sum.at[row ^ j], r.v_far.at[j - 1], r.z_sems, (j, 3), peer)
    )
    far_vec = along(lambda j, peer: send(r.vec_mine, r.vec_far.at[j - 1], r.z_sems, (j, 4), peer))
    for micro in range(batch):
        start(head_copies(micro))
        r.do_all[micro, band, :] = r.do_own[micro, me]
    wait(loads[12:])

    def out_rows(c, _):
        columns = at(c * step, step)
        weight = r.w2[:, :, columns].reshape(r.mixed.shape[1], step)
        for micro in range(batch):
            value = dot(r.mixed[micro * slot : (micro + 1) * slot, :], weight)
            r.y_all[micro, :, columns] = value.astype(LOW)
        return 0

    lax.fori_loop(0, width // step, out_rows, 0)
    y_rows(0).begin()
    wait(loads[5:6])

    def out_weight(d, _):
        a = r.a[:, :, at(d * cols, cols)].reshape(batch * tok, cols)
        grad = dot_tn(a, r.dz[...]).astype(LOW)
        for k in range(nf):
            r.go_all[d, k % 2, k // 2] = grad[k * rows_each : (k + 1) * rows_each]
        return 0

    lax.fori_loop(0, n, out_weight, 0)
    pair_o.start()
    wait(loads[6:12])
    left = lax.broadcasted_iota(jnp.int32, (1, 128), 1) < HDIM

    def one(micro, _):
        wait(head_copies(micro))

        def pair_of(two, _):
            def column(k):
                return at(k * cols + two * 128, 128)

            head = two * 2
            own_cols = at(two * 128, 128)
            sums = []
            k = r.qkv_all[micro, :, column(1)]
            v = r.qkv_all[micro, :, column(2)]
            for block in range(n):
                end = (block + 1) * tok
                rows = slice(block * tok, end)
                do = r.do_all[micro, rows, own_cols]
                out = []
                for side in range(2):
                    mine = left if side == 0 else jnp.logical_not(left)
                    probs = r.p_all[micro, head + side, rows, :end].astype(F32)
                    dp = dot_nt(jnp.where(mine, do, jnp.zeros_like(do)), v[:end])
                    delta = jnp.sum(probs * dp, axis=-1, keepdims=True)
                    ds = (probs * (dp - delta)).astype(LOW)
                    r.ds_all[side, rows, :end] = ds
                    out.append(dot(ds, k[:end]))
                    sums.append(jnp.sum(delta, axis=0, keepdims=True))
                dq = jnp.where(left, out[0], out[1]) * HDIM ** (-0.5)
                r.dqkv[micro, rows, column(0)] = dq.astype(LOW)
            q = r.qkv_all[micro, :, column(0)]
            do = r.do_all[micro, :, own_cols]
            for block in range(n):
                begin = block * tok
                keys = slice(begin, begin + tok)
                dk = [dot_tn(r.ds_all[side, begin:, keys], q[begin:]) for side in range(2)]
                dv = [
                    dot_tn(r.p_all[micro, head + side, begin:, keys], do[begin:])
                    for side in range(2)
                ]
                dk = jnp.where(left, dk[0], dk[1]) * HDIM ** (-0.5)
                r.dqkv[micro, keys, column(1)] = dk.astype(LOW)
                r.dqkv[micro, keys, column(2)] = jnp.where(left, dv[0], dv[1]).astype(LOW)
            spot = me * heads + head
            first = sum(sums[2::2], sums[0]) * (1.0 / r.scale[spot])
            second = sum(sums[3::2], sums[1]) * (1.0 / r.scale[spot + 1])
            r.vec[10:11, at(me * cols + two * 128, 128)] += jnp.where(left, first, second)

            @pl.when((micro == 0) & (two == 0))
            def _():
                g_turn(0)

            return 0

        lax.fori_loop(0, pairs, pair_of, 0)

        @pl.when(micro == 0)
        def _():
            pair_o.wait()
            for d in range(n):
                total = r.go_all[d, core].astype(F32) + r.go_pair[d].astype(F32)
                r.go_half[d] = total.astype(LOW)
            y_rows(0).turn()
            go.begin()

        @pl.when(micro == 1)
        def _():
            g_turn(1)
            go.turn()
            dh_rows(0).turn()

        def back_rows(d, _):
            total = dot_nt(r.dqkv[micro, :, :cols], r.w_qkv[0, d].reshape(cols, cols))
            for k in (1, 2):
                total = total + dot_nt(
                    r.dqkv[micro, :, k * cols : (k + 1) * cols],
                    r.w_qkv[k, d].reshape(cols, cols),
                )
            r.dh_all[micro, :, at(d * cols, cols)] = total.astype(LOW)
            return 0

        lax.fori_loop(0, n, back_rows, 0)
        dh_rows(micro).begin()
        grads = r.dqkv[micro].astype(F32)
        r.vec[4:5, place] += column_sum(grads[:, :cols])
        r.vec[5:6, place] += column_sum(grads[:, 2 * cols :])
        return 0

    lax.fori_loop(0, batch, one, 0)
    for micro in range(1, batch):
        y_rows(micro).begin()

    def weight_grads(d, _):
        h = r.h_all[:, :, at(d * cols, cols)].reshape(batch * slot, cols)
        grad = dot_tn(h, r.dqkv[...].reshape(batch * slot, 3 * cols)).astype(LOW)
        for k in range(nf):
            r.gq_all[d, k % 2, k // 2] = grad[k * rows_each : (k + 1) * rows_each]
        pair_q(d).start()
        return 0

    lax.fori_loop(0, n, weight_grads, 0)
    r.go_sum[...] = go.finish().astype(LOW)
    start(far_o)
    pair_v.wait()
    for k in range(nz):
        r.mid_sum[k] = r.mid[k, core] + r.mid_pair[k]
    start(far_v)

    def add_pair(d, _):
        pair_q(d).wait()
        total = r.gq_all[d, core].astype(F32) + r.gq_pair[d].astype(F32)
        r.gq_sum[d] = total.astype(LOW)
        return 0

    lax.fori_loop(0, n, add_pair, 0)
    start(far_q)
    for micro in range(1, batch):
        dh_rows(micro).turn()
    for micro in range(batch):
        grad = dh_rows(micro).finish()
        normed, inverse = normal(r.x[micro].astype(F32))
        r.vec[0:1, :] += column_sum(grad * normed)
        r.vec[3:4, :] += column_sum(grad)
        r.dx[micro] = r.dx1[micro] + normal_back(grad * r.wide[0:1, :], normed, inverse)
    spot = lax.broadcasted_iota(jnp.int32, (16, 1), 0)
    own_scales = r.vec[10:11, place]
    for d in range(n):
        block = jnp.where(spot >= 10, 0.0, r.vec[:, d * share : (d + 1) * share])
        r.vec_part[d] = jnp.where(spot == 10 + me, own_scales, block)
    start(shares)
    for micro in range(1, batch):
        y_rows(micro).turn()
    for micro in range(batch):
        total = r.x1[micro] + y_rows(micro).finish() + r.wide[9:10, :]
        r.out[micro] = total.astype(LOW)
    wait(shares)
    total = r.vec_part[me]
    for i in range(1, n):
        total = total + r.vec_got[i - 1]
    r.vec_mine[...] = total
    start(far_vec)
    halves = []
    for w in range(2):
        wait(g_second(w))
        total = r.g_mid[w, two_row].astype(F32)
        for j in range(1, nz // 2):
            total = total + r.g_far[j - 1, w].astype(F32)
        r.g_sum[w] = total.astype(LOW)
        for i, peer in enumerate(peers, 1):
            source = r.g_sum.at[w, :, at((me ^ i) * cols, cols)]
            halves.append(send(source, r.ffn_out.at[w, me], r.d_sems, (i, 4 + w), peer))
    own = [
        pltpu.make_async_copy(r.g_sum.at[w, :, place], r.ffn_out.at[w, me], r.own_sems.at[14 + w])
        for w in range(2)
    ]
    start(halves + own)
    wait(far_o)
    total = r.go_sum[row].astype(F32)
    for j in range(1, nz):
        total = total + r.o_far[j - 1].astype(F32)
    r.o_out[...] = total
    wait(far_v)
    total = r.mid_sum[row]
    for j in range(1, nz):
        total = total + r.v_far[j - 1]
    r.v_out[me] = total
    last = to_peers(
        lambda i, peer: send(r.v_out.at[me], r.v_out.at[me], r.d_sems, (i, 3), peer)
    )
    start(last)
    wait(far_vec)
    total = r.vec_mine[...]
    for j in range(1, nz):
        total = total + r.vec_far[j - 1]
    r.vec_out[...] = total
    r.vec_sum[...] = total
    pair_vec.start()
    wait(far_q)
    for d in range(n):
        total = r.gq_sum[d, row].astype(F32)
        for j in range(1, nz):
            total = total + r.q_far[j - 1, d].astype(F32)
        r.q_last[d] = total.astype(LOW)
    more = []
    for i, peer in enumerate(peers, 1):
        for k in range(3):
            source = r.q_last.at[me ^ i, :, k * cols : (k + 1) * cols]
            more.append(send(source, r.q_out.at[k, :, place], r.d_sems, (i, k), peer))
    own += [
        pltpu.make_async_copy(
            r.q_last.at[me, :, k * cols : (k + 1) * cols],
            r.q_out.at[k, :, place],
            r.own_sems.at[16 + k],
        )
        for k in range(3)
    ]
    start(more + own[2:])
    wait(last + more + own + halves + [pair_vec])
    r.vec_out[...] += r.vec_pair[...]


def backward(x, dy, kept, lens, scale, n, nf):
    batch, tok, width = x.shape
    _, _, _, rows, cols = kept["w_hbm"].shape
    part = kept["mid"].shape[3]
    slot, nz = n * tok, nf // 2
    share = width // n
    heads = cols // HDIM

    def low(*dims):
        return pltpu.VMEM(dims, LOW)

    def full(*dims):
        return pltpu.VMEM(dims, F32)

    names = ("x1_hbm", "z_hbm", "dh2_hbm", "a_hbm", "g_hbm", "out_hbm", "w_hbm", "h_hbm")
    names += ("qkv_hbm", "p_hbm", "mixed_hbm", "w2_hbm")
    inputs = {name: (kept[name], ANY) for name in names}
    inputs["x_hbm"] = (x, ANY)
    inputs["dy_hbm"] = (dy, ANY)
    inputs["wide"] = (kept["wide"], VMEM)
    inputs["mid"] = (kept["mid"], VMEM)
    inputs["lens"] = (lens, SMEM)
    inputs["scale"] = (scale, SMEM)
    outputs = {
        "out": (shape((batch, tok, width), LOW), VMEM),
        "dx": (shape((batch, tok, width), F32), VMEM),
        "q_out": (shape((3, rows, width), LOW), VMEM),
        "o_out": (shape((rows, width), F32), VMEM),
        "v_out": (shape((n, 8, part), F32), VMEM),
        "vec_out": (shape((16, share), F32), VMEM),
        "ffn_out": (shape((2, n, part, cols), LOW), VMEM),
    }
    scratch = {
        "x": low(batch, tok, width),
        "dy": low(batch, tok, width),
        "x1": full(batch, tok, width),
        "z": full(batch, tok, width),
        "dh2": full(batch, tok, width),
        "a": low(batch, tok, width),
        "wout": low(n, nf, rows, width),
        "w_qkv": low(3, n, nf, rows, cols),
        "h_all": low(batch, slot, width),
        "qkv_all": low(batch, slot, 3 * cols),
        "p_all": low(batch, heads, slot, slot),
        "mixed": low(*kept["mixed_hbm"].shape),
        "w2": low(*kept["w2_hbm"].shape),
        "y_all": low(batch, slot, width),
        "y_got": low(batch, 2, 2, tok, width // 2),
        "y_passed": low(batch, 2, tok, width // 2),
        "y_last": low(batch, 2, tok, width // 2),
        "dx1": full(batch, tok, width),
        "dz": low(batch * tok, width),
        "do_own": low(batch, n, tok, cols),
        "do_all": low(batch, slot, cols),
        "ds_all": low(2, slot, slot),
        "dqkv": low(batch, slot, 3 * cols),
        "dh_all": low(batch, slot, width),
        "dh_got": low(batch, 2, 2, tok, width // 2),
        "dh_passed": low(batch, 2, tok, width // 2),
        "dh_last": low(batch, 2, tok, width // 2),
        "go_all": low(n, 2, nz, rows, width),
        "go_pair": low(n, nz, rows, width),
        "go_half": low(n, nz, rows, width),
        "go_got": low(2, 2, nz, rows, width // 2),
        "go_passed": low(2, nz, rows, width // 2),
        "go_last": low(2, nz, rows, width // 2),
        "go_sum": low(nz, rows, width),
        "o_far": low(nz - 1, rows, width),
        "gq_all": low(n, 2, nz, rows, 3 * cols),
        "gq_pair": low(n, nz, rows, 3 * cols),
        "gq_sum": low(n, nz, rows, 3 * cols),
        "q_far": low(nz - 1, n, rows, 3 * cols),
        "q_last": low(n, rows, 3 * cols),
        "g_own": low(2, nz // 2, part, width),
        "g_pair": low(2, nz // 2, part, width),
        "g_mid": low(2, nz // 2, part, width),
        "g_far": low(nz // 2 - 1, 2, part, width),
        "g_sum": low(2, part, width),
        "mid_pair": full(nz, 8, part),
        "mid_sum": full(nz, 8, part),
        "v_far": full(nz - 1, 8, part),
        "vec": full(16, width),
        "vec_part": full(n, 16, share),
        "vec_got": full(n - 1, 16, share),
        "vec_mine": full(16, share),
        "vec_far": full(nz - 1, 16, share),
        "vec_sum": full(16, share),
        "vec_pair": full(16, share),
        "o_sems": DMA((2, batch, n)),
        "h_sems": DMA((2, batch, 2, 3)),
        "y_sems": DMA((2, batch, 2, 3)),
        "p_sems": DMA((2, 3)),
        "q_sems": DMA((2, n)),
        "e_sems": DMA((2, 2, 3)),
        "g_sems": DMA((2, nz // 2, 2)),
        "z_sems": DMA((2, nz, 5)),
        "d_sems": DMA((2, n, 7)),
        "own_sems": DMA((19,)),
    }
    return launch(
        lambda r: backward_kernel(n, nf, r), "backward", inputs, outputs, scratch, 1, 60
    )


def finish_kernel(n, nf, r):
    f = lax.axis_index("ffn")
    rows_each = r.gains.shape[1]
    part = r.mid.shape[2]
    cols, hid = r.w_in.shape
    r.out_to[...] = r.out[...]
    r.dx_to[...] = r.dx[...]
    r.q_to[...] = r.q_out[...].astype(F32)
    r.o_to[...] = r.o_out[...]
    r.w_in[...] = r.ffn[0].reshape(hid, cols).astype(F32).T
    r.w_out[...] = r.ffn[1].reshape(hid, cols).astype(F32)
    own = jnp.zeros((16, rows_each), F32)
    for k in range(nf):
        own = own + jnp.where(f == k, r.vec[:, k * rows_each : (k + 1) * rows_each], 0.0)
    r.gains[...] = own[:3]
    r.biases[...] = own[3:10]
    heads = r.heads.shape[1]
    lane = lax.broadcasted_iota(jnp.int32, (1, heads), 1)
    total = jnp.zeros((1, heads), F32)
    for head in range(heads):
        d, c = divmod(head, heads // n)
        value = r.vec[10 + d : 11 + d, c * HDIM : c * HDIM + 1]
        total = total + jnp.where(lane == head, value, 0.0)
    r.heads[...] = total
    for k, target in enumerate((r.mid_0, r.mid_1, r.mid_2)):
        for d in range(n):
            target[:, d * part : (d + 1) * part] = r.mid[d, k : k + 1]


def finish(done, heads, n, nf):
    out, dx, q_out, o_out = [done[name] for name in ("out", "dx", "q_out", "o_out")]
    vec, mid, ffn = done["vec_out"], done["v_out"], done["ffn_out"]
    _, _, part, cols = ffn.shape
    rows = o_out.shape[0]
    hid = n * part
    inputs = dict(out=out, dx=dx, q_out=q_out, o_out=o_out, vec=vec, mid=mid, ffn=ffn)
    outputs = dict(
        out_to=shape(out.shape, LOW),
        dx_to=shape(dx.shape, F32),
        q_to=shape(q_out.shape, F32),
        o_to=shape(o_out.shape, F32),
        heads=shape((1, heads), F32),
        gains=shape((3, rows), F32),
        biases=shape((7, rows), F32),
        w_in=shape((cols, hid), F32),
        mid_0=shape((1, hid), F32),
        mid_1=shape((1, hid), F32),
        mid_2=shape((1, hid), F32),
        w_out=shape((hid, cols), F32),
    )
    names = [*inputs, *outputs]
    return pl.pallas_call(
        lambda *refs: finish_kernel(n, nf, SimpleNamespace(**dict(zip(names, refs)))),
        name="finish",
        out_shape=tuple(outputs.values()),
        in_specs=[VMEM] * len(inputs),
        out_specs=(VMEM,) * len(outputs),
        compiler_params=pltpu.CompilerParams(vmem_limit_bytes=62 << 20),
    )(*inputs.values())


def on_device(
    tokens,
    seq_lens,
    qkv_weight,
    out_weight,
    head_scale,
    gains,
    biases,
    ffn_in,
    ffn_bias,
    mid_gain,
    mid_bias,
    ffn_out,
    out_cotangent,
):
    n = lax.axis_size("dp")
    nf = lax.axis_size("ffn")
    me = lax.axis_index("dp")
    batch, _, tok, width = tokens.shape
    heads = head_scale.shape[0]
    cols = width // n
    rows = qkv_weight.shape[1]
    hid = ffn_in.shape[1]
    part = hid // n

    vectors = lax.dynamic_index_in_dim(
        jnp.stack([ffn_bias, mid_gain, mid_bias]).reshape(3, n, part), me, 1, keepdims=False
    )
    x, dy = tokens[:, 0], out_cotangent[:, 0]
    lens = seq_lens.reshape(-1)
    kept = forward(
        x,
        qkv_weight,
        out_weight,
        (gains, biases, vectors),
        ffn_in,
        ffn_out.reshape(n, part, cols),
        dy,
        lens,
        head_scale,
        n,
        nf,
    )
    done = backward(x, dy, kept, lens, head_scale, n, nf)
    out, dx, q_grad, o_grad, head_grad, gain_grad, bias_grad, in_grad, *mids, last_grad = finish(
        done, heads, n, nf
    )
    return (
        out[:, None],
        dx[:, None],
        q_grad,
        o_grad,
        head_grad.reshape(heads),
        gain_grad,
        bias_grad,
        in_grad,
        *[mid.reshape(hid) for mid in mids],
        last_grad,
    )


def solution(mesh):
    seqs = P(None, "ffn", "dp", None)
    wide = P(None, ("dp", "ffn"))
    hidden = P("ffn")
    return jax.shard_map(
        on_device,
        mesh=mesh,
        in_specs=(
            seqs,
            P(None, "ffn"),
            P(None, ("dp", "ffn"), None),
            P(("dp", "ffn"), None),
            P(),
            wide,
            wide,
            P("dp", "ffn"),
            hidden,
            hidden,
            hidden,
            P("ffn", "dp"),
            seqs,
        ),
        out_specs=(
            seqs,
            seqs,
            P(None, ("dp", "ffn"), None),
            P(("dp", "ffn"), None),
            P(),
            wide,
            wide,
            P("dp", "ffn"),
            hidden,
            hidden,
            hidden,
            P("ffn", "dp"),
        ),
        check_vma=False,
    )
```

```python
from types import SimpleNamespace

import jax
import jax.numpy as jnp
from jax import lax
from jax.experimental import pallas as pl
from jax.experimental.pallas import tpu as pltpu
from jax.sharding import PartitionSpec as P

HDIM = 64
EPS = 1e-05
LOW = jnp.bfloat16
F32 = jnp.float32
ANY = pl.BlockSpec(memory_space=pl.ANY)
VMEM = pl.BlockSpec(memory_space=pltpu.VMEM)
SMEM = pl.BlockSpec(memory_space=pltpu.SMEM)
MESH = pl.DeviceIdType.MESH
DMA = pltpu.SemaphoreType.DMA


def dot(left, right):
    return jnp.dot(left, right, preferred_element_type=F32)


def dot_nt(left, right):
    return lax.dot_general(left, right, (((1,), (1,)), ((), ())), preferred_element_type=F32)


def dot_tn(left, right):
    return lax.dot_general(left, right, (((0,), (0,)), ((), ())), preferred_element_type=F32)


def shape(dims, kind):
    return jax.ShapeDtypeStruct(tuple(dims), kind)


def at(start, size, unit=128):
    return pl.ds(pl.multiple_of(start, unit), size)


def send(src, dst, sems, index, where):
    return pltpu.make_async_remote_copy(
        src_ref=src,
        dst_ref=dst,
        send_sem=sems.at[(0, *index)],
        recv_sem=sems.at[(1, *index)],
        device_id=where,
        device_id_type=MESH,
    )


def greet(peers):
    barrier = pltpu.get_barrier_semaphore()
    for peer in peers:
        pl.semaphore_signal(barrier, inc=1, device_id=peer, device_id_type=MESH)


def meet(peers):
    pl.semaphore_wait(pltpu.get_barrier_semaphore(), len(peers))


def dp_peers(n, me):
    return [{"dp": me ^ i} for i in range(1, n)]


def ffn_peers(nf, f):
    return [{"ffn": f ^ (2 * j)} for j in range(1, nf // 2)] + [{"ffn": f ^ 1}]


def start(copies):
    for copy in copies:
        copy.start()


def wait(copies):
    for copy in copies:
        copy.wait()


class Line:
    def __init__(self, nf, f, items, hop_sems, side_sems):
        self.nz, self.core, self.q, self.f = nf // 2, lax.rem(f, 2), lax.div(f, 2), f
        self.items, self.hop_sems, self.side_sems = items, hop_sems, side_sems
        self.next = [1] * len(items)

    def copy(self, sems, k, t, came, way, first, target):
        source, place = self.items[k]
        index = self.f if first else 2 * (self.q - t * way) + self.core
        spot = place(index)
        side = 0 if way > 0 else 1
        return pltpu.make_async_remote_copy(
            src_ref=source if first else spot,
            dst_ref=spot,
            send_sem=sems.at[0, side, k, t],
            recv_sem=sems.at[1, side, k, came],
            device_id={"ffn": target},
            device_id_type=MESH,
        )

    def hop(self, k, t, way, first=False):
        return self.copy(self.hop_sems, k, t, t + 1, way, first, self.f + 2 * way)

    def arrival(self, k, t, way):
        return self.copy(self.hop_sems, k, t, t, way, False, self.f + 2 * way)

    def over(self, k, t, way, first=False):
        return self.copy(self.side_sems, k, t, t, way, first, self.f ^ 1)

    def onward(self, way):
        return self.q < self.nz - 1 if way > 0 else self.q > 0

    def has(self, t, way):
        return self.q - t >= 0 if way > 0 else self.q + t <= self.nz - 1

    def begin(self, *items):
        for k in items:
            for way in (1, -1):

                @pl.when(self.onward(way))
                def _():
                    self.hop(k, 0, way, True).start()

        for k in items:
            self.over(k, 0, 1, True).start()

    def step(self, k, t):
        for way in (1, -1):

            @pl.when(self.has(t, way) & self.onward(way))
            def _():
                self.arrival(k, t, way).wait_recv()
                self.hop(k, t, way).start()

        for way in (1, -1):

            @pl.when(self.has(t, way))
            def _():
                @pl.when(jnp.logical_not(self.onward(way)))
                def _():
                    self.arrival(k, t, way).wait_recv()

                self.over(k, t, way).start()

    def advance(self, *items):
        for k in items:
            if self.next[k] < self.nz:
                self.step(k, self.next[k])
                self.next[k] += 1

    def arrive(self, *items):
        begin = self.next[items[0]]

        def rest(t, _):
            for k in items:
                self.step(k, t)
            return 0

        lax.fori_loop(begin, self.nz, rest, 0)

        def close(t, _):
            for k in items:
                for way in (1, -1):

                    @pl.when(self.has(t, way))
                    def _():
                        self.over(k, t, way).wait_recv()

            return 0

        for k in items:
            self.over(k, 0, 1, True).wait_recv()
        lax.fori_loop(1, self.nz, close, 0)

    def finish(self, *items):
        for k in items:
            self.over(k, 0, 1, True).wait_send()
            for way in (1, -1):

                @pl.when(self.onward(way))
                def _():
                    self.hop(k, 0, way, True).wait_send()

        def close(t, _):
            for k in items:
                for way in (1, -1):

                    @pl.when(self.has(t, way))
                    def _():
                        self.over(k, t, way).wait_send()

                    @pl.when(self.has(t, way) & self.onward(way))
                    def _():
                        self.hop(k, t, way).wait_send()

            return 0

        lax.fori_loop(1, self.nz, close, 0)


def line_meet(n, nf, me, f):
    barrier = pltpu.get_barrier_semaphore()
    q, nz = lax.div(f, 2), nf // 2
    greet(dp_peers(n, me) + [{"ffn": f ^ 1}])

    @pl.when(q < nz - 1)
    def _():
        greet([{"ffn": f + 2}])

    @pl.when(q > 0)
    def _():
        greet([{"ffn": f - 2}])

    count = n + jnp.where(q < nz - 1, 1, 0) + jnp.where(q > 0, 1, 0)
    pl.semaphore_wait(barrier, count)


class Gather:
    def __init__(self, me, source, place, size, sems, index):
        self.me, self.source, self.place, self.half = me, source, place, size // 2
        self.sems, self.index = sems, index

    def straight(self, k):
        spot = self.place(self.me, 0, 2 * self.half)
        return send(self.source, spot, self.sems, (*self.index, k), {"dp": self.me ^ (k + 1)})

    def relay(self, k):
        spot = self.place(self.me ^ (k + 1), k * self.half, self.half)
        return send(spot, spot, self.sems, (*self.index, 2 + k), {"dp": self.me ^ (2 - k)})

    def begin(self):
        for k in range(2):
            self.straight(k).start()

    def turn(self):
        for k in range(2):
            self.straight(k).wait()
            self.relay(k).start()

    def finish(self):
        for k in range(2):
            self.relay(k).wait()


class Reduce:
    def __init__(self, me, block, got, passed, last, sems, index):
        self.me, self.block, self.passed = me, block, passed
        self.got, self.last, self.sems, self.index = got, last, sems, index

    def first(self, side, far):
        step = side + 1
        owner = self.me ^ (3 if far else step)
        target = self.got.at[(*self.index, side, far)]
        spot = (*self.index, side, far)
        return send(self.block(owner, side), target, self.sems, spot, {"dp": self.me ^ step})

    def second(self, side):
        where = (*self.index, side)
        target = {"dp": self.me ^ (2 - side)}
        return send(self.passed.at[where], self.last.at[where], self.sems, (*where, 2), target)

    def begin(self):
        for far in (1, 0):
            for side in range(2):
                self.first(side, far).start()

    def turn(self):
        for side in range(2):
            self.first(side, 1).wait()
            total = self.block(self.me ^ (2 - side), side)[...].astype(F32)
            total = total + self.got[(*self.index, side, 1)].astype(F32)
            self.passed[(*self.index, side)] = total.astype(LOW)
            self.second(side).start()

    def finish(self):
        halves = []
        for side in range(2):
            self.first(side, 0).wait()
            self.second(side).wait()
            total = self.block(self.me, side)[...].astype(F32)
            total = total + self.got[(*self.index, side, 0)].astype(F32)
            halves.append(total + self.last[(*self.index, side)].astype(F32))
        return jnp.concatenate(halves, axis=-1)


def normal(values):
    center = values - jnp.mean(values, axis=-1, keepdims=True)
    inverse = lax.rsqrt(jnp.mean(center * center, axis=-1, keepdims=True) + EPS)
    return center * inverse, inverse


def normal_back(grad, normed, inverse):
    return inverse * (
        grad
        - jnp.mean(grad, axis=-1, keepdims=True)
        - normed * jnp.mean(grad * normed, axis=-1, keepdims=True)
    )


def column_sum(values):
    return jnp.sum(values, axis=0, keepdims=True)


def launch(body, name, inputs, outputs, scratch, number, limit):
    names = [*inputs, *outputs, *scratch]
    results = pl.pallas_call(
        lambda *refs: body(SimpleNamespace(**dict(zip(names, refs)))),
        name=name,
        out_shape=tuple(kind for kind, _ in outputs.values()),
        in_specs=[spec for _, spec in inputs.values()],
        out_specs=tuple(spec for _, spec in outputs.values()),
        scratch_shapes=list(scratch.values()),
        compiler_params=pltpu.CompilerParams(
            collective_id=number, has_side_effects=True, vmem_limit_bytes=limit << 20
        ),
    )(*[value for value, _ in inputs.values()])
    return dict(zip(outputs, results))


def forward_kernel(n, nf, part, r):
    me = lax.axis_index("dp")
    f = lax.axis_index("ffn")
    core, nz = lax.rem(f, 2), nf // 2
    batch, tok, width = r.x.shape
    rows_each = r.wout.shape[0]
    cols = width // n
    pairs = cols // 128
    slot = n * tok
    hid = nf * part
    ff = n * hid
    step = 256
    peers = dp_peers(n, me)
    pair = {"ffn": f ^ 1}
    place = at(me * cols, cols)
    band = at(me * tok, tok)

    own = [
        pltpu.make_async_copy(r.qkv.at[:, :, place], r.stage.at[:, me], r.own_sems.at[0]),
        pltpu.make_async_copy(r.small.at[0], r.small_stage.at[me], r.own_sems.at[1]),
        pltpu.make_async_copy(r.small.at[1], r.small_stage.at[n], r.own_sems.at[2]),
        pltpu.make_async_copy(r.wout, r.out_stage.at[me], r.own_sems.at[3]),
        pltpu.make_async_copy(r.first, r.first_in, r.own_sems.at[4]),
        pltpu.make_async_copy(r.second.at[me], r.second_stage.at[:, place], r.own_sems.at[5]),
        pltpu.make_async_copy(r.x, r.x_all.at[me], r.own_sems.at[6]),
        pltpu.make_async_copy(r.dy, r.dy_all.at[:, band, :], r.own_sems.at[7]),
    ]
    start(own[:1] + own[3:])
    line_meet(n, nf, me, f)

    def to_peers(make):
        return [make(i, peer) for i, peer in enumerate(peers, 1)]

    blocks = to_peers(
        lambda i, peer: send(
            r.qkv.at[:, :, at((me ^ i) * cols, cols)], r.stage.at[:, me], r.w_sems, (i, 0), peer
        )
    )
    smalls = to_peers(
        lambda i, peer: send(r.small.at[0], r.small_stage.at[me], r.w_sems, (i, 1), peer)
    )
    outs = to_peers(lambda i, peer: send(r.wout, r.out_stage.at[me], r.w_sems, (i, 2), peer))
    firsts = to_peers(
        lambda i, peer: send(
            r.first_all.at[me ^ i], r.first_stage.at[:, place], r.w_sems, (i, 3), peer
        )
    )
    seconds = to_peers(
        lambda i, peer: send(
            r.second.at[me ^ i], r.second_stage.at[:, place], r.w_sems, (i, 4), peer
        )
    )

    def x_rows(micro):
        def spot(owner, start, size):
            return r.x_all.at[owner, micro, start : start + size]

        return Gather(me, r.x.at[micro], spot, tok, r.x_sems, (micro,))

    def y_rows(micro):
        def spot(owner, start, size):
            return r.dy_all.at[micro, at(owner * tok + start, size, 64), :]

        return Gather(me, r.dy.at[micro], spot, tok, r.y_sems, (micro,))

    start(blocks)
    size = r.gains.shape[1]
    lanes = lax.broadcasted_iota(jnp.int32, (16, 128), 1)
    r.tile[...] = jnp.zeros_like(r.tile)
    for k in range(128 // size):
        r.tile[0, 0:3, k * size : (k + 1) * size] = r.gains[...].astype(F32)
        r.tile[0, 3:10, k * size : (k + 1) * size] = r.biases[...].astype(F32)
    for k in range(128 // part):
        r.tile[1, 0:3, k * part : (k + 1) * part] = r.hidden[...].astype(F32)
    for k, each_ in enumerate((size, part)):
        mine_ = lanes // each_ == lax.rem(f, 128 // each_)
        r.small[k] = jnp.where(mine_, r.tile[k], 0.0).astype(LOW)
    start(own[1:3] + smalls)
    x_rows(0).begin()
    wait(own[4:5])
    r.first_all[...] = r.first_in[...].T.reshape(r.first_all.shape)
    own[4] = pltpu.make_async_copy(
        r.first_all.at[me], r.first_stage.at[:, place], r.own_sems.at[4]
    )
    start(own[4:5])
    start(outs + firsts)
    line = Line(
        nf,
        f,
        [
            (r.stage, lambda index: r.w_all.at[:, :, index]),
            (r.small_stage, lambda index: r.small_all.at[index]),
            (r.out_stage, lambda index: r.out_all.at[:, index]),
            (r.first_stage, lambda index: r.w1.at[index]),
            (r.second_stage, lambda index: r.w2.at[index]),
        ],
        r.hop_sems,
        r.side_sems,
    )
    mine = [
        pltpu.make_async_copy(source, spot(f), r.own_sems.at[8 + k])
        for k, (source, spot) in enumerate(line.items)
    ]
    wait(blocks + smalls + own[:3])
    line.begin(0, 1)
    start(mine[:2])
    line.advance(0, 1)
    x_rows(0).turn()
    x_rows(1).begin()
    line.advance(0, 1)
    wait(outs + own[3:4])
    line.begin(2)
    start(mine[2:3])
    line.arrive(0, 1)
    wait(firsts + own[4:5])
    line.begin(3)
    start(mine[3:4])
    wait(mine[:2] + own[6:7])

    def lay_out(out_ref, index, begin, size):
        together = 128 // size
        for b in range(nf // together):
            total = r.small_all[b * together, index].astype(F32)
            for k in range(1, together):
                total = total + r.small_all[b * together + k, index].astype(F32)
            out_ref[:, begin + b * 128 : begin + (b + 1) * 128] = total

    for d in range(n):
        lay_out(r.wide, d, d * nf * rows_each, rows_each)
    lay_out(r.mids, n, 0, part)

    gain, shift = r.wide[0:1, :], r.wide[3:4, :]
    bias_q, bias_v = r.wide[4:5, place], r.wide[5:6, place]
    left = lax.broadcasted_iota(jnp.int32, (1, 128), 1) < HDIM

    def block_copies(micro):
        return to_peers(
            lambda i, peer: send(
                r.a_all.at[micro, me ^ i], r.a_own.at[micro, :, place], r.a_sems, (micro, i), peer
            )
        )

    def keep_copies(micro):
        return [
            pltpu.make_async_copy(source.at[micro], out.at[micro], r.keep_sems.at[micro, k])
            for k, (source, out) in enumerate(
                [(r.h_all, r.h_hbm), (r.qkv_all, r.qkv_hbm), (r.p_all, r.p_hbm)]
            )
        ]

    def after_first():
        line.advance(2)
        x_rows(1).turn()
        start(seconds)
        y_rows(0).begin()

    def after_second():
        line.advance(3)

    def after_third():
        line.advance(2)
        wait(seconds + own[5:6])
        line.begin(4)
        start(mine[4:5])

    def after_last():
        y_rows(0).turn()
        y_rows(1).begin()
        line.advance(3)

    def attend(index, _):
        micro, two = lax.div(index, pairs), lax.rem(index, pairs)

        @pl.when(two == 0)
        def _():
            x_rows(micro).finish()

            def norm_rows(d, _):
                values, _ = normal(r.x_all[d, micro].astype(F32))
                r.h_all[micro, at(d * tok, tok), :] = (values * gain + shift).astype(LOW)
                return 0

            lax.fori_loop(0, n, norm_rows, 0)
            for k, bias in enumerate((bias_q, None, bias_v)):
                weight = r.w_all[k].reshape(width, cols)
                value = dot(r.h_all[micro], weight)
                if bias is not None:
                    value = value + bias
                r.qkv_all[micro, :, k * cols : (k + 1) * cols] = value.astype(LOW)

        length = r.lens[micro]

        def column(k):
            return at(k * cols + two * 128, 128)

        head = two * 2
        scales = jnp.where(
            left, r.scale[me * 2 * pairs + head], r.scale[me * 2 * pairs + head + 1]
        )
        for block in range(n):
            end = (block + 1) * tok
            q = r.qkv_all[micro, block * tok : end, column(0)] * HDIM ** (-0.5)
            k = r.qkv_all[micro, :end, column(1)]
            v = r.qkv_all[micro, :end, column(2)]
            key = lax.broadcasted_iota(jnp.int32, (tok, end), 1)
            query = lax.broadcasted_iota(jnp.int32, (tok, end), 0) + block * tok
            mask = (key <= query) & (key < length)
            out = []
            for side in range(2):
                mine_ = left if side == 0 else jnp.logical_not(left)
                scores = dot_nt(jnp.where(mine_, q, jnp.zeros_like(q)), k)
                scores = jnp.where(mask, scores, -1e30)
                expo = jnp.exp(scores - jnp.max(scores, axis=-1, keepdims=True))
                probs = expo * (1.0 / jnp.sum(expo, axis=-1, keepdims=True))
                probs = probs.astype(LOW)
                r.p_all[micro, head + side, block * tok : end, :end] = probs
                out.append(dot(probs, v))
            joined = jnp.where(left, out[0], out[1]) * scales
            r.a_all[micro, block, :, at(two * 128, 128)] = joined.astype(LOW)

        @pl.when(two == pairs - 1)
        def _():
            start(block_copies(micro))
            start(keep_copies(micro))
            r.a_own[micro, :, place] = r.a_all[micro, me]

        work = [after_first, after_second, after_third, after_last]
        for k, act in enumerate(work[: batch * pairs]):
            pl.when(index == k)(act)
        return 0

    lax.fori_loop(0, batch * pairs, attend, 0)

    line.arrive(2)
    wait(mine[2:3])
    late = [
        pltpu.make_async_copy(source, target, r.own_sems.at[13 + k])
        for k, (source, target) in enumerate(
            [(r.w_all, r.w_hbm), (r.out_all, r.out_hbm), (r.z, r.z_hbm), (r.x1, r.x1_hbm),
             (r.a_own, r.a_hbm), (r.mixed, r.mixed_hbm), (r.pair_got, r.g_hbm), (r.dh2, r.dh2_hbm),
             (r.w2, r.w2_hbm)]
        )
    ]
    start(late[:2])

    def h2_rows(micro):
        def spot(owner, start, size):
            return r.h2_all.at[micro, at(owner * tok + start, size, 64), :]

        return Gather(me, r.h2_own.at[micro], spot, tok, r.h_sems, (micro,))

    for micro in range(batch):
        wait(block_copies(micro))
        z = dot(r.a_own[micro], r.out_all[...].reshape(width, width)) + r.wide[6:7, :]
        r.z[micro] = z
        values, _ = normal(z)
        x1 = r.x_all[me, micro].astype(F32) + values * r.wide[1:2, :] + r.wide[7:8, :]
        r.x1[micro] = x1
        values, _ = normal(x1)
        r.h2_own[micro] = (values * r.wide[2:3, :] + r.wide[8:9, :]).astype(LOW)
        h2_rows(micro).begin()
        r.h2_all[micro, band, :] = r.h2_own[micro]
    start(late[2:5])
    line.advance(4)
    h2_rows(0).turn()
    y_rows(1).turn()
    for micro in range(1, batch):
        h2_rows(micro).turn()
    line.arrive(3)
    wait(mine[3:4])

    def weights(ref, c):
        count = step // part
        return ref[pl.ds(c * count, count)].reshape(step, width)

    def w_columns(ref, columns):
        return ref[:, :, columns].reshape(hid, step)

    def sum_copies(micro):
        return to_peers(
            lambda i, peer: send(
                r.sums.at[micro], r.sums_all.at[micro, me], r.s_sems, (micro, i), peer
            )
        )

    def dh2_rows(micro):
        def block(owner, side):
            columns = slice(side * (width // 2), (side + 1) * (width // 2))
            return r.dh2_all.at[micro, at(owner * tok, tok), columns]

        return Reduce(me, block, r.dh2_got, r.dh2_passed, r.dh2_last, r.r_sems, (micro,))

    def fold(values):
        total = values[:, :128]
        for k in range(1, step // 128):
            total = total + values[:, k * 128 : (k + 1) * 128]
        return total

    def units(micro):
        h2_rows(micro).finish()

        def chunk(c, totals):
            rows = at(c * step, step)
            u = dot_nt(r.h2_all[micro], weights(r.w1, c)) + r.mids[0:1, rows]
            phi = 0.5 + 0.5 * lax.erf(u * (0.5**0.5))
            value = u * phi
            r.act[micro, :, rows] = value
            r.slope[micro, :, rows] = phi + u * jnp.exp(u * u * -0.5) * 0.3989422804014327
            return totals[0] + fold(value), totals[1] + fold(value * value)

        zero = jnp.zeros((slot, 128), F32)
        totals = lax.fori_loop(0, hid // step, chunk, (zero,) * 2)
        for k in range(2):
            r.sums[micro, k : k + 1, :] = column_sum(totals[k].T)

    def cotangents(micro):
        y_rows(micro).finish()
        valid = lax.broadcasted_iota(jnp.int32, (slot, 1), 0) < r.lens[micro]
        rows = r.dy_all[micro]
        r.dy_all[micro] = jnp.where(valid, rows, jnp.zeros_like(rows))

        def chunk(c, totals):
            rows = at(c * step, step)
            dm = dot_nt(r.dy_all[micro], weights(r.w2, c))
            r.dmix[micro, :, rows] = dm
            dn = dm * r.mids[1:2, rows]
            return totals[0] + fold(dn), totals[1] + fold(dn * r.act[micro, :, rows])

        zero = jnp.zeros((slot, 128), F32)
        totals = lax.fori_loop(0, hid // step, chunk, (zero,) * 2)
        for k in range(2):
            r.sums[micro, 2 + k : 3 + k, :] = column_sum(totals[k].T)
        r.sums[micro, 4:8, :] = jnp.zeros((4, slot), F32)
        start(sum_copies(micro))

    r.vec[...] = jnp.zeros_like(r.vec)

    def second_pass(micro, _):
        wait(sum_copies(micro))
        r.sums_all[micro, me] = r.sums[micro]
        total = r.sums_all[micro, 0]
        for d in range(1, n):
            total = total + r.sums_all[micro, d]
        total = total * (1.0 / ff)
        mean = total[0:1]
        inverse = lax.rsqrt(total[1:2] - mean * mean + EPS)
        back = total[2:3]
        cross = inverse * (total[3:4] - mean * back)
        table = jnp.concatenate([mean, inverse, back, cross] * 32, axis=0).T
        mean, inverse, back, cross = [table[:, k : k + 1] for k in range(4)]
        rows_of = at(micro * slot, slot)

        def chunk(c, _):
            rows = at(c * step, step)
            normed = (r.act[micro, :, rows] - mean) * inverse
            dm = r.dmix[micro, :, rows]
            gain = r.mids[1:2, rows]
            r.mixed[rows_of, rows] = (normed * gain + r.mids[2:3, rows]).astype(LOW)
            df = inverse * (dm * gain - back - normed * cross)
            low = (df * r.slope[micro, :, rows]).astype(LOW)
            r.du[rows_of, rows] = low
            r.vec[0:1, rows] += column_sum(low.astype(F32))
            r.vec[1:2, rows] += column_sum(dm * normed)
            r.vec[2:3, rows] += column_sum(dm)
            return 0

        lax.fori_loop(0, hid // step, chunk, 0)

        def back_rows(c, _):
            columns = at(c * step, step)
            value = dot(r.du[rows_of, :], w_columns(r.w1, columns))
            r.dh2_all[micro, :, columns] = value.astype(LOW)
            return 0

        lax.fori_loop(0, width // step, back_rows, 0)
        dh2_rows(micro).begin()
        return 0

    units(0)
    line.arrive(4)
    wait(mine[4:5] + own[7:8])
    cotangents(0)

    def passes(micro, _):
        @pl.when(micro + 1 < batch)
        def _():
            units(micro + 1)

        second_pass(micro, 0)

        @pl.when(micro + 1 < batch)
        def _():
            cotangents(micro + 1)

        @pl.when(micro > 0)
        def _():
            dh2_rows(micro - 1).turn()

        return 0

    lax.fori_loop(0, batch, passes, 0)
    start(late[5:6] + late[8:])
    each = step // part // 2

    def halved(index):
        return lax.div(index, 2), lax.rem(index, 2)

    def pair_copies(c):
        copies = []
        for k in range(each):
            index = c * (2 * each) + 2 * k
            for w in range(2):
                copies.append(
                    send(
                        r.grads.at[w, index + 1 - core],
                        r.pair_got.at[(w, *halved(c * each + k))],
                        r.p_sems,
                        (c, k, w),
                        pair,
                    )
                )
        return copies

    def weight_grads(c, _):
        rows = at(c * step, step)
        h2 = r.h2_all[...].reshape(batch * slot, width)
        dy = r.dy_all[...].reshape(batch * slot, width)
        first = dot_tn(r.du[:, rows], h2).astype(LOW)
        second = dot_tn(r.mixed[:, rows], dy).astype(LOW)
        for k in range(step // part):
            r.grads[0, c * (step // part) + k] = first[k * part : (k + 1) * part]
            r.grads[1, c * (step // part) + k] = second[k * part : (k + 1) * part]
        start(pair_copies(c))
        return 0

    lax.fori_loop(0, hid // step, weight_grads, 0)
    dh2_rows(batch - 1).turn()

    def pair_sum(c, _):
        wait(pair_copies(c))
        for k in range(each):
            for w in range(2):
                total = r.grads[w, c * (2 * each) + 2 * k + core].astype(F32)
                spot = (w, *halved(c * each + k))
                total = total + r.pair_got[spot].astype(F32)
                r.pair_got[spot] = total.astype(LOW)
        return 0

    lax.fori_loop(0, hid // step, pair_sum, 0)
    start(late[6:7])
    for k in range(nf):
        r.mid[k // 2, k % 2] = r.vec[:, k * part : (k + 1) * part]
    line.finish(0, 1, 2, 3, 4)
    for micro in range(batch):
        wait(keep_copies(micro))
    for micro in range(batch):
        r.dh2[micro] = dh2_rows(micro).finish()
    start(late[7:8])
    wait(late)


def forward(x, qkv, wout, small, first, second, dy, lens, scale, n, nf):
    batch, tok, width = x.shape
    rows = wout.shape[0]
    part = second.shape[1]
    cols = width // n
    slot, hid = n * tok, nf * part
    heads = cols // HDIM

    def low(*dims):
        return pltpu.VMEM(dims, LOW)

    def full(*dims):
        return pltpu.VMEM(dims, F32)

    inputs = {
        name: (value, ANY)
        for name, value in zip(
            ("x", "qkv", "wout", "first", "second", "dy"),
            (x, qkv, wout, first, second, dy),
        )
    }
    for name, value in zip(("gains", "biases", "hidden"), small):
        inputs[name] = (value, VMEM)
    inputs["lens"] = (lens, SMEM)
    inputs["scale"] = (scale, SMEM)
    outputs = {
        "wide": (shape((16, width), F32), VMEM),
        "w_hbm": (shape((3, n, nf, rows, cols), LOW), ANY),
        "out_hbm": (shape((n, nf, rows, width), LOW), ANY),
        "h_hbm": (shape((batch, slot, width), LOW), ANY),
        "qkv_hbm": (shape((batch, slot, 3 * cols), LOW), ANY),
        "p_hbm": (shape((batch, heads, slot, slot), LOW), ANY),
        "a_hbm": (shape((batch, tok, width), LOW), ANY),
        "z_hbm": (shape((batch, tok, width), F32), ANY),
        "x1_hbm": (shape((batch, tok, width), F32), ANY),
        "mixed_hbm": (shape((batch * slot, hid), LOW), ANY),
        "w2_hbm": (shape((nf, part, width), LOW), ANY),
        "g_hbm": (shape((2, nf // 4, 2, part, width), LOW), ANY),
        "dh2_hbm": (shape((batch, tok, width), F32), ANY),
        "mid": (shape((nf // 2, 2, 8, part), F32), VMEM),
    }
    scratch = {
        "mids": full(16, hid),
        "dh2": full(batch, tok, width),
        "vec": full(8, hid),
        "stage": low(3, n, rows, cols),
        "tile": full(2, 16, 128),
        "small": low(2, 16, 128),
        "small_stage": low(n + 1, 16, 128),
        "out_stage": low(n, rows, width),
        "first_in": low(*first.shape),
        "first_all": low(*second.shape),
        "first_stage": low(part, width),
        "second_stage": low(part, width),
        "small_all": low(nf, n + 1, 16, 128),
        "w_all": low(3, n, nf, rows, cols),
        "out_all": low(n, nf, rows, width),
        "w1": low(nf, part, width),
        "w2": low(nf, part, width),
        "x_all": low(n, batch, tok, width),
        "dy_all": low(batch, slot, width),
        "h_all": low(batch, slot, width),
        "qkv_all": low(batch, slot, 3 * cols),
        "p_all": low(batch, heads, slot, slot),
        "a_all": low(batch, n, tok, cols),
        "a_own": low(batch, tok, width),
        "z": full(batch, tok, width),
        "x1": full(batch, tok, width),
        "h2_own": low(batch, tok, width),
        "h2_all": low(batch, slot, width),
        "act": full(batch, slot, hid),
        "slope": full(batch, slot, hid),
        "dmix": full(batch, slot, hid),
        "mixed": low(batch * slot, hid),
        "du": low(batch * slot, hid),
        "sums": full(batch, 8, slot),
        "sums_all": full(batch, n, 8, slot),
        "dh2_all": low(batch, slot, width),
        "dh2_got": low(batch, 2, 2, tok, width // 2),
        "dh2_passed": low(batch, 2, tok, width // 2),
        "dh2_last": low(batch, 2, tok, width // 2),
        "grads": low(2, nf, part, width),
        "pair_got": low(2, nf // 4, 2, part, width),
        "w_sems": DMA((2, n, 5)),
        "x_sems": DMA((2, batch, 4)),
        "y_sems": DMA((2, batch, 4)),
        "a_sems": DMA((2, batch, n)),
        "h_sems": DMA((2, batch, 4)),
        "s_sems": DMA((2, batch, n)),
        "r_sems": DMA((2, batch, 2, 3)),
        "p_sems": DMA((2, hid // 256, 128 // part, 2)),
        "hop_sems": DMA((2, 2, 5, nf // 2)),
        "side_sems": DMA((2, 2, 5, nf // 2)),
        "keep_sems": DMA((batch, 3)),
        "own_sems": DMA((22,)),
    }
    return launch(
        lambda r: forward_kernel(n, nf, part, r), "forward", inputs, outputs, scratch, 0, 63
    )


def backward_kernel(n, nf, r):
    me = lax.axis_index("dp")
    f = lax.axis_index("ffn")
    core, row, nz = lax.rem(f, 2), lax.div(f, 2), nf // 2
    even, two_row = lax.rem(row, 2), lax.div(row, 2)
    batch, tok, width = r.dx.shape
    slot = n * tok
    cols = width // n
    rows_each = r.o_out.shape[0]
    pairs = cols // 128
    heads = cols // HDIM
    share = width // n
    step = 256
    peers = dp_peers(n, me)
    pair = {"ffn": f ^ 1}
    everyone = peers + ffn_peers(nf, f)
    greet(everyone)
    band = at(me * tok, tok)
    place = at(me * cols, cols)
    loads = [
        pltpu.make_async_copy(source, target, r.own_sems.at[k])
        for k, (source, target) in enumerate(
            [(r.x1_hbm, r.x1), (r.dh2_hbm, r.dh2), (r.dy_hbm, r.dy), (r.z_hbm, r.z),
             (r.out_hbm, r.wout), (r.a_hbm, r.a), (r.qkv_hbm, r.qkv_all), (r.p_hbm, r.p_all),
             (r.w_hbm, r.w_qkv), (r.h_hbm, r.h_all), (r.x_hbm, r.x), (r.g_hbm.at[:, :, even], r.g_own),
             (r.mixed_hbm, r.mixed), (r.w2_hbm, r.w2)]
        )
    ]
    start(loads)
    r.vec[...] = jnp.zeros_like(r.vec)

    def to_peers(make):
        return [make(i, peer) for i, peer in enumerate(peers, 1)]

    def along(make):
        return [make(j, {"ffn": f ^ (2 * j)}) for j in range(1, nz)]

    def columns_of(side):
        return slice(side * (width // 2), (side + 1) * (width // 2))

    def y_rows(micro):
        def block(owner, side):
            return r.y_all.at[micro, at(owner * tok, tok), columns_of(side)]

        return Reduce(me, block, r.y_got, r.y_passed, r.y_last, r.y_sems, (micro,))

    def dh_rows(micro):
        def block(owner, side):
            return r.dh_all.at[micro, at(owner * tok, tok), columns_of(side)]

        return Reduce(me, block, r.dh_got, r.dh_passed, r.dh_last, r.h_sems, (micro,))

    def go_block(owner, side):
        return r.go_half.at[owner, :, :, columns_of(side)]

    go = Reduce(me, go_block, r.go_got, r.go_passed, r.go_last, r.e_sems, ())

    def g_first(w):
        return send(
            r.g_hbm.at[w, :, 1 - even], r.g_pair.at[w], r.g_sems, (0, w), {"ffn": f ^ 2}
        )

    def g_second(w):
        return [
            send(r.g_mid.at[w, two_row ^ j], r.g_far.at[j - 1, w], r.g_sems, (j, w), {"ffn": f ^ (4 * j)})
            for j in range(1, nz // 2)
        ]

    def g_turn(w):
        g_first(w).wait()
        for k in range(nz // 2):
            total = r.g_own[w, k].astype(F32) + r.g_pair[w, k].astype(F32)
            r.g_mid[w, k] = total.astype(LOW)
        start(g_second(w))

    pair_v = send(r.mid.at[:, 1 - core], r.mid_pair, r.p_sems, (1,), pair)
    wait(loads[:4])
    meet(everyone)
    for w in range(2):
        g_first(w).start()
    pair_v.start()
    for micro in range(batch):
        normed, inverse = normal(r.x1[micro])
        grad = r.dh2[micro]
        r.vec[2:3, :] += column_sum(grad * normed)
        r.vec[8:9, :] += column_sum(grad)
        valid = lax.broadcasted_iota(jnp.int32, (tok, 1), 0) + me * tok < r.lens[micro]
        dy = jnp.where(valid, r.dy[micro].astype(F32), 0.0)
        r.vec[9:10, :] += column_sum(dy)
        grad = dy + normal_back(grad * r.wide[2:3, :], normed, inverse)
        r.dx1[micro] = grad
        normed, inverse = normal(r.z[micro])
        r.vec[1:2, :] += column_sum(grad * normed)
        r.vec[7:8, :] += column_sum(grad)
        low = normal_back(grad * r.wide[1:2, :], normed, inverse).astype(LOW)
        r.vec[6:7, :] += column_sum(low.astype(F32))
        r.dz[micro * tok : (micro + 1) * tok, :] = low
    wait(loads[4:5])
    for d in range(n):
        grad = dot_nt(r.dz[...], r.wout[d].reshape(cols, width))
        lane = lax.broadcasted_iota(jnp.int32, (1, cols), 1) // HDIM
        scales = jnp.zeros((1, cols), F32)
        for head in range(heads):
            scales = jnp.where(lane == head, r.scale[d * heads + head], scales)
        grad = (grad * scales).astype(LOW)
        for micro in range(batch):
            r.do_own[micro, d] = grad[micro * tok : (micro + 1) * tok]

    def head_copies(micro):
        return to_peers(
            lambda i, peer: send(
                r.do_own.at[micro, me ^ i], r.do_all.at[micro, band, :], r.o_sems, (micro, i), peer
            )
        )

    pair_o = send(r.go_all.at[:, 1 - core], r.go_pair, r.p_sems, (0,), pair)
    pair_vec = send(r.vec_sum, r.vec_pair, r.p_sems, (2,), pair)

    def pair_q(d):
        return send(r.gq_all.at[d, 1 - core], r.gq_pair.at[d], r.q_sems, (d,), pair)

    shares = to_peers(
        lambda i, peer: send(r.vec_part.at[me ^ i], r.vec_got.at[i - 1], r.d_sems, (i, 6), peer)
    )
    far_o = along(
        lambda j, peer: send(r.go_sum.at[row ^ j], r.o_far.at[j - 1], r.z_sems, (j, 1), peer)
    )
    def far_q(d):
        return along(
            lambda j, peer: send(
                r.gq_sum.at[d, row ^ j], r.q_far.at[j - 1, d], r.f_sems, (j, d), peer
            )
        )

    def add_pair(d):
        pair_q(d).wait()
        total = r.gq_all[d, core].astype(F32) + r.gq_pair[d].astype(F32)
        r.gq_sum[d] = total.astype(LOW)
        start(far_q(d))

    far_v = along(
        lambda j, peer: send(r.mid_sum.at[row ^ j], r.v_far.at[j - 1], r.z_sems, (j, 3), peer)
    )
    far_vec = along(lambda j, peer: send(r.vec_mine, r.vec_far.at[j - 1], r.z_sems, (j, 4), peer))
    for micro in range(batch):
        start(head_copies(micro))
        r.do_all[micro, band, :] = r.do_own[micro, me]
    wait(loads[12:])

    def out_rows(c, _):
        columns = at(c * step, step)
        weight = r.w2[:, :, columns].reshape(r.mixed.shape[1], step)
        for micro in range(batch):
            value = dot(r.mixed[micro * slot : (micro + 1) * slot, :], weight)
            r.y_all[micro, :, columns] = value.astype(LOW)
        return 0

    lax.fori_loop(0, width // step, out_rows, 0)
    y_rows(0).begin()
    wait(loads[5:6])

    def out_weight(d, _):
        a = r.a[:, :, at(d * cols, cols)].reshape(batch * tok, cols)
        grad = dot_tn(a, r.dz[...]).astype(LOW)
        for k in range(nf):
            r.go_all[d, k % 2, k // 2] = grad[k * rows_each : (k + 1) * rows_each]
        return 0

    lax.fori_loop(0, n, out_weight, 0)
    pair_o.start()
    wait(loads[6:12])
    left = lax.broadcasted_iota(jnp.int32, (1, 128), 1) < HDIM

    def one(micro, _):
        wait(head_copies(micro))

        def pair_of(two, _):
            def column(k):
                return at(k * cols + two * 128, 128)

            head = two * 2
            own_cols = at(two * 128, 128)
            sums = []
            k = r.qkv_all[micro, :, column(1)]
            v = r.qkv_all[micro, :, column(2)]
            for block in range(n):
                end = (block + 1) * tok
                rows = slice(block * tok, end)
                do = r.do_all[micro, rows, own_cols]
                out = []
                for side in range(2):
                    mine = left if side == 0 else jnp.logical_not(left)
                    probs = r.p_all[micro, head + side, rows, :end].astype(F32)
                    dp = dot_nt(jnp.where(mine, do, jnp.zeros_like(do)), v[:end])
                    delta = jnp.sum(probs * dp, axis=-1, keepdims=True)
                    ds = (probs * (dp - delta)).astype(LOW)
                    r.ds_all[side, rows, :end] = ds
                    out.append(dot(ds, k[:end]))
                    sums.append(jnp.sum(delta, axis=0, keepdims=True))
                dq = jnp.where(left, out[0], out[1]) * HDIM ** (-0.5)
                r.dqkv[micro, rows, column(0)] = dq.astype(LOW)
            q = r.qkv_all[micro, :, column(0)]
            do = r.do_all[micro, :, own_cols]
            for block in range(n):
                begin = block * tok
                keys = slice(begin, begin + tok)
                dk = [dot_tn(r.ds_all[side, begin:, keys], q[begin:]) for side in range(2)]
                dv = [
                    dot_tn(r.p_all[micro, head + side, begin:, keys], do[begin:])
                    for side in range(2)
                ]
                dk = jnp.where(left, dk[0], dk[1]) * HDIM ** (-0.5)
                r.dqkv[micro, keys, column(1)] = dk.astype(LOW)
                r.dqkv[micro, keys, column(2)] = jnp.where(left, dv[0], dv[1]).astype(LOW)
            spot = me * heads + head
            first = sum(sums[2::2], sums[0]) * (1.0 / r.scale[spot])
            second = sum(sums[3::2], sums[1]) * (1.0 / r.scale[spot + 1])
            r.vec[10:11, at(me * cols + two * 128, 128)] += jnp.where(left, first, second)

            @pl.when((micro == 0) & (two == 0))
            def _():
                g_turn(0)

            return 0

        lax.fori_loop(0, pairs, pair_of, 0)

        @pl.when(micro == 0)
        def _():
            pair_o.wait()
            for d in range(n):
                total = r.go_all[d, core].astype(F32) + r.go_pair[d].astype(F32)
                r.go_half[d] = total.astype(LOW)
            y_rows(0).turn()
            go.begin()

        @pl.when(micro == 1)
        def _():
            g_turn(1)
            go.turn()
            dh_rows(0).turn()

        def back_rows(d, _):
            total = dot_nt(r.dqkv[micro, :, :cols], r.w_qkv[0, d].reshape(cols, cols))
            for k in (1, 2):
                total = total + dot_nt(
                    r.dqkv[micro, :, k * cols : (k + 1) * cols],
                    r.w_qkv[k, d].reshape(cols, cols),
                )
            r.dh_all[micro, :, at(d * cols, cols)] = total.astype(LOW)
            return 0

        lax.fori_loop(0, n, back_rows, 0)
        dh_rows(micro).begin()
        grads = r.dqkv[micro].astype(F32)
        r.vec[4:5, place] += column_sum(grads[:, :cols])
        r.vec[5:6, place] += column_sum(grads[:, 2 * cols :])
        return 0

    lax.fori_loop(0, batch, one, 0)
    for micro in range(1, batch):
        y_rows(micro).begin()

    def weight_grads(d, _):
        h = r.h_all[:, :, at(d * cols, cols)].reshape(batch * slot, cols)
        grad = dot_tn(h, r.dqkv[...].reshape(batch * slot, 3 * cols)).astype(LOW)
        for k in range(nf):
            r.gq_all[d, k % 2, k // 2] = grad[k * rows_each : (k + 1) * rows_each]
        pair_q(d).start()

        @pl.when(d > 0)
        def _():
            add_pair(d - 1)

        return 0

    lax.fori_loop(0, n, weight_grads, 0)
    add_pair(n - 1)
    r.go_sum[...] = go.finish().astype(LOW)
    start(far_o)
    pair_v.wait()
    for k in range(nz):
        r.mid_sum[k] = r.mid[k, core] + r.mid_pair[k]
    start(far_v)

    for micro in range(1, batch):
        dh_rows(micro).turn()
    for micro in range(batch):
        grad = dh_rows(micro).finish()
        normed, inverse = normal(r.x[micro].astype(F32))
        r.vec[0:1, :] += column_sum(grad * normed)
        r.vec[3:4, :] += column_sum(grad)
        r.dx[micro] = r.dx1[micro] + normal_back(grad * r.wide[0:1, :], normed, inverse)
    spot = lax.broadcasted_iota(jnp.int32, (16, 1), 0)
    own_scales = r.vec[10:11, place]
    for d in range(n):
        block = jnp.where(spot >= 10, 0.0, r.vec[:, d * share : (d + 1) * share])
        r.vec_part[d] = jnp.where(spot == 10 + me, own_scales, block)
    start(shares)
    for micro in range(1, batch):
        y_rows(micro).turn()
    for micro in range(batch):
        total = r.x1[micro] + y_rows(micro).finish() + r.wide[9:10, :]
        r.out[micro] = total.astype(LOW)
    wait(shares)
    total = r.vec_part[me]
    for i in range(1, n):
        total = total + r.vec_got[i - 1]
    r.vec_mine[...] = total
    start(far_vec)
    halves = []
    for w in range(2):
        wait(g_second(w))
        total = r.g_mid[w, two_row].astype(F32)
        for j in range(1, nz // 2):
            total = total + r.g_far[j - 1, w].astype(F32)
        r.g_sum[w] = total.astype(LOW)
        for i, peer in enumerate(peers, 1):
            source = r.g_sum.at[w, :, at((me ^ i) * cols, cols)]
            halves.append(send(source, r.ffn_out.at[w, me], r.d_sems, (i, 4 + w), peer))
    own = [
        pltpu.make_async_copy(r.g_sum.at[w, :, place], r.ffn_out.at[w, me], r.own_sems.at[14 + w])
        for w in range(2)
    ]
    start(halves + own)
    wait(far_o)
    total = r.go_sum[row].astype(F32)
    for j in range(1, nz):
        total = total + r.o_far[j - 1].astype(F32)
    r.o_out[...] = total
    wait(far_v)
    total = r.mid_sum[row]
    for j in range(1, nz):
        total = total + r.v_far[j - 1]
    r.v_out[me] = total
    last = to_peers(
        lambda i, peer: send(r.v_out.at[me], r.v_out.at[me], r.d_sems, (i, 3), peer)
    )
    start(last)
    wait(far_vec)
    total = r.vec_mine[...]
    for j in range(1, nz):
        total = total + r.vec_far[j - 1]
    r.vec_out[...] = total
    r.vec_sum[...] = total
    pair_vec.start()
    for d in range(n):
        wait(far_q(d))
    for d in range(n):
        total = r.gq_sum[d, row].astype(F32)
        for j in range(1, nz):
            total = total + r.q_far[j - 1, d].astype(F32)
        r.q_last[d] = total.astype(LOW)
    more = []
    for i, peer in enumerate(peers, 1):
        for k in range(3):
            source = r.q_last.at[me ^ i, :, k * cols : (k + 1) * cols]
            more.append(send(source, r.q_out.at[k, :, place], r.d_sems, (i, k), peer))
    own += [
        pltpu.make_async_copy(
            r.q_last.at[me, :, k * cols : (k + 1) * cols],
            r.q_out.at[k, :, place],
            r.own_sems.at[16 + k],
        )
        for k in range(3)
    ]
    start(more + own[2:])
    wait(last + more + own + halves + [pair_vec])
    r.vec_out[...] += r.vec_pair[...]


def backward(x, dy, kept, lens, scale, n, nf):
    batch, tok, width = x.shape
    _, _, _, rows, cols = kept["w_hbm"].shape
    part = kept["mid"].shape[3]
    slot, nz = n * tok, nf // 2
    share = width // n
    heads = cols // HDIM

    def low(*dims):
        return pltpu.VMEM(dims, LOW)

    def full(*dims):
        return pltpu.VMEM(dims, F32)

    names = ("x1_hbm", "z_hbm", "dh2_hbm", "a_hbm", "g_hbm", "out_hbm", "w_hbm", "h_hbm")
    names += ("qkv_hbm", "p_hbm", "mixed_hbm", "w2_hbm")
    inputs = {name: (kept[name], ANY) for name in names}
    inputs["x_hbm"] = (x, ANY)
    inputs["dy_hbm"] = (dy, ANY)
    inputs["wide"] = (kept["wide"], VMEM)
    inputs["mid"] = (kept["mid"], VMEM)
    inputs["lens"] = (lens, SMEM)
    inputs["scale"] = (scale, SMEM)
    outputs = {
        "out": (shape((batch, tok, width), LOW), VMEM),
        "dx": (shape((batch, tok, width), F32), VMEM),
        "q_out": (shape((3, rows, width), LOW), VMEM),
        "o_out": (shape((rows, width), F32), VMEM),
        "v_out": (shape((n, 8, part), F32), VMEM),
        "vec_out": (shape((16, share), F32), VMEM),
        "ffn_out": (shape((2, n, part, cols), LOW), VMEM),
    }
    scratch = {
        "x": low(batch, tok, width),
        "dy": low(batch, tok, width),
        "x1": full(batch, tok, width),
        "z": full(batch, tok, width),
        "dh2": full(batch, tok, width),
        "a": low(batch, tok, width),
        "wout": low(n, nf, rows, width),
        "w_qkv": low(3, n, nf, rows, cols),
        "h_all": low(batch, slot, width),
        "qkv_all": low(batch, slot, 3 * cols),
        "p_all": low(batch, heads, slot, slot),
        "mixed": low(*kept["mixed_hbm"].shape),
        "w2": low(*kept["w2_hbm"].shape),
        "y_all": low(batch, slot, width),
        "y_got": low(batch, 2, 2, tok, width // 2),
        "y_passed": low(batch, 2, tok, width // 2),
        "y_last": low(batch, 2, tok, width // 2),
        "dx1": full(batch, tok, width),
        "dz": low(batch * tok, width),
        "do_own": low(batch, n, tok, cols),
        "do_all": low(batch, slot, cols),
        "ds_all": low(2, slot, slot),
        "dqkv": low(batch, slot, 3 * cols),
        "dh_all": low(batch, slot, width),
        "dh_got": low(batch, 2, 2, tok, width // 2),
        "dh_passed": low(batch, 2, tok, width // 2),
        "dh_last": low(batch, 2, tok, width // 2),
        "go_all": low(n, 2, nz, rows, width),
        "go_pair": low(n, nz, rows, width),
        "go_half": low(n, nz, rows, width),
        "go_got": low(2, 2, nz, rows, width // 2),
        "go_passed": low(2, nz, rows, width // 2),
        "go_last": low(2, nz, rows, width // 2),
        "go_sum": low(nz, rows, width),
        "o_far": low(nz - 1, rows, width),
        "gq_all": low(n, 2, nz, rows, 3 * cols),
        "gq_pair": low(n, nz, rows, 3 * cols),
        "gq_sum": low(n, nz, rows, 3 * cols),
        "q_far": low(nz - 1, n, rows, 3 * cols),
        "q_last": low(n, rows, 3 * cols),
        "g_own": low(2, nz // 2, part, width),
        "g_pair": low(2, nz // 2, part, width),
        "g_mid": low(2, nz // 2, part, width),
        "g_far": low(nz // 2 - 1, 2, part, width),
        "g_sum": low(2, part, width),
        "mid_pair": full(nz, 8, part),
        "mid_sum": full(nz, 8, part),
        "v_far": full(nz - 1, 8, part),
        "vec": full(16, width),
        "vec_part": full(n, 16, share),
        "vec_got": full(n - 1, 16, share),
        "vec_mine": full(16, share),
        "vec_far": full(nz - 1, 16, share),
        "vec_sum": full(16, share),
        "vec_pair": full(16, share),
        "o_sems": DMA((2, batch, n)),
        "h_sems": DMA((2, batch, 2, 3)),
        "y_sems": DMA((2, batch, 2, 3)),
        "p_sems": DMA((2, 3)),
        "q_sems": DMA((2, n)),
        "e_sems": DMA((2, 2, 3)),
        "g_sems": DMA((2, nz // 2, 2)),
        "z_sems": DMA((2, nz, 5)),
        "f_sems": DMA((2, nz, n)),
        "d_sems": DMA((2, n, 7)),
        "own_sems": DMA((19,)),
    }
    return launch(
        lambda r: backward_kernel(n, nf, r), "backward", inputs, outputs, scratch, 1, 60
    )


def finish_kernel(n, nf, r):
    f = lax.axis_index("ffn")
    rows_each = r.gains.shape[1]
    part = r.mid.shape[2]
    cols, hid = r.w_in.shape
    r.out_to[...] = r.out[...]
    r.dx_to[...] = r.dx[...]
    r.q_to[...] = r.q_out[...].astype(F32)
    r.o_to[...] = r.o_out[...]
    r.w_in[...] = r.ffn[0].reshape(hid, cols).astype(F32).T
    r.w_out[...] = r.ffn[1].reshape(hid, cols).astype(F32)
    own = jnp.zeros((16, rows_each), F32)
    for k in range(nf):
        own = own + jnp.where(f == k, r.vec[:, k * rows_each : (k + 1) * rows_each], 0.0)
    r.gains[...] = own[:3]
    r.biases[...] = own[3:10]
    heads = r.heads.shape[1]
    lane = lax.broadcasted_iota(jnp.int32, (1, heads), 1)
    total = jnp.zeros((1, heads), F32)
    for head in range(heads):
        d, c = divmod(head, heads // n)
        value = r.vec[10 + d : 11 + d, c * HDIM : c * HDIM + 1]
        total = total + jnp.where(lane == head, value, 0.0)
    r.heads[...] = total
    for k, target in enumerate((r.mid_0, r.mid_1, r.mid_2)):
        for d in range(n):
            target[:, d * part : (d + 1) * part] = r.mid[d, k : k + 1]


def finish(done, heads, n, nf):
    out, dx, q_out, o_out = [done[name] for name in ("out", "dx", "q_out", "o_out")]
    vec, mid, ffn = done["vec_out"], done["v_out"], done["ffn_out"]
    _, _, part, cols = ffn.shape
    rows = o_out.shape[0]
    hid = n * part
    inputs = dict(out=out, dx=dx, q_out=q_out, o_out=o_out, vec=vec, mid=mid, ffn=ffn)
    outputs = dict(
        out_to=shape(out.shape, LOW),
        dx_to=shape(dx.shape, F32),
        q_to=shape(q_out.shape, F32),
        o_to=shape(o_out.shape, F32),
        heads=shape((1, heads), F32),
        gains=shape((3, rows), F32),
        biases=shape((7, rows), F32),
        w_in=shape((cols, hid), F32),
        mid_0=shape((1, hid), F32),
        mid_1=shape((1, hid), F32),
        mid_2=shape((1, hid), F32),
        w_out=shape((hid, cols), F32),
    )
    names = [*inputs, *outputs]
    return pl.pallas_call(
        lambda *refs: finish_kernel(n, nf, SimpleNamespace(**dict(zip(names, refs)))),
        name="finish",
        out_shape=tuple(outputs.values()),
        in_specs=[VMEM] * len(inputs),
        out_specs=(VMEM,) * len(outputs),
        compiler_params=pltpu.CompilerParams(vmem_limit_bytes=62 << 20),
    )(*inputs.values())


def on_device(
    tokens,
    seq_lens,
    qkv_weight,
    out_weight,
    head_scale,
    gains,
    biases,
    ffn_in,
    ffn_bias,
    mid_gain,
    mid_bias,
    ffn_out,
    out_cotangent,
):
    n = lax.axis_size("dp")
    nf = lax.axis_size("ffn")
    me = lax.axis_index("dp")
    batch, _, tok, width = tokens.shape
    heads = head_scale.shape[0]
    cols = width // n
    rows = qkv_weight.shape[1]
    hid = ffn_in.shape[1]
    part = hid // n

    vectors = lax.dynamic_index_in_dim(
        jnp.stack([ffn_bias, mid_gain, mid_bias]).reshape(3, n, part), me, 1, keepdims=False
    )
    x, dy = tokens[:, 0], out_cotangent[:, 0]
    lens = seq_lens.reshape(-1)
    kept = forward(
        x,
        qkv_weight,
        out_weight,
        (gains, biases, vectors),
        ffn_in,
        ffn_out.reshape(n, part, cols),
        dy,
        lens,
        head_scale,
        n,
        nf,
    )
    done = backward(x, dy, kept, lens, head_scale, n, nf)
    out, dx, q_grad, o_grad, head_grad, gain_grad, bias_grad, in_grad, *mids, last_grad = finish(
        done, heads, n, nf
    )
    return (
        out[:, None],
        dx[:, None],
        q_grad,
        o_grad,
        head_grad.reshape(heads),
        gain_grad,
        bias_grad,
        in_grad,
        *[mid.reshape(hid) for mid in mids],
        last_grad,
    )


def solution(mesh):
    seqs = P(None, "ffn", "dp", None)
    wide = P(None, ("dp", "ffn"))
    hidden = P("ffn")
    return jax.shard_map(
        on_device,
        mesh=mesh,
        in_specs=(
            seqs,
            P(None, "ffn"),
            P(None, ("dp", "ffn"), None),
            P(("dp", "ffn"), None),
            P(),
            wide,
            wide,
            P("dp", "ffn"),
            hidden,
            hidden,
            hidden,
            P("ffn", "dp"),
            seqs,
        ),
        out_specs=(
            seqs,
            seqs,
            P(None, ("dp", "ffn"), None),
            P(("dp", "ffn"), None),
            P(),
            wide,
            wide,
            P("dp", "ffn"),
            hidden,
            hidden,
            hidden,
            P("ffn", "dp"),
        ),
        check_vma=False,
    )
```

```python
from types import SimpleNamespace

import jax
import jax.numpy as jnp
from jax import lax
from jax.experimental import pallas as pl
from jax.experimental.pallas import tpu as pltpu
from jax.sharding import PartitionSpec as P

HDIM = 64
EPS = 1e-05
LOW = jnp.bfloat16
F32 = jnp.float32
ANY = pl.BlockSpec(memory_space=pl.ANY)
VMEM = pl.BlockSpec(memory_space=pltpu.VMEM)
SMEM = pl.BlockSpec(memory_space=pltpu.SMEM)
MESH = pl.DeviceIdType.MESH
DMA = pltpu.SemaphoreType.DMA


def dot(left, right):
    return jnp.dot(left, right, preferred_element_type=F32)


def dot_nt(left, right):
    return lax.dot_general(left, right, (((1,), (1,)), ((), ())), preferred_element_type=F32)


def dot_tn(left, right):
    return lax.dot_general(left, right, (((0,), (0,)), ((), ())), preferred_element_type=F32)


def shape(dims, kind):
    return jax.ShapeDtypeStruct(tuple(dims), kind)


def at(start, size, unit=128):
    return pl.ds(pl.multiple_of(start, unit), size)


def send(src, dst, sems, index, where):
    return pltpu.make_async_remote_copy(
        src_ref=src,
        dst_ref=dst,
        send_sem=sems.at[(0, *index)],
        recv_sem=sems.at[(1, *index)],
        device_id=where,
        device_id_type=MESH,
    )


def greet(peers):
    barrier = pltpu.get_barrier_semaphore()
    for peer in peers:
        pl.semaphore_signal(barrier, inc=1, device_id=peer, device_id_type=MESH)


def meet(peers):
    pl.semaphore_wait(pltpu.get_barrier_semaphore(), len(peers))


def dp_peers(n, me):
    return [{"dp": me ^ i} for i in range(1, n)]


def ffn_peers(nf, f):
    return [{"ffn": f ^ (2 * j)} for j in range(1, nf // 2)] + [{"ffn": f ^ 1}]


def start(copies):
    for copy in copies:
        copy.start()


def wait(copies):
    for copy in copies:
        copy.wait()


class Line:
    def __init__(self, nf, f, items, hop_sems, side_sems):
        self.nz, self.core, self.q, self.f = nf // 2, lax.rem(f, 2), lax.div(f, 2), f
        self.items, self.hop_sems, self.side_sems = items, hop_sems, side_sems
        self.next = [1] * len(items)

    def copy(self, sems, k, t, came, way, first, target):
        source, place = self.items[k]
        index = self.f if first else 2 * (self.q - t * way) + self.core
        spot = place(index)
        side = 0 if way > 0 else 1
        return pltpu.make_async_remote_copy(
            src_ref=source if first else spot,
            dst_ref=spot,
            send_sem=sems.at[0, side, k, t],
            recv_sem=sems.at[1, side, k, came],
            device_id={"ffn": target},
            device_id_type=MESH,
        )

    def hop(self, k, t, way, first=False):
        return self.copy(self.hop_sems, k, t, t + 1, way, first, self.f + 2 * way)

    def arrival(self, k, t, way):
        return self.copy(self.hop_sems, k, t, t, way, False, self.f + 2 * way)

    def over(self, k, t, way, first=False):
        return self.copy(self.side_sems, k, t, t, way, first, self.f ^ 1)

    def onward(self, way):
        return self.q < self.nz - 1 if way > 0 else self.q > 0

    def has(self, t, way):
        return self.q - t >= 0 if way > 0 else self.q + t <= self.nz - 1

    def begin(self, *items):
        for k in items:
            for way in (1, -1):

                @pl.when(self.onward(way))
                def _():
                    self.hop(k, 0, way, True).start()

        for k in items:
            self.over(k, 0, 1, True).start()

    def step(self, k, t):
        for way in (1, -1):

            @pl.when(self.has(t, way) & self.onward(way))
            def _():
                self.arrival(k, t, way).wait_recv()
                self.hop(k, t, way).start()

        for way in (1, -1):

            @pl.when(self.has(t, way))
            def _():
                @pl.when(jnp.logical_not(self.onward(way)))
                def _():
                    self.arrival(k, t, way).wait_recv()

                self.over(k, t, way).start()

    def advance(self, *items):
        for k in items:
            if self.next[k] < self.nz:
                self.step(k, self.next[k])
                self.next[k] += 1

    def arrive(self, *items):
        begin = self.next[items[0]]

        def rest(t, _):
            for k in items:
                self.step(k, t)
            return 0

        lax.fori_loop(begin, self.nz, rest, 0)

        def close(t, _):
            for k in items:
                for way in (1, -1):

                    @pl.when(self.has(t, way))
                    def _():
                        self.over(k, t, way).wait_recv()

            return 0

        for k in items:
            self.over(k, 0, 1, True).wait_recv()
        lax.fori_loop(1, self.nz, close, 0)

    def finish(self, *items):
        for k in items:
            self.over(k, 0, 1, True).wait_send()
            for way in (1, -1):

                @pl.when(self.onward(way))
                def _():
                    self.hop(k, 0, way, True).wait_send()

        def close(t, _):
            for k in items:
                for way in (1, -1):

                    @pl.when(self.has(t, way))
                    def _():
                        self.over(k, t, way).wait_send()

                    @pl.when(self.has(t, way) & self.onward(way))
                    def _():
                        self.hop(k, t, way).wait_send()

            return 0

        lax.fori_loop(1, self.nz, close, 0)


def line_meet(n, nf, me, f):
    barrier = pltpu.get_barrier_semaphore()
    q, nz = lax.div(f, 2), nf // 2
    greet(dp_peers(n, me) + [{"ffn": f ^ 1}])

    @pl.when(q < nz - 1)
    def _():
        greet([{"ffn": f + 2}])

    @pl.when(q > 0)
    def _():
        greet([{"ffn": f - 2}])

    count = n + jnp.where(q < nz - 1, 1, 0) + jnp.where(q > 0, 1, 0)
    pl.semaphore_wait(barrier, count)


class Gather:
    def __init__(self, me, source, place, size, sems, index):
        self.me, self.source, self.place, self.half = me, source, place, size // 2
        self.sems, self.index = sems, index

    def straight(self, k):
        spot = self.place(self.me, 0, 2 * self.half)
        return send(self.source, spot, self.sems, (*self.index, k), {"dp": self.me ^ (k + 1)})

    def relay(self, k):
        spot = self.place(self.me ^ (k + 1), k * self.half, self.half)
        return send(spot, spot, self.sems, (*self.index, 2 + k), {"dp": self.me ^ (2 - k)})

    def begin(self):
        for k in range(2):
            self.straight(k).start()

    def turn(self):
        for k in range(2):
            self.straight(k).wait()
            self.relay(k).start()

    def finish(self):
        for k in range(2):
            self.relay(k).wait()


class Reduce:
    def __init__(self, me, block, got, passed, last, sems, index):
        self.me, self.block, self.passed = me, block, passed
        self.got, self.last, self.sems, self.index = got, last, sems, index

    def first(self, side, far):
        step = side + 1
        owner = self.me ^ (3 if far else step)
        target = self.got.at[(*self.index, side, far)]
        spot = (*self.index, side, far)
        return send(self.block(owner, side), target, self.sems, spot, {"dp": self.me ^ step})

    def second(self, side):
        where = (*self.index, side)
        target = {"dp": self.me ^ (2 - side)}
        return send(self.passed.at[where], self.last.at[where], self.sems, (*where, 2), target)

    def begin(self):
        for far in (1, 0):
            for side in range(2):
                self.first(side, far).start()

    def turn(self):
        for side in range(2):
            self.first(side, 1).wait()
            total = self.block(self.me ^ (2 - side), side)[...].astype(F32)
            total = total + self.got[(*self.index, side, 1)].astype(F32)
            self.passed[(*self.index, side)] = total.astype(LOW)
            self.second(side).start()

    def finish(self):
        halves = []
        for side in range(2):
            self.first(side, 0).wait()
            self.second(side).wait()
            total = self.block(self.me, side)[...].astype(F32)
            total = total + self.got[(*self.index, side, 0)].astype(F32)
            halves.append(total + self.last[(*self.index, side)].astype(F32))
        return jnp.concatenate(halves, axis=-1)


def normal(values):
    center = values - jnp.mean(values, axis=-1, keepdims=True)
    inverse = lax.rsqrt(jnp.mean(center * center, axis=-1, keepdims=True) + EPS)
    return center * inverse, inverse


def normal_back(grad, normed, inverse):
    return inverse * (
        grad
        - jnp.mean(grad, axis=-1, keepdims=True)
        - normed * jnp.mean(grad * normed, axis=-1, keepdims=True)
    )


def column_sum(values):
    return jnp.sum(values, axis=0, keepdims=True)


def launch(body, name, inputs, outputs, scratch, number, limit):
    names = [*inputs, *outputs, *scratch]
    results = pl.pallas_call(
        lambda *refs: body(SimpleNamespace(**dict(zip(names, refs)))),
        name=name,
        out_shape=tuple(kind for kind, _ in outputs.values()),
        in_specs=[spec for _, spec in inputs.values()],
        out_specs=tuple(spec for _, spec in outputs.values()),
        scratch_shapes=list(scratch.values()),
        compiler_params=pltpu.CompilerParams(
            collective_id=number, has_side_effects=True, vmem_limit_bytes=limit << 20
        ),
    )(*[value for value, _ in inputs.values()])
    return dict(zip(outputs, results))


def forward_kernel(n, nf, part, r):
    me = lax.axis_index("dp")
    f = lax.axis_index("ffn")
    core, nz = lax.rem(f, 2), nf // 2
    batch, tok, width = r.x.shape
    rows_each = r.wout.shape[0]
    cols = width // n
    pairs = cols // 128
    slot = n * tok
    hid = nf * part
    ff = n * hid
    step = 256
    peers = dp_peers(n, me)
    pair = {"ffn": f ^ 1}
    place = at(me * cols, cols)
    band = at(me * tok, tok)

    own = [
        pltpu.make_async_copy(r.qkv.at[:, :, place], r.stage.at[:, me], r.own_sems.at[0]),
        pltpu.make_async_copy(r.small.at[0], r.small_stage.at[me], r.own_sems.at[1]),
        pltpu.make_async_copy(r.small.at[1], r.small_stage.at[n], r.own_sems.at[2]),
        pltpu.make_async_copy(r.wout, r.out_stage.at[me], r.own_sems.at[3]),
        pltpu.make_async_copy(r.first, r.first_in, r.own_sems.at[4]),
        pltpu.make_async_copy(r.second.at[me], r.second_stage.at[:, place], r.own_sems.at[5]),
        pltpu.make_async_copy(r.x, r.x_all.at[me], r.own_sems.at[6]),
        pltpu.make_async_copy(r.dy, r.dy_all.at[:, band, :], r.own_sems.at[7]),
    ]
    start(own[:1] + own[3:])
    line_meet(n, nf, me, f)

    def to_peers(make):
        return [make(i, peer) for i, peer in enumerate(peers, 1)]

    blocks = to_peers(
        lambda i, peer: send(
            r.qkv.at[:, :, at((me ^ i) * cols, cols)], r.stage.at[:, me], r.w_sems, (i, 0), peer
        )
    )
    smalls = to_peers(
        lambda i, peer: send(r.small.at[0], r.small_stage.at[me], r.w_sems, (i, 1), peer)
    )
    outs = to_peers(lambda i, peer: send(r.wout, r.out_stage.at[me], r.w_sems, (i, 2), peer))
    firsts = to_peers(
        lambda i, peer: send(
            r.first_all.at[me ^ i], r.first_stage.at[:, place], r.w_sems, (i, 3), peer
        )
    )
    seconds = to_peers(
        lambda i, peer: send(
            r.second.at[me ^ i], r.second_stage.at[:, place], r.w_sems, (i, 4), peer
        )
    )

    def x_rows(micro):
        def spot(owner, start, size):
            return r.x_all.at[owner, micro, start : start + size]

        return Gather(me, r.x.at[micro], spot, tok, r.x_sems, (micro,))

    def y_rows(micro):
        def spot(owner, start, size):
            return r.dy_all.at[micro, at(owner * tok + start, size, 64), :]

        return Gather(me, r.dy.at[micro], spot, tok, r.y_sems, (micro,))

    start(blocks)
    size = r.gains.shape[1]
    lanes = lax.broadcasted_iota(jnp.int32, (16, 128), 1)
    r.tile[...] = jnp.zeros_like(r.tile)
    for k in range(128 // size):
        r.tile[0, 0:3, k * size : (k + 1) * size] = r.gains[...].astype(F32)
        r.tile[0, 3:10, k * size : (k + 1) * size] = r.biases[...].astype(F32)
    for k in range(128 // part):
        r.tile[1, 0:3, k * part : (k + 1) * part] = r.hidden[...].astype(F32)
    for k, each_ in enumerate((size, part)):
        mine_ = lanes // each_ == lax.rem(f, 128 // each_)
        r.small[k] = jnp.where(mine_, r.tile[k], 0.0).astype(LOW)
    start(own[1:3] + smalls)
    x_rows(0).begin()
    wait(own[4:5])
    r.first_all[...] = r.first_in[...].T.reshape(r.first_all.shape)
    own[4] = pltpu.make_async_copy(
        r.first_all.at[me], r.first_stage.at[:, place], r.own_sems.at[4]
    )
    start(own[4:5])
    start(outs + firsts)
    line = Line(
        nf,
        f,
        [
            (r.stage, lambda index: r.w_all.at[:, :, index]),
            (r.small_stage, lambda index: r.small_all.at[index]),
            (r.out_stage, lambda index: r.out_all.at[:, index]),
            (r.first_stage, lambda index: r.w1.at[index]),
            (r.second_stage, lambda index: r.w2.at[index]),
        ],
        r.hop_sems,
        r.side_sems,
    )
    mine = [
        pltpu.make_async_copy(source, spot(f), r.own_sems.at[8 + k])
        for k, (source, spot) in enumerate(line.items)
    ]
    wait(blocks + smalls + own[:3])
    line.begin(0, 1)
    start(mine[:2])
    line.advance(0, 1)
    x_rows(0).turn()
    x_rows(1).begin()
    line.advance(0, 1)
    wait(outs + own[3:4])
    line.begin(2)
    start(mine[2:3])
    line.arrive(0, 1)
    wait(firsts + own[4:5])
    line.begin(3)
    start(mine[3:4])
    wait(mine[:2] + own[6:7])

    def lay_out(out_ref, index, begin, size):
        together = 128 // size
        for b in range(nf // together):
            total = r.small_all[b * together, index].astype(F32)
            for k in range(1, together):
                total = total + r.small_all[b * together + k, index].astype(F32)
            out_ref[:, begin + b * 128 : begin + (b + 1) * 128] = total

    for d in range(n):
        lay_out(r.wide, d, d * nf * rows_each, rows_each)
    lay_out(r.mids, n, 0, part)

    gain, shift = r.wide[0:1, :], r.wide[3:4, :]
    bias_q, bias_v = r.wide[4:5, place], r.wide[5:6, place]
    left = lax.broadcasted_iota(jnp.int32, (1, 128), 1) < HDIM

    def block_copies(micro):
        return to_peers(
            lambda i, peer: send(
                r.a_all.at[micro, me ^ i], r.a_own.at[micro, :, place], r.a_sems, (micro, i), peer
            )
        )

    def keep_copies(micro):
        return [
            pltpu.make_async_copy(source.at[micro], out.at[micro], r.keep_sems.at[micro, k])
            for k, (source, out) in enumerate(
                [(r.h_all, r.h_hbm), (r.qkv_all, r.qkv_hbm), (r.p_all, r.p_hbm)]
            )
        ]

    def after_first():
        line.advance(2)
        x_rows(1).turn()
        start(seconds)
        y_rows(0).begin()

    def after_second():
        line.advance(3)

    def after_third():
        line.advance(2)
        wait(seconds + own[5:6])
        line.begin(4)
        start(mine[4:5])

    def after_last():
        y_rows(0).turn()
        y_rows(1).begin()
        line.advance(3)

    def attend(index, _):
        micro, two = lax.div(index, pairs), lax.rem(index, pairs)

        @pl.when(two == 0)
        def _():
            x_rows(micro).finish()

            def norm_rows(d, _):
                values, _ = normal(r.x_all[d, micro].astype(F32))
                r.h_all[micro, at(d * tok, tok), :] = (values * gain + shift).astype(LOW)
                return 0

            lax.fori_loop(0, n, norm_rows, 0)
            for k, bias in enumerate((bias_q, None, bias_v)):
                weight = r.w_all[k].reshape(width, cols)
                value = dot(r.h_all[micro], weight)
                if bias is not None:
                    value = value + bias
                r.qkv_all[micro, :, k * cols : (k + 1) * cols] = value.astype(LOW)

        length = r.lens[micro]

        def column(k):
            return at(k * cols + two * 128, 128)

        head = two * 2
        scales = jnp.where(
            left, r.scale[me * 2 * pairs + head], r.scale[me * 2 * pairs + head + 1]
        )
        for block in range(n):
            end = (block + 1) * tok
            q = r.qkv_all[micro, block * tok : end, column(0)] * HDIM ** (-0.5)
            k = r.qkv_all[micro, :end, column(1)]
            v = r.qkv_all[micro, :end, column(2)]
            key = lax.broadcasted_iota(jnp.int32, (tok, end), 1)
            query = lax.broadcasted_iota(jnp.int32, (tok, end), 0) + block * tok
            mask = (key <= query) & (key < length)
            out = []
            for side in range(2):
                mine_ = left if side == 0 else jnp.logical_not(left)
                scores = dot_nt(jnp.where(mine_, q, jnp.zeros_like(q)), k)
                scores = jnp.where(mask, scores, -1e30)
                expo = jnp.exp(scores - jnp.max(scores, axis=-1, keepdims=True))
                probs = expo * (1.0 / jnp.sum(expo, axis=-1, keepdims=True))
                probs = probs.astype(LOW)
                r.p_all[micro, head + side, block * tok : end, :end] = probs
                out.append(dot(probs, v))
            joined = jnp.where(left, out[0], out[1]) * scales
            r.a_all[micro, block, :, at(two * 128, 128)] = joined.astype(LOW)

        @pl.when(two == pairs - 1)
        def _():
            start(block_copies(micro))
            start(keep_copies(micro))
            r.a_own[micro, :, place] = r.a_all[micro, me]

        work = [after_first, after_second, after_third, after_last]
        for k, act in enumerate(work[: batch * pairs]):
            pl.when(index == k)(act)
        return 0

    lax.fori_loop(0, batch * pairs, attend, 0)

    line.arrive(2)
    wait(mine[2:3])
    late = [
        pltpu.make_async_copy(source, target, r.own_sems.at[13 + k])
        for k, (source, target) in enumerate(
            [(r.w_all, r.w_hbm), (r.out_all, r.out_hbm), (r.z, r.z_hbm), (r.x1, r.x1_hbm),
             (r.a_own, r.a_hbm), (r.mixed, r.mixed_hbm), (r.pair_got, r.g_hbm), (r.dh2, r.dh2_hbm),
             (r.w2, r.w2_hbm)]
        )
    ]
    start(late[:2])

    def h2_rows(micro):
        def spot(owner, start, size):
            return r.h2_all.at[micro, at(owner * tok + start, size, 64), :]

        return Gather(me, r.h2_own.at[micro], spot, tok, r.h_sems, (micro,))

    for micro in range(batch):
        wait(block_copies(micro))
        z = dot(r.a_own[micro], r.out_all[...].reshape(width, width)) + r.wide[6:7, :]
        r.z[micro] = z
        values, _ = normal(z)
        x1 = r.x_all[me, micro].astype(F32) + values * r.wide[1:2, :] + r.wide[7:8, :]
        r.x1[micro] = x1
        values, _ = normal(x1)
        r.h2_own[micro] = (values * r.wide[2:3, :] + r.wide[8:9, :]).astype(LOW)
        h2_rows(micro).begin()
        r.h2_all[micro, band, :] = r.h2_own[micro]
    start(late[2:5])
    line.advance(4)
    h2_rows(0).turn()
    y_rows(1).turn()
    for micro in range(1, batch):
        h2_rows(micro).turn()
    line.arrive(3)
    wait(mine[3:4])

    def weights(ref, c):
        count = step // part
        return ref[pl.ds(c * count, count)].reshape(step, width)

    def w_columns(ref, columns):
        return ref[:, :, columns].reshape(hid, step)

    def sum_copies(micro):
        return to_peers(
            lambda i, peer: send(
                r.sums.at[micro], r.sums_all.at[micro, me], r.s_sems, (micro, i), peer
            )
        )

    def dh2_rows(micro):
        def block(owner, side):
            columns = slice(side * (width // 2), (side + 1) * (width // 2))
            return r.dh2_all.at[micro, at(owner * tok, tok), columns]

        return Reduce(me, block, r.dh2_got, r.dh2_passed, r.dh2_last, r.r_sems, (micro,))

    def fold(values):
        total = values[:, :128]
        for k in range(1, step // 128):
            total = total + values[:, k * 128 : (k + 1) * 128]
        return total

    def units(micro):
        h2_rows(micro).finish()

        def chunk(c, totals):
            rows = at(c * step, step)
            u = dot_nt(r.h2_all[micro], weights(r.w1, c)) + r.mids[0:1, rows]
            phi = 0.5 + 0.5 * lax.erf(u * (0.5**0.5))
            value = u * phi
            r.act[micro, :, rows] = value
            r.slope[micro, :, rows] = phi + u * jnp.exp(u * u * -0.5) * 0.3989422804014327
            return totals[0] + fold(value), totals[1] + fold(value * value)

        zero = jnp.zeros((slot, 128), F32)
        totals = lax.fori_loop(0, hid // step, chunk, (zero,) * 2)
        for k in range(2):
            r.sums[micro, k : k + 1, :] = column_sum(totals[k].T)

    def cotangents(micro):
        y_rows(micro).finish()
        valid = lax.broadcasted_iota(jnp.int32, (slot, 1), 0) < r.lens[micro]
        rows = r.dy_all[micro]
        r.dy_all[micro] = jnp.where(valid, rows, jnp.zeros_like(rows))

        def chunk(c, totals):
            rows = at(c * step, step)
            dm = dot_nt(r.dy_all[micro], weights(r.w2, c))
            r.dmix[micro, :, rows] = dm
            dn = dm * r.mids[1:2, rows]
            return totals[0] + fold(dn), totals[1] + fold(dn * r.act[micro, :, rows])

        zero = jnp.zeros((slot, 128), F32)
        totals = lax.fori_loop(0, hid // step, chunk, (zero,) * 2)
        for k in range(2):
            r.sums[micro, 2 + k : 3 + k, :] = column_sum(totals[k].T)
        r.sums[micro, 4:8, :] = jnp.zeros((4, slot), F32)
        start(sum_copies(micro))

    r.vec[...] = jnp.zeros_like(r.vec)

    def second_pass(micro, _):
        wait(sum_copies(micro))
        r.sums_all[micro, me] = r.sums[micro]
        total = r.sums_all[micro, 0]
        for d in range(1, n):
            total = total + r.sums_all[micro, d]
        total = total * (1.0 / ff)
        mean = total[0:1]
        inverse = lax.rsqrt(total[1:2] - mean * mean + EPS)
        back = total[2:3]
        cross = inverse * (total[3:4] - mean * back)
        table = jnp.concatenate([mean, inverse, back, cross] * 32, axis=0).T
        mean, inverse, back, cross = [table[:, k : k + 1] for k in range(4)]
        rows_of = at(micro * slot, slot)

        def chunk(c, _):
            rows = at(c * step, step)
            normed = (r.act[micro, :, rows] - mean) * inverse
            dm = r.dmix[micro, :, rows]
            gain = r.mids[1:2, rows]
            r.mixed[rows_of, rows] = (normed * gain + r.mids[2:3, rows]).astype(LOW)
            df = inverse * (dm * gain - back - normed * cross)
            low = (df * r.slope[micro, :, rows]).astype(LOW)
            r.du[rows_of, rows] = low
            r.vec[0:1, rows] += column_sum(low.astype(F32))
            r.vec[1:2, rows] += column_sum(dm * normed)
            r.vec[2:3, rows] += column_sum(dm)
            return 0

        lax.fori_loop(0, hid // step, chunk, 0)

        def back_rows(c, _):
            columns = at(c * step, step)
            value = dot(r.du[rows_of, :], w_columns(r.w1, columns))
            r.dh2_all[micro, :, columns] = value.astype(LOW)
            return 0

        lax.fori_loop(0, width // step, back_rows, 0)
        dh2_rows(micro).begin()
        return 0

    def passes(micro, _):
        units(micro)

        @pl.when(micro == 0)
        def _():
            line.arrive(4)
            wait(mine[4:5] + own[7:8])

        cotangents(micro)

        @pl.when(micro > 0)
        def _():
            dh2_rows(micro - 1).turn()

        second_pass(micro, 0)
        return 0

    lax.fori_loop(0, batch, passes, 0)
    start(late[5:6] + late[8:])
    each = step // part // 2

    def halved(index):
        return lax.div(index, 2), lax.rem(index, 2)

    def pair_copies(c):
        copies = []
        for k in range(each):
            index = c * (2 * each) + 2 * k
            for w in range(2):
                copies.append(
                    send(
                        r.grads.at[w, index + 1 - core],
                        r.pair_got.at[(w, *halved(c * each + k))],
                        r.p_sems,
                        (c, k, w),
                        pair,
                    )
                )
        return copies

    def weight_grads(c, _):
        rows = at(c * step, step)
        h2 = r.h2_all[...].reshape(batch * slot, width)
        dy = r.dy_all[...].reshape(batch * slot, width)
        first = dot_tn(r.du[:, rows], h2).astype(LOW)
        second = dot_tn(r.mixed[:, rows], dy).astype(LOW)
        for k in range(step // part):
            r.grads[0, c * (step // part) + k] = first[k * part : (k + 1) * part]
            r.grads[1, c * (step // part) + k] = second[k * part : (k + 1) * part]
        start(pair_copies(c))
        return 0

    lax.fori_loop(0, hid // step, weight_grads, 0)
    dh2_rows(batch - 1).turn()

    def pair_sum(c, _):
        wait(pair_copies(c))
        for k in range(each):
            for w in range(2):
                total = r.grads[w, c * (2 * each) + 2 * k + core].astype(F32)
                spot = (w, *halved(c * each + k))
                total = total + r.pair_got[spot].astype(F32)
                r.pair_got[spot] = total.astype(LOW)
        return 0

    lax.fori_loop(0, hid // step, pair_sum, 0)
    start(late[6:7])
    for k in range(nf):
        r.mid[k // 2, k % 2] = r.vec[:, k * part : (k + 1) * part]
    line.finish(0, 1, 2, 3, 4)
    for micro in range(batch):
        wait(keep_copies(micro))
    for micro in range(batch):
        r.dh2[micro] = dh2_rows(micro).finish()
    start(late[7:8])
    wait(late)


def forward(x, qkv, wout, small, first, second, dy, lens, scale, n, nf):
    batch, tok, width = x.shape
    rows = wout.shape[0]
    part = second.shape[1]
    cols = width // n
    slot, hid = n * tok, nf * part
    heads = cols // HDIM

    def low(*dims):
        return pltpu.VMEM(dims, LOW)

    def full(*dims):
        return pltpu.VMEM(dims, F32)

    inputs = {
        name: (value, ANY)
        for name, value in zip(
            ("x", "qkv", "wout", "first", "second", "dy"),
            (x, qkv, wout, first, second, dy),
        )
    }
    for name, value in zip(("gains", "biases", "hidden"), small):
        inputs[name] = (value, VMEM)
    inputs["lens"] = (lens, SMEM)
    inputs["scale"] = (scale, SMEM)
    outputs = {
        "wide": (shape((16, width), F32), VMEM),
        "w_hbm": (shape((3, n, nf, rows, cols), LOW), ANY),
        "out_hbm": (shape((n, nf, rows, width), LOW), ANY),
        "h_hbm": (shape((batch, slot, width), LOW), ANY),
        "qkv_hbm": (shape((batch, slot, 3 * cols), LOW), ANY),
        "p_hbm": (shape((batch, heads, slot, slot), LOW), ANY),
        "a_hbm": (shape((batch, tok, width), LOW), ANY),
        "z_hbm": (shape((batch, tok, width), F32), ANY),
        "x1_hbm": (shape((batch, tok, width), F32), ANY),
        "mixed_hbm": (shape((batch * slot, hid), LOW), ANY),
        "w2_hbm": (shape((nf, part, width), LOW), ANY),
        "g_hbm": (shape((2, nf // 4, 2, part, width), LOW), ANY),
        "dh2_hbm": (shape((batch, tok, width), F32), ANY),
        "mid": (shape((nf // 2, 2, 8, part), F32), VMEM),
    }
    scratch = {
        "mids": full(16, hid),
        "dh2": full(batch, tok, width),
        "vec": full(8, hid),
        "stage": low(3, n, rows, cols),
        "tile": full(2, 16, 128),
        "small": low(2, 16, 128),
        "small_stage": low(n + 1, 16, 128),
        "out_stage": low(n, rows, width),
        "first_in": low(*first.shape),
        "first_all": low(*second.shape),
        "first_stage": low(part, width),
        "second_stage": low(part, width),
        "small_all": low(nf, n + 1, 16, 128),
        "w_all": low(3, n, nf, rows, cols),
        "out_all": low(n, nf, rows, width),
        "w1": low(nf, part, width),
        "w2": low(nf, part, width),
        "x_all": low(n, batch, tok, width),
        "dy_all": low(batch, slot, width),
        "h_all": low(batch, slot, width),
        "qkv_all": low(batch, slot, 3 * cols),
        "p_all": low(batch, heads, slot, slot),
        "a_all": low(batch, n, tok, cols),
        "a_own": low(batch, tok, width),
        "z": full(batch, tok, width),
        "x1": full(batch, tok, width),
        "h2_own": low(batch, tok, width),
        "h2_all": low(batch, slot, width),
        "act": full(batch, slot, hid),
        "slope": full(batch, slot, hid),
        "dmix": full(batch, slot, hid),
        "mixed": low(batch * slot, hid),
        "du": low(batch * slot, hid),
        "sums": full(batch, 8, slot),
        "sums_all": full(batch, n, 8, slot),
        "dh2_all": low(batch, slot, width),
        "dh2_got": low(batch, 2, 2, tok, width // 2),
        "dh2_passed": low(batch, 2, tok, width // 2),
        "dh2_last": low(batch, 2, tok, width // 2),
        "grads": low(2, nf, part, width),
        "pair_got": low(2, nf // 4, 2, part, width),
        "w_sems": DMA((2, n, 5)),
        "x_sems": DMA((2, batch, 4)),
        "y_sems": DMA((2, batch, 4)),
        "a_sems": DMA((2, batch, n)),
        "h_sems": DMA((2, batch, 4)),
        "s_sems": DMA((2, batch, n)),
        "r_sems": DMA((2, batch, 2, 3)),
        "p_sems": DMA((2, hid // 256, 128 // part, 2)),
        "hop_sems": DMA((2, 2, 5, nf // 2)),
        "side_sems": DMA((2, 2, 5, nf // 2)),
        "keep_sems": DMA((batch, 3)),
        "own_sems": DMA((22,)),
    }
    return launch(
        lambda r: forward_kernel(n, nf, part, r), "forward", inputs, outputs, scratch, 0, 63
    )


def backward_kernel(n, nf, r):
    me = lax.axis_index("dp")
    f = lax.axis_index("ffn")
    core, row, nz = lax.rem(f, 2), lax.div(f, 2), nf // 2
    even, two_row = lax.rem(row, 2), lax.div(row, 2)
    batch, tok, width = r.dx.shape
    slot = n * tok
    cols = width // n
    rows_each = r.o_out.shape[0]
    pairs = cols // 128
    heads = cols // HDIM
    share = width // n
    step = 256
    peers = dp_peers(n, me)
    pair = {"ffn": f ^ 1}
    everyone = peers + ffn_peers(nf, f)
    greet(everyone)
    band = at(me * tok, tok)
    place = at(me * cols, cols)
    loads = [
        pltpu.make_async_copy(source, target, r.own_sems.at[k])
        for k, (source, target) in enumerate(
            [(r.x1_hbm, r.x1), (r.dh2_hbm, r.dh2), (r.dy_hbm, r.dy), (r.z_hbm, r.z),
             (r.out_hbm, r.wout), (r.a_hbm, r.a), (r.qkv_hbm, r.qkv_all), (r.p_hbm, r.p_all),
             (r.w_hbm, r.w_qkv), (r.h_hbm, r.h_all), (r.x_hbm, r.x), (r.g_hbm.at[:, :, even], r.g_own),
             (r.mixed_hbm, r.mixed), (r.w2_hbm, r.w2)]
        )
    ]
    start(loads)
    r.vec[...] = jnp.zeros_like(r.vec)

    def to_peers(make):
        return [make(i, peer) for i, peer in enumerate(peers, 1)]

    def along(make):
        return [make(j, {"ffn": f ^ (2 * j)}) for j in range(1, nz)]

    def columns_of(side):
        return slice(side * (width // 2), (side + 1) * (width // 2))

    def y_rows(micro):
        def block(owner, side):
            return r.y_all.at[micro, at(owner * tok, tok), columns_of(side)]

        return Reduce(me, block, r.y_got, r.y_passed, r.y_last, r.y_sems, (micro,))

    def dh_rows(micro):
        def block(owner, side):
            return r.dh_all.at[micro, at(owner * tok, tok), columns_of(side)]

        return Reduce(me, block, r.dh_got, r.dh_passed, r.dh_last, r.h_sems, (micro,))

    def go_block(owner, side):
        return r.go_half.at[owner, :, :, columns_of(side)]

    go = Reduce(me, go_block, r.go_got, r.go_passed, r.go_last, r.e_sems, ())

    def g_first(w):
        return send(
            r.g_hbm.at[w, :, 1 - even], r.g_pair.at[w], r.g_sems, (0, w), {"ffn": f ^ 2}
        )

    def g_second(w):
        return [
            send(r.g_mid.at[w, two_row ^ j], r.g_far.at[j - 1, w], r.g_sems, (j, w), {"ffn": f ^ (4 * j)})
            for j in range(1, nz // 2)
        ]

    def g_turn(w):
        g_first(w).wait()
        for k in range(nz // 2):
            total = r.g_own[w, k].astype(F32) + r.g_pair[w, k].astype(F32)
            r.g_mid[w, k] = total.astype(LOW)
        start(g_second(w))

    pair_v = send(r.mid.at[:, 1 - core], r.mid_pair, r.p_sems, (1,), pair)
    wait(loads[:4])
    meet(everyone)
    for w in range(2):
        g_first(w).start()
    pair_v.start()
    for micro in range(batch):
        normed, inverse = normal(r.x1[micro])
        grad = r.dh2[micro]
        r.vec[2:3, :] += column_sum(grad * normed)
        r.vec[8:9, :] += column_sum(grad)
        valid = lax.broadcasted_iota(jnp.int32, (tok, 1), 0) + me * tok < r.lens[micro]
        dy = jnp.where(valid, r.dy[micro].astype(F32), 0.0)
        r.vec[9:10, :] += column_sum(dy)
        grad = dy + normal_back(grad * r.wide[2:3, :], normed, inverse)
        r.dx1[micro] = grad
        normed, inverse = normal(r.z[micro])
        r.vec[1:2, :] += column_sum(grad * normed)
        r.vec[7:8, :] += column_sum(grad)
        low = normal_back(grad * r.wide[1:2, :], normed, inverse).astype(LOW)
        r.vec[6:7, :] += column_sum(low.astype(F32))
        r.dz[micro * tok : (micro + 1) * tok, :] = low
    wait(loads[4:5])
    for d in range(n):
        grad = dot_nt(r.dz[...], r.wout[d].reshape(cols, width))
        lane = lax.broadcasted_iota(jnp.int32, (1, cols), 1) // HDIM
        scales = jnp.zeros((1, cols), F32)
        for head in range(heads):
            scales = jnp.where(lane == head, r.scale[d * heads + head], scales)
        grad = (grad * scales).astype(LOW)
        for micro in range(batch):
            r.do_own[micro, d] = grad[micro * tok : (micro + 1) * tok]

    def head_copies(micro):
        return to_peers(
            lambda i, peer: send(
                r.do_own.at[micro, me ^ i], r.do_all.at[micro, band, :], r.o_sems, (micro, i), peer
            )
        )

    pair_o = send(r.go_all.at[:, 1 - core], r.go_pair, r.p_sems, (0,), pair)
    pair_vec = send(r.vec_sum, r.vec_pair, r.p_sems, (2,), pair)

    def pair_q(d):
        return send(r.gq_all.at[d, 1 - core], r.gq_pair.at[d], r.q_sems, (d,), pair)

    shares = to_peers(
        lambda i, peer: send(r.vec_part.at[me ^ i], r.vec_got.at[i - 1], r.d_sems, (i, 6), peer)
    )
    far_o = along(
        lambda j, peer: send(r.go_sum.at[row ^ j], r.o_far.at[j - 1], r.z_sems, (j, 1), peer)
    )
    def far_q(d):
        return along(
            lambda j, peer: send(
                r.gq_sum.at[d, row ^ j], r.q_far.at[j - 1, d], r.f_sems, (j, d), peer
            )
        )

    def add_pair(d):
        pair_q(d).wait()
        total = r.gq_all[d, core].astype(F32) + r.gq_pair[d].astype(F32)
        r.gq_sum[d] = total.astype(LOW)
        start(far_q(d))

    far_v = along(
        lambda j, peer: send(r.mid_sum.at[row ^ j], r.v_far.at[j - 1], r.z_sems, (j, 3), peer)
    )
    far_vec = along(lambda j, peer: send(r.vec_mine, r.vec_far.at[j - 1], r.z_sems, (j, 4), peer))
    for micro in range(batch):
        start(head_copies(micro))
        r.do_all[micro, band, :] = r.do_own[micro, me]
    wait(loads[12:])

    def out_rows(c, _):
        columns = at(c * step, step)
        weight = r.w2[:, :, columns].reshape(r.mixed.shape[1], step)
        for micro in range(batch):
            value = dot(r.mixed[micro * slot : (micro + 1) * slot, :], weight)
            r.y_all[micro, :, columns] = value.astype(LOW)
        return 0

    lax.fori_loop(0, width // step, out_rows, 0)
    y_rows(0).begin()
    wait(loads[5:6])

    def out_weight(d, _):
        a = r.a[:, :, at(d * cols, cols)].reshape(batch * tok, cols)
        grad = dot_tn(a, r.dz[...]).astype(LOW)
        for k in range(nf):
            r.go_all[d, k % 2, k // 2] = grad[k * rows_each : (k + 1) * rows_each]
        return 0

    lax.fori_loop(0, n, out_weight, 0)
    pair_o.start()
    wait(loads[6:12])
    left = lax.broadcasted_iota(jnp.int32, (1, 128), 1) < HDIM

    def one(micro, _):
        wait(head_copies(micro))

        def pair_of(two, _):
            def column(k):
                return at(k * cols + two * 128, 128)

            head = two * 2
            own_cols = at(two * 128, 128)
            sums = []
            k = r.qkv_all[micro, :, column(1)]
            v = r.qkv_all[micro, :, column(2)]
            for block in range(n):
                end = (block + 1) * tok
                rows = slice(block * tok, end)
                do = r.do_all[micro, rows, own_cols]
                out = []
                for side in range(2):
                    mine = left if side == 0 else jnp.logical_not(left)
                    probs = r.p_all[micro, head + side, rows, :end].astype(F32)
                    dp = dot_nt(jnp.where(mine, do, jnp.zeros_like(do)), v[:end])
                    delta = jnp.sum(probs * dp, axis=-1, keepdims=True)
                    ds = (probs * (dp - delta)).astype(LOW)
                    r.ds_all[side, rows, :end] = ds
                    out.append(dot(ds, k[:end]))
                    sums.append(jnp.sum(delta, axis=0, keepdims=True))
                dq = jnp.where(left, out[0], out[1]) * HDIM ** (-0.5)
                r.dqkv[micro, rows, column(0)] = dq.astype(LOW)
            q = r.qkv_all[micro, :, column(0)]
            do = r.do_all[micro, :, own_cols]
            for block in range(n):
                begin = block * tok
                keys = slice(begin, begin + tok)
                dk = [dot_tn(r.ds_all[side, begin:, keys], q[begin:]) for side in range(2)]
                dv = [
                    dot_tn(r.p_all[micro, head + side, begin:, keys], do[begin:])
                    for side in range(2)
                ]
                dk = jnp.where(left, dk[0], dk[1]) * HDIM ** (-0.5)
                r.dqkv[micro, keys, column(1)] = dk.astype(LOW)
                r.dqkv[micro, keys, column(2)] = jnp.where(left, dv[0], dv[1]).astype(LOW)
            spot = me * heads + head
            first = sum(sums[2::2], sums[0]) * (1.0 / r.scale[spot])
            second = sum(sums[3::2], sums[1]) * (1.0 / r.scale[spot + 1])
            r.vec[10:11, at(me * cols + two * 128, 128)] += jnp.where(left, first, second)

            @pl.when((micro == 0) & (two == 0))
            def _():
                g_turn(0)

            return 0

        lax.fori_loop(0, pairs, pair_of, 0)

        @pl.when(micro == 0)
        def _():
            pair_o.wait()
            for d in range(n):
                total = r.go_all[d, core].astype(F32) + r.go_pair[d].astype(F32)
                r.go_half[d] = total.astype(LOW)
            y_rows(0).turn()
            go.begin()

        @pl.when(micro == 1)
        def _():
            g_turn(1)
            go.turn()
            dh_rows(0).turn()

        def back_rows(d, _):
            total = dot_nt(r.dqkv[micro, :, :cols], r.w_qkv[0, d].reshape(cols, cols))
            for k in (1, 2):
                total = total + dot_nt(
                    r.dqkv[micro, :, k * cols : (k + 1) * cols],
                    r.w_qkv[k, d].reshape(cols, cols),
                )
            r.dh_all[micro, :, at(d * cols, cols)] = total.astype(LOW)
            return 0

        lax.fori_loop(0, n, back_rows, 0)
        dh_rows(micro).begin()
        grads = r.dqkv[micro].astype(F32)
        r.vec[4:5, place] += column_sum(grads[:, :cols])
        r.vec[5:6, place] += column_sum(grads[:, 2 * cols :])
        return 0

    lax.fori_loop(0, batch, one, 0)
    for micro in range(1, batch):
        y_rows(micro).begin()

    def weight_grads(d, _):
        h = r.h_all[:, :, at(d * cols, cols)].reshape(batch * slot, cols)
        grad = dot_tn(h, r.dqkv[...].reshape(batch * slot, 3 * cols)).astype(LOW)
        for k in range(nf):
            r.gq_all[d, k % 2, k // 2] = grad[k * rows_each : (k + 1) * rows_each]
        pair_q(d).start()

        @pl.when(d > 0)
        def _():
            add_pair(d - 1)

        return 0

    lax.fori_loop(0, n, weight_grads, 0)
    add_pair(n - 1)
    r.go_sum[...] = go.finish().astype(LOW)
    start(far_o)
    pair_v.wait()
    for k in range(nz):
        r.mid_sum[k] = r.mid[k, core] + r.mid_pair[k]
    start(far_v)

    for micro in range(1, batch):
        dh_rows(micro).turn()
    for micro in range(batch):
        grad = dh_rows(micro).finish()
        normed, inverse = normal(r.x[micro].astype(F32))
        r.vec[0:1, :] += column_sum(grad * normed)
        r.vec[3:4, :] += column_sum(grad)
        r.dx[micro] = r.dx1[micro] + normal_back(grad * r.wide[0:1, :], normed, inverse)
    spot = lax.broadcasted_iota(jnp.int32, (16, 1), 0)
    own_scales = r.vec[10:11, place]
    for d in range(n):
        block = jnp.where(spot >= 10, 0.0, r.vec[:, d * share : (d + 1) * share])
        r.vec_part[d] = jnp.where(spot == 10 + me, own_scales, block)
    start(shares)
    for micro in range(1, batch):
        y_rows(micro).turn()
    for micro in range(batch):
        total = r.x1[micro] + y_rows(micro).finish() + r.wide[9:10, :]
        r.out[micro] = total.astype(LOW)
    wait(shares)
    total = r.vec_part[me]
    for i in range(1, n):
        total = total + r.vec_got[i - 1]
    r.vec_mine[...] = total
    start(far_vec)
    halves = []
    for w in range(2):
        wait(g_second(w))
        total = r.g_mid[w, two_row].astype(F32)
        for j in range(1, nz // 2):
            total = total + r.g_far[j - 1, w].astype(F32)
        r.g_sum[w] = total.astype(LOW)
        for i, peer in enumerate(peers, 1):
            source = r.g_sum.at[w, :, at((me ^ i) * cols, cols)]
            halves.append(send(source, r.ffn_out.at[w, me], r.d_sems, (i, 4 + w), peer))
    own = [
        pltpu.make_async_copy(r.g_sum.at[w, :, place], r.ffn_out.at[w, me], r.own_sems.at[14 + w])
        for w in range(2)
    ]
    start(halves + own)
    wait(far_o)
    total = r.go_sum[row].astype(F32)
    for j in range(1, nz):
        total = total + r.o_far[j - 1].astype(F32)
    r.o_out[...] = total
    wait(far_v)
    total = r.mid_sum[row]
    for j in range(1, nz):
        total = total + r.v_far[j - 1]
    r.v_out[me] = total
    last = to_peers(
        lambda i, peer: send(r.v_out.at[me], r.v_out.at[me], r.d_sems, (i, 3), peer)
    )
    start(last)
    wait(far_vec)
    total = r.vec_mine[...]
    for j in range(1, nz):
        total = total + r.vec_far[j - 1]
    r.vec_out[...] = total
    r.vec_sum[...] = total
    pair_vec.start()
    for d in range(n):
        wait(far_q(d))
    for d in range(n):
        total = r.gq_sum[d, row].astype(F32)
        for j in range(1, nz):
            total = total + r.q_far[j - 1, d].astype(F32)
        r.q_last[d] = total.astype(LOW)
    more = []
    for i, peer in enumerate(peers, 1):
        for k in range(3):
            source = r.q_last.at[me ^ i, :, k * cols : (k + 1) * cols]
            more.append(send(source, r.q_out.at[k, :, place], r.d_sems, (i, k), peer))
    own += [
        pltpu.make_async_copy(
            r.q_last.at[me, :, k * cols : (k + 1) * cols],
            r.q_out.at[k, :, place],
            r.own_sems.at[16 + k],
        )
        for k in range(3)
    ]
    start(more + own[2:])
    wait(last + more + own + halves + [pair_vec])
    r.vec_out[...] += r.vec_pair[...]


def backward(x, dy, kept, lens, scale, n, nf):
    batch, tok, width = x.shape
    _, _, _, rows, cols = kept["w_hbm"].shape
    part = kept["mid"].shape[3]
    slot, nz = n * tok, nf // 2
    share = width // n
    heads = cols // HDIM

    def low(*dims):
        return pltpu.VMEM(dims, LOW)

    def full(*dims):
        return pltpu.VMEM(dims, F32)

    names = ("x1_hbm", "z_hbm", "dh2_hbm", "a_hbm", "g_hbm", "out_hbm", "w_hbm", "h_hbm")
    names += ("qkv_hbm", "p_hbm", "mixed_hbm", "w2_hbm")
    inputs = {name: (kept[name], ANY) for name in names}
    inputs["x_hbm"] = (x, ANY)
    inputs["dy_hbm"] = (dy, ANY)
    inputs["wide"] = (kept["wide"], VMEM)
    inputs["mid"] = (kept["mid"], VMEM)
    inputs["lens"] = (lens, SMEM)
    inputs["scale"] = (scale, SMEM)
    outputs = {
        "out": (shape((batch, tok, width), LOW), VMEM),
        "dx": (shape((batch, tok, width), F32), VMEM),
        "q_out": (shape((3, rows, width), LOW), VMEM),
        "o_out": (shape((rows, width), F32), VMEM),
        "v_out": (shape((n, 8, part), F32), VMEM),
        "vec_out": (shape((16, share), F32), VMEM),
        "ffn_out": (shape((2, n, part, cols), LOW), VMEM),
    }
    scratch = {
        "x": low(batch, tok, width),
        "dy": low(batch, tok, width),
        "x1": full(batch, tok, width),
        "z": full(batch, tok, width),
        "dh2": full(batch, tok, width),
        "a": low(batch, tok, width),
        "wout": low(n, nf, rows, width),
        "w_qkv": low(3, n, nf, rows, cols),
        "h_all": low(batch, slot, width),
        "qkv_all": low(batch, slot, 3 * cols),
        "p_all": low(batch, heads, slot, slot),
        "mixed": low(*kept["mixed_hbm"].shape),
        "w2": low(*kept["w2_hbm"].shape),
        "y_all": low(batch, slot, width),
        "y_got": low(batch, 2, 2, tok, width // 2),
        "y_passed": low(batch, 2, tok, width // 2),
        "y_last": low(batch, 2, tok, width // 2),
        "dx1": full(batch, tok, width),
        "dz": low(batch * tok, width),
        "do_own": low(batch, n, tok, cols),
        "do_all": low(batch, slot, cols),
        "ds_all": low(2, slot, slot),
        "dqkv": low(batch, slot, 3 * cols),
        "dh_all": low(batch, slot, width),
        "dh_got": low(batch, 2, 2, tok, width // 2),
        "dh_passed": low(batch, 2, tok, width // 2),
        "dh_last": low(batch, 2, tok, width // 2),
        "go_all": low(n, 2, nz, rows, width),
        "go_pair": low(n, nz, rows, width),
        "go_half": low(n, nz, rows, width),
        "go_got": low(2, 2, nz, rows, width // 2),
        "go_passed": low(2, nz, rows, width // 2),
        "go_last": low(2, nz, rows, width // 2),
        "go_sum": low(nz, rows, width),
        "o_far": low(nz - 1, rows, width),
        "gq_all": low(n, 2, nz, rows, 3 * cols),
        "gq_pair": low(n, nz, rows, 3 * cols),
        "gq_sum": low(n, nz, rows, 3 * cols),
        "q_far": low(nz - 1, n, rows, 3 * cols),
        "q_last": low(n, rows, 3 * cols),
        "g_own": low(2, nz // 2, part, width),
        "g_pair": low(2, nz // 2, part, width),
        "g_mid": low(2, nz // 2, part, width),
        "g_far": low(nz // 2 - 1, 2, part, width),
        "g_sum": low(2, part, width),
        "mid_pair": full(nz, 8, part),
        "mid_sum": full(nz, 8, part),
        "v_far": full(nz - 1, 8, part),
        "vec": full(16, width),
        "vec_part": full(n, 16, share),
        "vec_got": full(n - 1, 16, share),
        "vec_mine": full(16, share),
        "vec_far": full(nz - 1, 16, share),
        "vec_sum": full(16, share),
        "vec_pair": full(16, share),
        "o_sems": DMA((2, batch, n)),
        "h_sems": DMA((2, batch, 2, 3)),
        "y_sems": DMA((2, batch, 2, 3)),
        "p_sems": DMA((2, 3)),
        "q_sems": DMA((2, n)),
        "e_sems": DMA((2, 2, 3)),
        "g_sems": DMA((2, nz // 2, 2)),
        "z_sems": DMA((2, nz, 5)),
        "f_sems": DMA((2, nz, n)),
        "d_sems": DMA((2, n, 7)),
        "own_sems": DMA((19,)),
    }
    return launch(
        lambda r: backward_kernel(n, nf, r), "backward", inputs, outputs, scratch, 1, 60
    )


def finish_kernel(n, nf, r):
    f = lax.axis_index("ffn")
    rows_each = r.gains.shape[1]
    part = r.mid.shape[2]
    cols, hid = r.w_in.shape
    r.out_to[...] = r.out[...]
    r.dx_to[...] = r.dx[...]
    r.q_to[...] = r.q_out[...].astype(F32)
    r.o_to[...] = r.o_out[...]
    r.w_in[...] = r.ffn[0].reshape(hid, cols).astype(F32).T
    r.w_out[...] = r.ffn[1].reshape(hid, cols).astype(F32)
    own = jnp.zeros((16, rows_each), F32)
    for k in range(nf):
        own = own + jnp.where(f == k, r.vec[:, k * rows_each : (k + 1) * rows_each], 0.0)
    r.gains[...] = own[:3]
    r.biases[...] = own[3:10]
    heads = r.heads.shape[1]
    lane = lax.broadcasted_iota(jnp.int32, (1, heads), 1)
    total = jnp.zeros((1, heads), F32)
    for head in range(heads):
        d, c = divmod(head, heads // n)
        value = r.vec[10 + d : 11 + d, c * HDIM : c * HDIM + 1]
        total = total + jnp.where(lane == head, value, 0.0)
    r.heads[...] = total
    for k, target in enumerate((r.mid_0, r.mid_1, r.mid_2)):
        for d in range(n):
            target[:, d * part : (d + 1) * part] = r.mid[d, k : k + 1]


def finish(done, heads, n, nf):
    out, dx, q_out, o_out = [done[name] for name in ("out", "dx", "q_out", "o_out")]
    vec, mid, ffn = done["vec_out"], done["v_out"], done["ffn_out"]
    _, _, part, cols = ffn.shape
    rows = o_out.shape[0]
    hid = n * part
    inputs = dict(out=out, dx=dx, q_out=q_out, o_out=o_out, vec=vec, mid=mid, ffn=ffn)
    outputs = dict(
        out_to=shape(out.shape, LOW),
        dx_to=shape(dx.shape, F32),
        q_to=shape(q_out.shape, F32),
        o_to=shape(o_out.shape, F32),
        heads=shape((1, heads), F32),
        gains=shape((3, rows), F32),
        biases=shape((7, rows), F32),
        w_in=shape((cols, hid), F32),
        mid_0=shape((1, hid), F32),
        mid_1=shape((1, hid), F32),
        mid_2=shape((1, hid), F32),
        w_out=shape((hid, cols), F32),
    )
    names = [*inputs, *outputs]
    return pl.pallas_call(
        lambda *refs: finish_kernel(n, nf, SimpleNamespace(**dict(zip(names, refs)))),
        name="finish",
        out_shape=tuple(outputs.values()),
        in_specs=[VMEM] * len(inputs),
        out_specs=(VMEM,) * len(outputs),
        compiler_params=pltpu.CompilerParams(vmem_limit_bytes=62 << 20),
    )(*inputs.values())


def on_device(
    tokens,
    seq_lens,
    qkv_weight,
    out_weight,
    head_scale,
    gains,
    biases,
    ffn_in,
    ffn_bias,
    mid_gain,
    mid_bias,
    ffn_out,
    out_cotangent,
):
    n = lax.axis_size("dp")
    nf = lax.axis_size("ffn")
    me = lax.axis_index("dp")
    batch, _, tok, width = tokens.shape
    heads = head_scale.shape[0]
    cols = width // n
    rows = qkv_weight.shape[1]
    hid = ffn_in.shape[1]
    part = hid // n

    vectors = lax.dynamic_index_in_dim(
        jnp.stack([ffn_bias, mid_gain, mid_bias]).reshape(3, n, part), me, 1, keepdims=False
    )
    x, dy = tokens[:, 0], out_cotangent[:, 0]
    lens = seq_lens.reshape(-1)
    kept = forward(
        x,
        qkv_weight,
        out_weight,
        (gains, biases, vectors),
        ffn_in,
        ffn_out.reshape(n, part, cols),
        dy,
        lens,
        head_scale,
        n,
        nf,
    )
    done = backward(x, dy, kept, lens, head_scale, n, nf)
    out, dx, q_grad, o_grad, head_grad, gain_grad, bias_grad, in_grad, *mids, last_grad = finish(
        done, heads, n, nf
    )
    return (
        out[:, None],
        dx[:, None],
        q_grad,
        o_grad,
        head_grad.reshape(heads),
        gain_grad,
        bias_grad,
        in_grad,
        *[mid.reshape(hid) for mid in mids],
        last_grad,
    )


def solution(mesh):
    seqs = P(None, "ffn", "dp", None)
    wide = P(None, ("dp", "ffn"))
    hidden = P("ffn")
    return jax.shard_map(
        on_device,
        mesh=mesh,
        in_specs=(
            seqs,
            P(None, "ffn"),
            P(None, ("dp", "ffn"), None),
            P(("dp", "ffn"), None),
            P(),
            wide,
            wide,
            P("dp", "ffn"),
            hidden,
            hidden,
            hidden,
            P("ffn", "dp"),
            seqs,
        ),
        out_specs=(
            seqs,
            seqs,
            P(None, ("dp", "ffn"), None),
            P(("dp", "ffn"), None),
            P(),
            wide,
            wide,
            P("dp", "ffn"),
            hidden,
            hidden,
            hidden,
            P("ffn", "dp"),
        ),
        check_vma=False,
    )
```
